32 devices in a mesh: dp: 4 (over z), lat: 4 (over y, core), lon: 2 (over x).
Axes of the slice: x: 2, y: 2, z: 4, core: 2. Of those that a mesh axis runs over, the one named last changes fastest.
Arguments:
- projected: bfloat16 [4, 4, 32, 16, 4608], P('dp', None, 'lat', 'lon'), may hold values from -52 to 52
- targets: bfloat16 [4, 4, 32, 16, 160], P('dp', None, 'lat', 'lon'), may hold values from -6 to 6
- valid_cells: int32 [32, 16], P('lat', 'lon'), may hold values 0 or 1
- w_out: bfloat16 [1536, 1536], P('dp'), may hold values from -0.15625 to 0.15625
- unpatch_matrix: bfloat16 [1536, 160], P('dp'), may hold values from -0.15625 to 0.15625
- norm_gain: bfloat16 [1536], P('dp'), may hold values from 0.099609375 to 1.8984375
- var_weight: float32 [5], replicated, may hold values from 0.3 to 3
Outputs:
- grad_context: bfloat16 [4, 4, 32, 16, 1536], P('dp', None, 'lat', 'lon')
- grad_recovery: float32 [1536, 160], P('dp')
- sample_penalty: float32 [4], P('dp')
The draws below stay inside these ranges and needn't reach their ends.
All inputs are finite; a program needn't handle non-finite values. No bound on the sum of `valid_cells` on one device may be relied on, other than what follows from the above.
Results may differ from the reference program's by a relative error of at most 0.011.
Values may be sent and summed in bfloat16 or wider, within the bound.
No kernel may reach another device: no remote copies, remote signals or barrier semaphores. Data moves between devices by JAX's collectives and lax.ppermute only.
A program may use at most 64 MiB of HBM per device.

```python
import math
import jax
import jax.numpy as jnp
from jax import lax

D = 1536
HEADS = 48
HDIM = 32
VARS = 5
CELLS_PER_PIECE = 32
TILE = 8
WLEV = 2
VERTICAL_LAYERS = 4
B = 4
GRID_PARALLELS = 32
GRID_MERIDIANS = 16
PREDICTED_ITEMS = 160


def draw_projected(key, part):
    drawn = jax.random.truncated_normal(key, -6.0, 6.0, (B, VERTICAL_LAYERS, GRID_PARALLELS, GRID_MERIDIANS, 3 * D), jnp.float32)
    return drawn.astype(jnp.bfloat16)


def set_ends(entries, stream_key, least, high):
    spot = [jax.random.randint(jax.random.fold_in(stream_key, axis), (), 0, length) for axis, length in enumerate(entries.shape)]
    widest = entries.shape.index(max(entries.shape))
    neighbour = spot[:widest] + [(spot[widest] + 1) % entries.shape[widest]] + spot[widest + 1:]
    return entries.at[tuple(spot)].set(least).at[tuple(neighbour)].set(high)


def level_of(rng, dims, pieces, smallest, largest):
    gain = 1.0
    for dim, shards_of in pieces:
        steps = jax.random.uniform(jax.random.fold_in(jax.random.fold_in(rng, 6), dim), (shards_of,), jnp.float32, smallest / len(pieces), largest / len(pieces))
        gain = gain * jnp.repeat(jnp.exp(steps), dims[dim] // shards_of).reshape((-1,) + (1,) * (len(dims) - 1 - dim))
    return gain


def scatter_about(own_key, dims, scale, bound, shards=(), held_as=jnp.bfloat16):
    result = scale * jax.random.normal(own_key, dims, jnp.float32)
    if shards:
        result = result * level_of(own_key, dims, shards, -0.22, 0.18)
    return jnp.clip(result, -bound, bound).astype(held_as)


def setup_inputs(seed: int = 0) -> dict:
    keys = jax.random.split(jax.random.key(seed), 8)
    projected = draw_projected(jax.random.fold_in(keys[7], 71), 0)
    targets = scatter_about(keys[1], (B, VERTICAL_LAYERS, GRID_PARALLELS, GRID_MERIDIANS, PREDICTED_ITEMS), 1.0, 6.0, ((0, 4), (2, 4), (3, 2)))
    valid_cells = set_ends((jax.random.randint(keys[2], (GRID_PARALLELS, GRID_MERIDIANS), 0, 8) < 7).astype(jnp.int32), jax.random.fold_in(keys[2], 1), 0, 1)
    w_out = scatter_about(keys[3], (D, D), D ** -0.5, 0.15625, ((0, 4),))
    unpatch_matrix = scatter_about(keys[4], (D, PREDICTED_ITEMS), D ** -0.5, 0.15625, ((0, 4),))
    norm_gain = jnp.clip(1.0 + 0.18 * jax.random.normal(keys[5], (D,), jnp.float32), 0.099609375, 1.8984375).astype(jnp.bfloat16)
    var_weight = jnp.clip(jnp.exp(jax.random.uniform(keys[6], (VARS,), jnp.float32, math.log(0.3), math.log(3.0))), 0.3, 3.0)
    return dict(projected=projected, targets=targets, valid_cells=valid_cells, w_out=w_out, unpatch_matrix=unpatch_matrix, norm_gain=norm_gain, var_weight=var_weight)


def to_windows(grid):
    chans = grid.shape[-1]
    split = grid.reshape(VERTICAL_LAYERS // WLEV, WLEV, GRID_PARALLELS // TILE, TILE, GRID_MERIDIANS // TILE, TILE, chans)
    return split.transpose(0, 2, 4, 1, 3, 5, 6).reshape(-1, WLEV * TILE * TILE, chans)

def from_windows(windows):
    chans = windows.shape[-1]
    split = windows.reshape(VERTICAL_LAYERS // WLEV, GRID_PARALLELS // TILE, GRID_MERIDIANS // TILE, WLEV, TILE, TILE, chans)
    return split.transpose(0, 3, 1, 4, 2, 5, 6).reshape(VERTICAL_LAYERS, GRID_PARALLELS, GRID_MERIDIANS, chans)

def attend(windows, region):
    win_count = windows.shape[0]
    tokw = windows.shape[1]
    queries = windows[..., :D].reshape(win_count, tokw, HEADS, HDIM).astype(jnp.float32)
    key_heads = windows[..., D:2 * D].reshape(win_count, tokw, HEADS, HDIM).astype(jnp.float32)
    value_heads = windows[..., 2 * D:].reshape(win_count, tokw, HEADS, HDIM).astype(jnp.float32)
    scores = jnp.einsum('wqhd,wkhd->whqk', queries, key_heads) * (1.0 / math.sqrt(HDIM))
    allowed = region[:, None, :, None] == region[:, None, None, :]
    scores = jnp.where(allowed, scores, -1e+30)
    row_peak = lax.optimization_barrier(jnp.max(scores, axis=-1, keepdims=True))
    lifted = jnp.exp(scores - row_peak)
    attn = (lifted / lax.optimization_barrier(jnp.sum(lifted, axis=-1, keepdims=True))).astype(jnp.bfloat16)
    context = jnp.einsum('whqk,wkhd->wqhd', attn.astype(jnp.float32), value_heads)
    return context.astype(jnp.bfloat16).reshape(win_count, tokw, D)

def one_sample(projected, targets, valid_cells, w_out, unpatch_matrix, norm_gain, var_weight):
    half_side = TILE // 2
    rolled = jnp.roll(projected, (-half_side, -half_side), axis=(1, 2))
    reference_field = jnp.roll(targets, (-half_side, -half_side), axis=(1, 2))
    valid = jnp.roll(valid_cells, (-half_side, -half_side), axis=(0, 1)).astype(jnp.float32)
    row_index = jnp.arange(GRID_PARALLELS)
    latitude = math.pi * ((row_index.astype(jnp.float32) + 0.5) / GRID_PARALLELS - 0.5)
    cosine = jnp.cos(latitude)
    lat_weight = jnp.roll(cosine / jnp.mean(cosine), -half_side)
    region_rows = (row_index >= GRID_PARALLELS - half_side).astype(jnp.int32)
    region = jnp.broadcast_to(region_rows[None, :, None, None], (VERTICAL_LAYERS, GRID_PARALLELS, GRID_MERIDIANS, 1))
    context = from_windows(attend(to_windows(rolled), to_windows(region)[..., 0])).reshape(-1, D)
    mixed_rows = jnp.dot(context, w_out, preferred_element_type=jnp.float32)
    centre = lax.optimization_barrier(jnp.mean(mixed_rows, axis=-1, keepdims=True))
    spread = lax.optimization_barrier(jnp.mean((mixed_rows - centre) ** 2, axis=-1, keepdims=True))
    inv_spread = lax.rsqrt(spread + 1e-05)
    normed = (mixed_rows - centre) * inv_spread
    gain_f = norm_gain.astype(jnp.float32)
    latent_activation = (normed * gain_f).astype(jnp.bfloat16)
    prediction_field = jnp.dot(latent_activation, unpatch_matrix, preferred_element_type=jnp.float32)
    prediction_misfit = prediction_field - reference_field.reshape(-1, PREDICTED_ITEMS).astype(jnp.float32)
    element_factor = jnp.broadcast_to(lat_weight[None, :, None] * valid[None], (VERTICAL_LAYERS, GRID_PARALLELS, GRID_MERIDIANS)).reshape(-1, 1)
    variable_factor = jnp.repeat(var_weight, CELLS_PER_PIECE)[None, :]
    sample_penalty = jnp.sum(element_factor * variable_factor * prediction_misfit * prediction_misfit) / (VERTICAL_LAYERS * GRID_PARALLELS * GRID_MERIDIANS * CELLS_PER_PIECE)
    prediction_gradient = (2.0 * element_factor * variable_factor * prediction_misfit).astype(jnp.bfloat16)
    term_rows = jnp.dot(latent_activation.T, prediction_gradient, preferred_element_type=jnp.float32)
    grad_hidden = jnp.dot(prediction_gradient, unpatch_matrix.T, preferred_element_type=jnp.float32)
    scaled_grad = grad_hidden * gain_f
    grad_mixed = inv_spread * (scaled_grad - lax.optimization_barrier(jnp.mean(scaled_grad, axis=-1, keepdims=True)) - normed * lax.optimization_barrier(jnp.mean(scaled_grad * normed, axis=-1, keepdims=True)))
    grad_mixed = grad_mixed.astype(jnp.bfloat16)
    grad_context = jnp.dot(grad_mixed, w_out.T, preferred_element_type=jnp.float32).astype(jnp.bfloat16)
    return (grad_context.reshape(VERTICAL_LAYERS, GRID_PARALLELS, GRID_MERIDIANS, D), term_rows, sample_penalty)

def reference(projected, targets, valid_cells, w_out, unpatch_matrix, norm_gain, var_weight):

    def per_sample(pair):
        return one_sample(pair[0], pair[1], valid_cells, w_out, unpatch_matrix, norm_gain, var_weight)
    grad_context, term_rows, sample_penalty = lax.map(per_sample, (projected, targets))
    grad_recovery = lax.optimization_barrier(jnp.sum(term_rows, axis=0)) / (VERTICAL_LAYERS * GRID_PARALLELS * GRID_MERIDIANS)
    return (grad_context, grad_recovery, sample_penalty)
```

```python
import math

import jax
import jax.numpy as jnp
import numpy as np
from jax import lax
from jax.experimental import pallas as pl
from jax.experimental.pallas import tpu as pltpu
from jax.sharding import PartitionSpec as P

HEADS = 48
HDIM = 32
WLEV = 2
BF = jnp.bfloat16
F32 = jnp.float32
EXTRA = 256
UGROWS = 256
VMEM = pl.BlockSpec(memory_space=pltpu.VMEM)
SMEM = pl.BlockSpec(memory_space=pltpu.SMEM)
ANY = pl.BlockSpec(memory_space=pl.ANY)


def from_behind(array, axis, by):
    length = lax.axis_size(axis)
    return lax.ppermute(array, axis, [(i, (i + by) % length) for i in range(length)])


def general_shards(projected, targets, valid_cells, w_out, unpatch_matrix, norm_gain, var_weight):
    tile_side = projected.shape[2]
    half_side = tile_side // 2
    levels = projected.shape[1]
    model_width = w_out.shape[1]
    predicted_span = unpatch_matrix.shape[1]
    lat_total = tile_side * lax.axis_size("lat")
    lon_total = tile_side * lax.axis_size("lon")
    lat_place = lax.axis_index("lat")
    moved = from_behind(
        (projected[:, :, :, :half_side], targets[:, :, :, :half_side], valid_cells[:, :half_side]),
        "lon",
        -1,
    )
    strip_proj = jnp.concatenate([projected[:, :, :, half_side:], moved[0]], axis=3)
    strip_goal = jnp.concatenate([targets[:, :, :, half_side:], moved[1]], axis=3)
    strip_valid = jnp.concatenate([valid_cells[:, half_side:], moved[2]], axis=1)
    moved_rows = from_behind(
        (strip_proj[:, :, :half_side], strip_goal[:, :, :half_side], strip_valid[:half_side]),
        "lat",
        -1,
    )
    local_proj = jnp.concatenate([strip_proj[:, :, half_side:], moved_rows[0]], axis=2)
    shard_reference = jnp.concatenate([strip_goal[:, :, half_side:], moved_rows[1]], axis=2)
    local_valid = jnp.concatenate([strip_valid[half_side:], moved_rows[2]], axis=0).astype(F32)
    win_count = levels // WLEV
    tokw = WLEV * tile_side * tile_side
    windows = local_proj.reshape(win_count, tokw, 3 * model_width)
    rows_here = lat_place * tile_side + jnp.arange(tile_side)
    region_rows = (rows_here >= lat_total - half_side).astype(jnp.int32)
    region = jnp.broadcast_to(region_rows[None, :, None], (WLEV, tile_side, tile_side)).reshape(-1)
    allowed = region[:, None] == region[None, :]
    queries = windows[..., :model_width].reshape(win_count, tokw, HEADS, -1)
    key_heads = windows[..., model_width : 2 * model_width].reshape(win_count, tokw, HEADS, -1)
    value_heads = windows[..., 2 * model_width :].reshape(win_count, tokw, HEADS, -1)
    scores = jnp.einsum("wqhd,wkhd->whqk", queries, key_heads, preferred_element_type=F32)
    scores = scores * (1.0 / math.sqrt(HDIM))
    scores = jnp.where(allowed[None, None], scores, -1e30)
    row_peak = jnp.max(scores, axis=-1, keepdims=True)
    lifted = jnp.exp(scores - row_peak)
    attn = (lifted / jnp.sum(lifted, axis=-1, keepdims=True)).astype(BF)
    context = jnp.einsum("whqk,wkhd->wqhd", attn, value_heads, preferred_element_type=F32)
    context = context.astype(BF).reshape(win_count * tokw, model_width)
    element_total = win_count * tokw
    out_all, unprojected_pieces, gain_all = (
        lax.all_gather(w_out, "dp", axis=0, tiled=True),
        lax.all_gather(unpatch_matrix, "dp", axis=0, tiled=True),
        lax.all_gather(norm_gain, "dp", axis=0, tiled=True),
    )
    mixed_rows = jnp.dot(context, out_all, preferred_element_type=F32)
    centre = jnp.mean(mixed_rows, axis=-1, keepdims=True)
    spread = jnp.mean((mixed_rows - centre) ** 2, axis=-1, keepdims=True)
    inv_spread = lax.rsqrt(spread + 1e-05)
    normed = (mixed_rows - centre) * inv_spread
    gain_f = gain_all.astype(F32)
    latent_activation = (normed * gain_f).astype(BF)
    prediction_field = jnp.dot(latent_activation, unprojected_pieces, preferred_element_type=F32)
    prediction_misfit = prediction_field - shard_reference.reshape(
        element_total, predicted_span
    ).astype(F32)
    all_rows = jnp.arange(lat_total).astype(F32)
    cosine_mean = jnp.mean(jnp.cos(math.pi * ((all_rows + 0.5) / lat_total - 0.5)))
    initial_rows = ((rows_here + half_side) % lat_total).astype(F32)
    lat_here = jnp.cos(math.pi * ((initial_rows + 0.5) / lat_total - 0.5)) / cosine_mean
    element_factor = jnp.broadcast_to(
        lat_here[None, :, None] * local_valid[None], (levels, tile_side, tile_side)
    ).reshape(element_total, 1)
    variable_factor = jnp.repeat(var_weight, predicted_span // var_weight.shape[0])[None, :]
    shard_penalty = jnp.sum(
        element_factor * variable_factor * prediction_misfit * prediction_misfit
    ) / (levels * lat_total * lon_total * (predicted_span // var_weight.shape[0]))
    prediction_gradient = (2.0 * element_factor * variable_factor * prediction_misfit).astype(BF)
    grad_shard = lax.psum_scatter(
        jnp.einsum(
            "td,to->do", latent_activation, prediction_gradient, preferred_element_type=F32
        ).astype(BF),
        "dp",
        scatter_dimension=0,
        tiled=True,
    ).astype(F32)
    grad_sum, loss_sum = lax.psum((grad_shard, shard_penalty), ("lat", "lon"))
    grad_recovery = grad_sum / (levels * lat_total * lon_total)
    grad_hidden = jnp.einsum(
        "to,do->td", prediction_gradient, unprojected_pieces, preferred_element_type=F32
    )
    scaled_grad = grad_hidden * gain_f
    grad_mixed = inv_spread * (
        scaled_grad
        - jnp.mean(scaled_grad, axis=-1, keepdims=True)
        - normed * jnp.mean(scaled_grad * normed, axis=-1, keepdims=True)
    )
    grad_mixed = grad_mixed.astype(BF)
    grad_context = jnp.einsum("tj,ij->ti", grad_mixed, out_all, preferred_element_type=F32)
    grad_context = grad_context.astype(BF).reshape(1, levels, tile_side, tile_side, model_width)
    return (grad_context, grad_recovery, loss_sum.reshape(1))


def params(mib=48):
    return pltpu.CompilerParams(vmem_limit_bytes=mib << 20)


def iota(shape, dim):
    return lax.broadcasted_iota(jnp.int32, shape, dim)


def pack_kernel(x_ref, t_ref, valid_ref, own_ref, east_ref, south_ref, diag_ref):
    count = x_ref.shape[0] * 64
    place = iota((count, count), 0)
    quad, rest = place // (count // 4), place % (count // 4)
    row = (rest // 4) % 4 + jnp.where(quad < 2, 4, 0)
    col = rest % 4 + jnp.where(quad % 2 == 0, 4, 0)
    source = (rest // 16) * 64 + row * 8 + col
    pick = (iota((count, count), 1) == source).astype(F32).astype(BF)
    refs = (own_ref, east_ref, south_ref, diag_ref)
    quarter = count // 4
    width = x_ref.shape[-1]
    step = 512
    for at in range(0, width, step):
        tokens = x_ref[:, :, :, at : at + step].reshape(count, step)
        out = jnp.dot(pick, tokens, preferred_element_type=F32).astype(BF)
        for q, ref in enumerate(refs):
            ref[:, at : at + step] = out[q * quarter : (q + 1) * quarter]
    goal = jnp.dot(pick, t_ref[...].reshape(count, t_ref.shape[-1]), preferred_element_type=F32)
    token = iota((count, 8), 0)
    row_hot = ((token // 8) % 8 == iota((count, 8), 1)).astype(F32)
    by_row = jnp.dot(row_hot, valid_ref[...].astype(F32), preferred_element_type=F32)
    natural = jnp.sum(jnp.where(token % 8 == iota((count, 8), 1), by_row, 0.0), axis=1, keepdims=True)
    spread = jnp.broadcast_to(natural, (count, 128)).astype(BF)
    column = jnp.dot(pick, spread, preferred_element_type=F32)
    span = goal.shape[1]
    extra = jnp.concatenate([goal, column[:, : EXTRA - span]], axis=1).astype(BF)
    for q, ref in enumerate(refs):
        ref[:, width:] = extra[q * quarter : (q + 1) * quarter]


def attention_kernel(last_ref, *refs):
    ctx_ref = refs[12]
    tiles = [refs[3 * q : 3 * q + 3] for q in range(4)]
    is_last = last_ref[0] == 1
    side = iota((128, 512), 0) // 64
    same = side == (iota((128, 512), 1) % 128) // 64
    keep = jnp.logical_or(same, jnp.logical_not(is_last))
    head = iota((128, 128), 1) // HDIM
    factor = math.log2(math.e) / math.sqrt(HDIM)
    for w in range(2):
        q, k, v = [
            jnp.concatenate([tiles[c][i][32 * w : 32 * w + 32] for c in range(4)], axis=0)
            for i in range(3)
        ]
        zero = jnp.zeros_like(k)
        k4 = jnp.concatenate([jnp.where(head == h, k, zero) for h in range(4)], axis=0)
        v4 = jnp.concatenate([jnp.where(head == h, v, zero) for h in range(4)], axis=0)
        s = lax.dot_general(q, k4, (((1,), (1,)), ((), ())), preferred_element_type=F32)
        s = jnp.where(keep, s, -1e30)
        parts = []
        for h in range(4):
            sh = s[:, 128 * h : 128 * h + 128]
            e = jnp.exp2((sh - jnp.max(sh, axis=1, keepdims=True)) * factor)
            parts.append((e / jnp.sum(e, axis=1, keepdims=True)).astype(BF))
        attn = jnp.concatenate(parts, axis=1)
        out = jnp.dot(attn, v4, preferred_element_type=F32)
        ctx_ref[128 * w : 128 * w + 128, :] = out.astype(BF)


def piece_copies(zi, half, own_w, own_ug, rings, swaps, w_all, ug_all, sems):
    rows = own_w.shape[0]
    hr = rows // 2
    steps = len(rings) + 1
    w_copies, u_copies = [], []

    def place(src, dst, to):
        at = sems.at[len(w_copies) + len(u_copies)]
        to.append(pltpu.make_async_copy(src, dst, at))

    base = pl.multiple_of(zi * rows, 128)
    place(own_w, w_all.at[pl.ds(base, rows), :], w_copies)
    place(own_ug, ug_all.at[:, pl.ds(base, rows)], u_copies)
    for k in range(1, steps):
        shard = lax.rem(zi - k + steps, steps)
        base = pl.multiple_of(shard * rows, 128)
        for piece, part in ((rings[k - 1], half), (swaps[k - 1], 1 - half)):
            row = pl.multiple_of(base + part * hr, 64)
            place(piece.at[pl.ds(0, hr), :], w_all.at[pl.ds(row, hr), :], w_copies)
            for j in range(4):
                urow = pl.multiple_of((4 * part + j) * 32, 32)
                place(
                    piece.at[pl.ds(hr, 32), pl.ds(j * rows, rows)],
                    ug_all.at[pl.ds(urow, 32), pl.ds(base, rows)],
                    u_copies,
                )
    return w_copies, u_copies


def split3(x):
    hi = x.astype(BF).astype(F32)
    mid = (x - hi).astype(BF).astype(F32)
    return hi, mid, x - hi - mid


def loss_block(value, rows):
    hi, mid, lo = split3(value)
    lane = iota((rows, 128), 1)
    return jnp.where(lane == 0, hi, jnp.where(lane == 1, mid, jnp.where(lane == 2, lo, 0.0)))


def forward_kernel(
    place_ref, lat_ref, var_ref, ctx_ref, e0, e1, e2, e3, own_w, own_ug, r1, r2, r3, c1, c2, c3,
    t0, t1, t2, t3, normed_ref, inv_ref, dfc_ref, hidden_ref, w_all, ug_all, term, sems,
):
    zi, half, lat_place = place_ref[0], place_ref[1], place_ref[2]
    w_copies, u_copies = piece_copies(
        zi, half, own_w, own_ug, (r1, r2, r3), (c1, c2, c3), w_all, ug_all, sems
    )
    for c in w_copies + u_copies:
        c.start()
    tokens, width = ctx_ref.shape
    span = dfc_ref.shape[1]
    extras = [e0, e1, e2, e3]
    extra = jnp.concatenate(
        [e[32 * w : 32 * w + 32, :] for w in range(2) for e in extras], axis=0
    ).astype(F32)
    goal, valid = extra[:, :span], extra[:, span : span + 1]
    token = iota((tokens, 1), 0)
    row = (token // 4) % 4 + jnp.where((token // 32) % 4 >= 2, 4, 0)
    lat_w = jnp.zeros((tokens, 1), F32)
    for r in range(8):
        lat_w = jnp.where(row == r, lat_ref[lat_place * 8 + r], lat_w)
    lane = iota((1, span), 1) // (span // var_ref.shape[0])
    var_w = jnp.zeros((1, span), F32)
    for n in range(var_ref.shape[0]):
        var_w = jnp.where(lane == n, var_ref[n], var_w)
    weight = lat_w * valid * var_w
    for c in w_copies:
        c.wait()
    mixed = jnp.dot(ctx_ref[...], w_all[...], preferred_element_type=F32)
    centre = jnp.mean(mixed, axis=-1, keepdims=True)
    off = mixed - centre
    inv = lax.rsqrt(jnp.mean(off * off, axis=-1, keepdims=True) + 1e-05)
    normed = off * inv
    normed_ref[...] = normed
    inv_ref[...] = jnp.broadcast_to(inv, inv_ref.shape)
    for c in u_copies:
        c.wait()
    gain = ug_all[pl.ds(span, 16), :][0:1].astype(F32)
    hidden_ref[...] = (normed * gain).astype(BF)
    field = lax.dot_general(
        hidden_ref[...], ug_all[0:span, :], (((1,), (1,)), ((), ())), preferred_element_type=F32
    )
    misfit = field - goal
    dfc = (2.0 * weight * misfit).astype(BF)
    dfc_ref[...] = dfc
    term[...] = lax.dot_general(
        dfc, hidden_ref[...], (((0,), (0,)), ((), ())), preferred_element_type=F32
    )
    loss = jnp.sum(jnp.sum(weight * misfit * misfit, axis=1, keepdims=True), axis=0, keepdims=True)
    rows = t0.shape[0]
    block = loss_block(loss, rows).astype(BF)
    for b, ref in enumerate((t0, t1, t2, t3)):
        at = pl.multiple_of((lat_place ^ b) * rows, 8)
        ref[:, :width] = term[pl.ds(at, rows), :].astype(BF)
        ref[:, width:] = block


def backward_kernel(
    place_ref, normed_ref, inv_ref, dfc_ref, own_w, own_ug, r1, r2, r3, c1, c2, c3,
    out_ref, w_all, ug_all, sems,
):
    zi, half = place_ref[0], place_ref[1]
    w_copies, u_copies = piece_copies(
        zi, half, own_w, own_ug, (r1, r2, r3), (c1, c2, c3), w_all, ug_all, sems
    )
    for c in u_copies + w_copies:
        c.start()
    tokens, width = normed_ref.shape
    span = dfc_ref.shape[1]
    for c in u_copies:
        c.wait()
    gain = ug_all[pl.ds(span, 16), :][0:1].astype(F32)
    g = jnp.dot(dfc_ref[...], ug_all[0:span, :], preferred_element_type=F32) * gain
    normed = normed_ref[...]
    mean_g = jnp.mean(g, axis=-1, keepdims=True)
    mean_gn = jnp.mean(g * normed, axis=-1, keepdims=True)
    dmixed = ((g - mean_g - normed * mean_gn) * inv_ref[:, 0:1]).astype(BF)
    place = iota((tokens, tokens), 0)
    row, col, level = (place // 8) % 8, place % 8, place // 64
    quad = jnp.where(row >= 4, 2, 0) + jnp.where(col >= 4, 1, 0)
    source = (level // 2) * 128 + quad * 32 + (level % 2) * 16 + (row % 4) * 4 + col % 4
    pick = (iota((tokens, tokens), 1) == source).astype(F32).astype(BF)
    dnat = jnp.dot(pick, dmixed, preferred_element_type=F32).astype(BF)
    for c in w_copies:
        c.wait()
    out = lax.dot_general(dnat, w_all[...], (((1,), (1,)), ((), ())), preferred_element_type=F32)
    out_ref[...] = out.astype(BF)


def lat_sum_kernel(a, b, c, d, s_ref):
    total = (a[...].astype(F32) + b[...].astype(F32)) + (c[...].astype(F32) + d[...].astype(F32))
    width = s_ref.shape[1] - 128
    s_ref[:, :width] = total[:, :width].astype(BF)
    loss = jnp.sum(total[0:1, width:], axis=1, keepdims=True)
    s_ref[:, width:] = loss_block(loss, s_ref.shape[0]).astype(BF)


def lon_sum_kernel(denominator, place_ref, a, b, z0, z1, z2, z3, loss_ref, total_ref):
    total = a[...].astype(F32) + b[...].astype(F32)
    total_ref[...] = total
    zi = place_ref[0]
    rows, width = z0.shape
    for k, ref in enumerate((z0, z1, z2, z3)):
        at = pl.multiple_of((zi ^ k) * width, 128)
        ref[...] = total_ref[:, pl.ds(at, width)].astype(BF)
    loss = jnp.sum(total[0:1, 4 * width :], axis=1, keepdims=True) / denominator
    loss_ref[...] = jnp.broadcast_to(loss, loss_ref.shape)


def dp_sum_kernel(denominator, a, b, c, d, o_ref):
    total = (a[...].astype(F32) + b[...].astype(F32)) + (c[...].astype(F32) + d[...].astype(F32))
    o_ref[...] = total / denominator


def join_kernel(place_ref, a, b, c, d, o_ref):
    rows = a.shape[0]
    lat_place = place_ref[2]
    for k, ref in enumerate((a, b, c, d)):
        at = pl.multiple_of((lat_place ^ k) * rows, 8)
        o_ref[pl.ds(at, rows), :] = ref[...]


def swap(array, axis, bit):
    return lax.ppermute(array, axis, [(i, i ^ bit) for i in range(lax.axis_size(axis))])


def shape(dims, dtype):
    return jax.ShapeDtypeStruct(dims, dtype)


def shards(projected, targets, valid_cells, w_out, unpatch_matrix, norm_gain, var_weight):
    dp, lat, lon = lax.axis_size("dp"), lax.axis_size("lat"), lax.axis_size("lon")
    rows, width = w_out.shape
    levels = projected.shape[1]
    span = unpatch_matrix.shape[1]
    tokens = levels * 64
    zi, lat_place = lax.axis_index("dp"), lax.axis_index("lat")
    half = lat_place % 2
    place = jnp.stack([zi, half, lat_place]).astype(jnp.int32)
    last = (lat_place == lat - 1).astype(jnp.int32).reshape(1)
    lat_total = 8 * lat
    angle = math.pi * ((np.arange(lat_total) + 0.5) / lat_total - 0.5)
    cosine = np.cos(angle)
    lat_table = jnp.asarray(np.roll(cosine / cosine.mean(), -4), F32)

    ug = jnp.concatenate(
        [unpatch_matrix.T, norm_gain[None], jnp.zeros((UGROWS - span - 1, rows), BF)], axis=0
    )
    ug_half = lax.dynamic_slice_in_dim(ug, half * (UGROWS // 2), UGROWS // 2, 0)
    ug_half = jnp.concatenate([ug_half[32 * j : 32 * j + 32] for j in range(4)], axis=1)
    payload = jnp.concatenate(
        [lax.dynamic_slice_in_dim(w_out, half * (rows // 2), rows // 2, 0), ug_half], axis=0
    )
    rings, swaps = [], []
    moving = payload
    for _ in range(dp - 1):
        moving = from_behind(moving, "dp", 1)
        rings.append(moving)
        swaps.append(swap(moving, "lat", 1))

    quads = pl.pallas_call(
        pack_kernel,
        out_shape=[shape((tokens // 4, 3 * width + EXTRA), BF)] * 4,
        in_specs=[VMEM] * 3,
        out_specs=[VMEM] * 4,
        compiler_params=params(),
        name="pack",
    )(projected.reshape(levels, 8, 8, 3 * width), targets.reshape(levels, 8, 8, span), valid_cells)
    own = quads[0]
    east = from_behind(quads[1], "lon", -1)
    south = from_behind(quads[2], "lat", -1)
    diag = lax.ppermute(
        quads[3],
        ("lat", "lon"),
        [
            (a * lon + b, ((a - 1) % lat) * lon + (b - 1) % lon)
            for a in range(lat)
            for b in range(lon)
        ],
    )
    tiles = (own, east, south, diag)
    groups = width // 128
    qkv_specs = [
        pl.BlockSpec((tokens // 4, 128), lambda g, i=i: (0, i * groups + g)) for i in range(3)
    ]
    ctx = pl.pallas_call(
        attention_kernel,
        grid=(groups,),
        out_shape=shape((tokens, width), BF),
        in_specs=[SMEM] + qkv_specs * 4,
        out_specs=pl.BlockSpec((tokens, 128), lambda g: (0, g)),
        compiler_params=params(),
        name="attention",
    )(last, *[t for t in tiles for _ in range(3)])

    piece = span // lat
    extra_spec = pl.BlockSpec((tokens // 4, EXTRA), lambda i: (0, 3 * width // EXTRA))
    copies = 2 + 2 * (dp - 1) * 5
    assembly = [
        pltpu.VMEM((dp * rows, width), BF),
        pltpu.VMEM((UGROWS, dp * rows), BF),
    ]
    t0, t1, t2, t3, normed, inv, dfc = pl.pallas_call(
        forward_kernel,
        grid=(1,),
        out_shape=[shape((piece, width + 128), BF)] * 4
        + [shape((tokens, width), F32), shape((tokens, 128), F32), shape((tokens, span), BF)],
        in_specs=[SMEM] * 3 + [VMEM] + [extra_spec] * 4 + [ANY] * 8,
        out_specs=[VMEM] * 7,
        scratch_shapes=[pltpu.VMEM((tokens, width), BF)]
        + assembly
        + [pltpu.VMEM((span, width), F32), pltpu.SemaphoreType.DMA((copies,))],
        compiler_params=params(),
        name="forward",
    )(place, lat_table, var_weight, ctx, *tiles, w_out, ug, *rings, *swaps)

    terms = [t0] + [swap(t, "lat", b) for b, t in ((1, t1), (2, t2), (3, t3))]
    grad_context = pl.pallas_call(
        backward_kernel,
        out_shape=shape((tokens, width), BF),
        in_specs=[SMEM] + [VMEM] * 3 + [ANY] * 8,
        out_specs=VMEM,
        scratch_shapes=assembly + [pltpu.SemaphoreType.DMA((copies,))],
        compiler_params=params(),
        name="backward",
    )(place, normed, inv, dfc, w_out, ug, *rings, *swaps)

    lat_sum = pl.pallas_call(
        lat_sum_kernel,
        out_shape=shape((piece, width + 128), BF),
        in_specs=[VMEM] * 4,
        out_specs=VMEM,
        name="lat_sum",
    )(*terms)
    denominator = levels * lat_total * 8 * lon
    *parts, loss = pl.pallas_call(
        lambda *refs: lon_sum_kernel(float(denominator * (span // var_weight.shape[0])), *refs),
        out_shape=[shape((piece, rows), BF)] * 4 + [shape((8, 128), F32)],
        in_specs=[SMEM] + [VMEM] * 2,
        out_specs=[VMEM] * 5,
        scratch_shapes=[pltpu.VMEM((piece, width + 128), F32)],
        name="lon_sum",
    )(place, lat_sum, swap(lat_sum, "lon", 1))
    parts = [parts[0]] + [swap(parts[k], "dp", k) for k in (1, 2, 3)]
    mine = pl.pallas_call(
        lambda *refs: dp_sum_kernel(float(denominator), *refs),
        out_shape=shape((piece, rows), F32),
        in_specs=[VMEM] * 4,
        out_specs=VMEM,
        name="dp_sum",
    )(*parts)
    joined = pl.pallas_call(
        join_kernel,
        out_shape=shape((span, rows), F32),
        in_specs=[SMEM] + [VMEM] * 4,
        out_specs=VMEM,
        name="join",
    )(place, mine, *[swap(mine, "lat", b) for b in (1, 2, 3)])
    return (
        grad_context.reshape(1, levels, 8, 8, width),
        joined.T,
        loss[0, 0:1],
    )


def solution(mesh):
    placed = (
        P("dp", None, "lat", "lon", None),
        P("dp", None, "lat", "lon", None),
        P("lat", "lon"),
        P("dp", None),
        P("dp", None),
        P("dp"),
        P(),
    )
    fits = mesh.shape["dp"] == 4 and mesh.shape["lat"] == 4 and mesh.shape["lon"] == 2

    def program(*arrays):
        body = shards if fits else general_shards
        return jax.shard_map(
            body,
            mesh=mesh,
            in_specs=placed,
            out_specs=(P("dp", None, "lat", "lon", None), P("dp", None), P("dp")),
            check_vma=False,
        )(*arrays)

    return program
```

```python
import math

import jax
import jax.numpy as jnp
import numpy as np
from jax import lax
from jax.experimental import pallas as pl
from jax.experimental.pallas import tpu as pltpu
from jax.sharding import PartitionSpec as P

HEADS = 48
HDIM = 32
WLEV = 2
BF = jnp.bfloat16
F32 = jnp.float32
EXTRA = 256
UGROWS = 256
VMEM = pl.BlockSpec(memory_space=pltpu.VMEM)
SMEM = pl.BlockSpec(memory_space=pltpu.SMEM)
ANY = pl.BlockSpec(memory_space=pl.ANY)


def from_behind(array, axis, by):
    length = lax.axis_size(axis)
    return lax.ppermute(array, axis, [(i, (i + by) % length) for i in range(length)])


def general_shards(projected, targets, valid_cells, w_out, unpatch_matrix, norm_gain, var_weight):
    tile_side = projected.shape[2]
    half_side = tile_side // 2
    levels = projected.shape[1]
    model_width = w_out.shape[1]
    predicted_span = unpatch_matrix.shape[1]
    lat_total = tile_side * lax.axis_size("lat")
    lon_total = tile_side * lax.axis_size("lon")
    lat_place = lax.axis_index("lat")
    moved = from_behind(
        (projected[:, :, :, :half_side], targets[:, :, :, :half_side], valid_cells[:, :half_side]),
        "lon",
        -1,
    )
    strip_proj = jnp.concatenate([projected[:, :, :, half_side:], moved[0]], axis=3)
    strip_goal = jnp.concatenate([targets[:, :, :, half_side:], moved[1]], axis=3)
    strip_valid = jnp.concatenate([valid_cells[:, half_side:], moved[2]], axis=1)
    moved_rows = from_behind(
        (strip_proj[:, :, :half_side], strip_goal[:, :, :half_side], strip_valid[:half_side]),
        "lat",
        -1,
    )
    local_proj = jnp.concatenate([strip_proj[:, :, half_side:], moved_rows[0]], axis=2)
    shard_reference = jnp.concatenate([strip_goal[:, :, half_side:], moved_rows[1]], axis=2)
    local_valid = jnp.concatenate([strip_valid[half_side:], moved_rows[2]], axis=0).astype(F32)
    win_count = levels // WLEV
    tokw = WLEV * tile_side * tile_side
    windows = local_proj.reshape(win_count, tokw, 3 * model_width)
    rows_here = lat_place * tile_side + jnp.arange(tile_side)
    region_rows = (rows_here >= lat_total - half_side).astype(jnp.int32)
    region = jnp.broadcast_to(region_rows[None, :, None], (WLEV, tile_side, tile_side)).reshape(-1)
    allowed = region[:, None] == region[None, :]
    queries = windows[..., :model_width].reshape(win_count, tokw, HEADS, -1)
    key_heads = windows[..., model_width : 2 * model_width].reshape(win_count, tokw, HEADS, -1)
    value_heads = windows[..., 2 * model_width :].reshape(win_count, tokw, HEADS, -1)
    scores = jnp.einsum("wqhd,wkhd->whqk", queries, key_heads, preferred_element_type=F32)
    scores = scores * (1.0 / math.sqrt(HDIM))
    scores = jnp.where(allowed[None, None], scores, -1e30)
    row_peak = jnp.max(scores, axis=-1, keepdims=True)
    lifted = jnp.exp(scores - row_peak)
    attn = (lifted / jnp.sum(lifted, axis=-1, keepdims=True)).astype(BF)
    context = jnp.einsum("whqk,wkhd->wqhd", attn, value_heads, preferred_element_type=F32)
    context = context.astype(BF).reshape(win_count * tokw, model_width)
    element_total = win_count * tokw
    out_all, unprojected_pieces, gain_all = (
        lax.all_gather(w_out, "dp", axis=0, tiled=True),
        lax.all_gather(unpatch_matrix, "dp", axis=0, tiled=True),
        lax.all_gather(norm_gain, "dp", axis=0, tiled=True),
    )
    mixed_rows = jnp.dot(context, out_all, preferred_element_type=F32)
    centre = jnp.mean(mixed_rows, axis=-1, keepdims=True)
    spread = jnp.mean((mixed_rows - centre) ** 2, axis=-1, keepdims=True)
    inv_spread = lax.rsqrt(spread + 1e-05)
    normed = (mixed_rows - centre) * inv_spread
    gain_f = gain_all.astype(F32)
    latent_activation = (normed * gain_f).astype(BF)
    prediction_field = jnp.dot(latent_activation, unprojected_pieces, preferred_element_type=F32)
    prediction_misfit = prediction_field - shard_reference.reshape(
        element_total, predicted_span
    ).astype(F32)
    all_rows = jnp.arange(lat_total).astype(F32)
    cosine_mean = jnp.mean(jnp.cos(math.pi * ((all_rows + 0.5) / lat_total - 0.5)))
    initial_rows = ((rows_here + half_side) % lat_total).astype(F32)
    lat_here = jnp.cos(math.pi * ((initial_rows + 0.5) / lat_total - 0.5)) / cosine_mean
    element_factor = jnp.broadcast_to(
        lat_here[None, :, None] * local_valid[None], (levels, tile_side, tile_side)
    ).reshape(element_total, 1)
    variable_factor = jnp.repeat(var_weight, predicted_span // var_weight.shape[0])[None, :]
    shard_penalty = jnp.sum(
        element_factor * variable_factor * prediction_misfit * prediction_misfit
    ) / (levels * lat_total * lon_total * (predicted_span // var_weight.shape[0]))
    prediction_gradient = (2.0 * element_factor * variable_factor * prediction_misfit).astype(BF)
    grad_shard = lax.psum_scatter(
        jnp.einsum(
            "td,to->do", latent_activation, prediction_gradient, preferred_element_type=F32
        ).astype(BF),
        "dp",
        scatter_dimension=0,
        tiled=True,
    ).astype(F32)
    grad_sum, loss_sum = lax.psum((grad_shard, shard_penalty), ("lat", "lon"))
    grad_recovery = grad_sum / (levels * lat_total * lon_total)
    grad_hidden = jnp.einsum(
        "to,do->td", prediction_gradient, unprojected_pieces, preferred_element_type=F32
    )
    scaled_grad = grad_hidden * gain_f
    grad_mixed = inv_spread * (
        scaled_grad
        - jnp.mean(scaled_grad, axis=-1, keepdims=True)
        - normed * jnp.mean(scaled_grad * normed, axis=-1, keepdims=True)
    )
    grad_mixed = grad_mixed.astype(BF)
    grad_context = jnp.einsum("tj,ij->ti", grad_mixed, out_all, preferred_element_type=F32)
    grad_context = grad_context.astype(BF).reshape(1, levels, tile_side, tile_side, model_width)
    return (grad_context, grad_recovery, loss_sum.reshape(1))


def params(mib):
    return pltpu.CompilerParams(vmem_limit_bytes=mib << 20)


def iota(shape, dim):
    return lax.broadcasted_iota(jnp.int32, shape, dim)


def pack_kernel(
    place_ref, x_ref, t_ref, valid_ref, w_ref, unpatch_ref, gain_ref,
    own0, own1, east0, east1, south0, south1, diag0, diag1, ug_ref, payload_ref, sems,
):
    half = place_ref[1]
    rows, width = w_ref.shape
    hr = rows // 2
    start = pl.multiple_of(half * hr, 64)
    copies = [
        pltpu.make_async_copy(
            w_ref.at[pl.ds(start, hr), :], payload_ref.at[pl.ds(0, hr), :], sems.at[0]
        )
    ]
    copies[0].start()
    span = t_ref.shape[-1]
    ug_ref[...] = jnp.concatenate(
        [
            unpatch_ref[...],
            jnp.broadcast_to(gain_ref[...], (16, rows)),
            jnp.zeros((UGROWS - span - 16, rows), BF),
        ],
        axis=0,
    )
    for j in range(4):
        at = pl.multiple_of((4 * half + j) * 32, 32)
        copies.append(
            pltpu.make_async_copy(
                ug_ref.at[pl.ds(at, 32), :],
                payload_ref.at[pl.ds(hr, 32), pl.ds(j * rows, rows)],
                sems.at[1 + j],
            )
        )
        copies[-1].start()
    count = x_ref.shape[0] * 64
    place = iota((count, count), 0)
    quad, rest = place // (count // 4), place % (count // 4)
    row = (rest // 4) % 4 + jnp.where(quad < 2, 4, 0)
    col = rest % 4 + jnp.where(quad % 2 == 0, 4, 0)
    source = (rest // 16) * 64 + row * 8 + col
    pick = (iota((count, count), 1) == source).astype(F32).astype(BF)
    firsts, seconds = (own0, east0, south0, diag0), (own1, east1, south1, diag1)
    quarter = count // 4
    part = width // 2
    step = part // 2
    for at in range(0, 3 * width, step):
        tokens = x_ref[:, :, :, at : at + step].reshape(count, step)
        out = jnp.dot(pick, tokens, preferred_element_type=F32).astype(BF)
        which, inner = at // width, at % width
        refs = firsts if inner < part else seconds
        to = which * part + inner % part
        for q, ref in enumerate(refs):
            ref[:, to : to + step] = out[q * quarter : (q + 1) * quarter]
    goal = jnp.dot(pick, t_ref[...].reshape(count, span), preferred_element_type=F32)
    token = iota((count, 8), 0)
    row_hot = ((token // 8) % 8 == iota((count, 8), 1)).astype(F32)
    by_row = jnp.dot(row_hot, valid_ref[...].astype(F32), preferred_element_type=F32)
    mine = token % 8 == iota((count, 8), 1)
    natural = jnp.sum(jnp.where(mine, by_row, 0.0), axis=1, keepdims=True)
    spread = jnp.broadcast_to(natural, (count, 128)).astype(BF)
    column = jnp.dot(pick, spread, preferred_element_type=F32)
    extra = jnp.concatenate([goal, column[:, : EXTRA - span]], axis=1).astype(BF)
    for q, ref in enumerate(seconds):
        ref[:, 3 * part :] = extra[q * quarter : (q + 1) * quarter]
    for c in copies:
        c.wait()


def attention_kernel(last_ref, *refs):
    ctx_ref = refs[12]
    tiles = [refs[3 * q : 3 * q + 3] for q in range(4)]
    is_last = last_ref[0] == 1
    side = iota((128, 512), 0) // 64
    same = side == (iota((128, 512), 1) % 128) // 64
    keep = jnp.logical_or(same, jnp.logical_not(is_last))
    head = iota((128, 128), 1) // HDIM
    factor = math.log2(math.e) / math.sqrt(HDIM)
    for w in range(2):
        q, k, v = [
            jnp.concatenate([tiles[c][i][32 * w : 32 * w + 32] for c in range(4)], axis=0)
            for i in range(3)
        ]
        zero = jnp.zeros_like(k)
        k4 = jnp.concatenate([jnp.where(head == h, k, zero) for h in range(4)], axis=0)
        v4 = jnp.concatenate([jnp.where(head == h, v, zero) for h in range(4)], axis=0)
        s = lax.dot_general(q, k4, (((1,), (1,)), ((), ())), preferred_element_type=F32)
        s = jnp.where(keep, s, -1e30)
        parts = []
        for h in range(4):
            sh = s[:, 128 * h : 128 * h + 128]
            e = jnp.exp2((sh - jnp.max(sh, axis=1, keepdims=True)) * factor)
            parts.append((e / jnp.sum(e, axis=1, keepdims=True)).astype(BF))
        attn = jnp.concatenate(parts, axis=1)
        out = jnp.dot(attn, v4, preferred_element_type=F32)
        ctx_ref[128 * w : 128 * w + 128, :] = out.astype(BF)


def piece_copies(zi, half, own_w, own_ug, rings, swaps, w_all, ug_all, sems):
    rows = own_w.shape[0]
    hr = rows // 2
    steps = len(rings) + 1
    w_copies, u_copies = [], []

    def place(src, dst, to):
        at = sems.at[len(w_copies) + len(u_copies)]
        to.append(pltpu.make_async_copy(src, dst, at))

    base = pl.multiple_of(zi * rows, 128)
    place(own_w, w_all.at[pl.ds(base, rows), :], w_copies)
    place(own_ug, ug_all.at[:, pl.ds(base, rows)], u_copies)
    for k in range(1, steps):
        shard = lax.rem(zi - k + steps, steps)
        base = pl.multiple_of(shard * rows, 128)
        for piece, part in ((rings[k - 1], half), (swaps[k - 1], 1 - half)):
            row = pl.multiple_of(base + part * hr, 64)
            place(piece.at[pl.ds(0, hr), :], w_all.at[pl.ds(row, hr), :], w_copies)
            for j in range(4):
                urow = pl.multiple_of((4 * part + j) * 32, 32)
                place(
                    piece.at[pl.ds(hr, 32), pl.ds(j * rows, rows)],
                    ug_all.at[pl.ds(urow, 32), pl.ds(base, rows)],
                    u_copies,
                )
    return w_copies, u_copies


def split3(x):
    hi = x.astype(BF).astype(F32)
    mid = (x - hi).astype(BF).astype(F32)
    return hi, mid, x - hi - mid


def loss_block(value, rows):
    hi, mid, lo = split3(value)
    lane = iota((rows, 128), 1)
    return jnp.where(lane == 0, hi, jnp.where(lane == 1, mid, jnp.where(lane == 2, lo, 0.0)))


def forward_kernel(
    place_ref, lat_ref, var_ref, ctx0_ref, ctx1_ref, e0, e1, e2, e3, own_w, own_ug, r1, r2, r3, c1, c2, c3,
    t0, t1, t2, t3, normed_ref, inv_ref, dfc_ref, hidden_ref, w_all, ug_all, term, sems,
):
    zi, half, lat_place = place_ref[0], place_ref[1], place_ref[2]
    w_copies, u_copies = piece_copies(
        zi, half, own_w, own_ug, (r1, r2, r3), (c1, c2, c3), w_all, ug_all, sems
    )
    for c in w_copies + u_copies:
        c.start()
    tokens, width = normed_ref.shape
    span = dfc_ref.shape[1]
    extras = [e0, e1, e2, e3]
    extra = jnp.concatenate(
        [e[32 * w : 32 * w + 32, :] for w in range(2) for e in extras], axis=0
    ).astype(F32)
    goal, valid = extra[:, :span], extra[:, span : span + 1]
    token = iota((tokens, 1), 0)
    row = (token // 4) % 4 + jnp.where((token // 32) % 4 >= 2, 4, 0)
    lat_w = jnp.zeros((tokens, 1), F32)
    for r in range(8):
        lat_w = jnp.where(row == r, lat_ref[lat_place * 8 + r], lat_w)
    lane = iota((1, span), 1) // (span // var_ref.shape[0])
    var_w = jnp.zeros((1, span), F32)
    for n in range(var_ref.shape[0]):
        var_w = jnp.where(lane == n, var_ref[n], var_w)
    weight = lat_w * valid * var_w
    for c in w_copies:
        c.wait()
    part = width // 2
    mixed = jnp.dot(ctx0_ref[...], w_all[0:part, :], preferred_element_type=F32)
    mixed += jnp.dot(ctx1_ref[...], w_all[part:, :], preferred_element_type=F32)
    centre = jnp.mean(mixed, axis=-1, keepdims=True)
    off = mixed - centre
    inv = lax.rsqrt(jnp.mean(off * off, axis=-1, keepdims=True) + 1e-05)
    normed = off * inv
    normed_ref[...] = normed
    inv_ref[...] = jnp.broadcast_to(inv, inv_ref.shape)
    for c in u_copies:
        c.wait()
    gain = ug_all[pl.ds(span, 16), :][0:1].astype(F32)
    hidden_ref[...] = (normed * gain).astype(BF)
    field = lax.dot_general(
        hidden_ref[...], ug_all[0:span, :], (((1,), (1,)), ((), ())), preferred_element_type=F32
    )
    misfit = field - goal
    dfc = (2.0 * weight * misfit).astype(BF)
    dfc_ref[...] = dfc
    term[...] = lax.dot_general(
        dfc, hidden_ref[...], (((0,), (0,)), ((), ())), preferred_element_type=F32
    )
    loss = jnp.sum(jnp.sum(weight * misfit * misfit, axis=1, keepdims=True), axis=0, keepdims=True)
    rows = t0.shape[0]
    block = loss_block(loss, rows).astype(BF)
    for b, ref in enumerate((t0, t1, t2, t3)):
        at = pl.multiple_of((lat_place ^ b) * rows, 8)
        ref[:, :width] = term[pl.ds(at, rows), :].astype(BF)
        ref[:, width:] = block


def backward_kernel(
    place_ref, normed_ref, inv_ref, dfc_ref, own_w, own_ug, r1, r2, r3, c1, c2, c3,
    out_ref, w_all, ug_all, sems,
):
    zi, half = place_ref[0], place_ref[1]
    w_copies, u_copies = piece_copies(
        zi, half, own_w, own_ug, (r1, r2, r3), (c1, c2, c3), w_all, ug_all, sems
    )
    for c in u_copies + w_copies:
        c.start()
    tokens, width = normed_ref.shape
    span = dfc_ref.shape[1]
    for c in u_copies:
        c.wait()
    gain = ug_all[pl.ds(span, 16), :][0:1].astype(F32)
    g = jnp.dot(dfc_ref[...], ug_all[0:span, :], preferred_element_type=F32) * gain
    normed = normed_ref[...]
    mean_g = jnp.mean(g, axis=-1, keepdims=True)
    mean_gn = jnp.mean(g * normed, axis=-1, keepdims=True)
    dmixed = ((g - mean_g - normed * mean_gn) * inv_ref[:, 0:1]).astype(BF)
    place = iota((tokens, tokens), 0)
    row, col, level = (place // 8) % 8, place % 8, place // 64
    quad = jnp.where(row >= 4, 2, 0) + jnp.where(col >= 4, 1, 0)
    source = (level // 2) * 128 + quad * 32 + (level % 2) * 16 + (row % 4) * 4 + col % 4
    pick = (iota((tokens, tokens), 1) == source).astype(F32).astype(BF)
    dnat = jnp.dot(pick, dmixed, preferred_element_type=F32).astype(BF)
    for c in w_copies:
        c.wait()
    out = lax.dot_general(dnat, w_all[...], (((1,), (1,)), ((), ())), preferred_element_type=F32)
    out_ref[...] = out.astype(BF)


def lat_sum_kernel(a, b, c, d, s_ref):
    total = (a[...].astype(F32) + b[...].astype(F32)) + (c[...].astype(F32) + d[...].astype(F32))
    width = s_ref.shape[1] - 128
    s_ref[:, :width] = total[:, :width].astype(BF)
    loss = jnp.sum(total[0:1, width:], axis=1, keepdims=True)
    s_ref[:, width:] = loss_block(loss, s_ref.shape[0]).astype(BF)


def lon_sum_kernel(denominator, place_ref, a, b, z0, z1, z2, z3, loss_ref, total_ref):
    total = a[...].astype(F32) + b[...].astype(F32)
    total_ref[...] = total
    zi = place_ref[0]
    rows, width = z0.shape
    for k, ref in enumerate((z0, z1, z2, z3)):
        at = pl.multiple_of((zi ^ k) * width, 128)
        ref[...] = total_ref[:, pl.ds(at, width)].astype(BF)
    loss = jnp.sum(total[0:1, 4 * width :], axis=1, keepdims=True) / denominator
    loss_ref[...] = jnp.broadcast_to(loss, loss_ref.shape)


def dp_sum_kernel(denominator, a, b, c, d, o_ref):
    total = (a[...].astype(F32) + b[...].astype(F32)) + (c[...].astype(F32) + d[...].astype(F32))
    o_ref[...] = total / denominator


def join_kernel(place_ref, a, b, c, d, o_ref):
    rows = a.shape[0]
    lat_place = place_ref[2]
    for k, ref in enumerate((a, b, c, d)):
        at = pl.multiple_of((lat_place ^ k) * rows, 8)
        o_ref[pl.ds(at, rows), :] = ref[...]


def swap(array, axis, bit):
    return lax.ppermute(array, axis, [(i, i ^ bit) for i in range(lax.axis_size(axis))])


def shape(dims, dtype):
    return jax.ShapeDtypeStruct(dims, dtype)


def shards(projected, targets, valid_cells, w_out, unpatch_matrix, norm_gain, var_weight):
    dp, lat, lon = lax.axis_size("dp"), lax.axis_size("lat"), lax.axis_size("lon")
    rows, width = w_out.shape
    levels = projected.shape[1]
    span = unpatch_matrix.shape[1]
    tokens = levels * 64
    zi, lat_place = lax.axis_index("dp"), lax.axis_index("lat")
    half = lat_place % 2
    place = jnp.stack([zi, half, lat_place]).astype(jnp.int32)
    last = (lat_place == lat - 1).astype(jnp.int32).reshape(1)
    lat_total = 8 * lat
    angle = math.pi * ((np.arange(lat_total) + 0.5) / lat_total - 0.5)
    cosine = np.cos(angle)
    lat_table = jnp.asarray(np.roll(cosine / cosine.mean(), -4), F32)

    part = width // 2
    quarter = tokens // 4
    widths = (3 * part, 3 * part + EXTRA)
    *packed, ug, payload = pl.pallas_call(
        pack_kernel,
        out_shape=[shape((quarter, w), BF) for _ in range(4) for w in widths]
        + [shape((UGROWS, rows), BF), shape((rows // 2 + 32, width), BF)],
        in_specs=[SMEM] + [VMEM] * 3 + [ANY] + [VMEM] * 2,
        out_specs=[VMEM] * 9 + [ANY],
        scratch_shapes=[pltpu.SemaphoreType.DMA((5,))],
        compiler_params=params(20),
        name="pack",
    )(
        place,
        projected.reshape(levels, 8, 8, 3 * width),
        targets.reshape(levels, 8, 8, span),
        valid_cells,
        w_out,
        unpatch_matrix.T,
        norm_gain.reshape(1, rows),
    )
    corner = [
        (a * lon + b, ((a - 1) % lat) * lon + (b - 1) % lon) for a in range(lat) for b in range(lon)
    ]
    tiles = []
    for g in range(2):
        own, east, south, diag = packed[g::2]
        tiles.append(
            (
                own,
                from_behind(east, "lon", -1),
                from_behind(south, "lat", -1),
                lax.ppermute(diag, ("lat", "lon"), corner),
            )
        )
    groups = part // 128

    def attend(chunk):
        specs = [
            pl.BlockSpec((quarter, 128), lambda g, i=i: (0, i * groups + g)) for i in range(3)
        ]
        return pl.pallas_call(
            attention_kernel,
            grid=(groups,),
            out_shape=shape((tokens, part), BF),
            in_specs=[SMEM] + specs * 4,
            out_specs=pl.BlockSpec((tokens, 128), lambda g: (0, g)),
            compiler_params=params(8),
            name="attention",
        )(last, *[t for t in chunk for _ in range(3)])

    ring1 = from_behind(payload, "dp", 1)
    ring1_after, *first = lax.optimization_barrier((ring1, *tiles[0][1:]))
    ring2 = from_behind(ring1_after, "dp", 1)
    ctx0 = attend((tiles[0][0], *first))
    ctx1 = attend(tiles[1])
    ring2_after, ctx0, ctx1 = lax.optimization_barrier((ring2, ctx0, ctx1))
    ring3 = from_behind(ring2_after, "dp", 1)
    rings = [ring1, ring2, ring3]
    swaps = [swap(r, "lat", 1) for r in rings]

    piece = span // lat
    extra_spec = pl.BlockSpec((tokens // 4, EXTRA), lambda i: (0, 3 * part // EXTRA))
    copies = 2 + 2 * (dp - 1) * 5
    assembly = [
        pltpu.VMEM((dp * rows, width), BF),
        pltpu.VMEM((UGROWS, dp * rows), BF),
    ]
    t0, t1, t2, t3, normed, inv, dfc = pl.pallas_call(
        forward_kernel,
        grid=(1,),
        out_shape=[shape((piece, width + 128), BF)] * 4
        + [shape((tokens, width), F32), shape((tokens, 128), F32), shape((tokens, span), BF)],
        in_specs=[SMEM] * 3 + [VMEM] * 2 + [extra_spec] * 4 + [ANY] * 8,
        out_specs=[VMEM] * 7,
        scratch_shapes=[pltpu.VMEM((tokens, width), BF)]
        + assembly
        + [pltpu.VMEM((span, width), F32), pltpu.SemaphoreType.DMA((copies,))],
        compiler_params=params(28),
        name="forward",
    )(place, lat_table, var_weight, ctx0, ctx1, *tiles[1], w_out, ug, *rings, *swaps)

    terms = [t0] + [swap(t, "lat", b) for b, t in ((1, t1), (2, t2), (3, t3))]
    grad_context = pl.pallas_call(
        backward_kernel,
        out_shape=shape((tokens, width), BF),
        in_specs=[SMEM] + [VMEM] * 3 + [ANY] * 8,
        out_specs=VMEM,
        scratch_shapes=assembly + [pltpu.SemaphoreType.DMA((copies,))],
        compiler_params=params(24),
        name="backward",
    )(place, normed, inv, dfc, w_out, ug, *rings, *swaps)

    *terms, grad_context = lax.optimization_barrier((*terms, grad_context))
    lat_sum = pl.pallas_call(
        lat_sum_kernel,
        out_shape=shape((piece, width + 128), BF),
        in_specs=[VMEM] * 4,
        out_specs=VMEM,
        compiler_params=params(4),
        name="lat_sum",
    )(*terms)
    denominator = levels * lat_total * 8 * lon
    *parts, loss = pl.pallas_call(
        lambda *refs: lon_sum_kernel(float(denominator * (span // var_weight.shape[0])), *refs),
        out_shape=[shape((piece, rows), BF)] * 4 + [shape((8, 128), F32)],
        in_specs=[SMEM] + [VMEM] * 2,
        out_specs=[VMEM] * 5,
        scratch_shapes=[pltpu.VMEM((piece, width + 128), F32)],
        compiler_params=params(4),
        name="lon_sum",
    )(place, lat_sum, swap(lat_sum, "lon", 1))
    parts = [parts[0]] + [swap(parts[k], "dp", k) for k in (1, 2, 3)]
    mine = pl.pallas_call(
        lambda *refs: dp_sum_kernel(float(denominator), *refs),
        out_shape=shape((piece, rows), F32),
        in_specs=[VMEM] * 4,
        out_specs=VMEM,
        compiler_params=params(4),
        name="dp_sum",
    )(*parts)
    joined = pl.pallas_call(
        join_kernel,
        out_shape=shape((span, rows), F32),
        in_specs=[SMEM] + [VMEM] * 4,
        out_specs=VMEM,
        compiler_params=params(4),
        name="join",
    )(place, mine, *[swap(mine, "lat", b) for b in (1, 2, 3)])
    return (
        grad_context.reshape(1, levels, 8, 8, width),
        joined.T,
        loss[0, 0:1],
    )


def solution(mesh):
    placed = (
        P("dp", None, "lat", "lon", None),
        P("dp", None, "lat", "lon", None),
        P("lat", "lon"),
        P("dp", None),
        P("dp", None),
        P("dp"),
        P(),
    )
    fits = mesh.shape["dp"] == 4 and mesh.shape["lat"] == 4 and mesh.shape["lon"] == 2

    def program(*arrays):
        body = shards if fits else general_shards
        return jax.shard_map(
            body,
            mesh=mesh,
            in_specs=placed,
            out_specs=(P("dp", None, "lat", "lon", None), P("dp", None), P("dp")),
            check_vma=False,
        )(*arrays)

    return program
```

```python
import math

import jax
import jax.numpy as jnp
import numpy as np
from jax import lax
from jax.experimental import pallas as pl
from jax.experimental.pallas import tpu as pltpu
from jax.sharding import PartitionSpec as P

HEADS = 48
HDIM = 32
WLEV = 2
BF = jnp.bfloat16
F32 = jnp.float32
EXTRA = 256
UGROWS = 256
CHUNKS = 3
PIECES = 12
VMEM = pl.BlockSpec(memory_space=pltpu.VMEM)
SMEM = pl.BlockSpec(memory_space=pltpu.SMEM)
ANY = pl.BlockSpec(memory_space=pl.ANY)
HBM = pl.BlockSpec(memory_space=pltpu.HBM)


def from_behind(array, axis, by):
    length = lax.axis_size(axis)
    return lax.ppermute(array, axis, [(i, (i + by) % length) for i in range(length)])


def general_shards(projected, targets, valid_cells, w_out, unpatch_matrix, norm_gain, var_weight):
    tile_side = projected.shape[2]
    half_side = tile_side // 2
    levels = projected.shape[1]
    model_width = w_out.shape[1]
    predicted_span = unpatch_matrix.shape[1]
    lat_total = tile_side * lax.axis_size("lat")
    lon_total = tile_side * lax.axis_size("lon")
    lat_place = lax.axis_index("lat")
    moved = from_behind(
        (projected[:, :, :, :half_side], targets[:, :, :, :half_side], valid_cells[:, :half_side]),
        "lon",
        -1,
    )
    strip_proj = jnp.concatenate([projected[:, :, :, half_side:], moved[0]], axis=3)
    strip_goal = jnp.concatenate([targets[:, :, :, half_side:], moved[1]], axis=3)
    strip_valid = jnp.concatenate([valid_cells[:, half_side:], moved[2]], axis=1)
    moved_rows = from_behind(
        (strip_proj[:, :, :half_side], strip_goal[:, :, :half_side], strip_valid[:half_side]),
        "lat",
        -1,
    )
    local_proj = jnp.concatenate([strip_proj[:, :, half_side:], moved_rows[0]], axis=2)
    shard_reference = jnp.concatenate([strip_goal[:, :, half_side:], moved_rows[1]], axis=2)
    local_valid = jnp.concatenate([strip_valid[half_side:], moved_rows[2]], axis=0).astype(F32)
    win_count = levels // WLEV
    tokw = WLEV * tile_side * tile_side
    windows = local_proj.reshape(win_count, tokw, 3 * model_width)
    rows_here = lat_place * tile_side + jnp.arange(tile_side)
    region_rows = (rows_here >= lat_total - half_side).astype(jnp.int32)
    region = jnp.broadcast_to(region_rows[None, :, None], (WLEV, tile_side, tile_side)).reshape(-1)
    allowed = region[:, None] == region[None, :]
    queries = windows[..., :model_width].reshape(win_count, tokw, HEADS, -1)
    key_heads = windows[..., model_width : 2 * model_width].reshape(win_count, tokw, HEADS, -1)
    value_heads = windows[..., 2 * model_width :].reshape(win_count, tokw, HEADS, -1)
    scores = jnp.einsum("wqhd,wkhd->whqk", queries, key_heads, preferred_element_type=F32)
    scores = scores * (1.0 / math.sqrt(HDIM))
    scores = jnp.where(allowed[None, None], scores, -1e30)
    row_peak = jnp.max(scores, axis=-1, keepdims=True)
    lifted = jnp.exp(scores - row_peak)
    attn = (lifted / jnp.sum(lifted, axis=-1, keepdims=True)).astype(BF)
    context = jnp.einsum("whqk,wkhd->wqhd", attn, value_heads, preferred_element_type=F32)
    context = context.astype(BF).reshape(win_count * tokw, model_width)
    element_total = win_count * tokw
    out_all, unprojected_pieces, gain_all = (
        lax.all_gather(w_out, "dp", axis=0, tiled=True),
        lax.all_gather(unpatch_matrix, "dp", axis=0, tiled=True),
        lax.all_gather(norm_gain, "dp", axis=0, tiled=True),
    )
    mixed_rows = jnp.dot(context, out_all, preferred_element_type=F32)
    centre = jnp.mean(mixed_rows, axis=-1, keepdims=True)
    spread = jnp.mean((mixed_rows - centre) ** 2, axis=-1, keepdims=True)
    inv_spread = lax.rsqrt(spread + 1e-05)
    normed = (mixed_rows - centre) * inv_spread
    gain_f = gain_all.astype(F32)
    latent_activation = (normed * gain_f).astype(BF)
    prediction_field = jnp.dot(latent_activation, unprojected_pieces, preferred_element_type=F32)
    prediction_misfit = prediction_field - shard_reference.reshape(
        element_total, predicted_span
    ).astype(F32)
    all_rows = jnp.arange(lat_total).astype(F32)
    cosine_mean = jnp.mean(jnp.cos(math.pi * ((all_rows + 0.5) / lat_total - 0.5)))
    initial_rows = ((rows_here + half_side) % lat_total).astype(F32)
    lat_here = jnp.cos(math.pi * ((initial_rows + 0.5) / lat_total - 0.5)) / cosine_mean
    element_factor = jnp.broadcast_to(
        lat_here[None, :, None] * local_valid[None], (levels, tile_side, tile_side)
    ).reshape(element_total, 1)
    variable_factor = jnp.repeat(var_weight, predicted_span // var_weight.shape[0])[None, :]
    shard_penalty = jnp.sum(
        element_factor * variable_factor * prediction_misfit * prediction_misfit
    ) / (levels * lat_total * lon_total * (predicted_span // var_weight.shape[0]))
    prediction_gradient = (2.0 * element_factor * variable_factor * prediction_misfit).astype(BF)
    grad_shard = lax.psum_scatter(
        jnp.einsum(
            "td,to->do", latent_activation, prediction_gradient, preferred_element_type=F32
        ).astype(BF),
        "dp",
        scatter_dimension=0,
        tiled=True,
    ).astype(F32)
    grad_sum, loss_sum = lax.psum((grad_shard, shard_penalty), ("lat", "lon"))
    grad_recovery = grad_sum / (levels * lat_total * lon_total)
    grad_hidden = jnp.einsum(
        "to,do->td", prediction_gradient, unprojected_pieces, preferred_element_type=F32
    )
    scaled_grad = grad_hidden * gain_f
    grad_mixed = inv_spread * (
        scaled_grad
        - jnp.mean(scaled_grad, axis=-1, keepdims=True)
        - normed * jnp.mean(scaled_grad * normed, axis=-1, keepdims=True)
    )
    grad_mixed = grad_mixed.astype(BF)
    grad_context = jnp.einsum("tj,ij->ti", grad_mixed, out_all, preferred_element_type=F32)
    grad_context = grad_context.astype(BF).reshape(1, levels, tile_side, tile_side, model_width)
    return (grad_context, grad_recovery, loss_sum.reshape(1))


def params(mib):
    return pltpu.CompilerParams(vmem_limit_bytes=mib << 20)


def iota(shape, dim):
    return lax.broadcasted_iota(jnp.int32, shape, dim)


def payload_kernel(place_ref, w_ref, unpatch_ref, gain_ref, ug_ref, payload_ref, u_in, sems):
    part = place_ref[1]
    rows, width = w_ref.shape
    qr = rows // 4
    span = unpatch_ref.shape[0]
    start = pl.multiple_of(part * qr, 32)
    w_copy = pltpu.make_async_copy(
        w_ref.at[pl.ds(start, qr), :], payload_ref.at[pl.ds(0, qr), :], sems.at[0]
    )
    u_copy = pltpu.make_async_copy(unpatch_ref, u_in, sems.at[1])
    w_copy.start()
    u_copy.start()
    gain = jnp.broadcast_to(gain_ref[...].astype(F32).reshape(1, rows), (16, rows)).astype(BF)
    ug_ref[pl.ds(span, 16), :] = gain
    ug_ref[pl.ds(span + 16, UGROWS - span - 16), :] = jnp.zeros((UGROWS - span - 16, rows), BF)
    u_copy.wait()
    ug_ref[pl.ds(0, span), :] = u_in[...]
    for j in range(4):
        at = pl.multiple_of((4 * part + j) * 16, 16)
        payload_ref[pl.ds(qr, 16), pl.ds(j * rows, rows)] = ug_ref[pl.ds(at, 16), :]
    w_copy.wait()


def pack_kernel(x_ref, t_ref, valid_ref, *refs):
    outs = refs[: 4 * CHUNKS]
    x_in, t_in, v_in, sems = refs[4 * CHUNKS :]
    width = x_ref.shape[-1] // 3
    span = t_ref.shape[-1]
    count = x_ref.shape[0] * 64
    part = width // CHUNKS
    copies = []
    for g in range(CHUNKS):
        for i in range(3):
            lanes = pl.ds(i * width + g * part, part)
            at = (slice(None), slice(None), slice(None), lanes)
            copies.append(
                pltpu.make_async_copy(x_ref.at[at], x_in.at[at], sems.at[3 * g + i])
            )
    copies.append(pltpu.make_async_copy(t_ref, t_in, sems.at[3 * CHUNKS]))
    copies.append(pltpu.make_async_copy(valid_ref, v_in, sems.at[3 * CHUNKS + 1]))
    for c in copies:
        c.start()
    place = iota((count, count), 0)
    quad, rest = place // (count // 4), place % (count // 4)
    row = (rest // 4) % 4 + jnp.where(quad < 2, 4, 0)
    col = rest % 4 + jnp.where(quad % 2 == 0, 4, 0)
    source = (rest // 16) * 64 + row * 8 + col
    pick = (iota((count, count), 1) == source).astype(F32).astype(BF)
    quarter = count // 4
    for g in range(CHUNKS):
        for i in range(3):
            copies[3 * g + i].wait()
            at = i * width + g * part
            tokens = x_in[:, :, :, at : at + part].reshape(count, part)
            out = jnp.dot(pick, tokens, preferred_element_type=F32).astype(BF)
            for q in range(4):
                outs[4 * g + q][:, i * part : (i + 1) * part] = out[q * quarter : (q + 1) * quarter]
    copies[-2].wait()
    copies[-1].wait()
    goal = jnp.dot(pick, t_in[...].reshape(count, span), preferred_element_type=F32)
    token = iota((count, 8), 0)
    row_hot = ((token // 8) % 8 == iota((count, 8), 1)).astype(F32)
    by_row = jnp.dot(row_hot, v_in[...].astype(F32), preferred_element_type=F32)
    mine = token % 8 == iota((count, 8), 1)
    natural = jnp.sum(jnp.where(mine, by_row, 0.0), axis=1, keepdims=True)
    spread = jnp.broadcast_to(natural, (count, 128)).astype(BF)
    column = jnp.dot(pick, spread, preferred_element_type=F32)
    extra = jnp.concatenate([goal, column[:, : EXTRA - span]], axis=1).astype(BF)
    for q in range(4):
        outs[4 * CHUNKS - 4 + q][:, 3 * part :] = extra[q * quarter : (q + 1) * quarter]


def attention_kernel(last_ref, *refs):
    ctx_ref = refs[12]
    tiles = [refs[3 * q : 3 * q + 3] for q in range(4)]
    is_last = last_ref[0] == 1
    side = iota((128, 512), 0) // 64
    same = side == (iota((128, 512), 1) % 128) // 64
    keep = jnp.logical_or(same, jnp.logical_not(is_last))
    head = iota((128, 128), 1) // HDIM
    factor = math.log2(math.e) / math.sqrt(HDIM)
    for w in range(2):
        q, k, v = [
            jnp.concatenate([tiles[c][i][32 * w : 32 * w + 32] for c in range(4)], axis=0)
            for i in range(3)
        ]
        zero = jnp.zeros_like(k)
        k4 = jnp.concatenate([jnp.where(head == h, k, zero) for h in range(4)], axis=0)
        v4 = jnp.concatenate([jnp.where(head == h, v, zero) for h in range(4)], axis=0)
        s = lax.dot_general(q, k4, (((1,), (1,)), ((), ())), preferred_element_type=F32)
        s = jnp.where(keep, s, -1e30)
        parts = []
        for h in range(4):
            sh = s[:, 128 * h : 128 * h + 128]
            e = jnp.exp2((sh - jnp.max(sh, axis=1, keepdims=True)) * factor)
            parts.append((e / jnp.sum(e, axis=1, keepdims=True)).astype(BF))
        attn = jnp.concatenate(parts, axis=1)
        out = jnp.dot(attn, v4, preferred_element_type=F32)
        ctx_ref[128 * w : 128 * w + 128, :] = out.astype(BF)


def piece_copies(zi, part, own_w, own_ug, pieces, w_all, ug_all, sems):
    rows = own_w.shape[0]
    qr = rows // 4
    steps = len(pieces) // 4 + 1
    w_copies, u_copies = [], []

    def place(src, dst, to):
        at = sems.at[len(w_copies) + len(u_copies)]
        to.append(pltpu.make_async_copy(src, dst, at))

    base = pl.multiple_of(zi * rows, 128)
    place(own_w, w_all.at[pl.ds(base, rows), :], w_copies)
    place(own_ug, ug_all.at[:, pl.ds(base, rows)], u_copies)
    for k in range(1, steps):
        shard = lax.rem(zi - k + steps, steps)
        base = pl.multiple_of(shard * rows, 128)
        for bits, piece in zip((0, 2, 1, 3), pieces[4 * k - 4 : 4 * k]):
            from_part = part ^ bits
            row = pl.multiple_of(base + from_part * qr, 32)
            place(piece.at[pl.ds(0, qr), :], w_all.at[pl.ds(row, qr), :], w_copies)
            for j in range(4):
                urow = pl.multiple_of((4 * from_part + j) * 16, 16)
                place(
                    piece.at[pl.ds(qr, 16), pl.ds(j * rows, rows)],
                    ug_all.at[pl.ds(urow, 16), pl.ds(base, rows)],
                    u_copies,
                )
    return w_copies, u_copies


def split3(x):
    hi = x.astype(BF).astype(F32)
    mid = (x - hi).astype(BF).astype(F32)
    return hi, mid, x - hi - mid


def loss_block(value, rows):
    hi, mid, lo = split3(value)
    lane = iota((rows, 128), 1)
    return jnp.where(lane == 0, hi, jnp.where(lane == 1, mid, jnp.where(lane == 2, lo, 0.0)))


def forward_kernel(place_ref, lat_ref, var_ref, *refs):
    ctx_refs, refs = refs[:CHUNKS], refs[CHUNKS:]
    extras, refs = refs[:4], refs[4:]
    (own_w, own_ug), refs = refs[:2], refs[2:]
    pieces, refs = refs[:PIECES], refs[PIECES:]
    ts, refs = refs[:4], refs[4:]
    normed_ref, inv_ref, dfc_ref, hidden_ref, w_all, ug_all, term, sems = refs
    zi, lat_place = place_ref[0], place_ref[1]
    w_copies, u_copies = piece_copies(zi, lat_place, own_w, own_ug, pieces, w_all, ug_all, sems)
    for c in w_copies + u_copies:
        c.start()
    tokens, width = normed_ref.shape
    span = dfc_ref.shape[1]
    extra = jnp.concatenate(
        [e[32 * w : 32 * w + 32, :] for w in range(2) for e in extras], axis=0
    ).astype(F32)
    goal, valid = extra[:, :span], extra[:, span : span + 1]
    token = iota((tokens, 1), 0)
    row = (token // 4) % 4 + jnp.where((token // 32) % 4 >= 2, 4, 0)
    lat_w = jnp.zeros((tokens, 1), F32)
    for r in range(8):
        lat_w = jnp.where(row == r, lat_ref[lat_place * 8 + r], lat_w)
    lane = iota((1, span), 1) // (span // var_ref.shape[0])
    var_w = jnp.zeros((1, span), F32)
    for n in range(var_ref.shape[0]):
        var_w = jnp.where(lane == n, var_ref[n], var_w)
    weight = lat_w * valid * var_w
    for c in w_copies:
        c.wait()
    part = width // CHUNKS
    mixed = jnp.dot(ctx_refs[0][...], w_all[0:part, :], preferred_element_type=F32)
    for g in range(1, CHUNKS):
        rows_g = w_all[g * part : (g + 1) * part, :]
        mixed += jnp.dot(ctx_refs[g][...], rows_g, preferred_element_type=F32)
    centre = jnp.mean(mixed, axis=-1, keepdims=True)
    off = mixed - centre
    inv = lax.rsqrt(jnp.mean(off * off, axis=-1, keepdims=True) + 1e-05)
    normed = off * inv
    normed_ref[...] = normed
    inv_ref[...] = jnp.broadcast_to(inv, inv_ref.shape)
    for c in u_copies:
        c.wait()
    gain = ug_all[pl.ds(span, 16), :][0:1].astype(F32)
    hidden_ref[...] = (normed * gain).astype(BF)
    field = lax.dot_general(
        hidden_ref[...], ug_all[0:span, :], (((1,), (1,)), ((), ())), preferred_element_type=F32
    )
    misfit = field - goal
    dfc = (2.0 * weight * misfit).astype(BF)
    dfc_ref[...] = dfc
    term[...] = lax.dot_general(
        dfc, hidden_ref[...], (((0,), (0,)), ((), ())), preferred_element_type=F32
    )
    loss = jnp.sum(jnp.sum(weight * misfit * misfit, axis=1, keepdims=True), axis=0, keepdims=True)
    rows = ts[0].shape[0]
    block = loss_block(loss, rows).astype(BF)
    for b, ref in enumerate(ts):
        at = pl.multiple_of((lat_place ^ b) * rows, 8)
        ref[:, :width] = term[pl.ds(at, rows), :].astype(BF)
        ref[:, width:] = block


def backward_kernel(place_ref, normed_ref, inv_ref, dfc_ref, own_w, own_ug, *refs):
    pieces, (out_ref, w_all, ug_all, sems) = refs[:PIECES], refs[PIECES:]
    zi, part = place_ref[0], place_ref[1]
    w_copies, u_copies = piece_copies(zi, part, own_w, own_ug, pieces, w_all, ug_all, sems)
    for c in u_copies + w_copies:
        c.start()
    tokens, width = normed_ref.shape
    span = dfc_ref.shape[1]
    for c in u_copies:
        c.wait()
    gain = ug_all[pl.ds(span, 16), :][0:1].astype(F32)
    g = jnp.dot(dfc_ref[...], ug_all[0:span, :], preferred_element_type=F32) * gain
    normed = normed_ref[...]
    mean_g = jnp.mean(g, axis=-1, keepdims=True)
    mean_gn = jnp.mean(g * normed, axis=-1, keepdims=True)
    dmixed = ((g - mean_g - normed * mean_gn) * inv_ref[:, 0:1]).astype(BF)
    place = iota((tokens, tokens), 0)
    row, col, level = (place // 8) % 8, place % 8, place // 64
    quad = jnp.where(row >= 4, 2, 0) + jnp.where(col >= 4, 1, 0)
    source = (level // 2) * 128 + quad * 32 + (level % 2) * 16 + (row % 4) * 4 + col % 4
    pick = (iota((tokens, tokens), 1) == source).astype(F32).astype(BF)
    dnat = jnp.dot(pick, dmixed, preferred_element_type=F32).astype(BF)
    for c in w_copies:
        c.wait()
    out = lax.dot_general(dnat, w_all[...], (((1,), (1,)), ((), ())), preferred_element_type=F32)
    out_ref[...] = out.astype(BF)


def add4(a, b, c, d):
    return (a[...].astype(F32) + b[...].astype(F32)) + (c[...].astype(F32) + d[...].astype(F32))


def lat_sum_kernel(place_ref, a, b, c, d, z0, z1, z2, z3, loss_ref, total_ref):
    total_ref[...] = add4(a, b, c, d)
    zi = place_ref[0]
    rows, width = z0.shape
    for k, ref in enumerate((z0, z1, z2, z3)):
        at = pl.multiple_of((zi ^ k) * width, 128)
        ref[...] = total_ref[:, pl.ds(at, width)].astype(BF)
    loss = jnp.sum(total_ref[0:1, 4 * width :], axis=1, keepdims=True)
    loss_ref[...] = jnp.broadcast_to(loss, loss_ref.shape)


def dp_sum_kernel(loss_ref, a, b, c, d, o_ref):
    rows, width = a.shape
    o_ref[0:rows, :] = add4(a, b, c, d).astype(BF)
    block = loss_block(loss_ref[0:1, 0:1], o_ref.shape[0] - rows)
    zeros = jnp.zeros((block.shape[0], width - 128), F32)
    o_ref[rows:, :] = jnp.concatenate([block, zeros], axis=1).astype(BF)


def join_kernel(counts, place_ref, *refs):
    pieces, (o_ref, loss_ref) = refs[:8], refs[8:]
    lat_place = place_ref[1]
    rows = o_ref.shape[0] // 4
    for a in range(4):
        at = pl.multiple_of((lat_place ^ a) * rows, 8)
        both = [pieces[2 * a + b][0:rows, :].astype(F32) for b in range(2)]
        o_ref[pl.ds(at, rows), :] = (both[0] + both[1]) / counts[0]
    sums = [
        jnp.sum(p[rows : rows + 1, 0:128].astype(F32), axis=1, keepdims=True) for p in pieces[:2]
    ]
    loss_ref[...] = jnp.broadcast_to((sums[0] + sums[1]) / counts[1], loss_ref.shape)


def swap(array, axis, bit):
    return lax.ppermute(array, axis, [(i, i ^ bit) for i in range(lax.axis_size(axis))])


def shape(dims, dtype):
    return jax.ShapeDtypeStruct(dims, dtype)


def shards(projected, targets, valid_cells, w_out, unpatch_matrix, norm_gain, var_weight):
    dp, lat, lon = lax.axis_size("dp"), lax.axis_size("lat"), lax.axis_size("lon")
    rows, width = w_out.shape
    levels = projected.shape[1]
    span = unpatch_matrix.shape[1]
    tokens = levels * 64
    quarter = tokens // 4
    part = width // CHUNKS
    lat_place = lax.axis_index("lat")
    place = jnp.stack([lax.axis_index("dp"), lat_place]).astype(jnp.int32)
    last = (lat_place == lat - 1).astype(jnp.int32).reshape(1)
    lat_total = 8 * lat
    angle = math.pi * ((np.arange(lat_total) + 0.5) / lat_total - 0.5)
    cosine = np.cos(angle)
    lat_table = jnp.asarray(np.roll(cosine / cosine.mean(), -4), F32)
    barrier = lax.optimization_barrier

    ug, payload = pl.pallas_call(
        payload_kernel,
        out_shape=[shape((UGROWS, rows), BF), shape((rows // 4 + 16, width), BF)],
        in_specs=[SMEM, HBM, HBM, VMEM],
        out_specs=[VMEM] * 2,
        scratch_shapes=[pltpu.VMEM((span, rows), BF), pltpu.SemaphoreType.DMA((2,))],
        compiler_params=params(62),
        name="payload",
    )(place, w_out, unpatch_matrix.T, norm_gain)
    ring1 = from_behind(payload, "dp", 1)

    widths = [3 * part] * (CHUNKS - 1) + [3 * part + EXTRA]
    packed = pl.pallas_call(
        pack_kernel,
        out_shape=[shape((quarter, w), BF) for w in widths for _ in range(4)],
        in_specs=[HBM] * 3,
        out_specs=[VMEM] * (4 * CHUNKS),
        scratch_shapes=[
            pltpu.VMEM((levels, 8, 8, 3 * width), BF),
            pltpu.VMEM((levels, 8, 8, span), BF),
            pltpu.VMEM((8, 8), jnp.int32),
            pltpu.SemaphoreType.DMA((3 * CHUNKS + 2,)),
        ],
        compiler_params=params(60),
        name="pack",
    )(projected.reshape(levels, 8, 8, 3 * width), targets.reshape(levels, 8, 8, span), valid_cells)
    corner = [
        (a * lon + b, ((a - 1) % lat) * lon + (b - 1) % lon) for a in range(lat) for b in range(lon)
    ]
    tiles = []
    for g in range(CHUNKS):
        own, east, south, diag = packed[4 * g : 4 * g + 4]
        tiles.append(
            [
                own,
                from_behind(east, "lon", -1),
                from_behind(south, "lat", -1),
                lax.ppermute(diag, ("lat", "lon"), corner),
            ]
        )
    groups = part // 128

    def attend(chunk):
        specs = [
            pl.BlockSpec((quarter, 128), lambda g, i=i: (0, i * groups + g)) for i in range(3)
        ]
        return pl.pallas_call(
            attention_kernel,
            grid=(groups,),
            out_shape=shape((tokens, part), BF),
            in_specs=[SMEM] + specs * 4,
            out_specs=pl.BlockSpec((tokens, 128), lambda g: (0, g)),
            compiler_params=params(8),
            name="attention",
        )(last, *[t for t in chunk for _ in range(3)])

    ring1_after, *tiles[0] = barrier((ring1, *tiles[0]))
    ring2 = from_behind(ring1_after, "dp", 1)
    across1 = swap(ring1, "lat", 2)
    ctx0 = attend(tiles[0])
    ring2_after, across1, ctx0, *tiles[1] = barrier((ring2, across1, ctx0, *tiles[1]))
    ring3 = from_behind(ring2_after, "dp", 1)
    across2 = swap(ring2, "lat", 2)
    ctx1 = attend(tiles[1])
    ring3_after, across2, ctx1, *tiles[2] = barrier((ring3, across2, ctx1, *tiles[2]))
    across3 = swap(ring3_after, "lat", 2)
    ctx2 = attend(tiles[2])
    pieces = []
    for ring, across in ((ring1, across1), (ring2, across2), (ring3, across3)):
        pieces += [ring, across, swap(ring, "lat", 1), swap(across, "lat", 1)]

    piece = span // lat
    extra_spec = pl.BlockSpec((quarter, EXTRA), lambda i: (0, 3 * part // EXTRA))
    copies = 2 + PIECES * 5
    assembly = [
        pltpu.VMEM((dp * rows, width), BF),
        pltpu.VMEM((UGROWS, dp * rows), BF),
    ]
    *terms, normed, inv, dfc = pl.pallas_call(
        forward_kernel,
        grid=(1,),
        out_shape=[shape((piece, width + 128), BF)] * 4
        + [shape((tokens, width), F32), shape((tokens, 128), F32), shape((tokens, span), BF)],
        in_specs=[SMEM] * 3 + [VMEM] * CHUNKS + [extra_spec] * 4 + [HBM] + [ANY] * (1 + PIECES),
        out_specs=[VMEM] * 7,
        scratch_shapes=[pltpu.VMEM((tokens, width), BF)]
        + assembly
        + [pltpu.VMEM((span, width), F32), pltpu.SemaphoreType.DMA((copies,))],
        compiler_params=params(28),
        name="forward",
    )(place, lat_table, var_weight, ctx0, ctx1, ctx2, *tiles[2], w_out, ug, *pieces)

    terms = [terms[0]] + [swap(terms[b], "lat", b) for b in (1, 2, 3)]
    grad_context = pl.pallas_call(
        backward_kernel,
        out_shape=shape((tokens, width), BF),
        in_specs=[SMEM] + [VMEM] * 3 + [HBM] + [ANY] * (1 + PIECES),
        out_specs=VMEM,
        scratch_shapes=assembly + [pltpu.SemaphoreType.DMA((copies,))],
        compiler_params=params(24),
        name="backward",
    )(place, normed, inv, dfc, w_out, ug, *pieces)
    *terms, grad_context = barrier((*terms, grad_context))

    *parts, loss = pl.pallas_call(
        lat_sum_kernel,
        out_shape=[shape((piece, rows), BF)] * 4 + [shape((8, 128), F32)],
        in_specs=[SMEM] + [VMEM] * 4,
        out_specs=[VMEM] * 5,
        scratch_shapes=[pltpu.VMEM((piece, width + 128), F32)],
        compiler_params=params(4),
        name="lat_sum",
    )(place, *terms)
    parts = [parts[0]] + [swap(parts[k], "dp", k) for k in (1, 2, 3)]
    mine = pl.pallas_call(
        dp_sum_kernel,
        out_shape=shape((piece + 8, rows), BF),
        in_specs=[VMEM] * 5,
        out_specs=VMEM,
        compiler_params=params(4),
        name="dp_sum",
    )(loss, *parts)
    plane = [mine]
    for a in range(4):
        for b in range(2):
            if a or b:
                pairs = [
                    (i * lon + j, (i ^ a) * lon + (j ^ b)) for i in range(lat) for j in range(lon)
                ]
                plane.append(lax.ppermute(mine, ("lat", "lon"), pairs))
    count = levels * lat_total * 8 * lon
    counts = (float(count), float(count * (span // var_weight.shape[0])))
    joined, loss = pl.pallas_call(
        lambda *refs: join_kernel(counts, *refs),
        out_shape=[shape((span, rows), F32), shape((1, 1), F32)],
        in_specs=[SMEM] + [VMEM] * 8,
        out_specs=[VMEM] * 2,
        compiler_params=params(4),
        name="join",
    )(place, *plane)
    return grad_context.reshape(1, levels, 8, 8, width), joined.T, loss.reshape(1)


def solution(mesh):
    placed = (
        P("dp", None, "lat", "lon", None),
        P("dp", None, "lat", "lon", None),
        P("lat", "lon"),
        P("dp", None),
        P("dp", None),
        P("dp"),
        P(),
    )
    fits = mesh.shape["dp"] == 4 and mesh.shape["lat"] == 4 and mesh.shape["lon"] == 2

    def program(*arrays):
        body = shards if fits else general_shards
        return jax.shard_map(
            body,
            mesh=mesh,
            in_specs=placed,
            out_specs=(P("dp", None, "lat", "lon", None), P("dp", None), P("dp")),
            check_vma=False,
        )(*arrays)

    return program
```

```python
import functools
import math

import jax
import jax.numpy as jnp
import numpy as np
from jax import lax
from jax.experimental import pallas as pl
from jax.experimental.pallas import tpu as pltpu
from jax.sharding import PartitionSpec as P

HEADS = 48
HDIM = 32
WLEV = 2
BF = jnp.bfloat16
F32 = jnp.float32
EXTRA = 256
UGROWS = 256
CHUNKS = (1, 4, 4, 3)
WITH_EXTRA = 2
PIECES = 12
VMEM = pl.BlockSpec(memory_space=pltpu.VMEM)
SMEM = pl.BlockSpec(memory_space=pltpu.SMEM)
ANY = pl.BlockSpec(memory_space=pl.ANY)
HBM = pl.BlockSpec(memory_space=pltpu.HBM)


def from_behind(array, axis, by):
    length = lax.axis_size(axis)
    return lax.ppermute(array, axis, [(i, (i + by) % length) for i in range(length)])


def general_shards(projected, targets, valid_cells, w_out, unpatch_matrix, norm_gain, var_weight):
    tile_side = projected.shape[2]
    half_side = tile_side // 2
    levels = projected.shape[1]
    model_width = w_out.shape[1]
    predicted_span = unpatch_matrix.shape[1]
    lat_total = tile_side * lax.axis_size("lat")
    lon_total = tile_side * lax.axis_size("lon")
    lat_place = lax.axis_index("lat")
    moved = from_behind(
        (projected[:, :, :, :half_side], targets[:, :, :, :half_side], valid_cells[:, :half_side]),
        "lon",
        -1,
    )
    strip_proj = jnp.concatenate([projected[:, :, :, half_side:], moved[0]], axis=3)
    strip_goal = jnp.concatenate([targets[:, :, :, half_side:], moved[1]], axis=3)
    strip_valid = jnp.concatenate([valid_cells[:, half_side:], moved[2]], axis=1)
    moved_rows = from_behind(
        (strip_proj[:, :, :half_side], strip_goal[:, :, :half_side], strip_valid[:half_side]),
        "lat",
        -1,
    )
    local_proj = jnp.concatenate([strip_proj[:, :, half_side:], moved_rows[0]], axis=2)
    shard_reference = jnp.concatenate([strip_goal[:, :, half_side:], moved_rows[1]], axis=2)
    local_valid = jnp.concatenate([strip_valid[half_side:], moved_rows[2]], axis=0).astype(F32)
    win_count = levels // WLEV
    tokw = WLEV * tile_side * tile_side
    windows = local_proj.reshape(win_count, tokw, 3 * model_width)
    rows_here = lat_place * tile_side + jnp.arange(tile_side)
    region_rows = (rows_here >= lat_total - half_side).astype(jnp.int32)
    region = jnp.broadcast_to(region_rows[None, :, None], (WLEV, tile_side, tile_side)).reshape(-1)
    allowed = region[:, None] == region[None, :]
    queries = windows[..., :model_width].reshape(win_count, tokw, HEADS, -1)
    key_heads = windows[..., model_width : 2 * model_width].reshape(win_count, tokw, HEADS, -1)
    value_heads = windows[..., 2 * model_width :].reshape(win_count, tokw, HEADS, -1)
    scores = jnp.einsum("wqhd,wkhd->whqk", queries, key_heads, preferred_element_type=F32)
    scores = scores * (1.0 / math.sqrt(HDIM))
    scores = jnp.where(allowed[None, None], scores, -1e30)
    row_peak = jnp.max(scores, axis=-1, keepdims=True)
    lifted = jnp.exp(scores - row_peak)
    attn = (lifted / jnp.sum(lifted, axis=-1, keepdims=True)).astype(BF)
    context = jnp.einsum("whqk,wkhd->wqhd", attn, value_heads, preferred_element_type=F32)
    context = context.astype(BF).reshape(win_count * tokw, model_width)
    element_total = win_count * tokw
    out_all, unprojected_pieces, gain_all = (
        lax.all_gather(w_out, "dp", axis=0, tiled=True),
        lax.all_gather(unpatch_matrix, "dp", axis=0, tiled=True),
        lax.all_gather(norm_gain, "dp", axis=0, tiled=True),
    )
    mixed_rows = jnp.dot(context, out_all, preferred_element_type=F32)
    centre = jnp.mean(mixed_rows, axis=-1, keepdims=True)
    spread = jnp.mean((mixed_rows - centre) ** 2, axis=-1, keepdims=True)
    inv_spread = lax.rsqrt(spread + 1e-05)
    normed = (mixed_rows - centre) * inv_spread
    gain_f = gain_all.astype(F32)
    latent_activation = (normed * gain_f).astype(BF)
    prediction_field = jnp.dot(latent_activation, unprojected_pieces, preferred_element_type=F32)
    prediction_misfit = prediction_field - shard_reference.reshape(
        element_total, predicted_span
    ).astype(F32)
    all_rows = jnp.arange(lat_total).astype(F32)
    cosine_mean = jnp.mean(jnp.cos(math.pi * ((all_rows + 0.5) / lat_total - 0.5)))
    initial_rows = ((rows_here + half_side) % lat_total).astype(F32)
    lat_here = jnp.cos(math.pi * ((initial_rows + 0.5) / lat_total - 0.5)) / cosine_mean
    element_factor = jnp.broadcast_to(
        lat_here[None, :, None] * local_valid[None], (levels, tile_side, tile_side)
    ).reshape(element_total, 1)
    variable_factor = jnp.repeat(var_weight, predicted_span // var_weight.shape[0])[None, :]
    shard_penalty = jnp.sum(
        element_factor * variable_factor * prediction_misfit * prediction_misfit
    ) / (levels * lat_total * lon_total * (predicted_span // var_weight.shape[0]))
    prediction_gradient = (2.0 * element_factor * variable_factor * prediction_misfit).astype(BF)
    grad_shard = lax.psum_scatter(
        jnp.einsum(
            "td,to->do", latent_activation, prediction_gradient, preferred_element_type=F32
        ).astype(BF),
        "dp",
        scatter_dimension=0,
        tiled=True,
    ).astype(F32)
    grad_sum, loss_sum = lax.psum((grad_shard, shard_penalty), ("lat", "lon"))
    grad_recovery = grad_sum / (levels * lat_total * lon_total)
    grad_hidden = jnp.einsum(
        "to,do->td", prediction_gradient, unprojected_pieces, preferred_element_type=F32
    )
    scaled_grad = grad_hidden * gain_f
    grad_mixed = inv_spread * (
        scaled_grad
        - jnp.mean(scaled_grad, axis=-1, keepdims=True)
        - normed * jnp.mean(scaled_grad * normed, axis=-1, keepdims=True)
    )
    grad_mixed = grad_mixed.astype(BF)
    grad_context = jnp.einsum("tj,ij->ti", grad_mixed, out_all, preferred_element_type=F32)
    grad_context = grad_context.astype(BF).reshape(1, levels, tile_side, tile_side, model_width)
    return (grad_context, grad_recovery, loss_sum.reshape(1))


def params(mib):
    return pltpu.CompilerParams(vmem_limit_bytes=mib << 20)


def iota(shape, dim):
    return lax.broadcasted_iota(jnp.int32, shape, dim)


def chunk_copies(x_ref, x_in, groups, sems, at):
    width = x_ref.shape[-1] // 3
    unit = width // sum(CHUNKS)
    copies = []
    to = 0
    for g in groups:
        part = unit * CHUNKS[g]
        base = unit * sum(CHUNKS[:g])
        for i in range(3):
            source = (slice(None),) * 3 + (pl.ds(i * width + base, part),)
            target = (slice(None),) * 3 + (pl.ds(to, part),)
            sem = sems.at[at + len(copies)]
            copies.append(
                (to, part, pltpu.make_async_copy(x_ref.at[source], x_in.at[target], sem))
            )
            to += part
    return copies


def quadrant_pick(count):
    place = iota((count, count), 0)
    quad, rest = place // (count // 4), place % (count // 4)
    row = (rest // 4) % 4 + jnp.where(quad < 2, 4, 0)
    col = rest % 4 + jnp.where(quad % 2 == 0, 4, 0)
    source = (rest // 16) * 64 + row * 8 + col
    return (iota((count, count), 1) == source).astype(F32).astype(BF)


def pack_chunk(pick, x_in, copies, outs):
    count = pick.shape[0]
    quarter = count // 4
    for i, (at, part, copy) in enumerate(copies):
        copy.wait()
        tokens = x_in[:, :, :, at : at + part].reshape(count, part)
        out = jnp.dot(pick, tokens, preferred_element_type=F32).astype(BF)
        for q in range(4):
            outs[q][:, i * part : (i + 1) * part] = out[q * quarter : (q + 1) * quarter]


def lead_kernel(
    place_ref, w_ref, unpatch_ref, gain_ref, x_ref, ug_ref, payload_ref, o0, o1, o2, o3,
    u_in, x_in, sems,
):
    part = place_ref[1]
    rows, width = w_ref.shape
    qr = rows // 4
    span = unpatch_ref.shape[0]
    start = pl.multiple_of(part * qr, 32)
    w_copy = pltpu.make_async_copy(
        w_ref.at[pl.ds(start, qr), :], payload_ref.at[pl.ds(0, qr), :], sems.at[0]
    )
    u_copy = pltpu.make_async_copy(unpatch_ref, u_in, sems.at[1])
    u_copy.start()
    w_copy.start()
    copies = chunk_copies(x_ref, x_in, (0,), sems, 2)
    for _, _, c in copies:
        c.start()
    pick = quadrant_pick(x_ref.shape[0] * 64)
    gain = jnp.broadcast_to(gain_ref[...].astype(F32).reshape(1, rows), (16, rows)).astype(BF)
    ug_ref[pl.ds(span, 16), :] = gain
    ug_ref[pl.ds(span + 16, UGROWS - span - 16), :] = jnp.zeros((UGROWS - span - 16, rows), BF)
    u_copy.wait()
    ug_ref[pl.ds(0, span), :] = u_in[...]
    for j in range(4):
        at = pl.multiple_of((4 * part + j) * 16, 16)
        payload_ref[pl.ds(qr, 16), pl.ds(j * rows, rows)] = ug_ref[pl.ds(at, 16), :]
    pack_chunk(pick, x_in, copies, (o0, o1, o2, o3))
    w_copy.wait()


def pack_kernel(x_ref, t_ref, valid_ref, *refs):
    later = range(1, len(CHUNKS))
    outs = refs[: 4 * len(later)]
    x_in, t_in, v_in, sems = refs[4 * len(later) :]
    span = t_ref.shape[-1]
    count = x_ref.shape[0] * 64
    quarter = count // 4
    copies = chunk_copies(x_ref, x_in, later, sems, 2)
    t_copy = pltpu.make_async_copy(t_ref, t_in, sems.at[0])
    v_copy = pltpu.make_async_copy(valid_ref, v_in, sems.at[1])
    for _, _, c in copies:
        c.start()
    t_copy.start()
    v_copy.start()
    pick = quadrant_pick(count)
    for n in range(len(later)):
        pack_chunk(pick, x_in, copies[3 * n : 3 * n + 3], outs[4 * n : 4 * n + 4])
    t_copy.wait()
    v_copy.wait()
    goal = jnp.dot(pick, t_in[...].reshape(count, span), preferred_element_type=F32)
    token = iota((count, 8), 0)
    row_hot = ((token // 8) % 8 == iota((count, 8), 1)).astype(F32)
    by_row = jnp.dot(row_hot, v_in[...].astype(F32), preferred_element_type=F32)
    mine = token % 8 == iota((count, 8), 1)
    natural = jnp.sum(jnp.where(mine, by_row, 0.0), axis=1, keepdims=True)
    spread = jnp.broadcast_to(natural, (count, 128)).astype(BF)
    column = jnp.dot(pick, spread, preferred_element_type=F32)
    extra = jnp.concatenate([goal, column[:, : EXTRA - span]], axis=1).astype(BF)
    for q in range(4):
        ref = outs[4 * (WITH_EXTRA - 1) + q]
        ref[:, ref.shape[1] - EXTRA :] = extra[q * quarter : (q + 1) * quarter]


def attention_kernel(last_ref, *refs):
    ctx_ref = refs[12]
    tiles = [refs[3 * q : 3 * q + 3] for q in range(4)]
    is_last = last_ref[0] == 1
    side = iota((128, 512), 0) // 64
    same = side == (iota((128, 512), 1) % 128) // 64
    keep = jnp.logical_or(same, jnp.logical_not(is_last))
    head = iota((128, 128), 1) // HDIM
    factor = math.log2(math.e) / math.sqrt(HDIM)
    for w in range(2):
        q, k, v = [
            jnp.concatenate([tiles[c][i][32 * w : 32 * w + 32] for c in range(4)], axis=0)
            for i in range(3)
        ]
        zero = jnp.zeros_like(k)
        k4 = jnp.concatenate([jnp.where(head == h, k, zero) for h in range(4)], axis=0)
        v4 = jnp.concatenate([jnp.where(head == h, v, zero) for h in range(4)], axis=0)
        s = lax.dot_general(q, k4, (((1,), (1,)), ((), ())), preferred_element_type=F32)
        s = jnp.where(keep, s, -1e30)
        parts = []
        for h in range(4):
            sh = s[:, 128 * h : 128 * h + 128]
            e = jnp.exp2((sh - jnp.max(sh, axis=1, keepdims=True)) * factor)
            parts.append((e / jnp.sum(e, axis=1, keepdims=True)).astype(BF))
        attn = jnp.concatenate(parts, axis=1)
        out = jnp.dot(attn, v4, preferred_element_type=F32)
        ctx_ref[128 * w : 128 * w + 128, :] = out.astype(BF)


def piece_copies(zi, part, own_w, own_ug, pieces, w_all, ug_all, sems):
    rows = own_w.shape[0]
    qr = rows // 4
    steps = len(pieces) // 4 + 1
    w_copies, u_copies = [], []

    def place(src, dst, to):
        at = sems.at[len(w_copies) + len(u_copies)]
        to.append(pltpu.make_async_copy(src, dst, at))

    base = pl.multiple_of(zi * rows, 128)
    place(own_w, w_all.at[pl.ds(base, rows), :], w_copies)
    place(own_ug, ug_all.at[:, pl.ds(base, rows)], u_copies)
    for k in range(1, steps):
        shard = lax.rem(zi - k + steps, steps)
        base = pl.multiple_of(shard * rows, 128)
        for bits, piece in zip((0, 2, 1, 3), pieces[4 * k - 4 : 4 * k]):
            from_part = part ^ bits
            row = pl.multiple_of(base + from_part * qr, 32)
            place(piece.at[pl.ds(0, qr), :], w_all.at[pl.ds(row, qr), :], w_copies)
            for j in range(4):
                urow = pl.multiple_of((4 * from_part + j) * 16, 16)
                place(
                    piece.at[pl.ds(qr, 16), pl.ds(j * rows, rows)],
                    ug_all.at[pl.ds(urow, 16), pl.ds(base, rows)],
                    u_copies,
                )
    return w_copies, u_copies


def split3(x):
    hi = x.astype(BF).astype(F32)
    mid = (x - hi).astype(BF).astype(F32)
    return hi, mid, x - hi - mid


def loss_block(value, rows):
    hi, mid, lo = split3(value)
    lane = iota((rows, 128), 1)
    return jnp.where(lane == 0, hi, jnp.where(lane == 1, mid, jnp.where(lane == 2, lo, 0.0)))


def forward_kernel(place_ref, lat_ref, var_ref, *refs):
    ctx_refs, refs = refs[: len(CHUNKS)], refs[len(CHUNKS) :]
    extras, refs = refs[:4], refs[4:]
    (own_w, own_ug), refs = refs[:2], refs[2:]
    pieces, refs = refs[:PIECES], refs[PIECES:]
    ts, refs = refs[:4], refs[4:]
    normed_ref, inv_ref, dfc_ref, hidden_ref, w_all, ug_all, term, sems = refs
    zi, lat_place = place_ref[0], place_ref[1]
    w_copies, u_copies = piece_copies(zi, lat_place, own_w, own_ug, pieces, w_all, ug_all, sems)
    for c in w_copies + u_copies:
        c.start()
    tokens, width = normed_ref.shape
    span = dfc_ref.shape[1]
    extra = jnp.concatenate(
        [e[32 * w : 32 * w + 32, :] for w in range(2) for e in extras], axis=0
    ).astype(F32)
    goal, valid = extra[:, :span], extra[:, span : span + 1]
    token = iota((tokens, 1), 0)
    row = (token // 4) % 4 + jnp.where((token // 32) % 4 >= 2, 4, 0)
    lat_w = jnp.zeros((tokens, 1), F32)
    for r in range(8):
        lat_w = jnp.where(row == r, lat_ref[lat_place * 8 + r], lat_w)
    lane = iota((1, span), 1) // (span // var_ref.shape[0])
    var_w = jnp.zeros((1, span), F32)
    for n in range(var_ref.shape[0]):
        var_w = jnp.where(lane == n, var_ref[n], var_w)
    weight = lat_w * valid * var_w
    for c in w_copies:
        c.wait()
    at = 0
    mixed = None
    for ref in ctx_refs:
        part = ref.shape[1]
        term_g = jnp.dot(ref[...], w_all[at : at + part, :], preferred_element_type=F32)
        mixed = term_g if mixed is None else mixed + term_g
        at += part
    centre = jnp.mean(mixed, axis=-1, keepdims=True)
    off = mixed - centre
    inv = lax.rsqrt(jnp.mean(off * off, axis=-1, keepdims=True) + 1e-05)
    normed = off * inv
    normed_ref[...] = normed
    inv_ref[...] = jnp.broadcast_to(inv, inv_ref.shape)
    for c in u_copies:
        c.wait()
    gain = ug_all[pl.ds(span, 16), :][0:1].astype(F32)
    hidden_ref[...] = (normed * gain).astype(BF)
    field = lax.dot_general(
        hidden_ref[...], ug_all[0:span, :], (((1,), (1,)), ((), ())), preferred_element_type=F32
    )
    misfit = field - goal
    dfc = (2.0 * weight * misfit).astype(BF)
    dfc_ref[...] = dfc
    term[...] = lax.dot_general(
        dfc, hidden_ref[...], (((0,), (0,)), ((), ())), preferred_element_type=F32
    )
    loss = jnp.sum(jnp.sum(weight * misfit * misfit, axis=1, keepdims=True), axis=0, keepdims=True)
    rows = ts[0].shape[0]
    block = loss_block(loss, rows).astype(BF)
    for b, ref in enumerate(ts):
        at = pl.multiple_of((lat_place ^ b) * rows, 8)
        ref[:, :width] = term[pl.ds(at, rows), :].astype(BF)
        ref[:, width:] = block


def backward_kernel(place_ref, normed_ref, inv_ref, dfc_ref, own_w, own_ug, *refs):
    pieces, (out_ref, w_all, ug_all, sems) = refs[:PIECES], refs[PIECES:]
    zi, part = place_ref[0], place_ref[1]
    w_copies, u_copies = piece_copies(zi, part, own_w, own_ug, pieces, w_all, ug_all, sems)
    for c in u_copies + w_copies:
        c.start()
    tokens, width = normed_ref.shape
    span = dfc_ref.shape[1]
    for c in u_copies:
        c.wait()
    gain = ug_all[pl.ds(span, 16), :][0:1].astype(F32)
    g = jnp.dot(dfc_ref[...], ug_all[0:span, :], preferred_element_type=F32) * gain
    normed = normed_ref[...]
    mean_g = jnp.mean(g, axis=-1, keepdims=True)
    mean_gn = jnp.mean(g * normed, axis=-1, keepdims=True)
    dmixed = ((g - mean_g - normed * mean_gn) * inv_ref[:, 0:1]).astype(BF)
    place = iota((tokens, tokens), 0)
    row, col, level = (place // 8) % 8, place % 8, place // 64
    quad = jnp.where(row >= 4, 2, 0) + jnp.where(col >= 4, 1, 0)
    source = (level // 2) * 128 + quad * 32 + (level % 2) * 16 + (row % 4) * 4 + col % 4
    pick = (iota((tokens, tokens), 1) == source).astype(F32).astype(BF)
    dnat = jnp.dot(pick, dmixed, preferred_element_type=F32).astype(BF)
    for c in w_copies:
        c.wait()
    out = lax.dot_general(dnat, w_all[...], (((1,), (1,)), ((), ())), preferred_element_type=F32)
    out_ref[...] = out.astype(BF)


def add4(a, b, c, d):
    return (a[...].astype(F32) + b[...].astype(F32)) + (c[...].astype(F32) + d[...].astype(F32))


def lat_sum_kernel(place_ref, a, b, c, d, z0, z1, z2, z3, loss_ref, total_ref):
    total_ref[...] = add4(a, b, c, d)
    zi = place_ref[0]
    rows, width = z0.shape
    for k, ref in enumerate((z0, z1, z2, z3)):
        at = pl.multiple_of((zi ^ k) * width, 128)
        ref[...] = total_ref[:, pl.ds(at, width)].astype(BF)
    loss = jnp.sum(total_ref[0:1, 4 * width :], axis=1, keepdims=True)
    loss_ref[...] = jnp.broadcast_to(loss, loss_ref.shape)


def dp_sum_kernel(loss_ref, a, b, c, d, o_ref):
    rows, width = a.shape
    o_ref[0:rows, :] = add4(a, b, c, d).astype(BF)
    block = loss_block(loss_ref[0:1, 0:1], o_ref.shape[0] - rows)
    zeros = jnp.zeros((block.shape[0], width - 128), F32)
    o_ref[rows:, :] = jnp.concatenate([block, zeros], axis=1).astype(BF)


def join_kernel(counts, place_ref, *refs):
    pieces, (o_ref, loss_ref) = refs[:8], refs[8:]
    lat_place = place_ref[1]
    rows = o_ref.shape[0] // 4
    for a in range(4):
        at = pl.multiple_of((lat_place ^ a) * rows, 8)
        both = [pieces[2 * a + b][0:rows, :].astype(F32) for b in range(2)]
        o_ref[pl.ds(at, rows), :] = (both[0] + both[1]) / counts[0]
    sums = [
        jnp.sum(p[rows : rows + 1, 0:128].astype(F32), axis=1, keepdims=True) for p in pieces[:2]
    ]
    loss_ref[...] = jnp.broadcast_to((sums[0] + sums[1]) / counts[1], loss_ref.shape)


def swap(array, axis, bit):
    return lax.ppermute(array, axis, [(i, i ^ bit) for i in range(lax.axis_size(axis))])


def shape(dims, dtype):
    return jax.ShapeDtypeStruct(dims, dtype)


def shards(projected, targets, valid_cells, w_out, unpatch_matrix, norm_gain, var_weight):
    dp, lat, lon = lax.axis_size("dp"), lax.axis_size("lat"), lax.axis_size("lon")
    rows, width = w_out.shape
    levels = projected.shape[1]
    span = unpatch_matrix.shape[1]
    tokens = levels * 64
    quarter = tokens // 4
    lat_place = lax.axis_index("lat")
    place = jnp.stack([lax.axis_index("dp"), lat_place]).astype(jnp.int32)
    last = (lat_place == lat - 1).astype(jnp.int32).reshape(1)
    lat_total = 8 * lat
    angle = math.pi * ((np.arange(lat_total) + 0.5) / lat_total - 0.5)
    cosine = np.cos(angle)
    lat_table = jnp.asarray(np.roll(cosine / cosine.mean(), -4), F32)
    barrier = lax.optimization_barrier

    x = projected.reshape(levels, 8, 8, 3 * width)
    parts_of = [width // sum(CHUNKS) * n for n in CHUNKS]
    widths = [3 * part + (EXTRA if g == WITH_EXTRA else 0) for g, part in enumerate(parts_of)]
    ug, payload, *packed = pl.pallas_call(
        lead_kernel,
        out_shape=[shape((UGROWS, rows), BF), shape((rows // 4 + 16, width), BF)]
        + [shape((quarter, widths[0]), BF)] * 4,
        in_specs=[SMEM, HBM, HBM, VMEM, HBM],
        out_specs=[VMEM] * 6,
        scratch_shapes=[
            pltpu.VMEM((span, rows), BF),
            pltpu.VMEM((levels, 8, 8, widths[0]), BF),
            pltpu.SemaphoreType.DMA((5,)),
        ],
        compiler_params=params(62),
        name="lead",
    )(place, w_out, unpatch_matrix.T, norm_gain, x)
    ring1 = from_behind(payload, "dp", 1)
    later = sum(parts_of[1:])
    packed += pl.pallas_call(
        pack_kernel,
        out_shape=[shape((quarter, w), BF) for w in widths[1:] for _ in range(4)],
        in_specs=[HBM] * 3,
        out_specs=[VMEM] * (4 * len(CHUNKS) - 4),
        scratch_shapes=[
            pltpu.VMEM((levels, 8, 8, 3 * later), BF),
            pltpu.VMEM((levels, 8, 8, span), BF),
            pltpu.VMEM((8, 8), jnp.int32),
            pltpu.SemaphoreType.DMA((3 * len(CHUNKS) - 1,)),
        ],
        compiler_params=params(62),
        name="pack",
    )(x, targets.reshape(levels, 8, 8, span), valid_cells)
    corner = [
        (a * lon + b, ((a - 1) % lat) * lon + (b - 1) % lon) for a in range(lat) for b in range(lon)
    ]

    def halo(east, south, diag):
        return [
            from_behind(east, "lon", -1),
            from_behind(south, "lat", -1),
            lax.ppermute(diag, ("lat", "lon"), corner),
        ]

    def attend(*chunk):
        part = chunk[0].shape[1] // 384 * 128
        groups = part // 128
        specs = [
            pl.BlockSpec((quarter, 128), lambda g, i=i: (0, i * groups + g)) for i in range(3)
        ]
        return pl.pallas_call(
            attention_kernel,
            grid=(groups,),
            out_shape=shape((tokens, part), BF),
            in_specs=[SMEM] + specs * 4,
            out_specs=pl.BlockSpec((tokens, 128), lambda g: (0, g)),
            compiler_params=params(8),
            name="attention",
        )(last, *[t for t in chunk for _ in range(3)])

    owns = packed[0::4]
    sends = [packed[4 * g + 1 : 4 * g + 4] for g in range(len(CHUNKS))]
    tiles0 = halo(*sends[0])
    ring1_after, sends[1][0], *tiles0 = barrier((ring1, sends[1][0], *tiles0))
    ring2 = from_behind(ring1_after, "dp", 1)
    across1 = swap(ring1, "lat", 2)
    *sends[1], tiles0[0] = barrier((*sends[1], tiles0[0]))
    tiles1 = halo(*sends[1])
    ctx0 = attend(owns[0], *tiles0)
    ring2_after, ctx0, *tiles1 = barrier((ring2, ctx0, *tiles1))
    ring3 = from_behind(ring2_after, "dp", 1)
    across2 = swap(ring2, "lat", 2)
    *sends[2], across1, tiles1[0] = barrier((*sends[2], across1, tiles1[0]))
    tiles2 = halo(*sends[2])
    ctx1 = attend(owns[1], *tiles1)
    ring3_after, ctx1, *tiles2 = barrier((ring3, ctx1, *tiles2))
    across3 = swap(ring3_after, "lat", 2)
    *sends[3], across2, tiles2[0] = barrier((*sends[3], across2, tiles2[0]))
    tiles3 = halo(*sends[3])
    ctx2 = attend(owns[2], *tiles2)
    ctx3 = attend(owns[3], *tiles3)
    across3, ctx2, ctx3 = barrier((across3, ctx2, ctx3))
    pieces = []
    for ring, across in ((ring1, across1), (ring2, across2), (ring3, across3)):
        pieces += [ring, across, swap(ring, "lat", 1), swap(across, "lat", 1)]

    piece = span // lat
    extra_spec = pl.BlockSpec((quarter, EXTRA), lambda i: (0, 3 * parts_of[WITH_EXTRA] // EXTRA))
    copies = 2 + PIECES * 5
    assembly = [
        pltpu.VMEM((dp * rows, width), BF),
        pltpu.VMEM((UGROWS, dp * rows), BF),
    ]
    *terms, normed, inv, dfc = pl.pallas_call(
        forward_kernel,
        grid=(1,),
        out_shape=[shape((piece, width + 128), BF)] * 4
        + [shape((tokens, width), F32), shape((tokens, 128), F32), shape((tokens, span), BF)],
        in_specs=[SMEM] * 3 + [VMEM] * len(CHUNKS) + [extra_spec] * 4 + [HBM] + [ANY] * (1 + PIECES),
        out_specs=[VMEM] * 7,
        scratch_shapes=[pltpu.VMEM((tokens, width), BF)]
        + assembly
        + [pltpu.VMEM((span, width), F32), pltpu.SemaphoreType.DMA((copies,))],
        compiler_params=params(28),
        name="forward",
    )(place, lat_table, var_weight, ctx0, ctx1, ctx2, ctx3, owns[2], *tiles2, w_out, ug, *pieces)

    terms = [terms[0]] + [swap(terms[b], "lat", b) for b in (1, 2, 3)]
    grad_context = pl.pallas_call(
        backward_kernel,
        out_shape=shape((tokens, width), BF),
        in_specs=[SMEM] + [VMEM] * 3 + [HBM] + [ANY] * (1 + PIECES),
        out_specs=VMEM,
        scratch_shapes=assembly + [pltpu.SemaphoreType.DMA((copies,))],
        compiler_params=params(24),
        name="backward",
    )(place, normed, inv, dfc, w_out, ug, *pieces)
    *terms, grad_context = barrier((*terms, grad_context))

    *parts, loss = pl.pallas_call(
        lat_sum_kernel,
        out_shape=[shape((piece, rows), BF)] * 4 + [shape((8, 128), F32)],
        in_specs=[SMEM] + [VMEM] * 4,
        out_specs=[VMEM] * 5,
        scratch_shapes=[pltpu.VMEM((piece, width + 128), F32)],
        compiler_params=params(4),
        name="lat_sum",
    )(place, *terms)
    parts = [parts[0]] + [swap(parts[k], "dp", k) for k in (1, 2, 3)]
    mine = pl.pallas_call(
        dp_sum_kernel,
        out_shape=shape((piece + 8, rows), BF),
        in_specs=[VMEM] * 5,
        out_specs=VMEM,
        compiler_params=params(4),
        name="dp_sum",
    )(loss, *parts)
    plane = [mine]
    for a in range(4):
        for b in range(2):
            if a or b:
                pairs = [
                    (i * lon + j, (i ^ a) * lon + (j ^ b)) for i in range(lat) for j in range(lon)
                ]
                plane.append(lax.ppermute(mine, ("lat", "lon"), pairs))
    count = levels * lat_total * 8 * lon
    counts = (float(count), float(count * (span // var_weight.shape[0])))
    joined, loss = pl.pallas_call(
        lambda *refs: join_kernel(counts, *refs),
        out_shape=[shape((span, rows), F32), shape((1, 1), F32)],
        in_specs=[SMEM] + [VMEM] * 8,
        out_specs=[VMEM] * 2,
        compiler_params=params(4),
        name="join",
    )(place, *plane)
    return grad_context.reshape(1, levels, 8, 8, width), joined.T, loss.reshape(1)


def solution(mesh):
    placed = (
        P("dp", None, "lat", "lon", None),
        P("dp", None, "lat", "lon", None),
        P("lat", "lon"),
        P("dp", None),
        P("dp", None),
        P("dp"),
        P(),
    )
    fits = mesh.shape["dp"] == 4 and mesh.shape["lat"] == 4 and mesh.shape["lon"] == 2

    def program(*arrays):
        body = shards if fits else general_shards
        return jax.shard_map(
            body,
            mesh=mesh,
            in_specs=placed,
            out_specs=(P("dp", None, "lat", "lon", None), P("dp", None), P("dp")),
            check_vma=False,
        )(*arrays)

    return program
```

```python
import functools
import math

import jax
import jax.numpy as jnp
import numpy as np
from jax import lax
from jax.experimental import pallas as pl
from jax.experimental.pallas import tpu as pltpu
from jax.sharding import PartitionSpec as P

HEADS = 48
HDIM = 32
WLEV = 2
BF = jnp.bfloat16
F32 = jnp.float32
EXTRA = 256
UGROWS = 256
CHUNKS = (1, 4, 4, 3)
WITH_EXTRA = 2
PIECES = 12
VMEM = pl.BlockSpec(memory_space=pltpu.VMEM)
SMEM = pl.BlockSpec(memory_space=pltpu.SMEM)
ANY = pl.BlockSpec(memory_space=pl.ANY)
HBM = pl.BlockSpec(memory_space=pltpu.HBM)


def from_behind(array, axis, by):
    length = lax.axis_size(axis)
    return lax.ppermute(array, axis, [(i, (i + by) % length) for i in range(length)])


def general_shards(projected, targets, valid_cells, w_out, unpatch_matrix, norm_gain, var_weight):
    tile_side = projected.shape[2]
    half_side = tile_side // 2
    levels = projected.shape[1]
    model_width = w_out.shape[1]
    predicted_span = unpatch_matrix.shape[1]
    lat_total = tile_side * lax.axis_size("lat")
    lon_total = tile_side * lax.axis_size("lon")
    lat_place = lax.axis_index("lat")
    moved = from_behind(
        (projected[:, :, :, :half_side], targets[:, :, :, :half_side], valid_cells[:, :half_side]),
        "lon",
        -1,
    )
    strip_proj = jnp.concatenate([projected[:, :, :, half_side:], moved[0]], axis=3)
    strip_goal = jnp.concatenate([targets[:, :, :, half_side:], moved[1]], axis=3)
    strip_valid = jnp.concatenate([valid_cells[:, half_side:], moved[2]], axis=1)
    moved_rows = from_behind(
        (strip_proj[:, :, :half_side], strip_goal[:, :, :half_side], strip_valid[:half_side]),
        "lat",
        -1,
    )
    local_proj = jnp.concatenate([strip_proj[:, :, half_side:], moved_rows[0]], axis=2)
    shard_reference = jnp.concatenate([strip_goal[:, :, half_side:], moved_rows[1]], axis=2)
    local_valid = jnp.concatenate([strip_valid[half_side:], moved_rows[2]], axis=0).astype(F32)
    win_count = levels // WLEV
    tokw = WLEV * tile_side * tile_side
    windows = local_proj.reshape(win_count, tokw, 3 * model_width)
    rows_here = lat_place * tile_side + jnp.arange(tile_side)
    region_rows = (rows_here >= lat_total - half_side).astype(jnp.int32)
    region = jnp.broadcast_to(region_rows[None, :, None], (WLEV, tile_side, tile_side)).reshape(-1)
    allowed = region[:, None] == region[None, :]
    queries = windows[..., :model_width].reshape(win_count, tokw, HEADS, -1)
    key_heads = windows[..., model_width : 2 * model_width].reshape(win_count, tokw, HEADS, -1)
    value_heads = windows[..., 2 * model_width :].reshape(win_count, tokw, HEADS, -1)
    scores = jnp.einsum("wqhd,wkhd->whqk", queries, key_heads, preferred_element_type=F32)
    scores = scores * (1.0 / math.sqrt(HDIM))
    scores = jnp.where(allowed[None, None], scores, -1e30)
    row_peak = jnp.max(scores, axis=-1, keepdims=True)
    lifted = jnp.exp(scores - row_peak)
    attn = (lifted / jnp.sum(lifted, axis=-1, keepdims=True)).astype(BF)
    context = jnp.einsum("whqk,wkhd->wqhd", attn, value_heads, preferred_element_type=F32)
    context = context.astype(BF).reshape(win_count * tokw, model_width)
    element_total = win_count * tokw
    out_all, unprojected_pieces, gain_all = (
        lax.all_gather(w_out, "dp", axis=0, tiled=True),
        lax.all_gather(unpatch_matrix, "dp", axis=0, tiled=True),
        lax.all_gather(norm_gain, "dp", axis=0, tiled=True),
    )
    mixed_rows = jnp.dot(context, out_all, preferred_element_type=F32)
    centre = jnp.mean(mixed_rows, axis=-1, keepdims=True)
    spread = jnp.mean((mixed_rows - centre) ** 2, axis=-1, keepdims=True)
    inv_spread = lax.rsqrt(spread + 1e-05)
    normed = (mixed_rows - centre) * inv_spread
    gain_f = gain_all.astype(F32)
    latent_activation = (normed * gain_f).astype(BF)
    prediction_field = jnp.dot(latent_activation, unprojected_pieces, preferred_element_type=F32)
    prediction_misfit = prediction_field - shard_reference.reshape(
        element_total, predicted_span
    ).astype(F32)
    all_rows = jnp.arange(lat_total).astype(F32)
    cosine_mean = jnp.mean(jnp.cos(math.pi * ((all_rows + 0.5) / lat_total - 0.5)))
    initial_rows = ((rows_here + half_side) % lat_total).astype(F32)
    lat_here = jnp.cos(math.pi * ((initial_rows + 0.5) / lat_total - 0.5)) / cosine_mean
    element_factor = jnp.broadcast_to(
        lat_here[None, :, None] * local_valid[None], (levels, tile_side, tile_side)
    ).reshape(element_total, 1)
    variable_factor = jnp.repeat(var_weight, predicted_span // var_weight.shape[0])[None, :]
    shard_penalty = jnp.sum(
        element_factor * variable_factor * prediction_misfit * prediction_misfit
    ) / (levels * lat_total * lon_total * (predicted_span // var_weight.shape[0]))
    prediction_gradient = (2.0 * element_factor * variable_factor * prediction_misfit).astype(BF)
    grad_shard = lax.psum_scatter(
        jnp.einsum(
            "td,to->do", latent_activation, prediction_gradient, preferred_element_type=F32
        ).astype(BF),
        "dp",
        scatter_dimension=0,
        tiled=True,
    ).astype(F32)
    grad_sum, loss_sum = lax.psum((grad_shard, shard_penalty), ("lat", "lon"))
    grad_recovery = grad_sum / (levels * lat_total * lon_total)
    grad_hidden = jnp.einsum(
        "to,do->td", prediction_gradient, unprojected_pieces, preferred_element_type=F32
    )
    scaled_grad = grad_hidden * gain_f
    grad_mixed = inv_spread * (
        scaled_grad
        - jnp.mean(scaled_grad, axis=-1, keepdims=True)
        - normed * jnp.mean(scaled_grad * normed, axis=-1, keepdims=True)
    )
    grad_mixed = grad_mixed.astype(BF)
    grad_context = jnp.einsum("tj,ij->ti", grad_mixed, out_all, preferred_element_type=F32)
    grad_context = grad_context.astype(BF).reshape(1, levels, tile_side, tile_side, model_width)
    return (grad_context, grad_recovery, loss_sum.reshape(1))


def params(mib):
    return pltpu.CompilerParams(vmem_limit_bytes=mib << 20)


def iota(shape, dim):
    return lax.broadcasted_iota(jnp.int32, shape, dim)


def chunk_copies(x_ref, x_in, groups, sems, at):
    width = x_ref.shape[-1] // 3
    unit = width // sum(CHUNKS)
    copies = []
    to = 0
    for g in groups:
        part = unit * CHUNKS[g]
        base = unit * sum(CHUNKS[:g])
        for i in range(3):
            source = (slice(None),) * 3 + (pl.ds(i * width + base, part),)
            target = (slice(None),) * 3 + (pl.ds(to, part),)
            sem = sems.at[at + len(copies)]
            copies.append(
                (to, part, pltpu.make_async_copy(x_ref.at[source], x_in.at[target], sem))
            )
            to += part
    return copies


def quadrant_pick(count):
    place = iota((count, count), 0)
    quad, rest = place // (count // 4), place % (count // 4)
    row = (rest // 4) % 4 + jnp.where(quad < 2, 4, 0)
    col = rest % 4 + jnp.where(quad % 2 == 0, 4, 0)
    source = (rest // 16) * 64 + row * 8 + col
    return (iota((count, count), 1) == source).astype(F32).astype(BF)


def pack_chunk(pick, x_in, copies, outs):
    count = pick.shape[0]
    quarter = count // 4
    for i, (at, part, copy) in enumerate(copies):
        copy.wait()
        tokens = x_in[:, :, :, at : at + part].reshape(count, part)
        out = jnp.dot(pick, tokens, preferred_element_type=F32).astype(BF)
        for q in range(4):
            outs[q][:, i * part : (i + 1) * part] = out[q * quarter : (q + 1) * quarter]


def lead_kernel(
    w_ref, unpatch_ref, gain_ref, x_ref, ug_ref, payload_ref, o0, o1, o2, o3,
    u_in, x_in, sems,
):
    part = lax.axis_index("lat")
    rows, width = w_ref.shape
    qr = rows // 4
    span = unpatch_ref.shape[0]
    start = pl.multiple_of(part * qr, 32)
    w_copy = pltpu.make_async_copy(
        w_ref.at[pl.ds(start, qr), :], payload_ref.at[pl.ds(0, qr), :], sems.at[0]
    )
    u_copy = pltpu.make_async_copy(unpatch_ref, u_in, sems.at[1])
    u_copy.start()
    w_copy.start()
    copies = chunk_copies(x_ref, x_in, (0,), sems, 2)
    for _, _, c in copies:
        c.start()
    pick = quadrant_pick(x_ref.shape[0] * 64)
    gain = jnp.broadcast_to(gain_ref[...].astype(F32).reshape(1, rows), (16, rows)).astype(BF)
    ug_ref[pl.ds(span, 16), :] = gain
    ug_ref[pl.ds(span + 16, UGROWS - span - 16), :] = jnp.zeros((UGROWS - span - 16, rows), BF)
    u_copy.wait()
    ug_ref[pl.ds(0, span), :] = u_in[...]
    for j in range(4):
        at = pl.multiple_of((4 * part + j) * 16, 16)
        payload_ref[pl.ds(qr, 16), pl.ds(j * rows, rows)] = ug_ref[pl.ds(at, 16), :]
    pack_chunk(pick, x_in, copies, (o0, o1, o2, o3))
    w_copy.wait()


def pack_kernel(x_ref, t_ref, valid_ref, *refs):
    later = range(1, len(CHUNKS))
    outs = refs[: 4 * len(later)]
    x_in, t_in, v_in, sems = refs[4 * len(later) :]
    span = t_ref.shape[-1]
    count = x_ref.shape[0] * 64
    quarter = count // 4
    copies = chunk_copies(x_ref, x_in, later, sems, 2)
    t_copy = pltpu.make_async_copy(t_ref, t_in, sems.at[0])
    v_copy = pltpu.make_async_copy(valid_ref, v_in, sems.at[1])
    for _, _, c in copies:
        c.start()
    t_copy.start()
    v_copy.start()
    pick = quadrant_pick(count)
    for n in range(len(later)):
        pack_chunk(pick, x_in, copies[3 * n : 3 * n + 3], outs[4 * n : 4 * n + 4])
    t_copy.wait()
    v_copy.wait()
    goal = jnp.dot(pick, t_in[...].reshape(count, span), preferred_element_type=F32)
    token = iota((count, 8), 0)
    row_hot = ((token // 8) % 8 == iota((count, 8), 1)).astype(F32)
    by_row = jnp.dot(row_hot, v_in[...].astype(F32), preferred_element_type=F32)
    mine = token % 8 == iota((count, 8), 1)
    natural = jnp.sum(jnp.where(mine, by_row, 0.0), axis=1, keepdims=True)
    spread = jnp.broadcast_to(natural, (count, 128)).astype(BF)
    column = jnp.dot(pick, spread, preferred_element_type=F32)
    extra = jnp.concatenate([goal, column[:, : EXTRA - span]], axis=1).astype(BF)
    for q in range(4):
        ref = outs[4 * (WITH_EXTRA - 1) + q]
        ref[:, ref.shape[1] - EXTRA :] = extra[q * quarter : (q + 1) * quarter]


def attention_kernel(own_ref, east_ref, south_ref, diag_ref, ctx_ref):
    tiles = (own_ref, east_ref, south_ref, diag_ref)
    part = ctx_ref.shape[1]
    is_last = lax.axis_index("lat") == lax.axis_size("lat") - 1
    same = (iota((512, 128), 0) % 128) // 64 == iota((512, 128), 1) // 64
    bias = jnp.where(jnp.logical_or(same, jnp.logical_not(is_last)), 0.0, -1e30)
    head = iota((128, 128), 1) // HDIM
    factor = math.log2(math.e) / math.sqrt(HDIM)
    for at in range(0, part, 128):
        for w in range(2):
            q, k, v = [
                jnp.concatenate(
                    [t[32 * w : 32 * w + 32, i * part + at : i * part + at + 128] for t in tiles],
                    axis=0,
                )
                for i in range(3)
            ]
            zero = jnp.zeros_like(k)
            k4 = jnp.concatenate([jnp.where(head == h, k, zero) for h in range(4)], axis=0)
            v4 = jnp.concatenate([jnp.where(head == h, v, zero) for h in range(4)], axis=0)
            s = lax.dot_general(k4, q, (((1,), (1,)), ((), ())), preferred_element_type=F32)
            s = s + bias
            parts = []
            for h in range(4):
                sh = s[128 * h : 128 * h + 128]
                e = jnp.exp2((sh - jnp.max(sh, axis=0, keepdims=True)) * factor)
                parts.append((e * (1.0 / jnp.sum(e, axis=0, keepdims=True))).astype(BF))
            attn = jnp.concatenate(parts, axis=0)
            out = lax.dot_general(attn, v4, (((0,), (0,)), ((), ())), preferred_element_type=F32)
            ctx_ref[128 * w : 128 * w + 128, at : at + 128] = out.astype(BF)


def piece_copies(zi, part, own_w, own_ug, pieces, w_all, ug_all, sems):
    rows = own_w.shape[0]
    qr = rows // 4
    steps = len(pieces) // 4 + 1
    w_copies, u_copies = [], []

    def place(src, dst, to):
        at = sems.at[len(w_copies) + len(u_copies)]
        to.append(pltpu.make_async_copy(src, dst, at))

    base = pl.multiple_of(zi * rows, 128)
    place(own_w, w_all.at[pl.ds(base, rows), :], w_copies)
    place(own_ug, ug_all.at[:, pl.ds(base, rows)], u_copies)
    for k in range(1, steps):
        shard = lax.rem(zi - k + steps, steps)
        base = pl.multiple_of(shard * rows, 128)
        for bits, piece in zip((0, 2, 1, 3), pieces[4 * k - 4 : 4 * k]):
            from_part = part ^ bits
            row = pl.multiple_of(base + from_part * qr, 32)
            place(piece.at[pl.ds(0, qr), :], w_all.at[pl.ds(row, qr), :], w_copies)
            for j in range(4):
                urow = pl.multiple_of((4 * from_part + j) * 16, 16)
                place(
                    piece.at[pl.ds(qr, 16), pl.ds(j * rows, rows)],
                    ug_all.at[pl.ds(urow, 16), pl.ds(base, rows)],
                    u_copies,
                )
    return w_copies, u_copies


def split3(x):
    hi = x.astype(BF).astype(F32)
    mid = (x - hi).astype(BF).astype(F32)
    return hi, mid, x - hi - mid


def loss_block(value, rows):
    hi, mid, lo = split3(value)
    lane = iota((rows, 128), 1)
    return jnp.where(lane == 0, hi, jnp.where(lane == 1, mid, jnp.where(lane == 2, lo, 0.0)))


def forward_kernel(lat_ref, var_ref, *refs):
    ctx_refs, refs = refs[: len(CHUNKS)], refs[len(CHUNKS) :]
    extras, refs = refs[:4], refs[4:]
    (own_w, own_ug), refs = refs[:2], refs[2:]
    pieces, refs = refs[:PIECES], refs[PIECES:]
    ts, refs = refs[:4], refs[4:]
    normed_ref, inv_ref, dfc_ref, hidden_ref, w_all, ug_all, term, sems = refs
    zi, lat_place = lax.axis_index("dp"), lax.axis_index("lat")
    w_copies, u_copies = piece_copies(zi, lat_place, own_w, own_ug, pieces, w_all, ug_all, sems)
    for c in w_copies + u_copies:
        c.start()
    tokens, width = normed_ref.shape
    span = dfc_ref.shape[1]
    extra = jnp.concatenate(
        [e[32 * w : 32 * w + 32, :] for w in range(2) for e in extras], axis=0
    ).astype(F32)
    goal, valid = extra[:, :span], extra[:, span : span + 1]
    token = iota((tokens, 1), 0)
    row = (token // 4) % 4 + jnp.where((token // 32) % 4 >= 2, 4, 0)
    lat_w = jnp.zeros((tokens, 1), F32)
    for r in range(8):
        lat_w = jnp.where(row == r, lat_ref[lat_place * 8 + r], lat_w)
    lane = iota((1, span), 1) // (span // var_ref.shape[0])
    var_w = jnp.zeros((1, span), F32)
    for n in range(var_ref.shape[0]):
        var_w = jnp.where(lane == n, var_ref[n], var_w)
    weight = lat_w * valid * var_w
    for c in w_copies:
        c.wait()
    at = 0
    mixed = None
    for ref in ctx_refs:
        part = ref.shape[1]
        term_g = jnp.dot(ref[...], w_all[at : at + part, :], preferred_element_type=F32)
        mixed = term_g if mixed is None else mixed + term_g
        at += part
    centre = jnp.mean(mixed, axis=-1, keepdims=True)
    off = mixed - centre
    inv = lax.rsqrt(jnp.mean(off * off, axis=-1, keepdims=True) + 1e-05)
    normed = off * inv
    normed_ref[...] = normed
    inv_ref[...] = jnp.broadcast_to(inv, inv_ref.shape)
    for c in u_copies:
        c.wait()
    gain = ug_all[pl.ds(span, 16), :][0:1].astype(F32)
    hidden_ref[...] = (normed * gain).astype(BF)
    field = lax.dot_general(
        hidden_ref[...], ug_all[0:span, :], (((1,), (1,)), ((), ())), preferred_element_type=F32
    )
    misfit = field - goal
    dfc = (2.0 * weight * misfit).astype(BF)
    dfc_ref[...] = dfc
    term[...] = lax.dot_general(
        dfc, hidden_ref[...], (((0,), (0,)), ((), ())), preferred_element_type=F32
    )
    loss = jnp.sum(jnp.sum(weight * misfit * misfit, axis=1, keepdims=True), axis=0, keepdims=True)
    rows = ts[0].shape[0]
    block = loss_block(loss, rows).astype(BF)
    for b, ref in enumerate(ts):
        at = pl.multiple_of((lat_place ^ b) * rows, 8)
        ref[:, :width] = term[pl.ds(at, rows), :].astype(BF)
        ref[:, width:] = block


def backward_kernel(normed_ref, inv_ref, dfc_ref, own_w, own_ug, *refs):
    pieces, (out_ref, w_all, ug_all, sems) = refs[:PIECES], refs[PIECES:]
    zi, part = lax.axis_index("dp"), lax.axis_index("lat")
    w_copies, u_copies = piece_copies(zi, part, own_w, own_ug, pieces, w_all, ug_all, sems)
    for c in u_copies + w_copies:
        c.start()
    tokens, width = normed_ref.shape
    span = dfc_ref.shape[1]
    for c in u_copies:
        c.wait()
    gain = ug_all[pl.ds(span, 16), :][0:1].astype(F32)
    g = jnp.dot(dfc_ref[...], ug_all[0:span, :], preferred_element_type=F32) * gain
    normed = normed_ref[...]
    mean_g = jnp.mean(g, axis=-1, keepdims=True)
    mean_gn = jnp.mean(g * normed, axis=-1, keepdims=True)
    dmixed = ((g - mean_g - normed * mean_gn) * inv_ref[:, 0:1]).astype(BF)
    place = iota((tokens, tokens), 0)
    row, col, level = (place // 8) % 8, place % 8, place // 64
    quad = jnp.where(row >= 4, 2, 0) + jnp.where(col >= 4, 1, 0)
    source = (level // 2) * 128 + quad * 32 + (level % 2) * 16 + (row % 4) * 4 + col % 4
    pick = (iota((tokens, tokens), 1) == source).astype(F32).astype(BF)
    dnat = jnp.dot(pick, dmixed, preferred_element_type=F32).astype(BF)
    for c in w_copies:
        c.wait()
    out = lax.dot_general(dnat, w_all[...], (((1,), (1,)), ((), ())), preferred_element_type=F32)
    out_ref[...] = out.astype(BF)


def add4(a, b, c, d):
    return (a[...].astype(F32) + b[...].astype(F32)) + (c[...].astype(F32) + d[...].astype(F32))


def lat_sum_kernel(a, b, c, d, z0, z1, z2, z3, loss_ref, total_ref):
    total_ref[...] = add4(a, b, c, d)
    zi = lax.axis_index("dp")
    rows, width = z0.shape
    for k, ref in enumerate((z0, z1, z2, z3)):
        at = pl.multiple_of((zi ^ k) * width, 128)
        ref[...] = total_ref[:, pl.ds(at, width)].astype(BF)
    loss = jnp.sum(total_ref[0:1, 4 * width :], axis=1, keepdims=True)
    loss_ref[...] = jnp.broadcast_to(loss, loss_ref.shape)


def dp_sum_kernel(loss_ref, a, b, c, d, o_ref):
    rows, width = a.shape
    o_ref[0:rows, :] = add4(a, b, c, d).astype(BF)
    block = loss_block(loss_ref[0:1, 0:1], o_ref.shape[0] - rows)
    zeros = jnp.zeros((block.shape[0], width - 128), F32)
    o_ref[rows:, :] = jnp.concatenate([block, zeros], axis=1).astype(BF)


def join_kernel(counts, *refs):
    pieces, (o_ref, loss_ref) = refs[:8], refs[8:]
    lat_place = lax.axis_index("lat")
    rows = o_ref.shape[0] // 4
    for a in range(4):
        at = pl.multiple_of((lat_place ^ a) * rows, 8)
        both = [pieces[2 * a + b][0:rows, :].astype(F32) for b in range(2)]
        o_ref[pl.ds(at, rows), :] = (both[0] + both[1]) / counts[0]
    sums = [
        jnp.sum(p[rows : rows + 1, 0:128].astype(F32), axis=1, keepdims=True) for p in pieces[:2]
    ]
    loss_ref[...] = jnp.broadcast_to((sums[0] + sums[1]) / counts[1], loss_ref.shape)


def swap(array, axis, bit):
    return lax.ppermute(array, axis, [(i, i ^ bit) for i in range(lax.axis_size(axis))])


def shape(dims, dtype):
    return jax.ShapeDtypeStruct(dims, dtype)


def shards(projected, targets, valid_cells, w_out, unpatch_matrix, norm_gain, var_weight):
    dp, lat, lon = lax.axis_size("dp"), lax.axis_size("lat"), lax.axis_size("lon")
    rows, width = w_out.shape
    levels = projected.shape[1]
    span = unpatch_matrix.shape[1]
    tokens = levels * 64
    quarter = tokens // 4
    lat_total = 8 * lat
    angle = math.pi * ((np.arange(lat_total) + 0.5) / lat_total - 0.5)
    cosine = np.cos(angle)
    lat_table = jnp.asarray(np.roll(cosine / cosine.mean(), -4), F32)
    barrier = lax.optimization_barrier

    x = projected.reshape(levels, 8, 8, 3 * width)
    parts_of = [width // sum(CHUNKS) * n for n in CHUNKS]
    widths = [3 * part + (EXTRA if g == WITH_EXTRA else 0) for g, part in enumerate(parts_of)]
    ug, payload, *packed = pl.pallas_call(
        lead_kernel,
        out_shape=[shape((UGROWS, rows), BF), shape((rows // 4 + 16, width), BF)]
        + [shape((quarter, widths[0]), BF)] * 4,
        in_specs=[HBM, HBM, VMEM, HBM],
        out_specs=[VMEM] * 6,
        scratch_shapes=[
            pltpu.VMEM((span, rows), BF),
            pltpu.VMEM((levels, 8, 8, widths[0]), BF),
            pltpu.SemaphoreType.DMA((5,)),
        ],
        compiler_params=params(62),
        name="lead",
    )(w_out, unpatch_matrix.T, norm_gain, x)
    ring1 = from_behind(payload, "dp", 1)
    later = sum(parts_of[1:])
    packed += pl.pallas_call(
        pack_kernel,
        out_shape=[shape((quarter, w), BF) for w in widths[1:] for _ in range(4)],
        in_specs=[HBM] * 3,
        out_specs=[VMEM] * (4 * len(CHUNKS) - 4),
        scratch_shapes=[
            pltpu.VMEM((levels, 8, 8, 3 * later), BF),
            pltpu.VMEM((levels, 8, 8, span), BF),
            pltpu.VMEM((8, 8), jnp.int32),
            pltpu.SemaphoreType.DMA((3 * len(CHUNKS) - 1,)),
        ],
        compiler_params=params(62),
        name="pack",
    )(x, targets.reshape(levels, 8, 8, span), valid_cells)
    corner = [
        (a * lon + b, ((a - 1) % lat) * lon + (b - 1) % lon) for a in range(lat) for b in range(lon)
    ]

    def halo(east, south, diag):
        return [
            from_behind(east, "lon", -1),
            from_behind(south, "lat", -1),
            lax.ppermute(diag, ("lat", "lon"), corner),
        ]

    def attend(*chunk):
        part = chunk[0].shape[1] // 384 * 128
        return pl.pallas_call(
            attention_kernel,
            out_shape=shape((tokens, part), BF),
            in_specs=[VMEM] * 4,
            out_specs=VMEM,
            compiler_params=params(8),
            name="attention",
        )(*chunk)

    owns = packed[0::4]
    sends = [packed[4 * g + 1 : 4 * g + 4] for g in range(len(CHUNKS))]
    tiles0 = halo(*sends[0])
    ring1_after, sends[1][0], *tiles0 = barrier((ring1, sends[1][0], *tiles0))
    ring2 = from_behind(ring1_after, "dp", 1)
    across1 = swap(ring1, "lat", 2)
    *sends[1], tiles0[0] = barrier((*sends[1], tiles0[0]))
    tiles1 = halo(*sends[1])
    ctx0 = attend(owns[0], *tiles0)
    ring2_after, ctx0, *tiles1 = barrier((ring2, ctx0, *tiles1))
    ring3 = from_behind(ring2_after, "dp", 1)
    across2 = swap(ring2, "lat", 2)
    *sends[2], across1, tiles1[0] = barrier((*sends[2], across1, tiles1[0]))
    tiles2 = halo(*sends[2])
    ctx1 = attend(owns[1], *tiles1)
    ring3_after, ctx1, *tiles2 = barrier((ring3, ctx1, *tiles2))
    across3 = swap(ring3_after, "lat", 2)
    *sends[3], tiles2[0] = barrier((*sends[3], tiles2[0]))
    tiles3 = halo(*sends[3])
    ctx2 = attend(owns[2], *tiles2)
    ring1, across1, tiles3[0] = barrier((ring1, across1, tiles3[0]))
    ctx3 = attend(owns[3], *tiles3)
    across3, ctx2, ctx3 = barrier((across3, ctx2, ctx3))
    pieces = []
    for ring, across in ((ring1, across1), (ring2, across2), (ring3, across3)):
        pieces += [ring, across, swap(ring, "lat", 1), swap(across, "lat", 1)]

    piece = span // lat
    extra_spec = pl.BlockSpec((quarter, EXTRA), lambda i: (0, 3 * parts_of[WITH_EXTRA] // EXTRA))
    copies = 2 + PIECES * 5
    assembly = [
        pltpu.VMEM((dp * rows, width), BF),
        pltpu.VMEM((UGROWS, dp * rows), BF),
    ]
    *terms, normed, inv, dfc = pl.pallas_call(
        forward_kernel,
        grid=(1,),
        out_shape=[shape((piece, width + 128), BF)] * 4
        + [shape((tokens, width), F32), shape((tokens, 128), F32), shape((tokens, span), BF)],
        in_specs=[SMEM] * 2 + [VMEM] * len(CHUNKS) + [extra_spec] * 4 + [HBM] + [ANY] * (1 + PIECES),
        out_specs=[VMEM] * 7,
        scratch_shapes=[pltpu.VMEM((tokens, width), BF)]
        + assembly
        + [pltpu.VMEM((span, width), F32), pltpu.SemaphoreType.DMA((copies,))],
        compiler_params=params(28),
        name="forward",
    )(lat_table, var_weight, ctx0, ctx1, ctx2, ctx3, owns[2], *tiles2, w_out, ug, *pieces)

    terms = [terms[0]] + [swap(terms[b], "lat", b) for b in (1, 2, 3)]
    grad_context = pl.pallas_call(
        backward_kernel,
        out_shape=shape((tokens, width), BF),
        in_specs=[VMEM] * 3 + [HBM] + [ANY] * (1 + PIECES),
        out_specs=VMEM,
        scratch_shapes=assembly + [pltpu.SemaphoreType.DMA((copies,))],
        compiler_params=params(24),
        name="backward",
    )(normed, inv, dfc, w_out, ug, *pieces)
    *terms, grad_context = barrier((*terms, grad_context))

    *parts, loss = pl.pallas_call(
        lat_sum_kernel,
        out_shape=[shape((piece, rows), BF)] * 4 + [shape((8, 128), F32)],
        in_specs=[VMEM] * 4,
        out_specs=[VMEM] * 5,
        scratch_shapes=[pltpu.VMEM((piece, width + 128), F32)],
        compiler_params=params(4),
        name="lat_sum",
    )(*terms)
    parts = [parts[0]] + [swap(parts[k], "dp", k) for k in (1, 2, 3)]
    mine = pl.pallas_call(
        dp_sum_kernel,
        out_shape=shape((piece + 8, rows), BF),
        in_specs=[VMEM] * 5,
        out_specs=VMEM,
        compiler_params=params(4),
        name="dp_sum",
    )(loss, *parts)
    plane = [mine]
    for a in range(4):
        for b in range(2):
            if a or b:
                pairs = [
                    (i * lon + j, (i ^ a) * lon + (j ^ b)) for i in range(lat) for j in range(lon)
                ]
                plane.append(lax.ppermute(mine, ("lat", "lon"), pairs))
    count = levels * lat_total * 8 * lon
    counts = (float(count), float(count * (span // var_weight.shape[0])))
    joined, loss = pl.pallas_call(
        lambda *refs: join_kernel(counts, *refs),
        out_shape=[shape((span, rows), F32), shape((1, 1), F32)],
        in_specs=[VMEM] * 8,
        out_specs=[VMEM] * 2,
        compiler_params=params(4),
        name="join",
    )(*plane)
    return grad_context.reshape(1, levels, 8, 8, width), joined.T, loss.reshape(1)


def solution(mesh):
    placed = (
        P("dp", None, "lat", "lon", None),
        P("dp", None, "lat", "lon", None),
        P("lat", "lon"),
        P("dp", None),
        P("dp", None),
        P("dp"),
        P(),
    )
    fits = mesh.shape["dp"] == 4 and mesh.shape["lat"] == 4 and mesh.shape["lon"] == 2

    def program(*arrays):
        body = shards if fits else general_shards
        return jax.shard_map(
            body,
            mesh=mesh,
            in_specs=placed,
            out_specs=(P("dp", None, "lat", "lon", None), P("dp", None), P("dp")),
            check_vma=False,
        )(*arrays)

    return program
```

```python
import functools
import math

import jax
import jax.numpy as jnp
import numpy as np
from jax import lax
from jax.experimental import pallas as pl
from jax.experimental.pallas import tpu as pltpu
from jax.sharding import PartitionSpec as P

HEADS = 48
HDIM = 32
WLEV = 2
BF = jnp.bfloat16
F32 = jnp.float32
EXTRA = 256
UGROWS = 256
PIECES = 12
VMEM = pl.BlockSpec(memory_space=pltpu.VMEM)
SMEM = pl.BlockSpec(memory_space=pltpu.SMEM)
ANY = pl.BlockSpec(memory_space=pl.ANY)
HBM = pl.BlockSpec(memory_space=pltpu.HBM)


def from_behind(array, axis, by):
    length = lax.axis_size(axis)
    return lax.ppermute(array, axis, [(i, (i + by) % length) for i in range(length)])


def general_shards(projected, targets, valid_cells, w_out, unpatch_matrix, norm_gain, var_weight):
    tile_side = projected.shape[2]
    half_side = tile_side // 2
    levels = projected.shape[1]
    model_width = w_out.shape[1]
    predicted_span = unpatch_matrix.shape[1]
    lat_total = tile_side * lax.axis_size("lat")
    lon_total = tile_side * lax.axis_size("lon")
    lat_place = lax.axis_index("lat")
    moved = from_behind(
        (projected[:, :, :, :half_side], targets[:, :, :, :half_side], valid_cells[:, :half_side]),
        "lon",
        -1,
    )
    strip_proj = jnp.concatenate([projected[:, :, :, half_side:], moved[0]], axis=3)
    strip_goal = jnp.concatenate([targets[:, :, :, half_side:], moved[1]], axis=3)
    strip_valid = jnp.concatenate([valid_cells[:, half_side:], moved[2]], axis=1)
    moved_rows = from_behind(
        (strip_proj[:, :, :half_side], strip_goal[:, :, :half_side], strip_valid[:half_side]),
        "lat",
        -1,
    )
    local_proj = jnp.concatenate([strip_proj[:, :, half_side:], moved_rows[0]], axis=2)
    shard_reference = jnp.concatenate([strip_goal[:, :, half_side:], moved_rows[1]], axis=2)
    local_valid = jnp.concatenate([strip_valid[half_side:], moved_rows[2]], axis=0).astype(F32)
    win_count = levels // WLEV
    tokw = WLEV * tile_side * tile_side
    windows = local_proj.reshape(win_count, tokw, 3 * model_width)
    rows_here = lat_place * tile_side + jnp.arange(tile_side)
    region_rows = (rows_here >= lat_total - half_side).astype(jnp.int32)
    region = jnp.broadcast_to(region_rows[None, :, None], (WLEV, tile_side, tile_side)).reshape(-1)
    allowed = region[:, None] == region[None, :]
    queries = windows[..., :model_width].reshape(win_count, tokw, HEADS, -1)
    key_heads = windows[..., model_width : 2 * model_width].reshape(win_count, tokw, HEADS, -1)
    value_heads = windows[..., 2 * model_width :].reshape(win_count, tokw, HEADS, -1)
    scores = jnp.einsum("wqhd,wkhd->whqk", queries, key_heads, preferred_element_type=F32)
    scores = scores * (1.0 / math.sqrt(HDIM))
    scores = jnp.where(allowed[None, None], scores, -1e30)
    row_peak = jnp.max(scores, axis=-1, keepdims=True)
    lifted = jnp.exp(scores - row_peak)
    attn = (lifted / jnp.sum(lifted, axis=-1, keepdims=True)).astype(BF)
    context = jnp.einsum("whqk,wkhd->wqhd", attn, value_heads, preferred_element_type=F32)
    context = context.astype(BF).reshape(win_count * tokw, model_width)
    element_total = win_count * tokw
    out_all, unprojected_pieces, gain_all = (
        lax.all_gather(w_out, "dp", axis=0, tiled=True),
        lax.all_gather(unpatch_matrix, "dp", axis=0, tiled=True),
        lax.all_gather(norm_gain, "dp", axis=0, tiled=True),
    )
    mixed_rows = jnp.dot(context, out_all, preferred_element_type=F32)
    centre = jnp.mean(mixed_rows, axis=-1, keepdims=True)
    spread = jnp.mean((mixed_rows - centre) ** 2, axis=-1, keepdims=True)
    inv_spread = lax.rsqrt(spread + 1e-05)
    normed = (mixed_rows - centre) * inv_spread
    gain_f = gain_all.astype(F32)
    latent_activation = (normed * gain_f).astype(BF)
    prediction_field = jnp.dot(latent_activation, unprojected_pieces, preferred_element_type=F32)
    prediction_misfit = prediction_field - shard_reference.reshape(
        element_total, predicted_span
    ).astype(F32)
    all_rows = jnp.arange(lat_total).astype(F32)
    cosine_mean = jnp.mean(jnp.cos(math.pi * ((all_rows + 0.5) / lat_total - 0.5)))
    initial_rows = ((rows_here + half_side) % lat_total).astype(F32)
    lat_here = jnp.cos(math.pi * ((initial_rows + 0.5) / lat_total - 0.5)) / cosine_mean
    element_factor = jnp.broadcast_to(
        lat_here[None, :, None] * local_valid[None], (levels, tile_side, tile_side)
    ).reshape(element_total, 1)
    variable_factor = jnp.repeat(var_weight, predicted_span // var_weight.shape[0])[None, :]
    shard_penalty = jnp.sum(
        element_factor * variable_factor * prediction_misfit * prediction_misfit
    ) / (levels * lat_total * lon_total * (predicted_span // var_weight.shape[0]))
    prediction_gradient = (2.0 * element_factor * variable_factor * prediction_misfit).astype(BF)
    grad_shard = lax.psum_scatter(
        jnp.einsum(
            "td,to->do", latent_activation, prediction_gradient, preferred_element_type=F32
        ).astype(BF),
        "dp",
        scatter_dimension=0,
        tiled=True,
    ).astype(F32)
    grad_sum, loss_sum = lax.psum((grad_shard, shard_penalty), ("lat", "lon"))
    grad_recovery = grad_sum / (levels * lat_total * lon_total)
    grad_hidden = jnp.einsum(
        "to,do->td", prediction_gradient, unprojected_pieces, preferred_element_type=F32
    )
    scaled_grad = grad_hidden * gain_f
    grad_mixed = inv_spread * (
        scaled_grad
        - jnp.mean(scaled_grad, axis=-1, keepdims=True)
        - normed * jnp.mean(scaled_grad * normed, axis=-1, keepdims=True)
    )
    grad_mixed = grad_mixed.astype(BF)
    grad_context = jnp.einsum("tj,ij->ti", grad_mixed, out_all, preferred_element_type=F32)
    grad_context = grad_context.astype(BF).reshape(1, levels, tile_side, tile_side, model_width)
    return (grad_context, grad_recovery, loss_sum.reshape(1))


def params(mib):
    return pltpu.CompilerParams(vmem_limit_bytes=mib << 20)


def iota(shape, dim):
    return lax.broadcasted_iota(jnp.int32, shape, dim)


def payload_kernel(w_ref, unpatch_ref, gain_ref, ug_ref, payload_ref, u_in, sems):
    part = lax.axis_index("lat")
    rows, width = w_ref.shape
    qr = rows // 4
    span = unpatch_ref.shape[0]
    start = pl.multiple_of(part * qr, 32)
    w_copy = pltpu.make_async_copy(
        w_ref.at[pl.ds(start, qr), :], payload_ref.at[pl.ds(0, qr), :], sems.at[0]
    )
    u_copy = pltpu.make_async_copy(unpatch_ref, u_in, sems.at[1])
    u_copy.start()
    w_copy.start()
    gain = jnp.broadcast_to(gain_ref[...].astype(F32).reshape(1, rows), (16, rows)).astype(BF)
    ug_ref[pl.ds(span, 16), :] = gain
    ug_ref[pl.ds(span + 16, UGROWS - span - 16), :] = jnp.zeros((UGROWS - span - 16, rows), BF)
    u_copy.wait()
    ug_ref[pl.ds(0, span), :] = u_in[...]
    for j in range(4):
        at = pl.multiple_of((4 * part + j) * 16, 16)
        payload_ref[pl.ds(qr, 16), pl.ds(j * rows, rows)] = ug_ref[pl.ds(at, 16), :]
    w_copy.wait()


def pack_kernel(x_ref, t_ref, valid_ref, o0, o1, o2, o3, x_in, t_in, v_in, sems):
    outs = (o0, o1, o2, o3)
    span = t_ref.shape[-1]
    count = x_ref.shape[0] * 64
    quarter = count // 4
    step = 512
    width = x_ref.shape[-1]
    copies = [
        pltpu.make_async_copy(t_ref, t_in, sems.at[0]),
        pltpu.make_async_copy(valid_ref, v_in, sems.at[1]),
    ]
    for at in range(0, width, step):
        lanes = (slice(None),) * 3 + (pl.ds(at, step),)
        copies.append(
            pltpu.make_async_copy(x_ref.at[lanes], x_in.at[lanes], sems.at[len(copies)])
        )
    for c in copies:
        c.start()
    place = iota((count, count), 0)
    quad, rest = place // quarter, place % quarter
    row = (rest // 4) % 4 + jnp.where(quad < 2, 4, 0)
    col = rest % 4 + jnp.where(quad % 2 == 0, 4, 0)
    source = (rest // 16) * 64 + row * 8 + col
    pick = (iota((count, count), 1) == source).astype(F32).astype(BF)
    copies[0].wait()
    copies[1].wait()
    goal = jnp.dot(pick, t_in[...].reshape(count, span), preferred_element_type=F32)
    token = iota((count, 8), 0)
    row_hot = ((token // 8) % 8 == iota((count, 8), 1)).astype(F32)
    by_row = jnp.dot(row_hot, v_in[...].astype(F32), preferred_element_type=F32)
    mine = token % 8 == iota((count, 8), 1)
    natural = jnp.sum(jnp.where(mine, by_row, 0.0), axis=1, keepdims=True)
    spread = jnp.broadcast_to(natural, (count, 128)).astype(BF)
    column = jnp.dot(pick, spread, preferred_element_type=F32)
    extra = jnp.concatenate([goal, column[:, : EXTRA - span]], axis=1).astype(BF)
    for q in range(4):
        outs[q][:, width:] = extra[q * quarter : (q + 1) * quarter]
    for n, at in enumerate(range(0, width, step)):
        copies[2 + n].wait()
        tokens = x_in[:, :, :, at : at + step].reshape(count, step)
        out = jnp.dot(pick, tokens, preferred_element_type=F32).astype(BF)
        for q in range(4):
            outs[q][:, at : at + step] = out[q * quarter : (q + 1) * quarter]


def attention_kernel(own_ref, east_ref, south_ref, diag_ref, ctx_ref):
    tiles = (own_ref, east_ref, south_ref, diag_ref)
    part = ctx_ref.shape[1]
    is_last = lax.axis_index("lat") == lax.axis_size("lat") - 1
    same = (iota((512, 128), 0) % 128) // 64 == iota((512, 128), 1) // 64
    bias = jnp.where(jnp.logical_or(same, jnp.logical_not(is_last)), 0.0, -1e30)
    head = iota((128, 128), 1) // HDIM
    factor = math.log2(math.e) / math.sqrt(HDIM)
    for at in range(0, part, 128):
        for w in range(2):
            q, k, v = [
                jnp.concatenate(
                    [t[32 * w : 32 * w + 32, i * part + at : i * part + at + 128] for t in tiles],
                    axis=0,
                )
                for i in range(3)
            ]
            zero = jnp.zeros_like(k)
            k4 = jnp.concatenate([jnp.where(head == h, k, zero) for h in range(4)], axis=0)
            v4 = jnp.concatenate([jnp.where(head == h, v, zero) for h in range(4)], axis=0)
            s = lax.dot_general(k4, q, (((1,), (1,)), ((), ())), preferred_element_type=F32)
            s = s + bias
            parts = []
            for h in range(4):
                sh = s[128 * h : 128 * h + 128]
                e = jnp.exp2((sh - jnp.max(sh, axis=0, keepdims=True)) * factor)
                parts.append((e * (1.0 / jnp.sum(e, axis=0, keepdims=True))).astype(BF))
            attn = jnp.concatenate(parts, axis=0)
            out = lax.dot_general(attn, v4, (((0,), (0,)), ((), ())), preferred_element_type=F32)
            ctx_ref[128 * w : 128 * w + 128, at : at + 128] = out.astype(BF)


def piece_copies(zi, part, own_w, own_ug, pieces, w_all, ug_all, sems):
    rows = own_w.shape[0]
    qr = rows // 4
    steps = len(pieces) // 4 + 1
    w_copies, u_copies = [], []

    def place(src, dst, to):
        at = sems.at[len(w_copies) + len(u_copies)]
        to.append(pltpu.make_async_copy(src, dst, at))

    base = pl.multiple_of(zi * rows, 128)
    place(own_w, w_all.at[pl.ds(base, rows), :], w_copies)
    place(own_ug, ug_all.at[:, pl.ds(base, rows)], u_copies)
    for k in range(1, steps):
        shard = lax.rem(zi - k + steps, steps)
        base = pl.multiple_of(shard * rows, 128)
        for bits, piece in zip((0, 2, 1, 3), pieces[4 * k - 4 : 4 * k]):
            from_part = part ^ bits
            row = pl.multiple_of(base + from_part * qr, 32)
            place(piece.at[pl.ds(0, qr), :], w_all.at[pl.ds(row, qr), :], w_copies)
            for j in range(4):
                urow = pl.multiple_of((4 * from_part + j) * 16, 16)
                place(
                    piece.at[pl.ds(qr, 16), pl.ds(j * rows, rows)],
                    ug_all.at[pl.ds(urow, 16), pl.ds(base, rows)],
                    u_copies,
                )
    return w_copies, u_copies


def split3(x):
    hi = x.astype(BF).astype(F32)
    mid = (x - hi).astype(BF).astype(F32)
    return hi, mid, x - hi - mid


def loss_block(value, rows):
    hi, mid, lo = split3(value)
    lane = iota((rows, 128), 1)
    return jnp.where(lane == 0, hi, jnp.where(lane == 1, mid, jnp.where(lane == 2, lo, 0.0)))


def forward_kernel(lat_ref, var_ref, *refs):
    ctx_ref, refs = refs[0], refs[1:]
    extras, refs = refs[:4], refs[4:]
    (own_w, own_ug), refs = refs[:2], refs[2:]
    pieces, refs = refs[:PIECES], refs[PIECES:]
    ts, refs = refs[:4], refs[4:]
    normed_ref, inv_ref, dfc_ref, hidden_ref, w_all, ug_all, term, sems = refs
    zi, lat_place = lax.axis_index("dp"), lax.axis_index("lat")
    w_copies, u_copies = piece_copies(zi, lat_place, own_w, own_ug, pieces, w_all, ug_all, sems)
    for c in w_copies + u_copies:
        c.start()
    tokens, width = normed_ref.shape
    span = dfc_ref.shape[1]
    extra = jnp.concatenate(
        [e[32 * w : 32 * w + 32, :] for w in range(2) for e in extras], axis=0
    ).astype(F32)
    goal, valid = extra[:, :span], extra[:, span : span + 1]
    token = iota((tokens, 1), 0)
    row = (token // 4) % 4 + jnp.where((token // 32) % 4 >= 2, 4, 0)
    lat_w = jnp.zeros((tokens, 1), F32)
    for r in range(8):
        lat_w = jnp.where(row == r, lat_ref[lat_place * 8 + r], lat_w)
    lane = iota((1, span), 1) // (span // var_ref.shape[0])
    var_w = jnp.zeros((1, span), F32)
    for n in range(var_ref.shape[0]):
        var_w = jnp.where(lane == n, var_ref[n], var_w)
    weight = lat_w * valid * var_w
    for c in w_copies:
        c.wait()
    mixed = jnp.dot(ctx_ref[...], w_all[...], preferred_element_type=F32)
    centre = jnp.mean(mixed, axis=-1, keepdims=True)
    off = mixed - centre
    inv = lax.rsqrt(jnp.mean(off * off, axis=-1, keepdims=True) + 1e-05)
    normed = off * inv
    normed_ref[...] = normed
    inv_ref[...] = jnp.broadcast_to(inv, inv_ref.shape)
    for c in u_copies:
        c.wait()
    gain = ug_all[pl.ds(span, 16), :][0:1].astype(F32)
    hidden_ref[...] = (normed * gain).astype(BF)
    field = lax.dot_general(
        hidden_ref[...], ug_all[0:span, :], (((1,), (1,)), ((), ())), preferred_element_type=F32
    )
    misfit = field - goal
    dfc = (2.0 * weight * misfit).astype(BF)
    dfc_ref[...] = dfc
    term[...] = lax.dot_general(
        dfc, hidden_ref[...], (((0,), (0,)), ((), ())), preferred_element_type=F32
    )
    loss = jnp.sum(jnp.sum(weight * misfit * misfit, axis=1, keepdims=True), axis=0, keepdims=True)
    rows = ts[0].shape[0]
    block = loss_block(loss, rows).astype(BF)
    for b, ref in enumerate(ts):
        at = pl.multiple_of((lat_place ^ b) * rows, 8)
        ref[:, :width] = term[pl.ds(at, rows), :].astype(BF)
        ref[:, width:] = block


def backward_kernel(normed_ref, inv_ref, dfc_ref, own_w, own_ug, *refs):
    pieces, (out_ref, w_all, ug_all, sems) = refs[:PIECES], refs[PIECES:]
    zi, part = lax.axis_index("dp"), lax.axis_index("lat")
    w_copies, u_copies = piece_copies(zi, part, own_w, own_ug, pieces, w_all, ug_all, sems)
    for c in u_copies + w_copies:
        c.start()
    tokens, width = normed_ref.shape
    span = dfc_ref.shape[1]
    for c in u_copies:
        c.wait()
    gain = ug_all[pl.ds(span, 16), :][0:1].astype(F32)
    g = jnp.dot(dfc_ref[...], ug_all[0:span, :], preferred_element_type=F32) * gain
    normed = normed_ref[...]
    mean_g = jnp.mean(g, axis=-1, keepdims=True)
    mean_gn = jnp.mean(g * normed, axis=-1, keepdims=True)
    dmixed = ((g - mean_g - normed * mean_gn) * inv_ref[:, 0:1]).astype(BF)
    place = iota((tokens, tokens), 0)
    row, col, level = (place // 8) % 8, place % 8, place // 64
    quad = jnp.where(row >= 4, 2, 0) + jnp.where(col >= 4, 1, 0)
    source = (level // 2) * 128 + quad * 32 + (level % 2) * 16 + (row % 4) * 4 + col % 4
    pick = (iota((tokens, tokens), 1) == source).astype(F32).astype(BF)
    dnat = jnp.dot(pick, dmixed, preferred_element_type=F32).astype(BF)
    for c in w_copies:
        c.wait()
    out = lax.dot_general(dnat, w_all[...], (((1,), (1,)), ((), ())), preferred_element_type=F32)
    out_ref[...] = out.astype(BF)


def add4(a, b, c, d):
    return (a[...].astype(F32) + b[...].astype(F32)) + (c[...].astype(F32) + d[...].astype(F32))


def lat_sum_kernel(a, b, c, d, z0, z1, z2, z3, loss_ref, total_ref):
    total_ref[...] = add4(a, b, c, d)
    zi = lax.axis_index("dp")
    rows, width = z0.shape
    for k, ref in enumerate((z0, z1, z2, z3)):
        at = pl.multiple_of((zi ^ k) * width, 128)
        ref[...] = total_ref[:, pl.ds(at, width)].astype(BF)
    loss = jnp.sum(total_ref[0:1, 4 * width :], axis=1, keepdims=True)
    loss_ref[...] = jnp.broadcast_to(loss, loss_ref.shape)


def dp_sum_kernel(loss_ref, a, b, c, d, o_ref):
    rows, width = a.shape
    o_ref[0:rows, :] = add4(a, b, c, d).astype(BF)
    block = loss_block(loss_ref[0:1, 0:1], o_ref.shape[0] - rows)
    zeros = jnp.zeros((block.shape[0], width - 128), F32)
    o_ref[rows:, :] = jnp.concatenate([block, zeros], axis=1).astype(BF)


def join_kernel(counts, *refs):
    pieces, (o_ref, loss_ref) = refs[:8], refs[8:]
    lat_place = lax.axis_index("lat")
    rows = o_ref.shape[0] // 4
    for a in range(4):
        at = pl.multiple_of((lat_place ^ a) * rows, 8)
        both = [pieces[2 * a + b][0:rows, :].astype(F32) for b in range(2)]
        o_ref[pl.ds(at, rows), :] = (both[0] + both[1]) / counts[0]
    sums = [
        jnp.sum(p[rows : rows + 1, 0:128].astype(F32), axis=1, keepdims=True) for p in pieces[:2]
    ]
    loss_ref[...] = jnp.broadcast_to((sums[0] + sums[1]) / counts[1], loss_ref.shape)


def swap(array, axis, bit):
    return lax.ppermute(array, axis, [(i, i ^ bit) for i in range(lax.axis_size(axis))])


def shape(dims, dtype):
    return jax.ShapeDtypeStruct(dims, dtype)


def shards(projected, targets, valid_cells, w_out, unpatch_matrix, norm_gain, var_weight):
    dp, lat, lon = lax.axis_size("dp"), lax.axis_size("lat"), lax.axis_size("lon")
    rows, width = w_out.shape
    levels = projected.shape[1]
    span = unpatch_matrix.shape[1]
    tokens = levels * 64
    quarter = tokens // 4
    lat_total = 8 * lat
    angle = math.pi * ((np.arange(lat_total) + 0.5) / lat_total - 0.5)
    cosine = np.cos(angle)
    lat_table = jnp.asarray(np.roll(cosine / cosine.mean(), -4), F32)
    barrier = lax.optimization_barrier

    ug, payload = pl.pallas_call(
        payload_kernel,
        out_shape=[shape((UGROWS, rows), BF), shape((rows // 4 + 16, width), BF)],
        in_specs=[HBM, HBM, VMEM],
        out_specs=[VMEM] * 2,
        scratch_shapes=[pltpu.VMEM((span, rows), BF), pltpu.SemaphoreType.DMA((2,))],
        compiler_params=params(62),
        name="payload",
    )(w_out, unpatch_matrix.T, norm_gain)
    ring1 = from_behind(payload, "dp", 1)
    own, *send = pl.pallas_call(
        pack_kernel,
        out_shape=[shape((quarter, 3 * width + EXTRA), BF)] * 4,
        in_specs=[HBM] * 3,
        out_specs=[VMEM] * 4,
        scratch_shapes=[
            pltpu.VMEM((levels, 8, 8, 3 * width), BF),
            pltpu.VMEM((levels, 8, 8, span), BF),
            pltpu.VMEM((8, 8), jnp.int32),
            pltpu.SemaphoreType.DMA((2 + 3 * width // 512,)),
        ],
        compiler_params=params(62),
        name="pack",
    )(
        projected.reshape(levels, 8, 8, 3 * width),
        targets.reshape(levels, 8, 8, span),
        valid_cells,
    )
    corner = [
        (a * lon + b, ((a - 1) % lat) * lon + (b - 1) % lon) for a in range(lat) for b in range(lon)
    ]
    ring1_after, _ = barrier((ring1, send[0]))
    tiles = (
        own,
        from_behind(send[0], "lon", -1),
        from_behind(send[1], "lat", -1),
        lax.ppermute(send[2], ("lat", "lon"), corner),
    )
    ring2 = from_behind(ring1_after, "dp", 1)
    across1 = swap(ring1, "lat", 2)
    ring2_after, across1 = barrier((ring2, across1))
    ring3 = from_behind(ring2_after, "dp", 1)
    across2 = swap(ring2, "lat", 2)
    across3 = swap(ring3, "lat", 2)
    ring1, across1, ring2, *tiles = barrier((ring1, across1, ring2, *tiles))
    ctx = pl.pallas_call(
        attention_kernel,
        out_shape=shape((tokens, width), BF),
        in_specs=[VMEM] * 4,
        out_specs=VMEM,
        compiler_params=params(16),
        name="attention",
    )(*tiles)
    across3, ctx = barrier((across3, ctx))
    pieces = []
    for ring, across in ((ring1, across1), (ring2, across2), (ring3, across3)):
        pieces += [ring, across, swap(ring, "lat", 1), swap(across, "lat", 1)]

    piece = span // lat
    extra_spec = pl.BlockSpec((quarter, EXTRA), lambda i: (0, 3 * width // EXTRA))
    copies = 2 + PIECES * 5
    assembly = [
        pltpu.VMEM((dp * rows, width), BF),
        pltpu.VMEM((UGROWS, dp * rows), BF),
    ]
    *terms, normed, inv, dfc = pl.pallas_call(
        forward_kernel,
        grid=(1,),
        out_shape=[shape((piece, width + 128), BF)] * 4
        + [shape((tokens, width), F32), shape((tokens, 128), F32), shape((tokens, span), BF)],
        in_specs=[SMEM] * 2 + [VMEM] + [extra_spec] * 4 + [HBM] + [ANY] * (1 + PIECES),
        out_specs=[VMEM] * 7,
        scratch_shapes=[pltpu.VMEM((tokens, width), BF)]
        + assembly
        + [pltpu.VMEM((span, width), F32), pltpu.SemaphoreType.DMA((copies,))],
        compiler_params=params(28),
        name="forward",
    )(lat_table, var_weight, ctx, *tiles, w_out, ug, *pieces)

    terms = [terms[0]] + [swap(terms[b], "lat", b) for b in (1, 2, 3)]
    grad_context = pl.pallas_call(
        backward_kernel,
        out_shape=shape((tokens, width), BF),
        in_specs=[VMEM] * 3 + [HBM] + [ANY] * (1 + PIECES),
        out_specs=VMEM,
        scratch_shapes=assembly + [pltpu.SemaphoreType.DMA((copies,))],
        compiler_params=params(24),
        name="backward",
    )(normed, inv, dfc, w_out, ug, *pieces)
    *terms, grad_context = barrier((*terms, grad_context))

    *parts, loss = pl.pallas_call(
        lat_sum_kernel,
        out_shape=[shape((piece, rows), BF)] * 4 + [shape((8, 128), F32)],
        in_specs=[VMEM] * 4,
        out_specs=[VMEM] * 5,
        scratch_shapes=[pltpu.VMEM((piece, width + 128), F32)],
        compiler_params=params(4),
        name="lat_sum",
    )(*terms)
    parts = [parts[0]] + [swap(parts[k], "dp", k) for k in (1, 2, 3)]
    mine = pl.pallas_call(
        dp_sum_kernel,
        out_shape=shape((piece + 8, rows), BF),
        in_specs=[VMEM] * 5,
        out_specs=VMEM,
        compiler_params=params(4),
        name="dp_sum",
    )(loss, *parts)
    plane = [mine]
    for a in range(4):
        for b in range(2):
            if a or b:
                pairs = [
                    (i * lon + j, (i ^ a) * lon + (j ^ b)) for i in range(lat) for j in range(lon)
                ]
                plane.append(lax.ppermute(mine, ("lat", "lon"), pairs))
    count = levels * lat_total * 8 * lon
    counts = (float(count), float(count * (span // var_weight.shape[0])))
    joined, loss = pl.pallas_call(
        lambda *refs: join_kernel(counts, *refs),
        out_shape=[shape((span, rows), F32), shape((1, 1), F32)],
        in_specs=[VMEM] * 8,
        out_specs=[VMEM] * 2,
        compiler_params=params(4),
        name="join",
    )(*plane)
    return grad_context.reshape(1, levels, 8, 8, width), joined.T, loss.reshape(1)


def solution(mesh):
    placed = (
        P("dp", None, "lat", "lon", None),
        P("dp", None, "lat", "lon", None),
        P("lat", "lon"),
        P("dp", None),
        P("dp", None),
        P("dp"),
        P(),
    )
    fits = mesh.shape["dp"] == 4 and mesh.shape["lat"] == 4 and mesh.shape["lon"] == 2

    def program(*arrays):
        body = shards if fits else general_shards
        return jax.shard_map(
            body,
            mesh=mesh,
            in_specs=placed,
            out_specs=(P("dp", None, "lat", "lon", None), P("dp", None), P("dp")),
            check_vma=False,
        )(*arrays)

    return program
```

```python
import functools
import math

import jax
import jax.numpy as jnp
import numpy as np
from jax import lax
from jax.experimental import pallas as pl
from jax.experimental.pallas import tpu as pltpu
from jax.sharding import PartitionSpec as P

HEADS = 48
HDIM = 32
WLEV = 2
BF = jnp.bfloat16
F32 = jnp.float32
EXTRA = 256
UGROWS = 256
PIECES = 12
VMEM = pl.BlockSpec(memory_space=pltpu.VMEM)
SMEM = pl.BlockSpec(memory_space=pltpu.SMEM)
ANY = pl.BlockSpec(memory_space=pl.ANY)
HBM = pl.BlockSpec(memory_space=pltpu.HBM)


def from_behind(array, axis, by):
    length = lax.axis_size(axis)
    return lax.ppermute(array, axis, [(i, (i + by) % length) for i in range(length)])


def general_shards(projected, targets, valid_cells, w_out, unpatch_matrix, norm_gain, var_weight):
    tile_side = projected.shape[2]
    half_side = tile_side // 2
    levels = projected.shape[1]
    model_width = w_out.shape[1]
    predicted_span = unpatch_matrix.shape[1]
    lat_total = tile_side * lax.axis_size("lat")
    lon_total = tile_side * lax.axis_size("lon")
    lat_place = lax.axis_index("lat")
    moved = from_behind(
        (projected[:, :, :, :half_side], targets[:, :, :, :half_side], valid_cells[:, :half_side]),
        "lon",
        -1,
    )
    strip_proj = jnp.concatenate([projected[:, :, :, half_side:], moved[0]], axis=3)
    strip_goal = jnp.concatenate([targets[:, :, :, half_side:], moved[1]], axis=3)
    strip_valid = jnp.concatenate([valid_cells[:, half_side:], moved[2]], axis=1)
    moved_rows = from_behind(
        (strip_proj[:, :, :half_side], strip_goal[:, :, :half_side], strip_valid[:half_side]),
        "lat",
        -1,
    )
    local_proj = jnp.concatenate([strip_proj[:, :, half_side:], moved_rows[0]], axis=2)
    shard_reference = jnp.concatenate([strip_goal[:, :, half_side:], moved_rows[1]], axis=2)
    local_valid = jnp.concatenate([strip_valid[half_side:], moved_rows[2]], axis=0).astype(F32)
    win_count = levels // WLEV
    tokw = WLEV * tile_side * tile_side
    windows = local_proj.reshape(win_count, tokw, 3 * model_width)
    rows_here = lat_place * tile_side + jnp.arange(tile_side)
    region_rows = (rows_here >= lat_total - half_side).astype(jnp.int32)
    region = jnp.broadcast_to(region_rows[None, :, None], (WLEV, tile_side, tile_side)).reshape(-1)
    allowed = region[:, None] == region[None, :]
    queries = windows[..., :model_width].reshape(win_count, tokw, HEADS, -1)
    key_heads = windows[..., model_width : 2 * model_width].reshape(win_count, tokw, HEADS, -1)
    value_heads = windows[..., 2 * model_width :].reshape(win_count, tokw, HEADS, -1)
    scores = jnp.einsum("wqhd,wkhd->whqk", queries, key_heads, preferred_element_type=F32)
    scores = scores * (1.0 / math.sqrt(HDIM))
    scores = jnp.where(allowed[None, None], scores, -1e30)
    row_peak = jnp.max(scores, axis=-1, keepdims=True)
    lifted = jnp.exp(scores - row_peak)
    attn = (lifted / jnp.sum(lifted, axis=-1, keepdims=True)).astype(BF)
    context = jnp.einsum("whqk,wkhd->wqhd", attn, value_heads, preferred_element_type=F32)
    context = context.astype(BF).reshape(win_count * tokw, model_width)
    element_total = win_count * tokw
    out_all, unprojected_pieces, gain_all = (
        lax.all_gather(w_out, "dp", axis=0, tiled=True),
        lax.all_gather(unpatch_matrix, "dp", axis=0, tiled=True),
        lax.all_gather(norm_gain, "dp", axis=0, tiled=True),
    )
    mixed_rows = jnp.dot(context, out_all, preferred_element_type=F32)
    centre = jnp.mean(mixed_rows, axis=-1, keepdims=True)
    spread = jnp.mean((mixed_rows - centre) ** 2, axis=-1, keepdims=True)
    inv_spread = lax.rsqrt(spread + 1e-05)
    normed = (mixed_rows - centre) * inv_spread
    gain_f = gain_all.astype(F32)
    latent_activation = (normed * gain_f).astype(BF)
    prediction_field = jnp.dot(latent_activation, unprojected_pieces, preferred_element_type=F32)
    prediction_misfit = prediction_field - shard_reference.reshape(
        element_total, predicted_span
    ).astype(F32)
    all_rows = jnp.arange(lat_total).astype(F32)
    cosine_mean = jnp.mean(jnp.cos(math.pi * ((all_rows + 0.5) / lat_total - 0.5)))
    initial_rows = ((rows_here + half_side) % lat_total).astype(F32)
    lat_here = jnp.cos(math.pi * ((initial_rows + 0.5) / lat_total - 0.5)) / cosine_mean
    element_factor = jnp.broadcast_to(
        lat_here[None, :, None] * local_valid[None], (levels, tile_side, tile_side)
    ).reshape(element_total, 1)
    variable_factor = jnp.repeat(var_weight, predicted_span // var_weight.shape[0])[None, :]
    shard_penalty = jnp.sum(
        element_factor * variable_factor * prediction_misfit * prediction_misfit
    ) / (levels * lat_total * lon_total * (predicted_span // var_weight.shape[0]))
    prediction_gradient = (2.0 * element_factor * variable_factor * prediction_misfit).astype(BF)
    grad_shard = lax.psum_scatter(
        jnp.einsum(
            "td,to->do", latent_activation, prediction_gradient, preferred_element_type=F32
        ).astype(BF),
        "dp",
        scatter_dimension=0,
        tiled=True,
    ).astype(F32)
    grad_sum, loss_sum = lax.psum((grad_shard, shard_penalty), ("lat", "lon"))
    grad_recovery = grad_sum / (levels * lat_total * lon_total)
    grad_hidden = jnp.einsum(
        "to,do->td", prediction_gradient, unprojected_pieces, preferred_element_type=F32
    )
    scaled_grad = grad_hidden * gain_f
    grad_mixed = inv_spread * (
        scaled_grad
        - jnp.mean(scaled_grad, axis=-1, keepdims=True)
        - normed * jnp.mean(scaled_grad * normed, axis=-1, keepdims=True)
    )
    grad_mixed = grad_mixed.astype(BF)
    grad_context = jnp.einsum("tj,ij->ti", grad_mixed, out_all, preferred_element_type=F32)
    grad_context = grad_context.astype(BF).reshape(1, levels, tile_side, tile_side, model_width)
    return (grad_context, grad_recovery, loss_sum.reshape(1))


def params(mib):
    return pltpu.CompilerParams(vmem_limit_bytes=mib << 20)


def iota(shape, dim):
    return lax.broadcasted_iota(jnp.int32, shape, dim)


def payload_kernel(w_ref, unpatch_ref, gain_ref, payload_ref, ug, sems):
    part = lax.axis_index("lat")
    rows, width = w_ref.shape
    qr = rows // 4
    span = unpatch_ref.shape[0]
    start = pl.multiple_of(part * qr, 32)
    u_copy = pltpu.make_async_copy(unpatch_ref, ug.at[pl.ds(0, span), :], sems.at[0])
    u_copy.start()
    w_copy = pltpu.make_async_copy(
        w_ref.at[pl.ds(start, qr), :], payload_ref.at[pl.ds(0, qr), :], sems.at[1]
    )
    w_copy.start()
    ug[pl.ds(span, 16), :] = gain_rows(gain_ref, rows)
    ug[pl.ds(span + 16, UGROWS - span - 16), :] = jnp.zeros((UGROWS - span - 16, rows), BF)
    u_copy.wait()
    copies = [w_copy]
    for j in range(4):
        at = pl.multiple_of((4 * part + j) * 16, 16)
        copies.append(
            pltpu.make_async_copy(
                ug.at[pl.ds(at, 16), :],
                payload_ref.at[pl.ds(qr, 16), pl.ds(j * rows, rows)],
                sems.at[2 + j],
            )
        )
        copies[-1].start()
    for c in copies:
        c.wait()


def gain_rows(gain_ref, rows):
    return jnp.broadcast_to(gain_ref[...].astype(F32).reshape(1, rows), (16, rows)).astype(BF)


def pack_kernel(x_ref, t_ref, valid_ref, o0, o1, o2, o3, o4, x_in, t_in, v_in, sems):
    span = t_ref.shape[-1]
    count = x_ref.shape[0] * 64
    quarter = count // 4
    step = 512
    width = x_ref.shape[-1]
    copies = [
        pltpu.make_async_copy(t_ref, t_in, sems.at[0]),
        pltpu.make_async_copy(valid_ref, v_in, sems.at[1]),
    ]
    for at in range(0, width, step):
        lanes = (slice(None),) * 3 + (pl.ds(at, step),)
        copies.append(
            pltpu.make_async_copy(x_ref.at[lanes], x_in.at[lanes], sems.at[len(copies)])
        )
    for c in copies:
        c.start()
    place = iota((count, count), 0)
    quad, rest = place // quarter, place % quarter
    row = (rest // 4) % 4 + jnp.where(quad < 2, 4, 0)
    col = rest % 4 + jnp.where(quad % 2 == 0, 4, 0)
    source = (rest // 16) * 64 + row * 8 + col
    pick = (iota((count, count), 1) == source).astype(F32).astype(BF)
    copies[0].wait()
    copies[1].wait()
    goal = jnp.dot(pick, t_in[...].reshape(count, span), preferred_element_type=F32)
    token = iota((count, 8), 0)
    row_hot = ((token // 8) % 8 == iota((count, 8), 1)).astype(F32)
    by_row = jnp.dot(row_hot, v_in[...].astype(F32), preferred_element_type=F32)
    mine = token % 8 == iota((count, 8), 1)
    natural = jnp.sum(jnp.where(mine, by_row, 0.0), axis=1, keepdims=True)
    spread = jnp.broadcast_to(natural, (count, 128)).astype(BF)
    column = jnp.dot(pick, spread, preferred_element_type=F32)
    extra = jnp.concatenate([goal, column[:, : EXTRA - span]], axis=1).astype(BF)
    outs = [(o0, 0), (o1, quarter), (o2, 2 * quarter), (o3, 3 * quarter), (o4, 7 * quarter // 2)]
    for ref, row in outs:
        ref[:, width:] = extra[row : row + ref.shape[0]]
    for n, at in enumerate(range(0, width, step)):
        copies[2 + n].wait()
        tokens = x_in[:, :, :, at : at + step].reshape(count, step)
        out = jnp.dot(pick, tokens, preferred_element_type=F32).astype(BF)
        for ref, row in outs:
            ref[:, at : at + step] = out[row : row + ref.shape[0]]


def attention_kernel(own_ref, east_ref, south_ref, diag0_ref, diag1_ref, ctx_ref):
    tiles = [[r.at[32 * w : 32 * w + 32] for r in (own_ref, east_ref, south_ref)] for w in range(2)]
    tiles[0].append(diag0_ref)
    tiles[1].append(diag1_ref)
    part = ctx_ref.shape[1]
    is_last = lax.axis_index("lat") == lax.axis_size("lat") - 1
    same = (iota((512, 128), 0) % 128) // 64 == iota((512, 128), 1) // 64
    bias = jnp.where(jnp.logical_or(same, jnp.logical_not(is_last)), 0.0, -1e30)
    head = iota((128, 128), 1) // HDIM
    factor = math.log2(math.e) / math.sqrt(HDIM)
    for at in range(0, part, 128):
        for w in range(2):
            q, k, v = [
                jnp.concatenate(
                    [t[:, i * part + at : i * part + at + 128] for t in tiles[w]],
                    axis=0,
                )
                for i in range(3)
            ]
            zero = jnp.zeros_like(k)
            k4 = jnp.concatenate([jnp.where(head == h, k, zero) for h in range(4)], axis=0)
            v4 = jnp.concatenate([jnp.where(head == h, v, zero) for h in range(4)], axis=0)
            s = lax.dot_general(k4, q, (((1,), (1,)), ((), ())), preferred_element_type=F32)
            s = s + bias
            parts = []
            for h in range(4):
                sh = s[128 * h : 128 * h + 128]
                e = jnp.exp2((sh - jnp.max(sh, axis=0, keepdims=True)) * factor)
                parts.append((e * (1.0 / jnp.sum(e, axis=0, keepdims=True))).astype(BF))
            attn = jnp.concatenate(parts, axis=0)
            out = lax.dot_general(attn, v4, (((0,), (0,)), ((), ())), preferred_element_type=F32)
            ctx_ref[128 * w : 128 * w + 128, at : at + 128] = out.astype(BF)


def assemble(own_w, own_u, own_gain, pieces, w_all, ug_all):
    zi, part = lax.axis_index("dp"), lax.axis_index("lat")
    rows = own_w.shape[0]
    qr = rows // 4
    steps = len(pieces) // 4 + 1
    base = pl.multiple_of(zi * rows, 128)
    w_all[pl.ds(base, rows), :] = own_w[...]
    span = own_u.shape[0]
    ug_all[0:span, pl.ds(base, rows)] = own_u[...]
    ug_all[span : span + 16, pl.ds(base, rows)] = gain_rows(own_gain, rows)
    for k in range(1, steps):
        shard = lax.rem(zi - k + steps, steps)
        base = pl.multiple_of(shard * rows, 128)
        for bits, piece in zip((0, 2, 1, 3), pieces[4 * k - 4 : 4 * k]):
            from_part = part ^ bits
            row = pl.multiple_of(base + from_part * qr, 32)
            w_all[pl.ds(row, qr), :] = piece[0:qr, :]
            for j in range(4):
                urow = pl.multiple_of((4 * from_part + j) * 16, 16)
                ug_all[pl.ds(urow, 16), pl.ds(base, rows)] = piece[
                    qr : qr + 16, j * rows : (j + 1) * rows
                ]


def split3(x):
    hi = x.astype(BF).astype(F32)
    mid = (x - hi).astype(BF).astype(F32)
    return hi, mid, x - hi - mid


def loss_block(value, rows):
    hi, mid, lo = split3(value)
    lane = iota((rows, 128), 1)
    return jnp.where(lane == 0, hi, jnp.where(lane == 1, mid, jnp.where(lane == 2, lo, 0.0)))


def forward_kernel(lat_ref, var_ref, *refs):
    ctx_ref, refs = refs[0], refs[1:]
    extras, refs = refs[:5], refs[5:]
    owned, refs = refs[:3], refs[3:]
    pieces, refs = refs[:PIECES], refs[PIECES:]
    ts, refs = refs[:4], refs[4:]
    normed_ref, inv_ref, dfc_ref, hidden_ref, w_all, ug_all, term = refs
    lat_place = lax.axis_index("lat")
    assemble(*owned, pieces, w_all, ug_all)
    tokens, width = normed_ref.shape
    span = dfc_ref.shape[1]
    extra = jnp.concatenate(
        [e[32 * w : 32 * w + 32, :] if n < 3 else extras[3 + w][...]
         for w in range(2) for n, e in enumerate(extras[:4])],
        axis=0,
    ).astype(F32)
    goal, valid = extra[:, :span], extra[:, span : span + 1]
    token = iota((tokens, 1), 0)
    row = (token // 4) % 4 + jnp.where((token // 32) % 4 >= 2, 4, 0)
    lat_w = jnp.zeros((tokens, 1), F32)
    for r in range(8):
        lat_w = jnp.where(row == r, lat_ref[lat_place * 8 + r], lat_w)
    lane = iota((1, span), 1) // (span // var_ref.shape[0])
    var_w = jnp.zeros((1, span), F32)
    for n in range(var_ref.shape[0]):
        var_w = jnp.where(lane == n, var_ref[n], var_w)
    weight = lat_w * valid * var_w
    mixed = jnp.dot(ctx_ref[...], w_all[...], preferred_element_type=F32)
    centre = jnp.mean(mixed, axis=-1, keepdims=True)
    off = mixed - centre
    inv = lax.rsqrt(jnp.mean(off * off, axis=-1, keepdims=True) + 1e-05)
    normed = off * inv
    normed_ref[...] = normed
    inv_ref[...] = jnp.broadcast_to(inv, inv_ref.shape)
    gain = ug_all[pl.ds(span, 16), :][0:1].astype(F32)
    hidden_ref[...] = (normed * gain).astype(BF)
    field = lax.dot_general(
        hidden_ref[...], ug_all[0:span, :], (((1,), (1,)), ((), ())), preferred_element_type=F32
    )
    misfit = field - goal
    dfc = (2.0 * weight * misfit).astype(BF)
    dfc_ref[...] = dfc
    term[...] = lax.dot_general(
        dfc, hidden_ref[...], (((0,), (0,)), ((), ())), preferred_element_type=F32
    )
    loss = jnp.sum(jnp.sum(weight * misfit * misfit, axis=1, keepdims=True), axis=0, keepdims=True)
    rows = ts[0].shape[0]
    block = loss_block(loss, rows).astype(BF)
    for b, ref in enumerate(ts):
        at = pl.multiple_of((lat_place ^ b) * rows, 8)
        ref[:, :width] = term[pl.ds(at, rows), :].astype(BF)
        ref[:, width:] = block


def backward_kernel(normed_ref, inv_ref, dfc_ref, *refs):
    owned, refs = refs[:3], refs[3:]
    pieces, (out_ref, w_all, ug_all) = refs[:PIECES], refs[PIECES:]
    assemble(*owned, pieces, w_all, ug_all)
    tokens, width = normed_ref.shape
    span = dfc_ref.shape[1]
    gain = ug_all[pl.ds(span, 16), :][0:1].astype(F32)
    g = jnp.dot(dfc_ref[...], ug_all[0:span, :], preferred_element_type=F32) * gain
    normed = normed_ref[...]
    mean_g = jnp.mean(g, axis=-1, keepdims=True)
    mean_gn = jnp.mean(g * normed, axis=-1, keepdims=True)
    dmixed = ((g - mean_g - normed * mean_gn) * inv_ref[:, 0:1]).astype(BF)
    place = iota((tokens, tokens), 0)
    row, col, level = (place // 8) % 8, place % 8, place // 64
    quad = jnp.where(row >= 4, 2, 0) + jnp.where(col >= 4, 1, 0)
    source = (level // 2) * 128 + quad * 32 + (level % 2) * 16 + (row % 4) * 4 + col % 4
    pick = (iota((tokens, tokens), 1) == source).astype(F32).astype(BF)
    dnat = jnp.dot(pick, dmixed, preferred_element_type=F32).astype(BF)
    out = lax.dot_general(dnat, w_all[...], (((1,), (1,)), ((), ())), preferred_element_type=F32)
    out_ref[...] = out.astype(BF)


def add4(a, b, c, d):
    return (a[...].astype(F32) + b[...].astype(F32)) + (c[...].astype(F32) + d[...].astype(F32))


def lat_sum_kernel(a, b, c, d, z0, z1, z2, z3, loss_ref, total_ref):
    total_ref[...] = add4(a, b, c, d)
    zi = lax.axis_index("dp")
    rows, width = z0.shape
    for k, ref in enumerate((z0, z1, z2, z3)):
        at = pl.multiple_of((zi ^ k) * width, 128)
        ref[...] = total_ref[:, pl.ds(at, width)].astype(BF)
    loss = jnp.sum(total_ref[0:1, 4 * width :], axis=1, keepdims=True)
    loss_ref[...] = jnp.broadcast_to(loss, loss_ref.shape)


def dp_sum_kernel(loss_ref, a, b, c, d, o_ref):
    rows, width = a.shape
    o_ref[0:rows, :] = add4(a, b, c, d).astype(BF)
    block = loss_block(loss_ref[0:1, 0:1], o_ref.shape[0] - rows)
    zeros = jnp.zeros((block.shape[0], width - 128), F32)
    o_ref[rows:, :] = jnp.concatenate([block, zeros], axis=1).astype(BF)


def join_kernel(counts, *refs):
    pieces, (o_ref, loss_ref) = refs[:8], refs[8:]
    lat_place = lax.axis_index("lat")
    rows = o_ref.shape[0] // 4
    for a in range(4):
        at = pl.multiple_of((lat_place ^ a) * rows, 8)
        both = [pieces[2 * a + b][0:rows, :].astype(F32) for b in range(2)]
        o_ref[pl.ds(at, rows), :] = (both[0] + both[1]) / counts[0]
    sums = [
        jnp.sum(p[rows : rows + 1, 0:128].astype(F32), axis=1, keepdims=True) for p in pieces[:2]
    ]
    loss_ref[...] = jnp.broadcast_to((sums[0] + sums[1]) / counts[1], loss_ref.shape)


def swap(array, axis, bit):
    return lax.ppermute(array, axis, [(i, i ^ bit) for i in range(lax.axis_size(axis))])


def shape(dims, dtype):
    return jax.ShapeDtypeStruct(dims, dtype)


def shards(projected, targets, valid_cells, w_out, unpatch_matrix, norm_gain, var_weight):
    dp, lat, lon = lax.axis_size("dp"), lax.axis_size("lat"), lax.axis_size("lon")
    rows, width = w_out.shape
    levels = projected.shape[1]
    span = unpatch_matrix.shape[1]
    tokens = levels * 64
    quarter = tokens // 4
    lat_total = 8 * lat
    angle = math.pi * ((np.arange(lat_total) + 0.5) / lat_total - 0.5)
    cosine = np.cos(angle)
    lat_table = jnp.asarray(np.roll(cosine / cosine.mean(), -4), F32)
    barrier = lax.optimization_barrier

    unpatch_t = unpatch_matrix.T
    payload = pl.pallas_call(
        payload_kernel,
        out_shape=shape((rows // 4 + 16, width), BF),
        in_specs=[HBM, HBM, VMEM],
        out_specs=HBM,
        scratch_shapes=[pltpu.VMEM((UGROWS, rows), BF), pltpu.SemaphoreType.DMA((6,))],
        compiler_params=params(62),
        name="payload",
    )(w_out, unpatch_t, norm_gain)
    ring1 = from_behind(payload, "dp", 1)
    own, *send = pl.pallas_call(
        pack_kernel,
        out_shape=[shape((quarter, 3 * width + EXTRA), BF)] * 3
        + [shape((quarter // 2, 3 * width + EXTRA), BF)] * 2,
        in_specs=[HBM] * 3,
        out_specs=[VMEM] * 5,
        scratch_shapes=[
            pltpu.VMEM((levels, 8, 8, 3 * width), BF),
            pltpu.VMEM((levels, 8, 8, span), BF),
            pltpu.VMEM((8, 8), jnp.int32),
            pltpu.SemaphoreType.DMA((2 + 3 * width // 512,)),
        ],
        compiler_params=params(62),
        name="pack",
    )(
        projected.reshape(levels, 8, 8, 3 * width),
        targets.reshape(levels, 8, 8, span),
        valid_cells,
    )
    corner = [
        (a * lon + b, ((a - 1) % lat) * lon + (b - 1) % lon) for a in range(lat) for b in range(lon)
    ]
    tiles = [
        own,
        from_behind(send[0], "lon", -1),
        from_behind(send[1], "lat", -1),
        lax.ppermute(send[2], ("lat", "lon"), corner),
        lax.ppermute(send[3], ("lat", "lon"), corner),
    ]
    ring1_after, tiles[3] = barrier((ring1, tiles[3]))
    ring2 = from_behind(ring1_after, "dp", 1)
    across1 = swap(ring1, "lat", 2)
    ring2_after, across1 = barrier((ring2, across1))
    ring3 = from_behind(ring2_after, "dp", 1)
    across2 = swap(ring2, "lat", 2)
    across3 = swap(ring3, "lat", 2)
    *tiles, ring1, across1, ring2 = barrier((*tiles, ring1, across1, ring2))
    ctx = pl.pallas_call(
        attention_kernel,
        out_shape=shape((tokens, width), BF),
        in_specs=[VMEM] * 5,
        out_specs=VMEM,
        compiler_params=params(16),
        name="attention",
    )(*tiles)
    ctx, across3 = barrier((ctx, across3))
    pieces = []
    for ring, across in ((ring1, across1), (ring2, across2), (ring3, across3)):
        pieces += [ring, across, swap(ring, "lat", 1), swap(across, "lat", 1)]

    piece = span // lat
    extra_specs = [
        pl.BlockSpec((t.shape[0], EXTRA), lambda i: (0, 3 * width // EXTRA)) for t in tiles
    ]
    assembly = [
        pltpu.VMEM((dp * rows, width), BF),
        pltpu.VMEM((UGROWS, dp * rows), BF),
    ]
    *terms, normed, inv, dfc = pl.pallas_call(
        forward_kernel,
        grid=(1,),
        out_shape=[shape((piece, width + 128), BF)] * 4
        + [shape((tokens, width), F32), shape((tokens, 128), F32), shape((tokens, span), BF)],
        in_specs=[SMEM] * 2 + [VMEM] + extra_specs + [VMEM] * (3 + PIECES),
        out_specs=[VMEM] * 7,
        scratch_shapes=[pltpu.VMEM((tokens, width), BF)]
        + assembly
        + [pltpu.VMEM((span, width), F32)],
        compiler_params=params(28),
        name="forward",
    )(lat_table, var_weight, ctx, *tiles, w_out, unpatch_t, norm_gain, *pieces)

    terms = [terms[0]] + [swap(terms[b], "lat", b) for b in (1, 2, 3)]
    grad_context = pl.pallas_call(
        backward_kernel,
        out_shape=shape((tokens, width), BF),
        in_specs=[VMEM] * (6 + PIECES),
        out_specs=VMEM,
        scratch_shapes=assembly,
        compiler_params=params(24),
        name="backward",
    )(normed, inv, dfc, w_out, unpatch_t, norm_gain, *pieces)
    *terms, grad_context = barrier((*terms, grad_context))

    *parts, loss = pl.pallas_call(
        lat_sum_kernel,
        out_shape=[shape((piece, rows), BF)] * 4 + [shape((8, 128), F32)],
        in_specs=[VMEM] * 4,
        out_specs=[VMEM] * 5,
        scratch_shapes=[pltpu.VMEM((piece, width + 128), F32)],
        compiler_params=params(4),
        name="lat_sum",
    )(*terms)
    parts = [parts[0]] + [swap(parts[k], "dp", k) for k in (1, 2, 3)]
    mine = pl.pallas_call(
        dp_sum_kernel,
        out_shape=shape((piece + 8, rows), BF),
        in_specs=[VMEM] * 5,
        out_specs=VMEM,
        compiler_params=params(4),
        name="dp_sum",
    )(loss, *parts)
    plane = [mine]
    for a in range(4):
        for b in range(2):
            if a or b:
                pairs = [
                    (i * lon + j, (i ^ a) * lon + (j ^ b)) for i in range(lat) for j in range(lon)
                ]
                plane.append(lax.ppermute(mine, ("lat", "lon"), pairs))
    count = levels * lat_total * 8 * lon
    counts = (float(count), float(count * (span // var_weight.shape[0])))
    joined, loss = pl.pallas_call(
        lambda *refs: join_kernel(counts, *refs),
        out_shape=[shape((span, rows), F32), shape((1, 1), F32)],
        in_specs=[VMEM] * 8,
        out_specs=[VMEM] * 2,
        compiler_params=params(4),
        name="join",
    )(*plane)
    return grad_context.reshape(1, levels, 8, 8, width), joined.T, loss.reshape(1)


def solution(mesh):
    placed = (
        P("dp", None, "lat", "lon", None),
        P("dp", None, "lat", "lon", None),
        P("lat", "lon"),
        P("dp", None),
        P("dp", None),
        P("dp"),
        P(),
    )
    fits = mesh.shape["dp"] == 4 and mesh.shape["lat"] == 4 and mesh.shape["lon"] == 2

    def program(*arrays):
        body = shards if fits else general_shards
        return jax.shard_map(
            body,
            mesh=mesh,
            in_specs=placed,
            out_specs=(P("dp", None, "lat", "lon", None), P("dp", None), P("dp")),
            check_vma=False,
        )(*arrays)

    return program
```

```python
import functools
import math

import jax
import jax.numpy as jnp
import numpy as np
from jax import lax
from jax.experimental import pallas as pl
from jax.experimental.pallas import tpu as pltpu
from jax.sharding import PartitionSpec as P

HEADS = 48
HDIM = 32
WLEV = 2
BF = jnp.bfloat16
F32 = jnp.float32
EXTRA = 256
UGROWS = 256
PIECES = 12
VMEM = pl.BlockSpec(memory_space=pltpu.VMEM)
SMEM = pl.BlockSpec(memory_space=pltpu.SMEM)
ANY = pl.BlockSpec(memory_space=pl.ANY)
HBM = pl.BlockSpec(memory_space=pltpu.HBM)


def from_behind(array, axis, by):
    length = lax.axis_size(axis)
    return lax.ppermute(array, axis, [(i, (i + by) % length) for i in range(length)])


def general_shards(projected, targets, valid_cells, w_out, unpatch_matrix, norm_gain, var_weight):
    tile_side = projected.shape[2]
    half_side = tile_side // 2
    levels = projected.shape[1]
    model_width = w_out.shape[1]
    predicted_span = unpatch_matrix.shape[1]
    lat_total = tile_side * lax.axis_size("lat")
    lon_total = tile_side * lax.axis_size("lon")
    lat_place = lax.axis_index("lat")
    moved = from_behind(
        (projected[:, :, :, :half_side], targets[:, :, :, :half_side], valid_cells[:, :half_side]),
        "lon",
        -1,
    )
    strip_proj = jnp.concatenate([projected[:, :, :, half_side:], moved[0]], axis=3)
    strip_goal = jnp.concatenate([targets[:, :, :, half_side:], moved[1]], axis=3)
    strip_valid = jnp.concatenate([valid_cells[:, half_side:], moved[2]], axis=1)
    moved_rows = from_behind(
        (strip_proj[:, :, :half_side], strip_goal[:, :, :half_side], strip_valid[:half_side]),
        "lat",
        -1,
    )
    local_proj = jnp.concatenate([strip_proj[:, :, half_side:], moved_rows[0]], axis=2)
    shard_reference = jnp.concatenate([strip_goal[:, :, half_side:], moved_rows[1]], axis=2)
    local_valid = jnp.concatenate([strip_valid[half_side:], moved_rows[2]], axis=0).astype(F32)
    win_count = levels // WLEV
    tokw = WLEV * tile_side * tile_side
    windows = local_proj.reshape(win_count, tokw, 3 * model_width)
    rows_here = lat_place * tile_side + jnp.arange(tile_side)
    region_rows = (rows_here >= lat_total - half_side).astype(jnp.int32)
    region = jnp.broadcast_to(region_rows[None, :, None], (WLEV, tile_side, tile_side)).reshape(-1)
    allowed = region[:, None] == region[None, :]
    queries = windows[..., :model_width].reshape(win_count, tokw, HEADS, -1)
    key_heads = windows[..., model_width : 2 * model_width].reshape(win_count, tokw, HEADS, -1)
    value_heads = windows[..., 2 * model_width :].reshape(win_count, tokw, HEADS, -1)
    scores = jnp.einsum("wqhd,wkhd->whqk", queries, key_heads, preferred_element_type=F32)
    scores = scores * (1.0 / math.sqrt(HDIM))
    scores = jnp.where(allowed[None, None], scores, -1e30)
    row_peak = jnp.max(scores, axis=-1, keepdims=True)
    lifted = jnp.exp(scores - row_peak)
    attn = (lifted / jnp.sum(lifted, axis=-1, keepdims=True)).astype(BF)
    context = jnp.einsum("whqk,wkhd->wqhd", attn, value_heads, preferred_element_type=F32)
    context = context.astype(BF).reshape(win_count * tokw, model_width)
    element_total = win_count * tokw
    out_all, unprojected_pieces, gain_all = (
        lax.all_gather(w_out, "dp", axis=0, tiled=True),
        lax.all_gather(unpatch_matrix, "dp", axis=0, tiled=True),
        lax.all_gather(norm_gain, "dp", axis=0, tiled=True),
    )
    mixed_rows = jnp.dot(context, out_all, preferred_element_type=F32)
    centre = jnp.mean(mixed_rows, axis=-1, keepdims=True)
    spread = jnp.mean((mixed_rows - centre) ** 2, axis=-1, keepdims=True)
    inv_spread = lax.rsqrt(spread + 1e-05)
    normed = (mixed_rows - centre) * inv_spread
    gain_f = gain_all.astype(F32)
    latent_activation = (normed * gain_f).astype(BF)
    prediction_field = jnp.dot(latent_activation, unprojected_pieces, preferred_element_type=F32)
    prediction_misfit = prediction_field - shard_reference.reshape(
        element_total, predicted_span
    ).astype(F32)
    all_rows = jnp.arange(lat_total).astype(F32)
    cosine_mean = jnp.mean(jnp.cos(math.pi * ((all_rows + 0.5) / lat_total - 0.5)))
    initial_rows = ((rows_here + half_side) % lat_total).astype(F32)
    lat_here = jnp.cos(math.pi * ((initial_rows + 0.5) / lat_total - 0.5)) / cosine_mean
    element_factor = jnp.broadcast_to(
        lat_here[None, :, None] * local_valid[None], (levels, tile_side, tile_side)
    ).reshape(element_total, 1)
    variable_factor = jnp.repeat(var_weight, predicted_span // var_weight.shape[0])[None, :]
    shard_penalty = jnp.sum(
        element_factor * variable_factor * prediction_misfit * prediction_misfit
    ) / (levels * lat_total * lon_total * (predicted_span // var_weight.shape[0]))
    prediction_gradient = (2.0 * element_factor * variable_factor * prediction_misfit).astype(BF)
    grad_shard = lax.psum_scatter(
        jnp.einsum(
            "td,to->do", latent_activation, prediction_gradient, preferred_element_type=F32
        ).astype(BF),
        "dp",
        scatter_dimension=0,
        tiled=True,
    ).astype(F32)
    grad_sum, loss_sum = lax.psum((grad_shard, shard_penalty), ("lat", "lon"))
    grad_recovery = grad_sum / (levels * lat_total * lon_total)
    grad_hidden = jnp.einsum(
        "to,do->td", prediction_gradient, unprojected_pieces, preferred_element_type=F32
    )
    scaled_grad = grad_hidden * gain_f
    grad_mixed = inv_spread * (
        scaled_grad
        - jnp.mean(scaled_grad, axis=-1, keepdims=True)
        - normed * jnp.mean(scaled_grad * normed, axis=-1, keepdims=True)
    )
    grad_mixed = grad_mixed.astype(BF)
    grad_context = jnp.einsum("tj,ij->ti", grad_mixed, out_all, preferred_element_type=F32)
    grad_context = grad_context.astype(BF).reshape(1, levels, tile_side, tile_side, model_width)
    return (grad_context, grad_recovery, loss_sum.reshape(1))


def params(mib):
    return pltpu.CompilerParams(vmem_limit_bytes=mib << 20)


def iota(shape, dim):
    return lax.broadcasted_iota(jnp.int32, shape, dim)


def payload_kernel(w_ref, unpatch_ref, gain_ref, payload_ref, ug, sems):
    part = lax.axis_index("lat")
    rows, width = w_ref.shape
    qr = rows // 4
    span = unpatch_ref.shape[0]
    start = pl.multiple_of(part * qr, 32)
    u_copy = pltpu.make_async_copy(unpatch_ref, ug.at[pl.ds(0, span), :], sems.at[0])
    u_copy.start()
    w_copy = pltpu.make_async_copy(
        w_ref.at[pl.ds(start, qr), :], payload_ref.at[pl.ds(0, qr), :], sems.at[1]
    )
    w_copy.start()
    ug[pl.ds(span, 16), :] = gain_rows(gain_ref, rows)
    ug[pl.ds(span + 16, UGROWS - span - 16), :] = jnp.zeros((UGROWS - span - 16, rows), BF)
    u_copy.wait()
    for j in range(4):
        at = pl.multiple_of((4 * part + j) * 16, 16)
        payload_ref[pl.ds(qr, 16), pl.ds(j * rows, rows)] = ug[pl.ds(at, 16), :]
    w_copy.wait()


def gain_rows(gain_ref, rows):
    return jnp.broadcast_to(gain_ref[...].astype(F32).reshape(1, rows), (16, rows)).astype(BF)


def pack_kernel(x_ref, t_ref, valid_ref, o0, o1, o2, o3, o4, x_in, t_in, v_in, sems):
    span = t_ref.shape[-1]
    count = x_ref.shape[0] * 64
    quarter = count // 4
    step = 512
    width = x_ref.shape[-1]
    copies = [
        pltpu.make_async_copy(t_ref, t_in, sems.at[0]),
        pltpu.make_async_copy(valid_ref, v_in, sems.at[1]),
    ]
    for at in range(0, width, step):
        lanes = (slice(None),) * 3 + (pl.ds(at, step),)
        copies.append(
            pltpu.make_async_copy(x_ref.at[lanes], x_in.at[lanes], sems.at[len(copies)])
        )
    for c in copies:
        c.start()
    place = iota((count, count), 0)
    quad, rest = place // quarter, place % quarter
    row = (rest // 4) % 4 + jnp.where(quad < 2, 4, 0)
    col = rest % 4 + jnp.where(quad % 2 == 0, 4, 0)
    source = (rest // 16) * 64 + row * 8 + col
    pick = (iota((count, count), 1) == source).astype(F32).astype(BF)
    copies[0].wait()
    copies[1].wait()
    goal = jnp.dot(pick, t_in[...].reshape(count, span), preferred_element_type=F32)
    token = iota((count, 8), 0)
    row_hot = ((token // 8) % 8 == iota((count, 8), 1)).astype(F32)
    by_row = jnp.dot(row_hot, v_in[...].astype(F32), preferred_element_type=F32)
    mine = token % 8 == iota((count, 8), 1)
    natural = jnp.sum(jnp.where(mine, by_row, 0.0), axis=1, keepdims=True)
    spread = jnp.broadcast_to(natural, (count, 128)).astype(BF)
    column = jnp.dot(pick, spread, preferred_element_type=F32)
    extra = jnp.concatenate([goal, column[:, : EXTRA - span]], axis=1).astype(BF)
    outs = [(o0, 0), (o1, quarter), (o2, 2 * quarter), (o3, 5 * quarter // 2), (o4, 3 * quarter)]
    for ref, row in outs:
        ref[:, width:] = extra[row : row + ref.shape[0]]
    for n, at in enumerate(range(0, width, step)):
        copies[2 + n].wait()
        tokens = x_in[:, :, :, at : at + step].reshape(count, step)
        out = jnp.dot(pick, tokens, preferred_element_type=F32).astype(BF)
        for ref, row in outs:
            ref[:, at : at + step] = out[row : row + ref.shape[0]]


def windows_of(own_ref, east_ref, south0_ref, south1_ref, diag_ref):
    return [
        (
            own_ref.at[32 * w : 32 * w + 32],
            east_ref.at[32 * w : 32 * w + 32],
            south,
            diag_ref.at[32 * w : 32 * w + 32],
        )
        for w, south in enumerate((south0_ref, south1_ref))
    ]


def attention_kernel(own_ref, east_ref, south0_ref, south1_ref, diag_ref, ctx_ref):
    tiles = windows_of(own_ref, east_ref, south0_ref, south1_ref, diag_ref)
    part = ctx_ref.shape[1]
    is_last = lax.axis_index("lat") == lax.axis_size("lat") - 1
    same = (iota((512, 128), 0) % 128) // 64 == iota((512, 128), 1) // 64
    bias = jnp.where(jnp.logical_or(same, jnp.logical_not(is_last)), 0.0, -1e30)
    head = iota((128, 128), 1) // HDIM
    factor = math.log2(math.e) / math.sqrt(HDIM)
    for at in range(0, part, 128):
        for w in range(2):
            q, k, v = [
                jnp.concatenate(
                    [t[:, i * part + at : i * part + at + 128] for t in tiles[w]],
                    axis=0,
                )
                for i in range(3)
            ]
            zero = jnp.zeros_like(k)
            k4 = jnp.concatenate([jnp.where(head == h, k, zero) for h in range(4)], axis=0)
            v4 = jnp.concatenate([jnp.where(head == h, v, zero) for h in range(4)], axis=0)
            s = lax.dot_general(k4, q, (((1,), (1,)), ((), ())), preferred_element_type=F32)
            s = s + bias
            parts = []
            for h in range(4):
                sh = s[128 * h : 128 * h + 128]
                e = jnp.exp2((sh - jnp.max(sh, axis=0, keepdims=True)) * factor)
                parts.append((e * (1.0 / jnp.sum(e, axis=0, keepdims=True))).astype(BF))
            attn = jnp.concatenate(parts, axis=0)
            out = lax.dot_general(attn, v4, (((0,), (0,)), ((), ())), preferred_element_type=F32)
            ctx_ref[128 * w : 128 * w + 128, at : at + 128] = out.astype(BF)


def assemble(own_w, own_u, own_gain, pieces, w_all, ug_all):
    zi, part = lax.axis_index("dp"), lax.axis_index("lat")
    rows = own_w.shape[0]
    qr = rows // 4
    steps = len(pieces) // 4 + 1
    base = pl.multiple_of(zi * rows, 128)
    w_all[pl.ds(base, rows), :] = own_w[...]
    span = own_u.shape[0]
    ug_all[0:span, pl.ds(base, rows)] = own_u[...]
    ug_all[span : span + 16, pl.ds(base, rows)] = gain_rows(own_gain, rows)
    for k in range(1, steps):
        shard = lax.rem(zi - k + steps, steps)
        base = pl.multiple_of(shard * rows, 128)
        for bits, piece in zip((0, 2, 1, 3), pieces[4 * k - 4 : 4 * k]):
            from_part = part ^ bits
            row = pl.multiple_of(base + from_part * qr, 32)
            w_all[pl.ds(row, qr), :] = piece[0:qr, :]
            for j in range(4):
                urow = pl.multiple_of((4 * from_part + j) * 16, 16)
                ug_all[pl.ds(urow, 16), pl.ds(base, rows)] = piece[
                    qr : qr + 16, j * rows : (j + 1) * rows
                ]


def split3(x):
    hi = x.astype(BF).astype(F32)
    mid = (x - hi).astype(BF).astype(F32)
    return hi, mid, x - hi - mid


def loss_block(value, rows):
    hi, mid, lo = split3(value)
    lane = iota((rows, 128), 1)
    return jnp.where(lane == 0, hi, jnp.where(lane == 1, mid, jnp.where(lane == 2, lo, 0.0)))


def forward_kernel(lat_ref, var_ref, *refs):
    ctx_ref, refs = refs[0], refs[1:]
    extras, refs = refs[:5], refs[5:]
    owned, refs = refs[:3], refs[3:]
    pieces, refs = refs[:PIECES], refs[PIECES:]
    ts, refs = refs[:4], refs[4:]
    normed_ref, inv_ref, dfc_ref, hidden_ref, w_all, ug_all, term = refs
    lat_place = lax.axis_index("lat")
    assemble(*owned, pieces, w_all, ug_all)
    tokens, width = normed_ref.shape
    span = dfc_ref.shape[1]
    extra = jnp.concatenate([t[...] for tiles in windows_of(*extras) for t in tiles], axis=0)
    extra = extra.astype(F32)
    goal, valid = extra[:, :span], extra[:, span : span + 1]
    token = iota((tokens, 1), 0)
    row = (token // 4) % 4 + jnp.where((token // 32) % 4 >= 2, 4, 0)
    lat_w = jnp.zeros((tokens, 1), F32)
    for r in range(8):
        lat_w = jnp.where(row == r, lat_ref[lat_place * 8 + r], lat_w)
    lane = iota((1, span), 1) // (span // var_ref.shape[0])
    var_w = jnp.zeros((1, span), F32)
    for n in range(var_ref.shape[0]):
        var_w = jnp.where(lane == n, var_ref[n], var_w)
    weight = lat_w * valid * var_w
    mixed = jnp.dot(ctx_ref[...], w_all[...], preferred_element_type=F32)
    centre = jnp.mean(mixed, axis=-1, keepdims=True)
    off = mixed - centre
    inv = lax.rsqrt(jnp.mean(off * off, axis=-1, keepdims=True) + 1e-05)
    normed = off * inv
    normed_ref[...] = normed
    inv_ref[...] = jnp.broadcast_to(inv, inv_ref.shape)
    gain = ug_all[pl.ds(span, 16), :][0:1].astype(F32)
    hidden_ref[...] = (normed * gain).astype(BF)
    field = lax.dot_general(
        hidden_ref[...], ug_all[0:span, :], (((1,), (1,)), ((), ())), preferred_element_type=F32
    )
    misfit = field - goal
    dfc = (2.0 * weight * misfit).astype(BF)
    dfc_ref[...] = dfc
    term[...] = lax.dot_general(
        dfc, hidden_ref[...], (((0,), (0,)), ((), ())), preferred_element_type=F32
    )
    loss = jnp.sum(jnp.sum(weight * misfit * misfit, axis=1, keepdims=True), axis=0, keepdims=True)
    rows = ts[0].shape[0]
    block = loss_block(loss, rows).astype(BF)
    for b, ref in enumerate(ts):
        at = pl.multiple_of((lat_place ^ b) * rows, 8)
        ref[:, :width] = term[pl.ds(at, rows), :].astype(BF)
        ref[:, width:] = block


def backward_kernel(normed_ref, inv_ref, dfc_ref, *refs):
    owned, refs = refs[:3], refs[3:]
    pieces, (out_ref, w_all, ug_all) = refs[:PIECES], refs[PIECES:]
    assemble(*owned, pieces, w_all, ug_all)
    tokens, width = normed_ref.shape
    span = dfc_ref.shape[1]
    gain = ug_all[pl.ds(span, 16), :][0:1].astype(F32)
    g = jnp.dot(dfc_ref[...], ug_all[0:span, :], preferred_element_type=F32) * gain
    normed = normed_ref[...]
    mean_g = jnp.mean(g, axis=-1, keepdims=True)
    mean_gn = jnp.mean(g * normed, axis=-1, keepdims=True)
    dmixed = ((g - mean_g - normed * mean_gn) * inv_ref[:, 0:1]).astype(BF)
    place = iota((tokens, tokens), 0)
    row, col, level = (place // 8) % 8, place % 8, place // 64
    quad = jnp.where(row >= 4, 2, 0) + jnp.where(col >= 4, 1, 0)
    source = (level // 2) * 128 + quad * 32 + (level % 2) * 16 + (row % 4) * 4 + col % 4
    pick = (iota((tokens, tokens), 1) == source).astype(F32).astype(BF)
    dnat = jnp.dot(pick, dmixed, preferred_element_type=F32).astype(BF)
    out = lax.dot_general(dnat, w_all[...], (((1,), (1,)), ((), ())), preferred_element_type=F32)
    out_ref[...] = out.astype(BF)


def add4(a, b, c, d):
    return (a[...].astype(F32) + b[...].astype(F32)) + (c[...].astype(F32) + d[...].astype(F32))


def lat_sum_kernel(a, b, c, d, z0, z1, z2, z3, loss_ref, total_ref):
    total_ref[...] = add4(a, b, c, d)
    zi = lax.axis_index("dp")
    rows, width = z0.shape
    for k, ref in enumerate((z0, z1, z2, z3)):
        at = pl.multiple_of((zi ^ k) * width, 128)
        ref[...] = total_ref[:, pl.ds(at, width)].astype(BF)
    loss = jnp.sum(total_ref[0:1, 4 * width :], axis=1, keepdims=True)
    loss_ref[...] = jnp.broadcast_to(loss, loss_ref.shape)


def dp_sum_kernel(loss_ref, a, b, c, d, o_ref):
    rows, width = a.shape
    o_ref[0:rows, :] = add4(a, b, c, d).astype(BF)
    block = loss_block(loss_ref[0:1, 0:1], o_ref.shape[0] - rows)
    zeros = jnp.zeros((block.shape[0], width - 128), F32)
    o_ref[rows:, :] = jnp.concatenate([block, zeros], axis=1).astype(BF)


def join_kernel(counts, *refs):
    pieces, (o_ref, loss_ref) = refs[:8], refs[8:]
    lat_place = lax.axis_index("lat")
    rows = o_ref.shape[0] // 4
    for a in range(4):
        at = pl.multiple_of((lat_place ^ a) * rows, 8)
        both = [pieces[2 * a + b][0:rows, :].astype(F32) for b in range(2)]
        o_ref[pl.ds(at, rows), :] = (both[0] + both[1]) / counts[0]
    sums = [
        jnp.sum(p[rows : rows + 1, 0:128].astype(F32), axis=1, keepdims=True) for p in pieces[:2]
    ]
    loss_ref[...] = jnp.broadcast_to((sums[0] + sums[1]) / counts[1], loss_ref.shape)


def swap(array, axis, bit):
    return lax.ppermute(array, axis, [(i, i ^ bit) for i in range(lax.axis_size(axis))])


def shape(dims, dtype):
    return jax.ShapeDtypeStruct(dims, dtype)


def shards(projected, targets, valid_cells, w_out, unpatch_matrix, norm_gain, var_weight):
    dp, lat, lon = lax.axis_size("dp"), lax.axis_size("lat"), lax.axis_size("lon")
    rows, width = w_out.shape
    levels = projected.shape[1]
    span = unpatch_matrix.shape[1]
    tokens = levels * 64
    quarter = tokens // 4
    lat_total = 8 * lat
    angle = math.pi * ((np.arange(lat_total) + 0.5) / lat_total - 0.5)
    cosine = np.cos(angle)
    lat_table = jnp.asarray(np.roll(cosine / cosine.mean(), -4), F32)
    barrier = lax.optimization_barrier

    unpatch_t = unpatch_matrix.T
    payload = pl.pallas_call(
        payload_kernel,
        out_shape=shape((rows // 4 + 16, width), BF),
        in_specs=[HBM, HBM, VMEM],
        out_specs=VMEM,
        scratch_shapes=[pltpu.VMEM((UGROWS, rows), BF), pltpu.SemaphoreType.DMA((2,))],
        compiler_params=params(60),
        name="payload",
    )(w_out, unpatch_t, norm_gain)
    ring1 = from_behind(payload, "dp", 1)
    own, *send = pl.pallas_call(
        pack_kernel,
        out_shape=[shape((quarter, 3 * width + EXTRA), BF)] * 2
        + [shape((quarter // 2, 3 * width + EXTRA), BF)] * 2
        + [shape((quarter, 3 * width + EXTRA), BF)],
        in_specs=[HBM] * 3,
        out_specs=[VMEM] * 5,
        scratch_shapes=[
            pltpu.VMEM((levels, 8, 8, 3 * width), BF),
            pltpu.VMEM((levels, 8, 8, span), BF),
            pltpu.VMEM((8, 8), jnp.int32),
            pltpu.SemaphoreType.DMA((2 + 3 * width // 512,)),
        ],
        compiler_params=params(62),
        name="pack",
    )(
        projected.reshape(levels, 8, 8, 3 * width),
        targets.reshape(levels, 8, 8, span),
        valid_cells,
    )
    corner = [
        (a * lon + b, ((a - 1) % lat) * lon + (b - 1) % lon) for a in range(lat) for b in range(lon)
    ]
    tiles = [
        own,
        from_behind(send[0], "lon", -1),
        from_behind(send[1], "lat", -1),
        from_behind(send[2], "lat", -1),
        lax.ppermute(send[3], ("lat", "lon"), corner),
    ]
    ring1_after, tiles[2] = barrier((ring1, tiles[2]))
    ring2 = from_behind(ring1_after, "dp", 1)
    across1 = swap(ring1, "lat", 2)
    ring2_after, across1 = barrier((ring2, across1))
    ring3 = from_behind(ring2_after, "dp", 1)
    across2 = swap(ring2, "lat", 2)
    across3 = swap(ring3, "lat", 2)
    *tiles, ring1, across1, ring2 = barrier((*tiles, ring1, across1, ring2))
    ctx = pl.pallas_call(
        attention_kernel,
        out_shape=shape((tokens, width), BF),
        in_specs=[VMEM] * 5,
        out_specs=VMEM,
        compiler_params=params(16),
        name="attention",
    )(*tiles)
    ctx, across3 = barrier((ctx, across3))
    pieces = []
    for ring, across in ((ring1, across1), (ring2, across2), (ring3, across3)):
        pieces += [ring, across, swap(ring, "lat", 1), swap(across, "lat", 1)]

    piece = span // lat
    extra_specs = [
        pl.BlockSpec((t.shape[0], EXTRA), lambda i: (0, 3 * width // EXTRA)) for t in tiles
    ]
    assembly = [
        pltpu.VMEM((dp * rows, width), BF),
        pltpu.VMEM((UGROWS, dp * rows), BF),
    ]
    *terms, normed, inv, dfc = pl.pallas_call(
        forward_kernel,
        grid=(1,),
        out_shape=[shape((piece, width + 128), BF)] * 4
        + [shape((tokens, width), F32), shape((tokens, 128), F32), shape((tokens, span), BF)],
        in_specs=[SMEM] * 2 + [VMEM] + extra_specs + [VMEM] * (3 + PIECES),
        out_specs=[VMEM] * 7,
        scratch_shapes=[pltpu.VMEM((tokens, width), BF)]
        + assembly
        + [pltpu.VMEM((span, width), F32)],
        compiler_params=params(28),
        name="forward",
    )(lat_table, var_weight, ctx, *tiles, w_out, unpatch_t, norm_gain, *pieces)

    terms = [terms[0]] + [swap(terms[b], "lat", b) for b in (1, 2, 3)]
    grad_context = pl.pallas_call(
        backward_kernel,
        out_shape=shape((tokens, width), BF),
        in_specs=[VMEM] * (6 + PIECES),
        out_specs=VMEM,
        scratch_shapes=assembly,
        compiler_params=params(24),
        name="backward",
    )(normed, inv, dfc, w_out, unpatch_t, norm_gain, *pieces)
    *terms, grad_context = barrier((*terms, grad_context))

    *parts, loss = pl.pallas_call(
        lat_sum_kernel,
        out_shape=[shape((piece, rows), BF)] * 4 + [shape((8, 128), F32)],
        in_specs=[VMEM] * 4,
        out_specs=[VMEM] * 5,
        scratch_shapes=[pltpu.VMEM((piece, width + 128), F32)],
        compiler_params=params(4),
        name="lat_sum",
    )(*terms)
    parts = [parts[0]] + [swap(parts[k], "dp", k) for k in (1, 2, 3)]
    mine = pl.pallas_call(
        dp_sum_kernel,
        out_shape=shape((piece + 8, rows), BF),
        in_specs=[VMEM] * 5,
        out_specs=VMEM,
        compiler_params=params(4),
        name="dp_sum",
    )(loss, *parts)
    plane = [mine]
    for a in range(4):
        for b in range(2):
            if a or b:
                pairs = [
                    (i * lon + j, (i ^ a) * lon + (j ^ b)) for i in range(lat) for j in range(lon)
                ]
                plane.append(lax.ppermute(mine, ("lat", "lon"), pairs))
    count = levels * lat_total * 8 * lon
    counts = (float(count), float(count * (span // var_weight.shape[0])))
    joined, loss = pl.pallas_call(
        lambda *refs: join_kernel(counts, *refs),
        out_shape=[shape((span, rows), F32), shape((1, 1), F32)],
        in_specs=[VMEM] * 8,
        out_specs=[VMEM] * 2,
        compiler_params=params(4),
        name="join",
    )(*plane)
    return grad_context.reshape(1, levels, 8, 8, width), joined.T, loss.reshape(1)


def solution(mesh):
    placed = (
        P("dp", None, "lat", "lon", None),
        P("dp", None, "lat", "lon", None),
        P("lat", "lon"),
        P("dp", None),
        P("dp", None),
        P("dp"),
        P(),
    )
    fits = mesh.shape["dp"] == 4 and mesh.shape["lat"] == 4 and mesh.shape["lon"] == 2

    def program(*arrays):
        body = shards if fits else general_shards
        return jax.shard_map(
            body,
            mesh=mesh,
            in_specs=placed,
            out_specs=(P("dp", None, "lat", "lon", None), P("dp", None), P("dp")),
            check_vma=False,
        )(*arrays)

    return program
```

```python
import functools
import math

import jax
import jax.numpy as jnp
import numpy as np
from jax import lax
from jax.experimental import pallas as pl
from jax.experimental.pallas import tpu as pltpu
from jax.sharding import PartitionSpec as P

HEADS = 48
HDIM = 32
WLEV = 2
BF = jnp.bfloat16
F32 = jnp.float32
EXTRA = 256
UGROWS = 256
PIECES = 12
VMEM = pl.BlockSpec(memory_space=pltpu.VMEM)
SMEM = pl.BlockSpec(memory_space=pltpu.SMEM)
ANY = pl.BlockSpec(memory_space=pl.ANY)
HBM = pl.BlockSpec(memory_space=pltpu.HBM)


def from_behind(array, axis, by):
    length = lax.axis_size(axis)
    return lax.ppermute(array, axis, [(i, (i + by) % length) for i in range(length)])


def general_shards(projected, targets, valid_cells, w_out, unpatch_matrix, norm_gain, var_weight):
    tile_side = projected.shape[2]
    half_side = tile_side // 2
    levels = projected.shape[1]
    model_width = w_out.shape[1]
    predicted_span = unpatch_matrix.shape[1]
    lat_total = tile_side * lax.axis_size("lat")
    lon_total = tile_side * lax.axis_size("lon")
    lat_place = lax.axis_index("lat")
    moved = from_behind(
        (projected[:, :, :, :half_side], targets[:, :, :, :half_side], valid_cells[:, :half_side]),
        "lon",
        -1,
    )
    strip_proj = jnp.concatenate([projected[:, :, :, half_side:], moved[0]], axis=3)
    strip_goal = jnp.concatenate([targets[:, :, :, half_side:], moved[1]], axis=3)
    strip_valid = jnp.concatenate([valid_cells[:, half_side:], moved[2]], axis=1)
    moved_rows = from_behind(
        (strip_proj[:, :, :half_side], strip_goal[:, :, :half_side], strip_valid[:half_side]),
        "lat",
        -1,
    )
    local_proj = jnp.concatenate([strip_proj[:, :, half_side:], moved_rows[0]], axis=2)
    shard_reference = jnp.concatenate([strip_goal[:, :, half_side:], moved_rows[1]], axis=2)
    local_valid = jnp.concatenate([strip_valid[half_side:], moved_rows[2]], axis=0).astype(F32)
    win_count = levels // WLEV
    tokw = WLEV * tile_side * tile_side
    windows = local_proj.reshape(win_count, tokw, 3 * model_width)
    rows_here = lat_place * tile_side + jnp.arange(tile_side)
    region_rows = (rows_here >= lat_total - half_side).astype(jnp.int32)
    region = jnp.broadcast_to(region_rows[None, :, None], (WLEV, tile_side, tile_side)).reshape(-1)
    allowed = region[:, None] == region[None, :]
    queries = windows[..., :model_width].reshape(win_count, tokw, HEADS, -1)
    key_heads = windows[..., model_width : 2 * model_width].reshape(win_count, tokw, HEADS, -1)
    value_heads = windows[..., 2 * model_width :].reshape(win_count, tokw, HEADS, -1)
    scores = jnp.einsum("wqhd,wkhd->whqk", queries, key_heads, preferred_element_type=F32)
    scores = scores * (1.0 / math.sqrt(HDIM))
    scores = jnp.where(allowed[None, None], scores, -1e30)
    row_peak = jnp.max(scores, axis=-1, keepdims=True)
    lifted = jnp.exp(scores - row_peak)
    attn = (lifted / jnp.sum(lifted, axis=-1, keepdims=True)).astype(BF)
    context = jnp.einsum("whqk,wkhd->wqhd", attn, value_heads, preferred_element_type=F32)
    context = context.astype(BF).reshape(win_count * tokw, model_width)
    element_total = win_count * tokw
    out_all, unprojected_pieces, gain_all = (
        lax.all_gather(w_out, "dp", axis=0, tiled=True),
        lax.all_gather(unpatch_matrix, "dp", axis=0, tiled=True),
        lax.all_gather(norm_gain, "dp", axis=0, tiled=True),
    )
    mixed_rows = jnp.dot(context, out_all, preferred_element_type=F32)
    centre = jnp.mean(mixed_rows, axis=-1, keepdims=True)
    spread = jnp.mean((mixed_rows - centre) ** 2, axis=-1, keepdims=True)
    inv_spread = lax.rsqrt(spread + 1e-05)
    normed = (mixed_rows - centre) * inv_spread
    gain_f = gain_all.astype(F32)
    latent_activation = (normed * gain_f).astype(BF)
    prediction_field = jnp.dot(latent_activation, unprojected_pieces, preferred_element_type=F32)
    prediction_misfit = prediction_field - shard_reference.reshape(
        element_total, predicted_span
    ).astype(F32)
    all_rows = jnp.arange(lat_total).astype(F32)
    cosine_mean = jnp.mean(jnp.cos(math.pi * ((all_rows + 0.5) / lat_total - 0.5)))
    initial_rows = ((rows_here + half_side) % lat_total).astype(F32)
    lat_here = jnp.cos(math.pi * ((initial_rows + 0.5) / lat_total - 0.5)) / cosine_mean
    element_factor = jnp.broadcast_to(
        lat_here[None, :, None] * local_valid[None], (levels, tile_side, tile_side)
    ).reshape(element_total, 1)
    variable_factor = jnp.repeat(var_weight, predicted_span // var_weight.shape[0])[None, :]
    shard_penalty = jnp.sum(
        element_factor * variable_factor * prediction_misfit * prediction_misfit
    ) / (levels * lat_total * lon_total * (predicted_span // var_weight.shape[0]))
    prediction_gradient = (2.0 * element_factor * variable_factor * prediction_misfit).astype(BF)
    grad_shard = lax.psum_scatter(
        jnp.einsum(
            "td,to->do", latent_activation, prediction_gradient, preferred_element_type=F32
        ).astype(BF),
        "dp",
        scatter_dimension=0,
        tiled=True,
    ).astype(F32)
    grad_sum, loss_sum = lax.psum((grad_shard, shard_penalty), ("lat", "lon"))
    grad_recovery = grad_sum / (levels * lat_total * lon_total)
    grad_hidden = jnp.einsum(
        "to,do->td", prediction_gradient, unprojected_pieces, preferred_element_type=F32
    )
    scaled_grad = grad_hidden * gain_f
    grad_mixed = inv_spread * (
        scaled_grad
        - jnp.mean(scaled_grad, axis=-1, keepdims=True)
        - normed * jnp.mean(scaled_grad * normed, axis=-1, keepdims=True)
    )
    grad_mixed = grad_mixed.astype(BF)
    grad_context = jnp.einsum("tj,ij->ti", grad_mixed, out_all, preferred_element_type=F32)
    grad_context = grad_context.astype(BF).reshape(1, levels, tile_side, tile_side, model_width)
    return (grad_context, grad_recovery, loss_sum.reshape(1))


def params(mib):
    return pltpu.CompilerParams(vmem_limit_bytes=mib << 20)


def iota(shape, dim):
    return lax.broadcasted_iota(jnp.int32, shape, dim)


def payload_kernel(w_ref, unpatch_ref, gain_ref, payload_ref, ug, sems):
    part = lax.axis_index("lat")
    rows, width = w_ref.shape
    qr = rows // 4
    span = unpatch_ref.shape[0]
    start = pl.multiple_of(part * qr, 32)
    u_copy = pltpu.make_async_copy(unpatch_ref, ug.at[pl.ds(0, span), :], sems.at[0])
    u_copy.start()
    w_copy = pltpu.make_async_copy(
        w_ref.at[pl.ds(start, qr), :], payload_ref.at[pl.ds(0, qr), :], sems.at[1]
    )
    w_copy.start()
    ug[pl.ds(span, 16), :] = gain_rows(gain_ref, rows)
    ug[pl.ds(span + 16, UGROWS - span - 16), :] = jnp.zeros((UGROWS - span - 16, rows), BF)
    u_copy.wait()
    for j in range(4):
        at = pl.multiple_of((4 * part + j) * 16, 16)
        payload_ref[pl.ds(qr, 16), pl.ds(j * rows, rows)] = ug[pl.ds(at, 16), :]
    w_copy.wait()


def gain_rows(gain_ref, rows):
    return jnp.broadcast_to(gain_ref[...].astype(F32).reshape(1, rows), (16, rows)).astype(BF)


def pack_kernel(x_ref, t_ref, valid_ref, o0, o1, o2, o3, o4, x_in, t_in, v_in, sems):
    span = t_ref.shape[-1]
    count = x_ref.shape[0] * 64
    quarter = count // 4
    step = 512
    width = x_ref.shape[-1]
    copies = [
        pltpu.make_async_copy(t_ref, t_in, sems.at[0]),
        pltpu.make_async_copy(valid_ref, v_in, sems.at[1]),
    ]
    for at in range(0, width, step):
        lanes = (slice(None),) * 3 + (pl.ds(at, step),)
        copies.append(
            pltpu.make_async_copy(x_ref.at[lanes], x_in.at[lanes], sems.at[len(copies)])
        )
    for c in copies:
        c.start()
    place = iota((count, count), 0)
    quad, rest = place // quarter, place % quarter
    row = (rest // 4) % 4 + jnp.where(quad < 2, 4, 0)
    col = rest % 4 + jnp.where(quad % 2 == 0, 4, 0)
    source = (rest // 16) * 64 + row * 8 + col
    pick = (iota((count, count), 1) == source).astype(F32).astype(BF)
    copies[0].wait()
    copies[1].wait()
    goal = jnp.dot(pick, t_in[...].reshape(count, span), preferred_element_type=F32)
    token = iota((count, 8), 0)
    row_hot = ((token // 8) % 8 == iota((count, 8), 1)).astype(F32)
    by_row = jnp.dot(row_hot, v_in[...].astype(F32), preferred_element_type=F32)
    mine = token % 8 == iota((count, 8), 1)
    natural = jnp.sum(jnp.where(mine, by_row, 0.0), axis=1, keepdims=True)
    spread = jnp.broadcast_to(natural, (count, 128)).astype(BF)
    column = jnp.dot(pick, spread, preferred_element_type=F32)
    extra = jnp.concatenate([goal, column[:, : EXTRA - span]], axis=1).astype(BF)
    outs = [(o0, 0), (o1, quarter), (o2, 2 * quarter), (o3, 5 * quarter // 2), (o4, 3 * quarter)]
    for ref, row in outs:
        ref[:, width:] = extra[row : row + ref.shape[0]]
    for n, at in enumerate(range(0, width, step)):
        copies[2 + n].wait()
        tokens = x_in[:, :, :, at : at + step].reshape(count, step)
        out = jnp.dot(pick, tokens, preferred_element_type=F32).astype(BF)
        for ref, row in outs:
            ref[:, at : at + step] = out[row : row + ref.shape[0]]


def windows_of(own_ref, east_ref, south0_ref, south1_ref, diag_ref):
    return [
        (
            own_ref.at[32 * w : 32 * w + 32],
            east_ref.at[32 * w : 32 * w + 32],
            south,
            diag_ref.at[32 * w : 32 * w + 32],
        )
        for w, south in enumerate((south0_ref, south1_ref))
    ]


def attention_kernel(own_ref, east_ref, south0_ref, south1_ref, diag_ref, ctx_ref):
    tiles = windows_of(own_ref, east_ref, south0_ref, south1_ref, diag_ref)
    part = ctx_ref.shape[1]
    is_last = lax.axis_index("lat") == lax.axis_size("lat") - 1
    same = (iota((512, 128), 0) % 128) // 64 == iota((512, 128), 1) // 64
    bias = jnp.where(jnp.logical_or(same, jnp.logical_not(is_last)), 0.0, -1e30)
    head = iota((128, 128), 1) // HDIM
    factor = math.log2(math.e) / math.sqrt(HDIM)
    for at in range(0, part, 128):
        for w in range(2):
            q, k, v = [
                jnp.concatenate(
                    [t[:, i * part + at : i * part + at + 128] for t in tiles[w]],
                    axis=0,
                )
                for i in range(3)
            ]
            zero = jnp.zeros_like(k)
            k4 = jnp.concatenate([jnp.where(head == h, k, zero) for h in range(4)], axis=0)
            v4 = jnp.concatenate([jnp.where(head == h, v, zero) for h in range(4)], axis=0)
            s = lax.dot_general(k4, q, (((1,), (1,)), ((), ())), preferred_element_type=F32)
            s = s + bias
            parts = []
            for h in range(4):
                sh = s[128 * h : 128 * h + 128]
                e = jnp.exp2((sh - jnp.max(sh, axis=0, keepdims=True)) * factor)
                parts.append((e * (1.0 / jnp.sum(e, axis=0, keepdims=True))).astype(BF))
            attn = jnp.concatenate(parts, axis=0)
            out = lax.dot_general(attn, v4, (((0,), (0,)), ((), ())), preferred_element_type=F32)
            ctx_ref[128 * w : 128 * w + 128, at : at + 128] = out.astype(BF)


def assemble(own_w, own_u, own_gain, pieces, w_all, ug_all):
    zi, part = lax.axis_index("dp"), lax.axis_index("lat")
    rows = own_w.shape[0]
    qr = rows // 4
    steps = len(pieces) // 4 + 1
    base = pl.multiple_of(zi * rows, 128)
    w_all[pl.ds(base, rows), :] = own_w[...]
    span = own_u.shape[0]
    ug_all[0:span, pl.ds(base, rows)] = own_u[...]
    ug_all[span : span + 16, pl.ds(base, rows)] = gain_rows(own_gain, rows)
    for k in range(1, steps):
        shard = lax.rem(zi - k + steps, steps)
        base = pl.multiple_of(shard * rows, 128)
        for bits, piece in zip((0, 2, 1, 3), pieces[4 * k - 4 : 4 * k]):
            from_part = part ^ bits
            row = pl.multiple_of(base + from_part * qr, 32)
            w_all[pl.ds(row, qr), :] = piece[0:qr, :]
            for j in range(4):
                urow = pl.multiple_of((4 * from_part + j) * 16, 16)
                ug_all[pl.ds(urow, 16), pl.ds(base, rows)] = piece[
                    qr : qr + 16, j * rows : (j + 1) * rows
                ]


def split3(x):
    hi = x.astype(BF).astype(F32)
    mid = (x - hi).astype(BF).astype(F32)
    return hi, mid, x - hi - mid


def loss_block(value, rows):
    hi, mid, lo = split3(value)
    lane = iota((rows, 128), 1)
    return jnp.where(lane == 0, hi, jnp.where(lane == 1, mid, jnp.where(lane == 2, lo, 0.0)))


def forward_kernel(lat_ref, var_ref, *refs):
    ctx_ref, refs = refs[0], refs[1:]
    extras, refs = refs[:5], refs[5:]
    owned, refs = refs[:3], refs[3:]
    pieces, refs = refs[:PIECES], refs[PIECES:]
    ts, refs = refs[:4], refs[4:]
    normed_ref, inv_ref, dfc_ref, hidden_ref, w_all, ug_all, term = refs
    lat_place = lax.axis_index("lat")
    assemble(*owned, pieces, w_all, ug_all)
    tokens, width = normed_ref.shape
    span = dfc_ref.shape[1]
    extra = jnp.concatenate([t[...] for tiles in windows_of(*extras) for t in tiles], axis=0)
    extra = extra.astype(F32)
    goal, valid = extra[:, :span], extra[:, span : span + 1]
    token = iota((tokens, 1), 0)
    row = (token // 4) % 4 + jnp.where((token // 32) % 4 >= 2, 4, 0)
    lat_w = jnp.zeros((tokens, 1), F32)
    for r in range(8):
        lat_w = jnp.where(row == r, lat_ref[lat_place * 8 + r], lat_w)
    lane = iota((1, span), 1) // (span // var_ref.shape[0])
    var_w = jnp.zeros((1, span), F32)
    for n in range(var_ref.shape[0]):
        var_w = jnp.where(lane == n, var_ref[n], var_w)
    weight = lat_w * valid * var_w
    mixed = jnp.dot(ctx_ref[...], w_all[...], preferred_element_type=F32)
    centre = jnp.mean(mixed, axis=-1, keepdims=True)
    off = mixed - centre
    inv = lax.rsqrt(jnp.mean(off * off, axis=-1, keepdims=True) + 1e-05)
    normed = off * inv
    normed_ref[...] = normed
    inv_ref[...] = jnp.broadcast_to(inv, inv_ref.shape)
    gain = ug_all[pl.ds(span, 16), :][0:1].astype(F32)
    hidden_ref[...] = (normed * gain).astype(BF)
    field = lax.dot_general(
        hidden_ref[...], ug_all[0:span, :], (((1,), (1,)), ((), ())), preferred_element_type=F32
    )
    misfit = field - goal
    dfc = (2.0 * weight * misfit).astype(BF)
    dfc_ref[...] = dfc
    term[...] = lax.dot_general(
        dfc, hidden_ref[...], (((0,), (0,)), ((), ())), preferred_element_type=F32
    )
    loss = jnp.sum(jnp.sum(weight * misfit * misfit, axis=1, keepdims=True), axis=0, keepdims=True)
    rows = ts[0].shape[0]
    block = loss_block(loss, rows).astype(BF)
    for b, ref in enumerate(ts):
        at = pl.multiple_of((lat_place ^ b) * rows, 8)
        ref[:, :width] = term[pl.ds(at, rows), :].astype(BF)
        ref[:, width:] = block


def backward_kernel(normed_ref, inv_ref, dfc_ref, *refs):
    owned, refs = refs[:3], refs[3:]
    pieces, (out_ref, w_all, ug_all) = refs[:PIECES], refs[PIECES:]
    assemble(*owned, pieces, w_all, ug_all)
    tokens, width = normed_ref.shape
    span = dfc_ref.shape[1]
    gain = ug_all[pl.ds(span, 16), :][0:1].astype(F32)
    g = jnp.dot(dfc_ref[...], ug_all[0:span, :], preferred_element_type=F32) * gain
    normed = normed_ref[...]
    mean_g = jnp.mean(g, axis=-1, keepdims=True)
    mean_gn = jnp.mean(g * normed, axis=-1, keepdims=True)
    dmixed = ((g - mean_g - normed * mean_gn) * inv_ref[:, 0:1]).astype(BF)
    place = iota((tokens, tokens), 0)
    row, col, level = (place // 8) % 8, place % 8, place // 64
    quad = jnp.where(row >= 4, 2, 0) + jnp.where(col >= 4, 1, 0)
    source = (level // 2) * 128 + quad * 32 + (level % 2) * 16 + (row % 4) * 4 + col % 4
    pick = (iota((tokens, tokens), 1) == source).astype(F32).astype(BF)
    dnat = jnp.dot(pick, dmixed, preferred_element_type=F32).astype(BF)
    out = lax.dot_general(dnat, w_all[...], (((1,), (1,)), ((), ())), preferred_element_type=F32)
    out_ref[...] = out.astype(BF)


def add4(a, b, c, d):
    return (a[...].astype(F32) + b[...].astype(F32)) + (c[...].astype(F32) + d[...].astype(F32))


def lat_sum_kernel(a, b, c, d, z0, z1, z2, z3, loss_ref, total_ref):
    total_ref[...] = add4(a, b, c, d)
    zi = lax.axis_index("dp")
    rows, width = z0.shape
    for k, ref in enumerate((z0, z1, z2, z3)):
        at = pl.multiple_of((zi ^ k) * width, 128)
        ref[...] = total_ref[:, pl.ds(at, width)].astype(BF)
    loss = jnp.sum(total_ref[0:1, 4 * width :], axis=1, keepdims=True)
    loss_ref[...] = jnp.broadcast_to(loss, loss_ref.shape)


def dp_sum_kernel(loss_ref, a, b, c, d, o_ref):
    rows, width = a.shape
    o_ref[0:rows, :] = add4(a, b, c, d).astype(BF)
    block = loss_block(loss_ref[0:1, 0:1], o_ref.shape[0] - rows)
    zeros = jnp.zeros((block.shape[0], width - 128), F32)
    o_ref[rows:, :] = jnp.concatenate([block, zeros], axis=1).astype(BF)


def join_kernel(counts, *refs):
    pieces, (o_ref, loss_ref) = refs[:8], refs[8:]
    lat_place = lax.axis_index("lat")
    rows = o_ref.shape[0] // 4
    for a in range(4):
        at = pl.multiple_of((lat_place ^ a) * rows, 8)
        both = [pieces[2 * a + b][0:rows, :].astype(F32) for b in range(2)]
        o_ref[pl.ds(at, rows), :] = (both[0] + both[1]) / counts[0]
    sums = [
        jnp.sum(p[rows : rows + 1, 0:128].astype(F32), axis=1, keepdims=True) for p in pieces[:2]
    ]
    loss_ref[...] = jnp.broadcast_to((sums[0] + sums[1]) / counts[1], loss_ref.shape)


def swap(array, axis, bit):
    return lax.ppermute(array, axis, [(i, i ^ bit) for i in range(lax.axis_size(axis))])


def shape(dims, dtype):
    return jax.ShapeDtypeStruct(dims, dtype)


def shards(projected, targets, valid_cells, w_out, unpatch_matrix, norm_gain, var_weight):
    dp, lat, lon = lax.axis_size("dp"), lax.axis_size("lat"), lax.axis_size("lon")
    rows, width = w_out.shape
    levels = projected.shape[1]
    span = unpatch_matrix.shape[1]
    tokens = levels * 64
    quarter = tokens // 4
    lat_total = 8 * lat
    angle = math.pi * ((np.arange(lat_total) + 0.5) / lat_total - 0.5)
    cosine = np.cos(angle)
    lat_table = jnp.asarray(np.roll(cosine / cosine.mean(), -4), F32)
    barrier = lax.optimization_barrier

    unpatch_t = unpatch_matrix.T
    payload = pl.pallas_call(
        payload_kernel,
        out_shape=shape((rows // 4 + 16, width), BF),
        in_specs=[HBM, HBM, VMEM],
        out_specs=VMEM,
        scratch_shapes=[pltpu.VMEM((UGROWS, rows), BF), pltpu.SemaphoreType.DMA((2,))],
        compiler_params=params(60),
        name="payload",
    )(w_out, unpatch_t, norm_gain)
    ring1 = from_behind(payload, "dp", 1)
    own, *send = pl.pallas_call(
        pack_kernel,
        out_shape=[shape((quarter, 3 * width + EXTRA), BF)] * 2
        + [shape((quarter // 2, 3 * width + EXTRA), BF)] * 2
        + [shape((quarter, 3 * width + EXTRA), BF)],
        in_specs=[HBM] * 3,
        out_specs=[VMEM] * 5,
        scratch_shapes=[
            pltpu.VMEM((levels, 8, 8, 3 * width), BF),
            pltpu.VMEM((levels, 8, 8, span), BF),
            pltpu.VMEM((8, 8), jnp.int32),
            pltpu.SemaphoreType.DMA((2 + 3 * width // 512,)),
        ],
        compiler_params=params(62),
        name="pack",
    )(
        projected.reshape(levels, 8, 8, 3 * width),
        targets.reshape(levels, 8, 8, span),
        valid_cells,
    )
    corner = [
        (a * lon + b, ((a - 1) % lat) * lon + (b - 1) % lon) for a in range(lat) for b in range(lon)
    ]
    tiles = [
        own,
        from_behind(send[0], "lon", -1),
        from_behind(send[1], "lat", -1),
        from_behind(send[2], "lat", -1),
        lax.ppermute(send[3], ("lat", "lon"), corner),
    ]
    ring1_after, tiles[2] = barrier((ring1, tiles[2]))
    ring2 = from_behind(ring1_after, "dp", 1)
    across1 = swap(ring1, "lat", 2)
    ring2_after, across1, tiles[3] = barrier((ring2, across1, tiles[3]))
    ring3 = from_behind(ring2_after, "dp", 1)
    across2 = swap(ring2, "lat", 2)
    across3 = swap(ring3, "lat", 2)
    *tiles, ring1, across1, ring2 = barrier((*tiles, ring1, across1, ring2))
    ctx = pl.pallas_call(
        attention_kernel,
        out_shape=shape((tokens, width), BF),
        in_specs=[VMEM] * 5,
        out_specs=VMEM,
        compiler_params=params(16),
        name="attention",
    )(*tiles)
    ctx, across3 = barrier((ctx, across3))
    pieces = []
    for ring, across in ((ring1, across1), (ring2, across2), (ring3, across3)):
        pieces += [ring, across, swap(ring, "lat", 1), swap(across, "lat", 1)]

    piece = span // lat
    extra_specs = [
        pl.BlockSpec((t.shape[0], EXTRA), lambda i: (0, 3 * width // EXTRA)) for t in tiles
    ]
    assembly = [
        pltpu.VMEM((dp * rows, width), BF),
        pltpu.VMEM((UGROWS, dp * rows), BF),
    ]
    *terms, normed, inv, dfc = pl.pallas_call(
        forward_kernel,
        grid=(1,),
        out_shape=[shape((piece, width + 128), BF)] * 4
        + [shape((tokens, width), F32), shape((tokens, 128), F32), shape((tokens, span), BF)],
        in_specs=[SMEM] * 2 + [VMEM] + extra_specs + [VMEM] * (3 + PIECES),
        out_specs=[VMEM] * 7,
        scratch_shapes=[pltpu.VMEM((tokens, width), BF)]
        + assembly
        + [pltpu.VMEM((span, width), F32)],
        compiler_params=params(28),
        name="forward",
    )(lat_table, var_weight, ctx, *tiles, w_out, unpatch_t, norm_gain, *pieces)

    terms = [terms[0]] + [swap(terms[b], "lat", b) for b in (1, 2, 3)]
    grad_context = pl.pallas_call(
        backward_kernel,
        out_shape=shape((tokens, width), BF),
        in_specs=[VMEM] * (6 + PIECES),
        out_specs=VMEM,
        scratch_shapes=assembly,
        compiler_params=params(24),
        name="backward",
    )(normed, inv, dfc, w_out, unpatch_t, norm_gain, *pieces)
    *terms, grad_context = barrier((*terms, grad_context))

    *parts, loss = pl.pallas_call(
        lat_sum_kernel,
        out_shape=[shape((piece, rows), BF)] * 4 + [shape((8, 128), F32)],
        in_specs=[VMEM] * 4,
        out_specs=[VMEM] * 5,
        scratch_shapes=[pltpu.VMEM((piece, width + 128), F32)],
        compiler_params=params(4),
        name="lat_sum",
    )(*terms)
    parts = [parts[0]] + [swap(parts[k], "dp", k) for k in (1, 2, 3)]
    mine = pl.pallas_call(
        dp_sum_kernel,
        out_shape=shape((piece + 8, rows), BF),
        in_specs=[VMEM] * 5,
        out_specs=VMEM,
        compiler_params=params(4),
        name="dp_sum",
    )(loss, *parts)
    plane = [mine]
    for a in range(4):
        for b in range(2):
            if a or b:
                pairs = [
                    (i * lon + j, (i ^ a) * lon + (j ^ b)) for i in range(lat) for j in range(lon)
                ]
                plane.append(lax.ppermute(mine, ("lat", "lon"), pairs))
    count = levels * lat_total * 8 * lon
    counts = (float(count), float(count * (span // var_weight.shape[0])))
    joined, loss = pl.pallas_call(
        lambda *refs: join_kernel(counts, *refs),
        out_shape=[shape((span, rows), F32), shape((1, 1), F32)],
        in_specs=[VMEM] * 8,
        out_specs=[VMEM] * 2,
        compiler_params=params(4),
        name="join",
    )(*plane)
    return grad_context.reshape(1, levels, 8, 8, width), joined.T, loss.reshape(1)


def solution(mesh):
    placed = (
        P("dp", None, "lat", "lon", None),
        P("dp", None, "lat", "lon", None),
        P("lat", "lon"),
        P("dp", None),
        P("dp", None),
        P("dp"),
        P(),
    )
    fits = mesh.shape["dp"] == 4 and mesh.shape["lat"] == 4 and mesh.shape["lon"] == 2

    def program(*arrays):
        body = shards if fits else general_shards
        return jax.shard_map(
            body,
            mesh=mesh,
            in_specs=placed,
            out_specs=(P("dp", None, "lat", "lon", None), P("dp", None), P("dp")),
            check_vma=False,
        )(*arrays)

    return program
```

```python
import functools
import math

import jax
import jax.numpy as jnp
import numpy as np
from jax import lax
from jax.experimental import pallas as pl
from jax.experimental.pallas import tpu as pltpu
from jax.sharding import PartitionSpec as P

HEADS = 48
HDIM = 32
WLEV = 2
BF = jnp.bfloat16
F32 = jnp.float32
EXTRA = 256
UGROWS = 256
PIECES = 12
VMEM = pl.BlockSpec(memory_space=pltpu.VMEM)
SMEM = pl.BlockSpec(memory_space=pltpu.SMEM)
ANY = pl.BlockSpec(memory_space=pl.ANY)
HBM = pl.BlockSpec(memory_space=pltpu.HBM)


def from_behind(array, axis, by):
    length = lax.axis_size(axis)
    return lax.ppermute(array, axis, [(i, (i + by) % length) for i in range(length)])


def general_shards(projected, targets, valid_cells, w_out, unpatch_matrix, norm_gain, var_weight):
    tile_side = projected.shape[2]
    half_side = tile_side // 2
    levels = projected.shape[1]
    model_width = w_out.shape[1]
    predicted_span = unpatch_matrix.shape[1]
    lat_total = tile_side * lax.axis_size("lat")
    lon_total = tile_side * lax.axis_size("lon")
    lat_place = lax.axis_index("lat")
    moved = from_behind(
        (projected[:, :, :, :half_side], targets[:, :, :, :half_side], valid_cells[:, :half_side]),
        "lon",
        -1,
    )
    strip_proj = jnp.concatenate([projected[:, :, :, half_side:], moved[0]], axis=3)
    strip_goal = jnp.concatenate([targets[:, :, :, half_side:], moved[1]], axis=3)
    strip_valid = jnp.concatenate([valid_cells[:, half_side:], moved[2]], axis=1)
    moved_rows = from_behind(
        (strip_proj[:, :, :half_side], strip_goal[:, :, :half_side], strip_valid[:half_side]),
        "lat",
        -1,
    )
    local_proj = jnp.concatenate([strip_proj[:, :, half_side:], moved_rows[0]], axis=2)
    shard_reference = jnp.concatenate([strip_goal[:, :, half_side:], moved_rows[1]], axis=2)
    local_valid = jnp.concatenate([strip_valid[half_side:], moved_rows[2]], axis=0).astype(F32)
    win_count = levels // WLEV
    tokw = WLEV * tile_side * tile_side
    windows = local_proj.reshape(win_count, tokw, 3 * model_width)
    rows_here = lat_place * tile_side + jnp.arange(tile_side)
    region_rows = (rows_here >= lat_total - half_side).astype(jnp.int32)
    region = jnp.broadcast_to(region_rows[None, :, None], (WLEV, tile_side, tile_side)).reshape(-1)
    allowed = region[:, None] == region[None, :]
    queries = windows[..., :model_width].reshape(win_count, tokw, HEADS, -1)
    key_heads = windows[..., model_width : 2 * model_width].reshape(win_count, tokw, HEADS, -1)
    value_heads = windows[..., 2 * model_width :].reshape(win_count, tokw, HEADS, -1)
    scores = jnp.einsum("wqhd,wkhd->whqk", queries, key_heads, preferred_element_type=F32)
    scores = scores * (1.0 / math.sqrt(HDIM))
    scores = jnp.where(allowed[None, None], scores, -1e30)
    row_peak = jnp.max(scores, axis=-1, keepdims=True)
    lifted = jnp.exp(scores - row_peak)
    attn = (lifted / jnp.sum(lifted, axis=-1, keepdims=True)).astype(BF)
    context = jnp.einsum("whqk,wkhd->wqhd", attn, value_heads, preferred_element_type=F32)
    context = context.astype(BF).reshape(win_count * tokw, model_width)
    element_total = win_count * tokw
    out_all, unprojected_pieces, gain_all = (
        lax.all_gather(w_out, "dp", axis=0, tiled=True),
        lax.all_gather(unpatch_matrix, "dp", axis=0, tiled=True),
        lax.all_gather(norm_gain, "dp", axis=0, tiled=True),
    )
    mixed_rows = jnp.dot(context, out_all, preferred_element_type=F32)
    centre = jnp.mean(mixed_rows, axis=-1, keepdims=True)
    spread = jnp.mean((mixed_rows - centre) ** 2, axis=-1, keepdims=True)
    inv_spread = lax.rsqrt(spread + 1e-05)
    normed = (mixed_rows - centre) * inv_spread
    gain_f = gain_all.astype(F32)
    latent_activation = (normed * gain_f).astype(BF)
    prediction_field = jnp.dot(latent_activation, unprojected_pieces, preferred_element_type=F32)
    prediction_misfit = prediction_field - shard_reference.reshape(
        element_total, predicted_span
    ).astype(F32)
    all_rows = jnp.arange(lat_total).astype(F32)
    cosine_mean = jnp.mean(jnp.cos(math.pi * ((all_rows + 0.5) / lat_total - 0.5)))
    initial_rows = ((rows_here + half_side) % lat_total).astype(F32)
    lat_here = jnp.cos(math.pi * ((initial_rows + 0.5) / lat_total - 0.5)) / cosine_mean
    element_factor = jnp.broadcast_to(
        lat_here[None, :, None] * local_valid[None], (levels, tile_side, tile_side)
    ).reshape(element_total, 1)
    variable_factor = jnp.repeat(var_weight, predicted_span // var_weight.shape[0])[None, :]
    shard_penalty = jnp.sum(
        element_factor * variable_factor * prediction_misfit * prediction_misfit
    ) / (levels * lat_total * lon_total * (predicted_span // var_weight.shape[0]))
    prediction_gradient = (2.0 * element_factor * variable_factor * prediction_misfit).astype(BF)
    grad_shard = lax.psum_scatter(
        jnp.einsum(
            "td,to->do", latent_activation, prediction_gradient, preferred_element_type=F32
        ).astype(BF),
        "dp",
        scatter_dimension=0,
        tiled=True,
    ).astype(F32)
    grad_sum, loss_sum = lax.psum((grad_shard, shard_penalty), ("lat", "lon"))
    grad_recovery = grad_sum / (levels * lat_total * lon_total)
    grad_hidden = jnp.einsum(
        "to,do->td", prediction_gradient, unprojected_pieces, preferred_element_type=F32
    )
    scaled_grad = grad_hidden * gain_f
    grad_mixed = inv_spread * (
        scaled_grad
        - jnp.mean(scaled_grad, axis=-1, keepdims=True)
        - normed * jnp.mean(scaled_grad * normed, axis=-1, keepdims=True)
    )
    grad_mixed = grad_mixed.astype(BF)
    grad_context = jnp.einsum("tj,ij->ti", grad_mixed, out_all, preferred_element_type=F32)
    grad_context = grad_context.astype(BF).reshape(1, levels, tile_side, tile_side, model_width)
    return (grad_context, grad_recovery, loss_sum.reshape(1))


def params(mib):
    return pltpu.CompilerParams(vmem_limit_bytes=mib << 20)


def iota(shape, dim):
    return lax.broadcasted_iota(jnp.int32, shape, dim)


def payload_kernel(w_ref, unpatch_ref, gain_ref, payload_ref, ug, sems):
    part = lax.axis_index("lat")
    rows, width = w_ref.shape
    qr = rows // 4
    span = unpatch_ref.shape[0]
    start = pl.multiple_of(part * qr, 32)
    u_copy = pltpu.make_async_copy(unpatch_ref, ug.at[pl.ds(0, span), :], sems.at[0])
    u_copy.start()
    w_copy = pltpu.make_async_copy(
        w_ref.at[pl.ds(start, qr), :], payload_ref.at[pl.ds(0, qr), :], sems.at[1]
    )
    w_copy.start()
    ug[pl.ds(span, 16), :] = gain_rows(gain_ref, rows)
    ug[pl.ds(span + 16, UGROWS - span - 16), :] = jnp.zeros((UGROWS - span - 16, rows), BF)
    u_copy.wait()
    for j in range(4):
        at = pl.multiple_of((4 * part + j) * 16, 16)
        payload_ref[pl.ds(qr, 16), pl.ds(j * rows, rows)] = ug[pl.ds(at, 16), :]
    w_copy.wait()


def gain_rows(gain_ref, rows):
    return jnp.broadcast_to(gain_ref[...].astype(F32).reshape(1, rows), (16, rows)).astype(BF)


def pack_kernel(x_ref, t_ref, valid_ref, *refs):
    outs, (x_in, t_in, v_in, sems) = refs[:4], refs[4:]
    span = t_ref.shape[-1]
    count = x_ref.shape[0] * 64
    quarter = count // 4
    step = 512
    width = x_ref.shape[-1]
    copies = [
        pltpu.make_async_copy(t_ref, t_in, sems.at[0]),
        pltpu.make_async_copy(valid_ref, v_in, sems.at[1]),
    ]
    for at in range(0, width, step):
        lanes = (slice(None),) * 3 + (pl.ds(at, step),)
        copies.append(
            pltpu.make_async_copy(x_ref.at[lanes], x_in.at[lanes], sems.at[len(copies)])
        )
    for c in copies:
        c.start()
    place = iota((count, count), 0)
    quad, rest = place // quarter, place % quarter
    row = (rest // 4) % 4 + jnp.where(quad < 2, 4, 0)
    col = rest % 4 + jnp.where(quad % 2 == 0, 4, 0)
    source = (rest // 16) * 64 + row * 8 + col
    pick = (iota((count, count), 1) == source).astype(F32).astype(BF)
    copies[0].wait()
    copies[1].wait()
    goal = jnp.dot(pick, t_in[...].reshape(count, span), preferred_element_type=F32)
    token = iota((count, 8), 0)
    row_hot = ((token // 8) % 8 == iota((count, 8), 1)).astype(F32)
    by_row = jnp.dot(row_hot, v_in[...].astype(F32), preferred_element_type=F32)
    mine = token % 8 == iota((count, 8), 1)
    natural = jnp.sum(jnp.where(mine, by_row, 0.0), axis=1, keepdims=True)
    spread = jnp.broadcast_to(natural, (count, 128)).astype(BF)
    column = jnp.dot(pick, spread, preferred_element_type=F32)
    extra = jnp.concatenate([goal, column[:, : EXTRA - span]], axis=1).astype(BF)
    starts = [sum(o.shape[0] for o in outs[:n]) for n in range(4)]
    outs = list(zip(outs, starts))
    for ref, row in outs:
        ref[:, width:] = extra[row : row + ref.shape[0]]
    for n, at in enumerate(range(0, width, step)):
        copies[2 + n].wait()
        tokens = x_in[:, :, :, at : at + step].reshape(count, step)
        out = jnp.dot(pick, tokens, preferred_element_type=F32).astype(BF)
        for ref, row in outs:
            ref[:, at : at + step] = out[row : row + ref.shape[0]]


def windows_of(*tiles):
    return [[t.at[32 * w : 32 * w + 32] for t in tiles] for w in range(2)]


def attention_kernel(*refs):
    tiles, ctx_ref = windows_of(*refs[:4]), refs[4]
    part = ctx_ref.shape[1]
    is_last = lax.axis_index("lat") == lax.axis_size("lat") - 1
    same = (iota((512, 128), 0) % 128) // 64 == iota((512, 128), 1) // 64
    bias = jnp.where(jnp.logical_or(same, jnp.logical_not(is_last)), 0.0, -1e30)
    head = iota((128, 128), 1) // HDIM
    factor = math.log2(math.e) / math.sqrt(HDIM)
    for at in range(0, part, 128):
        for w in range(2):
            q, k, v = [
                jnp.concatenate(
                    [t[:, i * part + at : i * part + at + 128] for t in tiles[w]],
                    axis=0,
                )
                for i in range(3)
            ]
            zero = jnp.zeros_like(k)
            k4 = jnp.concatenate([jnp.where(head == h, k, zero) for h in range(4)], axis=0)
            v4 = jnp.concatenate([jnp.where(head == h, v, zero) for h in range(4)], axis=0)
            s = lax.dot_general(k4, q, (((1,), (1,)), ((), ())), preferred_element_type=F32)
            s = s + bias
            parts = []
            for h in range(4):
                sh = s[128 * h : 128 * h + 128]
                e = jnp.exp2((sh - jnp.max(sh, axis=0, keepdims=True)) * factor)
                parts.append((e * (1.0 / jnp.sum(e, axis=0, keepdims=True))).astype(BF))
            attn = jnp.concatenate(parts, axis=0)
            out = lax.dot_general(attn, v4, (((0,), (0,)), ((), ())), preferred_element_type=F32)
            ctx_ref[128 * w : 128 * w + 128, at : at + 128] = out.astype(BF)


def assemble(own_w, own_u, own_gain, pieces, w_all, ug_all):
    zi, part = lax.axis_index("dp"), lax.axis_index("lat")
    rows = own_w.shape[0]
    qr = rows // 4
    steps = len(pieces) // 4 + 1
    base = pl.multiple_of(zi * rows, 128)
    w_all[pl.ds(base, rows), :] = own_w[...]
    span = own_u.shape[0]
    ug_all[0:span, pl.ds(base, rows)] = own_u[...]
    ug_all[span : span + 16, pl.ds(base, rows)] = gain_rows(own_gain, rows)
    for k in range(1, steps):
        shard = lax.rem(zi - k + steps, steps)
        base = pl.multiple_of(shard * rows, 128)
        for bits, piece in zip((0, 2, 1, 3), pieces[4 * k - 4 : 4 * k]):
            from_part = part ^ bits
            row = pl.multiple_of(base + from_part * qr, 32)
            w_all[pl.ds(row, qr), :] = piece[0:qr, :]
            for j in range(4):
                urow = pl.multiple_of((4 * from_part + j) * 16, 16)
                ug_all[pl.ds(urow, 16), pl.ds(base, rows)] = piece[
                    qr : qr + 16, j * rows : (j + 1) * rows
                ]


def split3(x):
    hi = x.astype(BF).astype(F32)
    mid = (x - hi).astype(BF).astype(F32)
    return hi, mid, x - hi - mid


def loss_block(value, rows):
    hi, mid, lo = split3(value)
    lane = iota((rows, 128), 1)
    return jnp.where(lane == 0, hi, jnp.where(lane == 1, mid, jnp.where(lane == 2, lo, 0.0)))


def forward_kernel(lat_ref, var_ref, *refs):
    ctx_ref, refs = refs[0], refs[1:]
    extras, refs = refs[:4], refs[4:]
    owned, refs = refs[:3], refs[3:]
    pieces, refs = refs[:PIECES], refs[PIECES:]
    ts, refs = refs[:4], refs[4:]
    normed_ref, inv_ref, dfc_ref, hidden_ref, w_all, ug_all, term = refs
    lat_place = lax.axis_index("lat")
    assemble(*owned, pieces, w_all, ug_all)
    tokens, width = normed_ref.shape
    span = dfc_ref.shape[1]
    extra = jnp.concatenate([t[...] for tiles in windows_of(*extras) for t in tiles], axis=0)
    extra = extra.astype(F32)
    goal, valid = extra[:, :span], extra[:, span : span + 1]
    token = iota((tokens, 1), 0)
    row = (token // 4) % 4 + jnp.where((token // 32) % 4 >= 2, 4, 0)
    lat_w = jnp.zeros((tokens, 1), F32)
    for r in range(8):
        lat_w = jnp.where(row == r, lat_ref[lat_place * 8 + r], lat_w)
    lane = iota((1, span), 1) // (span // var_ref.shape[0])
    var_w = jnp.zeros((1, span), F32)
    for n in range(var_ref.shape[0]):
        var_w = jnp.where(lane == n, var_ref[n], var_w)
    weight = lat_w * valid * var_w
    mixed = jnp.dot(ctx_ref[...], w_all[...], preferred_element_type=F32)
    centre = jnp.mean(mixed, axis=-1, keepdims=True)
    off = mixed - centre
    inv = lax.rsqrt(jnp.mean(off * off, axis=-1, keepdims=True) + 1e-05)
    normed = off * inv
    normed_ref[...] = normed
    inv_ref[...] = jnp.broadcast_to(inv, inv_ref.shape)
    gain = ug_all[pl.ds(span, 16), :][0:1].astype(F32)
    hidden_ref[...] = (normed * gain).astype(BF)
    field = lax.dot_general(
        hidden_ref[...], ug_all[0:span, :], (((1,), (1,)), ((), ())), preferred_element_type=F32
    )
    misfit = field - goal
    dfc = (2.0 * weight * misfit).astype(BF)
    dfc_ref[...] = dfc
    term[...] = lax.dot_general(
        dfc, hidden_ref[...], (((0,), (0,)), ((), ())), preferred_element_type=F32
    )
    loss = jnp.sum(jnp.sum(weight * misfit * misfit, axis=1, keepdims=True), axis=0, keepdims=True)
    rows = ts[0].shape[0]
    block = loss_block(loss, rows).astype(BF)
    for b, ref in enumerate(ts):
        at = pl.multiple_of((lat_place ^ b) * rows, 8)
        ref[:, :width] = term[pl.ds(at, rows), :].astype(BF)
        ref[:, width:] = block


def backward_kernel(normed_ref, inv_ref, dfc_ref, *refs):
    owned, refs = refs[:3], refs[3:]
    pieces, (out_ref, w_all, ug_all) = refs[:PIECES], refs[PIECES:]
    assemble(*owned, pieces, w_all, ug_all)
    tokens, width = normed_ref.shape
    span = dfc_ref.shape[1]
    gain = ug_all[pl.ds(span, 16), :][0:1].astype(F32)
    g = jnp.dot(dfc_ref[...], ug_all[0:span, :], preferred_element_type=F32) * gain
    normed = normed_ref[...]
    mean_g = jnp.mean(g, axis=-1, keepdims=True)
    mean_gn = jnp.mean(g * normed, axis=-1, keepdims=True)
    dmixed = ((g - mean_g - normed * mean_gn) * inv_ref[:, 0:1]).astype(BF)
    place = iota((tokens, tokens), 0)
    row, col, level = (place // 8) % 8, place % 8, place // 64
    quad = jnp.where(row >= 4, 2, 0) + jnp.where(col >= 4, 1, 0)
    source = (level // 2) * 128 + quad * 32 + (level % 2) * 16 + (row % 4) * 4 + col % 4
    pick = (iota((tokens, tokens), 1) == source).astype(F32).astype(BF)
    dnat = jnp.dot(pick, dmixed, preferred_element_type=F32).astype(BF)
    out = lax.dot_general(dnat, w_all[...], (((1,), (1,)), ((), ())), preferred_element_type=F32)
    out_ref[...] = out.astype(BF)


def add4(a, b, c, d):
    return (a[...].astype(F32) + b[...].astype(F32)) + (c[...].astype(F32) + d[...].astype(F32))


def lat_sum_kernel(a, b, c, d, z0, z1, z2, z3, loss_ref, total_ref):
    total_ref[...] = add4(a, b, c, d)
    zi = lax.axis_index("dp")
    rows, width = z0.shape
    for k, ref in enumerate((z0, z1, z2, z3)):
        at = pl.multiple_of((zi ^ k) * width, 128)
        ref[...] = total_ref[:, pl.ds(at, width)].astype(BF)
    loss = jnp.sum(total_ref[0:1, 4 * width :], axis=1, keepdims=True)
    loss_ref[...] = jnp.broadcast_to(loss, loss_ref.shape)


def dp_sum_kernel(loss_ref, a, b, c, d, o_ref):
    rows, width = a.shape
    o_ref[0:rows, :] = add4(a, b, c, d).astype(BF)
    block = loss_block(loss_ref[0:1, 0:1], o_ref.shape[0] - rows)
    zeros = jnp.zeros((block.shape[0], width - 128), F32)
    o_ref[rows:, :] = jnp.concatenate([block, zeros], axis=1).astype(BF)


def join_kernel(counts, *refs):
    pieces, (o_ref, loss_ref) = refs[:8], refs[8:]
    lat_place = lax.axis_index("lat")
    rows = o_ref.shape[0] // 4
    for a in range(4):
        at = pl.multiple_of((lat_place ^ a) * rows, 8)
        both = [pieces[2 * a + b][0:rows, :].astype(F32) for b in range(2)]
        o_ref[pl.ds(at, rows), :] = (both[0] + both[1]) / counts[0]
    sums = [
        jnp.sum(p[rows : rows + 1, 0:128].astype(F32), axis=1, keepdims=True) for p in pieces[:2]
    ]
    loss_ref[...] = jnp.broadcast_to((sums[0] + sums[1]) / counts[1], loss_ref.shape)


def swap(array, axis, bit):
    return lax.ppermute(array, axis, [(i, i ^ bit) for i in range(lax.axis_size(axis))])


def shape(dims, dtype):
    return jax.ShapeDtypeStruct(dims, dtype)


def shards(projected, targets, valid_cells, w_out, unpatch_matrix, norm_gain, var_weight):
    dp, lat, lon = lax.axis_size("dp"), lax.axis_size("lat"), lax.axis_size("lon")
    rows, width = w_out.shape
    levels = projected.shape[1]
    span = unpatch_matrix.shape[1]
    tokens = levels * 64
    lat_total = 8 * lat
    angle = math.pi * ((np.arange(lat_total) + 0.5) / lat_total - 0.5)
    cosine = np.cos(angle)
    lat_table = jnp.asarray(np.roll(cosine / cosine.mean(), -4), F32)
    barrier = lax.optimization_barrier

    unpatch_t = unpatch_matrix.T
    payload = pl.pallas_call(
        payload_kernel,
        out_shape=shape((rows // 4 + 16, width), BF),
        in_specs=[HBM, HBM, VMEM],
        out_specs=VMEM,
        scratch_shapes=[pltpu.VMEM((UGROWS, rows), BF), pltpu.SemaphoreType.DMA((2,))],
        compiler_params=params(60),
        name="payload",
    )(w_out, unpatch_t, norm_gain)
    ring1 = from_behind(payload, "dp", 1)
    own, *send = pl.pallas_call(
        pack_kernel,
        out_shape=[shape((n, 3 * width + EXTRA), BF) for n in (64, 64, 64, 64)],
        in_specs=[HBM] * 3,
        out_specs=[VMEM] * 4,
        scratch_shapes=[
            pltpu.VMEM((levels, 8, 8, 3 * width), BF),
            pltpu.VMEM((levels, 8, 8, span), BF),
            pltpu.VMEM((8, 8), jnp.int32),
            pltpu.SemaphoreType.DMA((2 + 3 * width // 512,)),
        ],
        compiler_params=params(62),
        name="pack",
    )(
        projected.reshape(levels, 8, 8, 3 * width),
        targets.reshape(levels, 8, 8, span),
        valid_cells,
    )
    corner = [
        (a * lon + b, ((a - 1) % lat) * lon + (b - 1) % lon) for a in range(lat) for b in range(lon)
    ]
    south = from_behind(send[1], "lat", -1)
    diag = lax.ppermute(send[2], ("lat", "lon"), corner)
    ring2 = from_behind(ring1, "dp", 1)
    across2 = swap(ring2, "lat", 2)
    ring2_after, east, south, diag = barrier((ring2, send[0], south, diag))
    ring3 = from_behind(ring2_after, "dp", 1)
    east = from_behind(east, "lon", -1)
    across3 = from_behind(across2, "dp", 1)
    ring1_late, across2 = barrier((ring1, across2))
    across1 = swap(ring1_late, "lat", 2)
    tiles = [own, east, south, diag]
    *tiles, ring1, across1, ring2 = barrier((*tiles, ring1, across1, ring2))
    ctx = pl.pallas_call(
        attention_kernel,
        out_shape=shape((tokens, width), BF),
        in_specs=[VMEM] * 4,
        out_specs=VMEM,
        compiler_params=params(16),
        name="attention",
    )(*tiles)
    ctx, across3 = barrier((ctx, across3))
    pieces = []
    for ring, across in ((ring1, across1), (ring2, across2), (ring3, across3)):
        pieces += [ring, across, swap(ring, "lat", 1), swap(across, "lat", 1)]

    piece = span // lat
    extra_specs = [
        pl.BlockSpec((t.shape[0], EXTRA), lambda i: (0, 3 * width // EXTRA)) for t in tiles
    ]
    assembly = [
        pltpu.VMEM((dp * rows, width), BF),
        pltpu.VMEM((UGROWS, dp * rows), BF),
    ]
    *terms, normed, inv, dfc = pl.pallas_call(
        forward_kernel,
        grid=(1,),
        out_shape=[shape((piece, width + 128), BF)] * 4
        + [shape((tokens, width), F32), shape((tokens, 128), F32), shape((tokens, span), BF)],
        in_specs=[SMEM] * 2 + [VMEM] + extra_specs + [VMEM] * (3 + PIECES),
        out_specs=[VMEM] * 7,
        scratch_shapes=[pltpu.VMEM((tokens, width), BF)]
        + assembly
        + [pltpu.VMEM((span, width), F32)],
        compiler_params=params(28),
        name="forward",
    )(lat_table, var_weight, ctx, *tiles, w_out, unpatch_t, norm_gain, *pieces)

    terms = [terms[0]] + [swap(terms[b], "lat", b) for b in (1, 2, 3)]
    grad_context = pl.pallas_call(
        backward_kernel,
        out_shape=shape((tokens, width), BF),
        in_specs=[VMEM] * (6 + PIECES),
        out_specs=VMEM,
        scratch_shapes=assembly,
        compiler_params=params(24),
        name="backward",
    )(normed, inv, dfc, w_out, unpatch_t, norm_gain, *pieces)
    *terms, grad_context = barrier((*terms, grad_context))

    *parts, loss = pl.pallas_call(
        lat_sum_kernel,
        out_shape=[shape((piece, rows), BF)] * 4 + [shape((8, 128), F32)],
        in_specs=[VMEM] * 4,
        out_specs=[VMEM] * 5,
        scratch_shapes=[pltpu.VMEM((piece, width + 128), F32)],
        compiler_params=params(4),
        name="lat_sum",
    )(*terms)
    parts = [parts[0]] + [swap(parts[k], "dp", k) for k in (1, 2, 3)]
    mine = pl.pallas_call(
        dp_sum_kernel,
        out_shape=shape((piece + 8, rows), BF),
        in_specs=[VMEM] * 5,
        out_specs=VMEM,
        compiler_params=params(4),
        name="dp_sum",
    )(loss, *parts)
    plane = [mine]
    for a in range(4):
        for b in range(2):
            if a or b:
                pairs = [
                    (i * lon + j, (i ^ a) * lon + (j ^ b)) for i in range(lat) for j in range(lon)
                ]
                plane.append(lax.ppermute(mine, ("lat", "lon"), pairs))
    count = levels * lat_total * 8 * lon
    counts = (float(count), float(count * (span // var_weight.shape[0])))
    joined, loss = pl.pallas_call(
        lambda *refs: join_kernel(counts, *refs),
        out_shape=[shape((span, rows), F32), shape((1, 1), F32)],
        in_specs=[VMEM] * 8,
        out_specs=[VMEM] * 2,
        compiler_params=params(4),
        name="join",
    )(*plane)
    return grad_context.reshape(1, levels, 8, 8, width), joined.T, loss.reshape(1)


def solution(mesh):
    placed = (
        P("dp", None, "lat", "lon", None),
        P("dp", None, "lat", "lon", None),
        P("lat", "lon"),
        P("dp", None),
        P("dp", None),
        P("dp"),
        P(),
    )
    fits = mesh.shape["dp"] == 4 and mesh.shape["lat"] == 4 and mesh.shape["lon"] == 2

    def program(*arrays):
        body = shards if fits else general_shards
        return jax.shard_map(
            body,
            mesh=mesh,
            in_specs=placed,
            out_specs=(P("dp", None, "lat", "lon", None), P("dp", None), P("dp")),
            check_vma=False,
        )(*arrays)

    return program
```

```python
import functools
import math

import jax
import jax.numpy as jnp
import numpy as np
from jax import lax
from jax.experimental import pallas as pl
from jax.experimental.pallas import tpu as pltpu
from jax.sharding import PartitionSpec as P

HEADS = 48
HDIM = 32
WLEV = 2
BF = jnp.bfloat16
F32 = jnp.float32
EXTRA = 256
UGROWS = 256
PIECES = 12
VMEM = pl.BlockSpec(memory_space=pltpu.VMEM)
SMEM = pl.BlockSpec(memory_space=pltpu.SMEM)
ANY = pl.BlockSpec(memory_space=pl.ANY)
HBM = pl.BlockSpec(memory_space=pltpu.HBM)


def from_behind(array, axis, by):
    length = lax.axis_size(axis)
    return lax.ppermute(array, axis, [(i, (i + by) % length) for i in range(length)])


def general_shards(projected, targets, valid_cells, w_out, unpatch_matrix, norm_gain, var_weight):
    tile_side = projected.shape[2]
    half_side = tile_side // 2
    levels = projected.shape[1]
    model_width = w_out.shape[1]
    predicted_span = unpatch_matrix.shape[1]
    lat_total = tile_side * lax.axis_size("lat")
    lon_total = tile_side * lax.axis_size("lon")
    lat_place = lax.axis_index("lat")
    moved = from_behind(
        (projected[:, :, :, :half_side], targets[:, :, :, :half_side], valid_cells[:, :half_side]),
        "lon",
        -1,
    )
    strip_proj = jnp.concatenate([projected[:, :, :, half_side:], moved[0]], axis=3)
    strip_goal = jnp.concatenate([targets[:, :, :, half_side:], moved[1]], axis=3)
    strip_valid = jnp.concatenate([valid_cells[:, half_side:], moved[2]], axis=1)
    moved_rows = from_behind(
        (strip_proj[:, :, :half_side], strip_goal[:, :, :half_side], strip_valid[:half_side]),
        "lat",
        -1,
    )
    local_proj = jnp.concatenate([strip_proj[:, :, half_side:], moved_rows[0]], axis=2)
    shard_reference = jnp.concatenate([strip_goal[:, :, half_side:], moved_rows[1]], axis=2)
    local_valid = jnp.concatenate([strip_valid[half_side:], moved_rows[2]], axis=0).astype(F32)
    win_count = levels // WLEV
    tokw = WLEV * tile_side * tile_side
    windows = local_proj.reshape(win_count, tokw, 3 * model_width)
    rows_here = lat_place * tile_side + jnp.arange(tile_side)
    region_rows = (rows_here >= lat_total - half_side).astype(jnp.int32)
    region = jnp.broadcast_to(region_rows[None, :, None], (WLEV, tile_side, tile_side)).reshape(-1)
    allowed = region[:, None] == region[None, :]
    queries = windows[..., :model_width].reshape(win_count, tokw, HEADS, -1)
    key_heads = windows[..., model_width : 2 * model_width].reshape(win_count, tokw, HEADS, -1)
    value_heads = windows[..., 2 * model_width :].reshape(win_count, tokw, HEADS, -1)
    scores = jnp.einsum("wqhd,wkhd->whqk", queries, key_heads, preferred_element_type=F32)
    scores = scores * (1.0 / math.sqrt(HDIM))
    scores = jnp.where(allowed[None, None], scores, -1e30)
    row_peak = jnp.max(scores, axis=-1, keepdims=True)
    lifted = jnp.exp(scores - row_peak)
    attn = (lifted / jnp.sum(lifted, axis=-1, keepdims=True)).astype(BF)
    context = jnp.einsum("whqk,wkhd->wqhd", attn, value_heads, preferred_element_type=F32)
    context = context.astype(BF).reshape(win_count * tokw, model_width)
    element_total = win_count * tokw
    out_all, unprojected_pieces, gain_all = (
        lax.all_gather(w_out, "dp", axis=0, tiled=True),
        lax.all_gather(unpatch_matrix, "dp", axis=0, tiled=True),
        lax.all_gather(norm_gain, "dp", axis=0, tiled=True),
    )
    mixed_rows = jnp.dot(context, out_all, preferred_element_type=F32)
    centre = jnp.mean(mixed_rows, axis=-1, keepdims=True)
    spread = jnp.mean((mixed_rows - centre) ** 2, axis=-1, keepdims=True)
    inv_spread = lax.rsqrt(spread + 1e-05)
    normed = (mixed_rows - centre) * inv_spread
    gain_f = gain_all.astype(F32)
    latent_activation = (normed * gain_f).astype(BF)
    prediction_field = jnp.dot(latent_activation, unprojected_pieces, preferred_element_type=F32)
    prediction_misfit = prediction_field - shard_reference.reshape(
        element_total, predicted_span
    ).astype(F32)
    all_rows = jnp.arange(lat_total).astype(F32)
    cosine_mean = jnp.mean(jnp.cos(math.pi * ((all_rows + 0.5) / lat_total - 0.5)))
    initial_rows = ((rows_here + half_side) % lat_total).astype(F32)
    lat_here = jnp.cos(math.pi * ((initial_rows + 0.5) / lat_total - 0.5)) / cosine_mean
    element_factor = jnp.broadcast_to(
        lat_here[None, :, None] * local_valid[None], (levels, tile_side, tile_side)
    ).reshape(element_total, 1)
    variable_factor = jnp.repeat(var_weight, predicted_span // var_weight.shape[0])[None, :]
    shard_penalty = jnp.sum(
        element_factor * variable_factor * prediction_misfit * prediction_misfit
    ) / (levels * lat_total * lon_total * (predicted_span // var_weight.shape[0]))
    prediction_gradient = (2.0 * element_factor * variable_factor * prediction_misfit).astype(BF)
    grad_shard = lax.psum_scatter(
        jnp.einsum(
            "td,to->do", latent_activation, prediction_gradient, preferred_element_type=F32
        ).astype(BF),
        "dp",
        scatter_dimension=0,
        tiled=True,
    ).astype(F32)
    grad_sum, loss_sum = lax.psum((grad_shard, shard_penalty), ("lat", "lon"))
    grad_recovery = grad_sum / (levels * lat_total * lon_total)
    grad_hidden = jnp.einsum(
        "to,do->td", prediction_gradient, unprojected_pieces, preferred_element_type=F32
    )
    scaled_grad = grad_hidden * gain_f
    grad_mixed = inv_spread * (
        scaled_grad
        - jnp.mean(scaled_grad, axis=-1, keepdims=True)
        - normed * jnp.mean(scaled_grad * normed, axis=-1, keepdims=True)
    )
    grad_mixed = grad_mixed.astype(BF)
    grad_context = jnp.einsum("tj,ij->ti", grad_mixed, out_all, preferred_element_type=F32)
    grad_context = grad_context.astype(BF).reshape(1, levels, tile_side, tile_side, model_width)
    return (grad_context, grad_recovery, loss_sum.reshape(1))


def params(mib):
    return pltpu.CompilerParams(vmem_limit_bytes=mib << 20)


def iota(shape, dim):
    return lax.broadcasted_iota(jnp.int32, shape, dim)


def payload_kernel(w_ref, unpatch_ref, gain_ref, payload_ref, ug, sems):
    part = lax.axis_index("lat")
    rows, width = w_ref.shape
    qr = rows // 4
    span = unpatch_ref.shape[0]
    start = pl.multiple_of(part * qr, 32)
    u_copy = pltpu.make_async_copy(unpatch_ref, ug.at[pl.ds(0, span), :], sems.at[0])
    u_copy.start()
    w_copy = pltpu.make_async_copy(
        w_ref.at[pl.ds(start, qr), :], payload_ref.at[pl.ds(0, qr), :], sems.at[1]
    )
    w_copy.start()
    ug[pl.ds(span, 16), :] = gain_rows(gain_ref, rows)
    ug[pl.ds(span + 16, UGROWS - span - 16), :] = jnp.zeros((UGROWS - span - 16, rows), BF)
    u_copy.wait()
    for j in range(4):
        at = pl.multiple_of((4 * part + j) * 16, 16)
        payload_ref[pl.ds(qr, 16), pl.ds(j * rows, rows)] = ug[pl.ds(at, 16), :]
    w_copy.wait()


def gain_rows(gain_ref, rows):
    return jnp.broadcast_to(gain_ref[...].astype(F32).reshape(1, rows), (16, rows)).astype(BF)


def pack_kernel(x_ref, t_ref, valid_ref, *refs):
    outs, (x_in, t_in, v_in, sems) = refs[:4], refs[4:]
    span = t_ref.shape[-1]
    count = x_ref.shape[0] * 64
    quarter = count // 4
    step = 512
    width = x_ref.shape[-1]
    copies = [
        pltpu.make_async_copy(t_ref, t_in, sems.at[0]),
        pltpu.make_async_copy(valid_ref, v_in, sems.at[1]),
    ]
    for at in range(0, width, step):
        lanes = (slice(None),) * 3 + (pl.ds(at, step),)
        copies.append(
            pltpu.make_async_copy(x_ref.at[lanes], x_in.at[lanes], sems.at[len(copies)])
        )
    for c in copies:
        c.start()
    place = iota((count, count), 0)
    quad, rest = place // quarter, place % quarter
    row = (rest // 4) % 4 + jnp.where(quad < 2, 4, 0)
    col = rest % 4 + jnp.where(quad % 2 == 0, 4, 0)
    source = (rest // 16) * 64 + row * 8 + col
    pick = (iota((count, count), 1) == source).astype(F32).astype(BF)
    copies[0].wait()
    copies[1].wait()
    goal = jnp.dot(pick, t_in[...].reshape(count, span), preferred_element_type=F32)
    token = iota((count, 8), 0)
    row_hot = ((token // 8) % 8 == iota((count, 8), 1)).astype(F32)
    by_row = jnp.dot(row_hot, v_in[...].astype(F32), preferred_element_type=F32)
    mine = token % 8 == iota((count, 8), 1)
    natural = jnp.sum(jnp.where(mine, by_row, 0.0), axis=1, keepdims=True)
    spread = jnp.broadcast_to(natural, (count, 128)).astype(BF)
    column = jnp.dot(pick, spread, preferred_element_type=F32)
    extra = jnp.concatenate([goal, column[:, : EXTRA - span]], axis=1).astype(BF)
    starts = [sum(o.shape[0] for o in outs[:n]) for n in range(4)]
    outs = list(zip(outs, starts))
    for ref, row in outs:
        ref[:, width:] = extra[row : row + ref.shape[0]]
    for n, at in enumerate(range(0, width, step)):
        copies[2 + n].wait()
        tokens = x_in[:, :, :, at : at + step].reshape(count, step)
        out = jnp.dot(pick, tokens, preferred_element_type=F32).astype(BF)
        for ref, row in outs:
            ref[:, at : at + step] = out[row : row + ref.shape[0]]


def windows_of(*tiles):
    return [[t.at[32 * w : 32 * w + 32] for t in tiles] for w in range(2)]


def attention_kernel(*refs):
    tiles, ctx_ref = windows_of(*refs[:4]), refs[4]
    part = ctx_ref.shape[1]
    is_last = lax.axis_index("lat") == lax.axis_size("lat") - 1
    same = (iota((512, 128), 0) % 128) // 64 == iota((512, 128), 1) // 64
    bias = jnp.where(jnp.logical_or(same, jnp.logical_not(is_last)), 0.0, -1e30)
    head = iota((128, 128), 1) // HDIM
    factor = math.log2(math.e) / math.sqrt(HDIM)
    for at in range(0, part, 128):
        for w in range(2):
            q, k, v = [
                jnp.concatenate(
                    [t[:, i * part + at : i * part + at + 128] for t in tiles[w]],
                    axis=0,
                )
                for i in range(3)
            ]
            zero = jnp.zeros_like(k)
            k4 = jnp.concatenate([jnp.where(head == h, k, zero) for h in range(4)], axis=0)
            v4 = jnp.concatenate([jnp.where(head == h, v, zero) for h in range(4)], axis=0)
            s = lax.dot_general(k4, q, (((1,), (1,)), ((), ())), preferred_element_type=F32)
            s = s + bias
            parts = []
            for h in range(4):
                sh = s[128 * h : 128 * h + 128]
                e = jnp.exp2((sh - jnp.max(sh, axis=0, keepdims=True)) * factor)
                parts.append((e * (1.0 / jnp.sum(e, axis=0, keepdims=True))).astype(BF))
            attn = jnp.concatenate(parts, axis=0)
            out = lax.dot_general(attn, v4, (((0,), (0,)), ((), ())), preferred_element_type=F32)
            ctx_ref[128 * w : 128 * w + 128, at : at + 128] = out.astype(BF)


def assemble(own_w, own_u, own_gain, pieces, w_all, ug_all):
    zi, part = lax.axis_index("dp"), lax.axis_index("lat")
    rows = own_w.shape[0]
    qr = rows // 4
    steps = len(pieces) // 4 + 1
    base = pl.multiple_of(zi * rows, 128)
    w_all[pl.ds(base, rows), :] = own_w[...]
    span = own_u.shape[0]
    ug_all[0:span, pl.ds(base, rows)] = own_u[...]
    ug_all[span : span + 16, pl.ds(base, rows)] = gain_rows(own_gain, rows)
    for k in range(1, steps):
        shard = lax.rem(zi - k + steps, steps)
        base = pl.multiple_of(shard * rows, 128)
        for bits, piece in zip((0, 2, 1, 3), pieces[4 * k - 4 : 4 * k]):
            from_part = part ^ bits
            row = pl.multiple_of(base + from_part * qr, 32)
            w_all[pl.ds(row, qr), :] = piece[0:qr, :]
            for j in range(4):
                urow = pl.multiple_of((4 * from_part + j) * 16, 16)
                ug_all[pl.ds(urow, 16), pl.ds(base, rows)] = piece[
                    qr : qr + 16, j * rows : (j + 1) * rows
                ]


def split3(x):
    hi = x.astype(BF).astype(F32)
    mid = (x - hi).astype(BF).astype(F32)
    return hi, mid, x - hi - mid


def loss_block(value, rows):
    hi, mid, lo = split3(value)
    lane = iota((rows, 128), 1)
    return jnp.where(lane == 0, hi, jnp.where(lane == 1, mid, jnp.where(lane == 2, lo, 0.0)))


def forward_kernel(lat_ref, var_ref, *refs):
    ctx_ref, refs = refs[0], refs[1:]
    extras, refs = refs[:4], refs[4:]
    owned, refs = refs[:3], refs[3:]
    pieces, refs = refs[:PIECES], refs[PIECES:]
    ts, refs = refs[:4], refs[4:]
    normed_ref, inv_ref, dfc_ref, hidden_ref, w_all, ug_all, term = refs
    lat_place = lax.axis_index("lat")
    assemble(*owned, pieces, w_all, ug_all)
    tokens, width = normed_ref.shape
    span = dfc_ref.shape[1]
    extra = jnp.concatenate([t[...] for tiles in windows_of(*extras) for t in tiles], axis=0)
    extra = extra.astype(F32)
    goal, valid = extra[:, :span], extra[:, span : span + 1]
    token = iota((tokens, 1), 0)
    row = (token // 4) % 4 + jnp.where((token // 32) % 4 >= 2, 4, 0)
    lat_w = jnp.zeros((tokens, 1), F32)
    for r in range(8):
        lat_w = jnp.where(row == r, lat_ref[lat_place * 8 + r], lat_w)
    lane = iota((1, span), 1) // (span // var_ref.shape[0])
    var_w = jnp.zeros((1, span), F32)
    for n in range(var_ref.shape[0]):
        var_w = jnp.where(lane == n, var_ref[n], var_w)
    weight = lat_w * valid * var_w
    mixed = jnp.dot(ctx_ref[...], w_all[...], preferred_element_type=F32)
    centre = jnp.mean(mixed, axis=-1, keepdims=True)
    off = mixed - centre
    inv = lax.rsqrt(jnp.mean(off * off, axis=-1, keepdims=True) + 1e-05)
    normed = off * inv
    normed_ref[...] = normed
    inv_ref[...] = jnp.broadcast_to(inv, inv_ref.shape)
    gain = ug_all[pl.ds(span, 16), :][0:1].astype(F32)
    hidden_ref[...] = (normed * gain).astype(BF)
    field = lax.dot_general(
        hidden_ref[...], ug_all[0:span, :], (((1,), (1,)), ((), ())), preferred_element_type=F32
    )
    misfit = field - goal
    dfc = (2.0 * weight * misfit).astype(BF)
    dfc_ref[...] = dfc
    term[...] = lax.dot_general(
        dfc, hidden_ref[...], (((0,), (0,)), ((), ())), preferred_element_type=F32
    )
    loss = jnp.sum(jnp.sum(weight * misfit * misfit, axis=1, keepdims=True), axis=0, keepdims=True)
    rows = ts[0].shape[0]
    block = loss_block(loss, rows).astype(BF)
    for b, ref in enumerate(ts):
        at = pl.multiple_of((lat_place ^ b) * rows, 8)
        ref[:, :width] = term[pl.ds(at, rows), :].astype(BF)
        ref[:, width:] = block


def backward_kernel(normed_ref, inv_ref, dfc_ref, *refs):
    owned, refs = refs[:3], refs[3:]
    pieces, (out_ref, w_all, ug_all) = refs[:PIECES], refs[PIECES:]
    assemble(*owned, pieces, w_all, ug_all)
    tokens, width = normed_ref.shape
    span = dfc_ref.shape[1]
    gain = ug_all[pl.ds(span, 16), :][0:1].astype(F32)
    g = jnp.dot(dfc_ref[...], ug_all[0:span, :], preferred_element_type=F32) * gain
    normed = normed_ref[...]
    mean_g = jnp.mean(g, axis=-1, keepdims=True)
    mean_gn = jnp.mean(g * normed, axis=-1, keepdims=True)
    dmixed = ((g - mean_g - normed * mean_gn) * inv_ref[:, 0:1]).astype(BF)
    place = iota((tokens, tokens), 0)
    row, col, level = (place // 8) % 8, place % 8, place // 64
    quad = jnp.where(row >= 4, 2, 0) + jnp.where(col >= 4, 1, 0)
    source = (level // 2) * 128 + quad * 32 + (level % 2) * 16 + (row % 4) * 4 + col % 4
    pick = (iota((tokens, tokens), 1) == source).astype(F32).astype(BF)
    dnat = jnp.dot(pick, dmixed, preferred_element_type=F32).astype(BF)
    out = lax.dot_general(dnat, w_all[...], (((1,), (1,)), ((), ())), preferred_element_type=F32)
    out_ref[...] = out.astype(BF)


def add4(a, b, c, d):
    return (a[...].astype(F32) + b[...].astype(F32)) + (c[...].astype(F32) + d[...].astype(F32))


def lat_sum_kernel(a, b, c, d, z0, z1, z2, z3, loss_ref, total_ref):
    total_ref[...] = add4(a, b, c, d)
    zi = lax.axis_index("dp")
    rows, width = z0.shape
    for k, ref in enumerate((z0, z1, z2, z3)):
        at = pl.multiple_of((zi ^ k) * width, 128)
        ref[...] = total_ref[:, pl.ds(at, width)].astype(BF)
    loss = jnp.sum(total_ref[0:1, 4 * width :], axis=1, keepdims=True)
    loss_ref[...] = jnp.broadcast_to(loss, loss_ref.shape)


def dp_sum_kernel(loss_ref, a, b, c, d, o_ref):
    rows, width = a.shape
    o_ref[0:rows, :] = add4(a, b, c, d).astype(BF)
    block = loss_block(loss_ref[0:1, 0:1], o_ref.shape[0] - rows)
    zeros = jnp.zeros((block.shape[0], width - 128), F32)
    o_ref[rows:, :] = jnp.concatenate([block, zeros], axis=1).astype(BF)


def pair_kernel(mine_ref, other_ref, o_ref):
    rows = mine_ref.shape[0]
    odd = lax.axis_index("lat") % 2
    o_ref[pl.ds(pl.multiple_of(odd * rows, 8), rows), :] = mine_ref[...]
    o_ref[pl.ds(pl.multiple_of((1 - odd) * rows, 8), rows), :] = other_ref[...]


def join_kernel(counts, *refs):
    pieces, (o_ref, loss_ref) = refs[:4], refs[4:]
    chip = lax.axis_index("lat") // 2
    held = pieces[0].shape[0] // 2
    rows = held - 8
    for a in range(2):
        for n in range(2):
            at = pl.multiple_of((2 * (chip ^ a) + n) * rows, 8)
            both = [pieces[2 * a + b][held * n : held * n + rows, :].astype(F32) for b in range(2)]
            o_ref[pl.ds(at, rows), :] = (both[0] + both[1]) / counts[0]
    sums = [
        jnp.sum(p[rows : rows + 1, 0:128].astype(F32), axis=1, keepdims=True) for p in pieces[:2]
    ]
    loss_ref[...] = jnp.broadcast_to((sums[0] + sums[1]) / counts[1], loss_ref.shape)


def swap(array, axis, bit):
    return lax.ppermute(array, axis, [(i, i ^ bit) for i in range(lax.axis_size(axis))])


def shape(dims, dtype):
    return jax.ShapeDtypeStruct(dims, dtype)


def shards(projected, targets, valid_cells, w_out, unpatch_matrix, norm_gain, var_weight):
    dp, lat, lon = lax.axis_size("dp"), lax.axis_size("lat"), lax.axis_size("lon")
    rows, width = w_out.shape
    levels = projected.shape[1]
    span = unpatch_matrix.shape[1]
    tokens = levels * 64
    lat_total = 8 * lat
    angle = math.pi * ((np.arange(lat_total) + 0.5) / lat_total - 0.5)
    cosine = np.cos(angle)
    lat_table = jnp.asarray(np.roll(cosine / cosine.mean(), -4), F32)
    barrier = lax.optimization_barrier

    unpatch_t = unpatch_matrix.T
    payload = pl.pallas_call(
        payload_kernel,
        out_shape=shape((rows // 4 + 16, width), BF),
        in_specs=[HBM, HBM, VMEM],
        out_specs=VMEM,
        scratch_shapes=[pltpu.VMEM((UGROWS, rows), BF), pltpu.SemaphoreType.DMA((2,))],
        compiler_params=params(60),
        name="payload",
    )(w_out, unpatch_t, norm_gain)
    ring1 = from_behind(payload, "dp", 1)
    own, *send = pl.pallas_call(
        pack_kernel,
        out_shape=[shape((n, 3 * width + EXTRA), BF) for n in (64, 64, 64, 64)],
        in_specs=[HBM] * 3,
        out_specs=[VMEM] * 4,
        scratch_shapes=[
            pltpu.VMEM((levels, 8, 8, 3 * width), BF),
            pltpu.VMEM((levels, 8, 8, span), BF),
            pltpu.VMEM((8, 8), jnp.int32),
            pltpu.SemaphoreType.DMA((2 + 3 * width // 512,)),
        ],
        compiler_params=params(62),
        name="pack",
    )(
        projected.reshape(levels, 8, 8, 3 * width),
        targets.reshape(levels, 8, 8, span),
        valid_cells,
    )
    corner = [
        (a * lon + b, ((a - 1) % lat) * lon + (b - 1) % lon) for a in range(lat) for b in range(lon)
    ]
    south = from_behind(send[1], "lat", -1)
    diag = lax.ppermute(send[2], ("lat", "lon"), corner)
    ring2 = from_behind(ring1, "dp", 1)
    across2 = swap(ring2, "lat", 2)
    ring2_after, east, south, diag = barrier((ring2, send[0], south, diag))
    ring3 = from_behind(ring2_after, "dp", 1)
    east = from_behind(east, "lon", -1)
    across3 = from_behind(across2, "dp", 1)
    ring1_late, across2 = barrier((ring1, across2))
    across1 = swap(ring1_late, "lat", 2)
    tiles = [own, east, south, diag]
    *tiles, ring1, across1, ring2, across3 = barrier((*tiles, ring1, across1, ring2, across3))
    ctx = pl.pallas_call(
        attention_kernel,
        out_shape=shape((tokens, width), BF),
        in_specs=[VMEM] * 4,
        out_specs=VMEM,
        compiler_params=params(16),
        name="attention",
    )(*tiles)
    pieces = []
    for ring, across in ((ring1, across1), (ring2, across2), (ring3, across3)):
        pieces += [ring, across, swap(ring, "lat", 1), swap(across, "lat", 1)]

    piece = span // lat
    extra_specs = [
        pl.BlockSpec((t.shape[0], EXTRA), lambda i: (0, 3 * width // EXTRA)) for t in tiles
    ]
    assembly = [
        pltpu.VMEM((dp * rows, width), BF),
        pltpu.VMEM((UGROWS, dp * rows), BF),
    ]
    *terms, normed, inv, dfc = pl.pallas_call(
        forward_kernel,
        grid=(1,),
        out_shape=[shape((piece, width + 128), BF)] * 4
        + [shape((tokens, width), F32), shape((tokens, 128), F32), shape((tokens, span), BF)],
        in_specs=[SMEM] * 2 + [VMEM] + extra_specs + [VMEM] * (3 + PIECES),
        out_specs=[VMEM] * 7,
        scratch_shapes=[pltpu.VMEM((tokens, width), BF)]
        + assembly
        + [pltpu.VMEM((span, width), F32)],
        compiler_params=params(28),
        name="forward",
    )(lat_table, var_weight, ctx, *tiles, w_out, unpatch_t, norm_gain, *pieces)

    terms = [terms[0]] + [swap(terms[b], "lat", b) for b in (1, 2, 3)]
    grad_context = pl.pallas_call(
        backward_kernel,
        out_shape=shape((tokens, width), BF),
        in_specs=[VMEM] * (6 + PIECES),
        out_specs=VMEM,
        scratch_shapes=assembly,
        compiler_params=params(24),
        name="backward",
    )(normed, inv, dfc, w_out, unpatch_t, norm_gain, *pieces)
    *terms, grad_context = barrier((*terms, grad_context))

    *parts, loss = pl.pallas_call(
        lat_sum_kernel,
        out_shape=[shape((piece, rows), BF)] * 4 + [shape((8, 128), F32)],
        in_specs=[VMEM] * 4,
        out_specs=[VMEM] * 5,
        scratch_shapes=[pltpu.VMEM((piece, width + 128), F32)],
        compiler_params=params(4),
        name="lat_sum",
    )(*terms)
    parts = [parts[0]] + [swap(parts[k], "dp", k) for k in (1, 2, 3)]
    mine = pl.pallas_call(
        dp_sum_kernel,
        out_shape=shape((piece + 8, rows), BF),
        in_specs=[VMEM] * 5,
        out_specs=VMEM,
        compiler_params=params(4),
        name="dp_sum",
    )(loss, *parts)
    chip = pl.pallas_call(
        pair_kernel,
        out_shape=shape((2 * piece + 16, rows), BF),
        in_specs=[VMEM] * 2,
        out_specs=VMEM,
        compiler_params=params(4),
        name="pair",
    )(mine, swap(mine, "lat", 1))
    plane = [chip]
    for a, b in ((0, 1), (2, 0), (2, 1)):
        pairs = [(i * lon + j, (i ^ a) * lon + (j ^ b)) for i in range(lat) for j in range(lon)]
        plane.append(lax.ppermute(chip, ("lat", "lon"), pairs))
    count = levels * lat_total * 8 * lon
    counts = (float(count), float(count * (span // var_weight.shape[0])))
    joined, loss = pl.pallas_call(
        lambda *refs: join_kernel(counts, *refs),
        out_shape=[shape((span, rows), F32), shape((1, 1), F32)],
        in_specs=[VMEM] * 4,
        out_specs=[VMEM] * 2,
        compiler_params=params(4),
        name="join",
    )(*plane)
    return grad_context.reshape(1, levels, 8, 8, width), joined.T, loss.reshape(1)


def solution(mesh):
    placed = (
        P("dp", None, "lat", "lon", None),
        P("dp", None, "lat", "lon", None),
        P("lat", "lon"),
        P("dp", None),
        P("dp", None),
        P("dp"),
        P(),
    )
    fits = mesh.shape["dp"] == 4 and mesh.shape["lat"] == 4 and mesh.shape["lon"] == 2

    def program(*arrays):
        body = shards if fits else general_shards
        return jax.shard_map(
            body,
            mesh=mesh,
            in_specs=placed,
            out_specs=(P("dp", None, "lat", "lon", None), P("dp", None), P("dp")),
            check_vma=False,
        )(*arrays)

    return program
```

```python
import functools
import math

import jax
import jax.numpy as jnp
import numpy as np
from jax import lax
from jax.experimental import pallas as pl
from jax.experimental.pallas import tpu as pltpu
from jax.sharding import PartitionSpec as P

HEADS = 48
HDIM = 32
WLEV = 2
BF = jnp.bfloat16
F32 = jnp.float32
EXTRA = 256
UGROWS = 256
PIECES = 12
VMEM = pl.BlockSpec(memory_space=pltpu.VMEM)
SMEM = pl.BlockSpec(memory_space=pltpu.SMEM)
ANY = pl.BlockSpec(memory_space=pl.ANY)
HBM = pl.BlockSpec(memory_space=pltpu.HBM)


def from_behind(array, axis, by):
    length = lax.axis_size(axis)
    return lax.ppermute(array, axis, [(i, (i + by) % length) for i in range(length)])


def general_shards(projected, targets, valid_cells, w_out, unpatch_matrix, norm_gain, var_weight):
    tile_side = projected.shape[2]
    half_side = tile_side // 2
    levels = projected.shape[1]
    model_width = w_out.shape[1]
    predicted_span = unpatch_matrix.shape[1]
    lat_total = tile_side * lax.axis_size("lat")
    lon_total = tile_side * lax.axis_size("lon")
    lat_place = lax.axis_index("lat")
    moved = from_behind(
        (projected[:, :, :, :half_side], targets[:, :, :, :half_side], valid_cells[:, :half_side]),
        "lon",
        -1,
    )
    strip_proj = jnp.concatenate([projected[:, :, :, half_side:], moved[0]], axis=3)
    strip_goal = jnp.concatenate([targets[:, :, :, half_side:], moved[1]], axis=3)
    strip_valid = jnp.concatenate([valid_cells[:, half_side:], moved[2]], axis=1)
    moved_rows = from_behind(
        (strip_proj[:, :, :half_side], strip_goal[:, :, :half_side], strip_valid[:half_side]),
        "lat",
        -1,
    )
    local_proj = jnp.concatenate([strip_proj[:, :, half_side:], moved_rows[0]], axis=2)
    shard_reference = jnp.concatenate([strip_goal[:, :, half_side:], moved_rows[1]], axis=2)
    local_valid = jnp.concatenate([strip_valid[half_side:], moved_rows[2]], axis=0).astype(F32)
    win_count = levels // WLEV
    tokw = WLEV * tile_side * tile_side
    windows = local_proj.reshape(win_count, tokw, 3 * model_width)
    rows_here = lat_place * tile_side + jnp.arange(tile_side)
    region_rows = (rows_here >= lat_total - half_side).astype(jnp.int32)
    region = jnp.broadcast_to(region_rows[None, :, None], (WLEV, tile_side, tile_side)).reshape(-1)
    allowed = region[:, None] == region[None, :]
    queries = windows[..., :model_width].reshape(win_count, tokw, HEADS, -1)
    key_heads = windows[..., model_width : 2 * model_width].reshape(win_count, tokw, HEADS, -1)
    value_heads = windows[..., 2 * model_width :].reshape(win_count, tokw, HEADS, -1)
    scores = jnp.einsum("wqhd,wkhd->whqk", queries, key_heads, preferred_element_type=F32)
    scores = scores * (1.0 / math.sqrt(HDIM))
    scores = jnp.where(allowed[None, None], scores, -1e30)
    row_peak = jnp.max(scores, axis=-1, keepdims=True)
    lifted = jnp.exp(scores - row_peak)
    attn = (lifted / jnp.sum(lifted, axis=-1, keepdims=True)).astype(BF)
    context = jnp.einsum("whqk,wkhd->wqhd", attn, value_heads, preferred_element_type=F32)
    context = context.astype(BF).reshape(win_count * tokw, model_width)
    element_total = win_count * tokw
    out_all, unprojected_pieces, gain_all = (
        lax.all_gather(w_out, "dp", axis=0, tiled=True),
        lax.all_gather(unpatch_matrix, "dp", axis=0, tiled=True),
        lax.all_gather(norm_gain, "dp", axis=0, tiled=True),
    )
    mixed_rows = jnp.dot(context, out_all, preferred_element_type=F32)
    centre = jnp.mean(mixed_rows, axis=-1, keepdims=True)
    spread = jnp.mean((mixed_rows - centre) ** 2, axis=-1, keepdims=True)
    inv_spread = lax.rsqrt(spread + 1e-05)
    normed = (mixed_rows - centre) * inv_spread
    gain_f = gain_all.astype(F32)
    latent_activation = (normed * gain_f).astype(BF)
    prediction_field = jnp.dot(latent_activation, unprojected_pieces, preferred_element_type=F32)
    prediction_misfit = prediction_field - shard_reference.reshape(
        element_total, predicted_span
    ).astype(F32)
    all_rows = jnp.arange(lat_total).astype(F32)
    cosine_mean = jnp.mean(jnp.cos(math.pi * ((all_rows + 0.5) / lat_total - 0.5)))
    initial_rows = ((rows_here + half_side) % lat_total).astype(F32)
    lat_here = jnp.cos(math.pi * ((initial_rows + 0.5) / lat_total - 0.5)) / cosine_mean
    element_factor = jnp.broadcast_to(
        lat_here[None, :, None] * local_valid[None], (levels, tile_side, tile_side)
    ).reshape(element_total, 1)
    variable_factor = jnp.repeat(var_weight, predicted_span // var_weight.shape[0])[None, :]
    shard_penalty = jnp.sum(
        element_factor * variable_factor * prediction_misfit * prediction_misfit
    ) / (levels * lat_total * lon_total * (predicted_span // var_weight.shape[0]))
    prediction_gradient = (2.0 * element_factor * variable_factor * prediction_misfit).astype(BF)
    grad_shard = lax.psum_scatter(
        jnp.einsum(
            "td,to->do", latent_activation, prediction_gradient, preferred_element_type=F32
        ).astype(BF),
        "dp",
        scatter_dimension=0,
        tiled=True,
    ).astype(F32)
    grad_sum, loss_sum = lax.psum((grad_shard, shard_penalty), ("lat", "lon"))
    grad_recovery = grad_sum / (levels * lat_total * lon_total)
    grad_hidden = jnp.einsum(
        "to,do->td", prediction_gradient, unprojected_pieces, preferred_element_type=F32
    )
    scaled_grad = grad_hidden * gain_f
    grad_mixed = inv_spread * (
        scaled_grad
        - jnp.mean(scaled_grad, axis=-1, keepdims=True)
        - normed * jnp.mean(scaled_grad * normed, axis=-1, keepdims=True)
    )
    grad_mixed = grad_mixed.astype(BF)
    grad_context = jnp.einsum("tj,ij->ti", grad_mixed, out_all, preferred_element_type=F32)
    grad_context = grad_context.astype(BF).reshape(1, levels, tile_side, tile_side, model_width)
    return (grad_context, grad_recovery, loss_sum.reshape(1))


def params(mib):
    return pltpu.CompilerParams(vmem_limit_bytes=mib << 20)


def iota(shape, dim):
    return lax.broadcasted_iota(jnp.int32, shape, dim)


def payload_kernel(bits, w_ref, unpatch_ref, gain_ref, payload_ref, ug, sems):
    part = lax.axis_index("lat") ^ bits
    rows, width = w_ref.shape
    qr = rows // 4
    span = unpatch_ref.shape[0]
    start = pl.multiple_of(part * qr, 32)
    u_copy = pltpu.make_async_copy(unpatch_ref, ug.at[pl.ds(0, span), :], sems.at[0])
    u_copy.start()
    w_copy = pltpu.make_async_copy(
        w_ref.at[pl.ds(start, qr), :], payload_ref.at[pl.ds(0, qr), :], sems.at[1]
    )
    w_copy.start()
    ug[pl.ds(span, 16), :] = gain_rows(gain_ref, rows)
    ug[pl.ds(span + 16, UGROWS - span - 16), :] = jnp.zeros((UGROWS - span - 16, rows), BF)
    u_copy.wait()
    for j in range(4):
        at = pl.multiple_of((4 * part + j) * 16, 16)
        payload_ref[pl.ds(qr, 16), pl.ds(j * rows, rows)] = ug[pl.ds(at, 16), :]
    w_copy.wait()


def gain_rows(gain_ref, rows):
    return jnp.broadcast_to(gain_ref[...].astype(F32).reshape(1, rows), (16, rows)).astype(BF)


def pack_kernel(x_ref, t_ref, valid_ref, *refs):
    outs, (x_in, t_in, v_in, sems) = refs[:4], refs[4:]
    span = t_ref.shape[-1]
    count = x_ref.shape[0] * 64
    quarter = count // 4
    step = 512
    width = x_ref.shape[-1]
    copies = [
        pltpu.make_async_copy(t_ref, t_in, sems.at[0]),
        pltpu.make_async_copy(valid_ref, v_in, sems.at[1]),
    ]
    for at in range(0, width, step):
        lanes = (slice(None),) * 3 + (pl.ds(at, step),)
        copies.append(
            pltpu.make_async_copy(x_ref.at[lanes], x_in.at[lanes], sems.at[len(copies)])
        )
    for c in copies:
        c.start()
    place = iota((count, count), 0)
    quad, rest = place // quarter, place % quarter
    row = (rest // 4) % 4 + jnp.where(quad < 2, 4, 0)
    col = rest % 4 + jnp.where(quad % 2 == 0, 4, 0)
    source = (rest // 16) * 64 + row * 8 + col
    pick = (iota((count, count), 1) == source).astype(F32).astype(BF)
    copies[0].wait()
    copies[1].wait()
    goal = jnp.dot(pick, t_in[...].reshape(count, span), preferred_element_type=F32)
    token = iota((count, 8), 0)
    row_hot = ((token // 8) % 8 == iota((count, 8), 1)).astype(F32)
    by_row = jnp.dot(row_hot, v_in[...].astype(F32), preferred_element_type=F32)
    mine = token % 8 == iota((count, 8), 1)
    natural = jnp.sum(jnp.where(mine, by_row, 0.0), axis=1, keepdims=True)
    spread = jnp.broadcast_to(natural, (count, 128)).astype(BF)
    column = jnp.dot(pick, spread, preferred_element_type=F32)
    extra = jnp.concatenate([goal, column[:, : EXTRA - span]], axis=1).astype(BF)
    starts = [sum(o.shape[0] for o in outs[:n]) for n in range(4)]
    outs = list(zip(outs, starts))
    for ref, row in outs:
        ref[:, width:] = extra[row : row + ref.shape[0]]
    for n, at in enumerate(range(0, width, step)):
        copies[2 + n].wait()
        tokens = x_in[:, :, :, at : at + step].reshape(count, step)
        out = jnp.dot(pick, tokens, preferred_element_type=F32).astype(BF)
        for ref, row in outs:
            ref[:, at : at + step] = out[row : row + ref.shape[0]]


def windows_of(*tiles):
    return [[t.at[32 * w : 32 * w + 32] for t in tiles] for w in range(2)]


def attention_kernel(*refs):
    tiles, ctx_ref = windows_of(*refs[:4]), refs[4]
    part = ctx_ref.shape[1]
    is_last = lax.axis_index("lat") == lax.axis_size("lat") - 1
    same = (iota((512, 128), 0) % 128) // 64 == iota((512, 128), 1) // 64
    bias = jnp.where(jnp.logical_or(same, jnp.logical_not(is_last)), 0.0, -1e30)
    head = iota((128, 128), 1) // HDIM
    factor = math.log2(math.e) / math.sqrt(HDIM)
    for at in range(0, part, 128):
        for w in range(2):
            q, k, v = [
                jnp.concatenate(
                    [t[:, i * part + at : i * part + at + 128] for t in tiles[w]],
                    axis=0,
                )
                for i in range(3)
            ]
            zero = jnp.zeros_like(k)
            k4 = jnp.concatenate([jnp.where(head == h, k, zero) for h in range(4)], axis=0)
            v4 = jnp.concatenate([jnp.where(head == h, v, zero) for h in range(4)], axis=0)
            s = lax.dot_general(k4, q, (((1,), (1,)), ((), ())), preferred_element_type=F32)
            s = s + bias
            parts = []
            for h in range(4):
                sh = s[128 * h : 128 * h + 128]
                e = jnp.exp2((sh - jnp.max(sh, axis=0, keepdims=True)) * factor)
                parts.append((e * (1.0 / jnp.sum(e, axis=0, keepdims=True))).astype(BF))
            attn = jnp.concatenate(parts, axis=0)
            out = lax.dot_general(attn, v4, (((0,), (0,)), ((), ())), preferred_element_type=F32)
            ctx_ref[128 * w : 128 * w + 128, at : at + 128] = out.astype(BF)


def assemble(own_w, own_u, own_gain, pieces, w_all, ug_all):
    zi, part = lax.axis_index("dp"), lax.axis_index("lat")
    rows = own_w.shape[0]
    qr = rows // 4
    steps = len(pieces) // 4 + 1
    base = pl.multiple_of(zi * rows, 128)
    w_all[pl.ds(base, rows), :] = own_w[...]
    span = own_u.shape[0]
    ug_all[0:span, pl.ds(base, rows)] = own_u[...]
    ug_all[span : span + 16, pl.ds(base, rows)] = gain_rows(own_gain, rows)
    for k in range(1, steps):
        shard = lax.rem(zi - k + steps, steps)
        base = pl.multiple_of(shard * rows, 128)
        for bits, piece in zip((0, 2, 1, 3), pieces[4 * k - 4 : 4 * k]):
            from_part = part ^ bits
            row = pl.multiple_of(base + from_part * qr, 32)
            w_all[pl.ds(row, qr), :] = piece[0:qr, :]
            for j in range(4):
                urow = pl.multiple_of((4 * from_part + j) * 16, 16)
                ug_all[pl.ds(urow, 16), pl.ds(base, rows)] = piece[
                    qr : qr + 16, j * rows : (j + 1) * rows
                ]


def split3(x):
    hi = x.astype(BF).astype(F32)
    mid = (x - hi).astype(BF).astype(F32)
    return hi, mid, x - hi - mid


def loss_block(value, rows):
    hi, mid, lo = split3(value)
    lane = iota((rows, 128), 1)
    return jnp.where(lane == 0, hi, jnp.where(lane == 1, mid, jnp.where(lane == 2, lo, 0.0)))


def forward_kernel(lat_ref, var_ref, *refs):
    ctx_ref, refs = refs[0], refs[1:]
    extras, refs = refs[:4], refs[4:]
    owned, refs = refs[:3], refs[3:]
    pieces, refs = refs[:PIECES], refs[PIECES:]
    ts, refs = refs[:4], refs[4:]
    normed_ref, inv_ref, dfc_ref, hidden_ref, w_all, ug_all, term = refs
    lat_place = lax.axis_index("lat")
    assemble(*owned, pieces, w_all, ug_all)
    tokens, width = normed_ref.shape
    span = dfc_ref.shape[1]
    extra = jnp.concatenate([t[...] for tiles in windows_of(*extras) for t in tiles], axis=0)
    extra = extra.astype(F32)
    goal, valid = extra[:, :span], extra[:, span : span + 1]
    token = iota((tokens, 1), 0)
    row = (token // 4) % 4 + jnp.where((token // 32) % 4 >= 2, 4, 0)
    lat_w = jnp.zeros((tokens, 1), F32)
    for r in range(8):
        lat_w = jnp.where(row == r, lat_ref[lat_place * 8 + r], lat_w)
    lane = iota((1, span), 1) // (span // var_ref.shape[0])
    var_w = jnp.zeros((1, span), F32)
    for n in range(var_ref.shape[0]):
        var_w = jnp.where(lane == n, var_ref[n], var_w)
    weight = lat_w * valid * var_w
    mixed = jnp.dot(ctx_ref[...], w_all[...], preferred_element_type=F32)
    centre = jnp.mean(mixed, axis=-1, keepdims=True)
    off = mixed - centre
    inv = lax.rsqrt(jnp.mean(off * off, axis=-1, keepdims=True) + 1e-05)
    normed = off * inv
    normed_ref[...] = normed
    inv_ref[...] = jnp.broadcast_to(inv, inv_ref.shape)
    gain = ug_all[pl.ds(span, 16), :][0:1].astype(F32)
    hidden_ref[...] = (normed * gain).astype(BF)
    field = lax.dot_general(
        hidden_ref[...], ug_all[0:span, :], (((1,), (1,)), ((), ())), preferred_element_type=F32
    )
    misfit = field - goal
    dfc = (2.0 * weight * misfit).astype(BF)
    dfc_ref[...] = dfc
    term[...] = lax.dot_general(
        dfc, hidden_ref[...], (((0,), (0,)), ((), ())), preferred_element_type=F32
    )
    loss = jnp.sum(jnp.sum(weight * misfit * misfit, axis=1, keepdims=True), axis=0, keepdims=True)
    rows = ts[0].shape[0]
    block = loss_block(loss, rows).astype(BF)
    for b, ref in enumerate(ts):
        at = pl.multiple_of((lat_place ^ b) * rows, 8)
        ref[:, :width] = term[pl.ds(at, rows), :].astype(BF)
        ref[:, width:] = block


def backward_kernel(normed_ref, inv_ref, dfc_ref, *refs):
    owned, refs = refs[:3], refs[3:]
    pieces, (out_ref, w_all, ug_all) = refs[:PIECES], refs[PIECES:]
    assemble(*owned, pieces, w_all, ug_all)
    tokens, width = normed_ref.shape
    span = dfc_ref.shape[1]
    gain = ug_all[pl.ds(span, 16), :][0:1].astype(F32)
    g = jnp.dot(dfc_ref[...], ug_all[0:span, :], preferred_element_type=F32) * gain
    normed = normed_ref[...]
    mean_g = jnp.mean(g, axis=-1, keepdims=True)
    mean_gn = jnp.mean(g * normed, axis=-1, keepdims=True)
    dmixed = ((g - mean_g - normed * mean_gn) * inv_ref[:, 0:1]).astype(BF)
    place = iota((tokens, tokens), 0)
    row, col, level = (place // 8) % 8, place % 8, place // 64
    quad = jnp.where(row >= 4, 2, 0) + jnp.where(col >= 4, 1, 0)
    source = (level // 2) * 128 + quad * 32 + (level % 2) * 16 + (row % 4) * 4 + col % 4
    pick = (iota((tokens, tokens), 1) == source).astype(F32).astype(BF)
    dnat = jnp.dot(pick, dmixed, preferred_element_type=F32).astype(BF)
    out = lax.dot_general(dnat, w_all[...], (((1,), (1,)), ((), ())), preferred_element_type=F32)
    out_ref[...] = out.astype(BF)


def add4(a, b, c, d):
    return (a[...].astype(F32) + b[...].astype(F32)) + (c[...].astype(F32) + d[...].astype(F32))


def lat_sum_kernel(a, b, c, d, z0, z1, z2, z3, loss_ref, total_ref):
    total_ref[...] = add4(a, b, c, d)
    zi = lax.axis_index("dp")
    rows, width = z0.shape
    for k, ref in enumerate((z0, z1, z2, z3)):
        at = pl.multiple_of((zi ^ k) * width, 128)
        ref[...] = total_ref[:, pl.ds(at, width)].astype(BF)
    loss = jnp.sum(total_ref[0:1, 4 * width :], axis=1, keepdims=True)
    loss_ref[...] = jnp.broadcast_to(loss, loss_ref.shape)


def dp_sum_kernel(loss_ref, a, b, c, d, o_ref):
    rows, width = a.shape
    o_ref[0:rows, :] = add4(a, b, c, d).astype(BF)
    block = loss_block(loss_ref[0:1, 0:1], o_ref.shape[0] - rows)
    zeros = jnp.zeros((block.shape[0], width - 128), F32)
    o_ref[rows:, :] = jnp.concatenate([block, zeros], axis=1).astype(BF)


def pair_kernel(mine_ref, other_ref, o_ref):
    rows = mine_ref.shape[0]
    odd = lax.axis_index("lat") % 2
    o_ref[pl.ds(pl.multiple_of(odd * rows, 8), rows), :] = mine_ref[...]
    o_ref[pl.ds(pl.multiple_of((1 - odd) * rows, 8), rows), :] = other_ref[...]


def join_kernel(counts, *refs):
    pieces, (o_ref, loss_ref) = refs[:4], refs[4:]
    chip = lax.axis_index("lat") // 2
    held = pieces[0].shape[0] // 2
    rows = held - 8
    for a in range(2):
        for n in range(2):
            at = pl.multiple_of((2 * (chip ^ a) + n) * rows, 8)
            both = [pieces[2 * a + b][held * n : held * n + rows, :].astype(F32) for b in range(2)]
            o_ref[pl.ds(at, rows), :] = (both[0] + both[1]) / counts[0]
    sums = [
        jnp.sum(p[rows : rows + 1, 0:128].astype(F32), axis=1, keepdims=True) for p in pieces[:2]
    ]
    loss_ref[...] = jnp.broadcast_to((sums[0] + sums[1]) / counts[1], loss_ref.shape)


def swap(array, axis, bit):
    return lax.ppermute(array, axis, [(i, i ^ bit) for i in range(lax.axis_size(axis))])


def shape(dims, dtype):
    return jax.ShapeDtypeStruct(dims, dtype)


def shards(projected, targets, valid_cells, w_out, unpatch_matrix, norm_gain, var_weight):
    dp, lat, lon = lax.axis_size("dp"), lax.axis_size("lat"), lax.axis_size("lon")
    rows, width = w_out.shape
    levels = projected.shape[1]
    span = unpatch_matrix.shape[1]
    tokens = levels * 64
    lat_total = 8 * lat
    angle = math.pi * ((np.arange(lat_total) + 0.5) / lat_total - 0.5)
    cosine = np.cos(angle)
    lat_table = jnp.asarray(np.roll(cosine / cosine.mean(), -4), F32)
    barrier = lax.optimization_barrier

    unpatch_t = unpatch_matrix.T

    def quarter_of(bits):
        return pl.pallas_call(
            functools.partial(payload_kernel, bits),
            out_shape=shape((rows // 4 + 16, width), BF),
            in_specs=[HBM, HBM, VMEM],
            out_specs=VMEM,
            scratch_shapes=[pltpu.VMEM((UGROWS, rows), BF), pltpu.SemaphoreType.DMA((2,))],
            compiler_params=params(62),
            name="payload",
        )(w_out, unpatch_t, norm_gain)

    payload = quarter_of(0)
    second = quarter_of(2)
    ring1 = from_behind(payload, "dp", 1)
    own, *send = pl.pallas_call(
        pack_kernel,
        out_shape=[shape((n, 3 * width + EXTRA), BF) for n in (64, 64, 64, 64)],
        in_specs=[HBM] * 3,
        out_specs=[VMEM] * 4,
        scratch_shapes=[
            pltpu.VMEM((levels, 8, 8, 3 * width), BF),
            pltpu.VMEM((levels, 8, 8, span), BF),
            pltpu.VMEM((8, 8), jnp.int32),
            pltpu.SemaphoreType.DMA((2 + 3 * width // 512,)),
        ],
        compiler_params=params(62),
        name="pack",
    )(
        projected.reshape(levels, 8, 8, 3 * width),
        targets.reshape(levels, 8, 8, span),
        barrier((valid_cells, payload))[0],
    )
    corner = [
        (a * lon + b, ((a - 1) % lat) * lon + (b - 1) % lon) for a in range(lat) for b in range(lon)
    ]
    south = from_behind(send[1], "lat", -1)
    diag = lax.ppermute(send[2], ("lat", "lon"), corner)
    ring1_after, second = barrier((ring1, second))
    ring2 = from_behind(ring1_after, "dp", 1)
    across2 = swap(ring2, "lat", 2)
    ring2_late, east, south, diag = barrier((ring2, send[0], south, diag))
    east = from_behind(east, "lon", -1)
    first, second, ring1_late, ring2 = barrier((payload, second, ring1, ring2_late))
    back = from_behind(first, "dp", -1)
    back_across = from_behind(second, "dp", -1)
    across1 = swap(ring1_late, "lat", 2)
    tiles = barrier((own, east, south, diag))
    ctx = pl.pallas_call(
        attention_kernel,
        out_shape=shape((tokens, width), BF),
        in_specs=[VMEM] * 4,
        out_specs=VMEM,
        compiler_params=params(16),
        name="attention",
    )(*tiles)
    across2, back_across, ctx = barrier((across2, back_across, ctx))
    pieces = []
    for ring, across in ((ring1, across1), (ring2, across2), (back, back_across)):
        pieces += [ring, across, swap(ring, "lat", 1), swap(across, "lat", 1)]

    piece = span // lat
    extra_specs = [
        pl.BlockSpec((t.shape[0], EXTRA), lambda i: (0, 3 * width // EXTRA)) for t in tiles
    ]
    assembly = [
        pltpu.VMEM((dp * rows, width), BF),
        pltpu.VMEM((UGROWS, dp * rows), BF),
    ]
    *terms, normed, inv, dfc = pl.pallas_call(
        forward_kernel,
        grid=(1,),
        out_shape=[shape((piece, width + 128), BF)] * 4
        + [shape((tokens, width), F32), shape((tokens, 128), F32), shape((tokens, span), BF)],
        in_specs=[SMEM] * 2 + [VMEM] + extra_specs + [VMEM] * (3 + PIECES),
        out_specs=[VMEM] * 7,
        scratch_shapes=[pltpu.VMEM((tokens, width), BF)]
        + assembly
        + [pltpu.VMEM((span, width), F32)],
        compiler_params=params(28),
        name="forward",
    )(lat_table, var_weight, ctx, *tiles, w_out, unpatch_t, norm_gain, *pieces)

    terms = [terms[0]] + [swap(terms[b], "lat", b) for b in (1, 2, 3)]
    grad_context = pl.pallas_call(
        backward_kernel,
        out_shape=shape((tokens, width), BF),
        in_specs=[VMEM] * (6 + PIECES),
        out_specs=VMEM,
        scratch_shapes=assembly,
        compiler_params=params(24),
        name="backward",
    )(normed, inv, dfc, w_out, unpatch_t, norm_gain, *pieces)
    *terms, grad_context = barrier((*terms, grad_context))

    *parts, loss = pl.pallas_call(
        lat_sum_kernel,
        out_shape=[shape((piece, rows), BF)] * 4 + [shape((8, 128), F32)],
        in_specs=[VMEM] * 4,
        out_specs=[VMEM] * 5,
        scratch_shapes=[pltpu.VMEM((piece, width + 128), F32)],
        compiler_params=params(4),
        name="lat_sum",
    )(*terms)
    parts = [parts[0]] + [swap(parts[k], "dp", k) for k in (1, 2, 3)]
    mine = pl.pallas_call(
        dp_sum_kernel,
        out_shape=shape((piece + 8, rows), BF),
        in_specs=[VMEM] * 5,
        out_specs=VMEM,
        compiler_params=params(4),
        name="dp_sum",
    )(loss, *parts)
    chip = pl.pallas_call(
        pair_kernel,
        out_shape=shape((2 * piece + 16, rows), BF),
        in_specs=[VMEM] * 2,
        out_specs=VMEM,
        compiler_params=params(4),
        name="pair",
    )(mine, swap(mine, "lat", 1))
    plane = [chip]
    for a, b in ((0, 1), (2, 0), (2, 1)):
        pairs = [(i * lon + j, (i ^ a) * lon + (j ^ b)) for i in range(lat) for j in range(lon)]
        plane.append(lax.ppermute(chip, ("lat", "lon"), pairs))
    count = levels * lat_total * 8 * lon
    counts = (float(count), float(count * (span // var_weight.shape[0])))
    joined, loss = pl.pallas_call(
        lambda *refs: join_kernel(counts, *refs),
        out_shape=[shape((span, rows), F32), shape((1, 1), F32)],
        in_specs=[VMEM] * 4,
        out_specs=[VMEM] * 2,
        compiler_params=params(4),
        name="join",
    )(*plane)
    return grad_context.reshape(1, levels, 8, 8, width), joined.T, loss.reshape(1)


def solution(mesh):
    placed = (
        P("dp", None, "lat", "lon", None),
        P("dp", None, "lat", "lon", None),
        P("lat", "lon"),
        P("dp", None),
        P("dp", None),
        P("dp"),
        P(),
    )
    fits = mesh.shape["dp"] == 4 and mesh.shape["lat"] == 4 and mesh.shape["lon"] == 2

    def program(*arrays):
        body = shards if fits else general_shards
        return jax.shard_map(
            body,
            mesh=mesh,
            in_specs=placed,
            out_specs=(P("dp", None, "lat", "lon", None), P("dp", None), P("dp")),
            check_vma=False,
        )(*arrays)

    return program
```

```python
import functools
import math

import jax
import jax.numpy as jnp
import numpy as np
from jax import lax
from jax.experimental import pallas as pl
from jax.experimental.pallas import tpu as pltpu
from jax.sharding import PartitionSpec as P

HEADS = 48
HDIM = 32
WLEV = 2
BF = jnp.bfloat16
F32 = jnp.float32
EXTRA = 256
UGROWS = 256
PIECES = 12
VMEM = pl.BlockSpec(memory_space=pltpu.VMEM)
SMEM = pl.BlockSpec(memory_space=pltpu.SMEM)
ANY = pl.BlockSpec(memory_space=pl.ANY)
HBM = pl.BlockSpec(memory_space=pltpu.HBM)


def from_behind(array, axis, by):
    length = lax.axis_size(axis)
    return lax.ppermute(array, axis, [(i, (i + by) % length) for i in range(length)])


def general_shards(projected, targets, valid_cells, w_out, unpatch_matrix, norm_gain, var_weight):
    tile_side = projected.shape[2]
    half_side = tile_side // 2
    levels = projected.shape[1]
    model_width = w_out.shape[1]
    predicted_span = unpatch_matrix.shape[1]
    lat_total = tile_side * lax.axis_size("lat")
    lon_total = tile_side * lax.axis_size("lon")
    lat_place = lax.axis_index("lat")
    moved = from_behind(
        (projected[:, :, :, :half_side], targets[:, :, :, :half_side], valid_cells[:, :half_side]),
        "lon",
        -1,
    )
    strip_proj = jnp.concatenate([projected[:, :, :, half_side:], moved[0]], axis=3)
    strip_goal = jnp.concatenate([targets[:, :, :, half_side:], moved[1]], axis=3)
    strip_valid = jnp.concatenate([valid_cells[:, half_side:], moved[2]], axis=1)
    moved_rows = from_behind(
        (strip_proj[:, :, :half_side], strip_goal[:, :, :half_side], strip_valid[:half_side]),
        "lat",
        -1,
    )
    local_proj = jnp.concatenate([strip_proj[:, :, half_side:], moved_rows[0]], axis=2)
    shard_reference = jnp.concatenate([strip_goal[:, :, half_side:], moved_rows[1]], axis=2)
    local_valid = jnp.concatenate([strip_valid[half_side:], moved_rows[2]], axis=0).astype(F32)
    win_count = levels // WLEV
    tokw = WLEV * tile_side * tile_side
    windows = local_proj.reshape(win_count, tokw, 3 * model_width)
    rows_here = lat_place * tile_side + jnp.arange(tile_side)
    region_rows = (rows_here >= lat_total - half_side).astype(jnp.int32)
    region = jnp.broadcast_to(region_rows[None, :, None], (WLEV, tile_side, tile_side)).reshape(-1)
    allowed = region[:, None] == region[None, :]
    queries = windows[..., :model_width].reshape(win_count, tokw, HEADS, -1)
    key_heads = windows[..., model_width : 2 * model_width].reshape(win_count, tokw, HEADS, -1)
    value_heads = windows[..., 2 * model_width :].reshape(win_count, tokw, HEADS, -1)
    scores = jnp.einsum("wqhd,wkhd->whqk", queries, key_heads, preferred_element_type=F32)
    scores = scores * (1.0 / math.sqrt(HDIM))
    scores = jnp.where(allowed[None, None], scores, -1e30)
    row_peak = jnp.max(scores, axis=-1, keepdims=True)
    lifted = jnp.exp(scores - row_peak)
    attn = (lifted / jnp.sum(lifted, axis=-1, keepdims=True)).astype(BF)
    context = jnp.einsum("whqk,wkhd->wqhd", attn, value_heads, preferred_element_type=F32)
    context = context.astype(BF).reshape(win_count * tokw, model_width)
    element_total = win_count * tokw
    out_all, unprojected_pieces, gain_all = (
        lax.all_gather(w_out, "dp", axis=0, tiled=True),
        lax.all_gather(unpatch_matrix, "dp", axis=0, tiled=True),
        lax.all_gather(norm_gain, "dp", axis=0, tiled=True),
    )
    mixed_rows = jnp.dot(context, out_all, preferred_element_type=F32)
    centre = jnp.mean(mixed_rows, axis=-1, keepdims=True)
    spread = jnp.mean((mixed_rows - centre) ** 2, axis=-1, keepdims=True)
    inv_spread = lax.rsqrt(spread + 1e-05)
    normed = (mixed_rows - centre) * inv_spread
    gain_f = gain_all.astype(F32)
    latent_activation = (normed * gain_f).astype(BF)
    prediction_field = jnp.dot(latent_activation, unprojected_pieces, preferred_element_type=F32)
    prediction_misfit = prediction_field - shard_reference.reshape(
        element_total, predicted_span
    ).astype(F32)
    all_rows = jnp.arange(lat_total).astype(F32)
    cosine_mean = jnp.mean(jnp.cos(math.pi * ((all_rows + 0.5) / lat_total - 0.5)))
    initial_rows = ((rows_here + half_side) % lat_total).astype(F32)
    lat_here = jnp.cos(math.pi * ((initial_rows + 0.5) / lat_total - 0.5)) / cosine_mean
    element_factor = jnp.broadcast_to(
        lat_here[None, :, None] * local_valid[None], (levels, tile_side, tile_side)
    ).reshape(element_total, 1)
    variable_factor = jnp.repeat(var_weight, predicted_span // var_weight.shape[0])[None, :]
    shard_penalty = jnp.sum(
        element_factor * variable_factor * prediction_misfit * prediction_misfit
    ) / (levels * lat_total * lon_total * (predicted_span // var_weight.shape[0]))
    prediction_gradient = (2.0 * element_factor * variable_factor * prediction_misfit).astype(BF)
    grad_shard = lax.psum_scatter(
        jnp.einsum(
            "td,to->do", latent_activation, prediction_gradient, preferred_element_type=F32
        ).astype(BF),
        "dp",
        scatter_dimension=0,
        tiled=True,
    ).astype(F32)
    grad_sum, loss_sum = lax.psum((grad_shard, shard_penalty), ("lat", "lon"))
    grad_recovery = grad_sum / (levels * lat_total * lon_total)
    grad_hidden = jnp.einsum(
        "to,do->td", prediction_gradient, unprojected_pieces, preferred_element_type=F32
    )
    scaled_grad = grad_hidden * gain_f
    grad_mixed = inv_spread * (
        scaled_grad
        - jnp.mean(scaled_grad, axis=-1, keepdims=True)
        - normed * jnp.mean(scaled_grad * normed, axis=-1, keepdims=True)
    )
    grad_mixed = grad_mixed.astype(BF)
    grad_context = jnp.einsum("tj,ij->ti", grad_mixed, out_all, preferred_element_type=F32)
    grad_context = grad_context.astype(BF).reshape(1, levels, tile_side, tile_side, model_width)
    return (grad_context, grad_recovery, loss_sum.reshape(1))


def params(mib):
    return pltpu.CompilerParams(vmem_limit_bytes=mib << 20)


def iota(shape, dim):
    return lax.broadcasted_iota(jnp.int32, shape, dim)


def payload_kernel(w_ref, unpatch_ref, gain_ref, payload_ref, ug, sems):
    part = lax.axis_index("lat")
    rows, width = w_ref.shape
    qr = rows // 4
    span = unpatch_ref.shape[0]
    start = pl.multiple_of(part * qr, 32)
    u_copy = pltpu.make_async_copy(unpatch_ref, ug.at[pl.ds(0, span), :], sems.at[0])
    u_copy.start()
    w_copy = pltpu.make_async_copy(
        w_ref.at[pl.ds(start, qr), :], payload_ref.at[pl.ds(0, qr), :], sems.at[1]
    )
    w_copy.start()
    ug[pl.ds(span, 16), :] = gain_rows(gain_ref, rows)
    ug[pl.ds(span + 16, UGROWS - span - 16), :] = jnp.zeros((UGROWS - span - 16, rows), BF)
    u_copy.wait()
    for j in range(4):
        at = pl.multiple_of((4 * part + j) * 16, 16)
        payload_ref[pl.ds(qr, 16), pl.ds(j * rows, rows)] = ug[pl.ds(at, 16), :]
    w_copy.wait()


def gain_rows(gain_ref, rows):
    return jnp.broadcast_to(gain_ref[...].astype(F32).reshape(1, rows), (16, rows)).astype(BF)


def pack_kernel(x_ref, t_ref, valid_ref, *refs):
    outs, (x_in, t_in, v_in, sems) = refs[:4], refs[4:]
    span = t_ref.shape[-1]
    count = x_ref.shape[0] * 64
    quarter = count // 4
    step = 512
    width = x_ref.shape[-1]
    copies = [
        pltpu.make_async_copy(t_ref, t_in, sems.at[0]),
        pltpu.make_async_copy(valid_ref, v_in, sems.at[1]),
    ]
    for at in range(0, width, step):
        lanes = (slice(None),) * 3 + (pl.ds(at, step),)
        copies.append(
            pltpu.make_async_copy(x_ref.at[lanes], x_in.at[lanes], sems.at[len(copies)])
        )
    for c in copies:
        c.start()
    place = iota((count, count), 0)
    quad, rest = place // quarter, place % quarter
    row = (rest // 4) % 4 + jnp.where(quad < 2, 4, 0)
    col = rest % 4 + jnp.where(quad % 2 == 0, 4, 0)
    source = (rest // 16) * 64 + row * 8 + col
    pick = (iota((count, count), 1) == source).astype(F32).astype(BF)
    copies[0].wait()
    copies[1].wait()
    goal = jnp.dot(pick, t_in[...].reshape(count, span), preferred_element_type=F32)
    token = iota((count, 8), 0)
    row_hot = ((token // 8) % 8 == iota((count, 8), 1)).astype(F32)
    by_row = jnp.dot(row_hot, v_in[...].astype(F32), preferred_element_type=F32)
    mine = token % 8 == iota((count, 8), 1)
    natural = jnp.sum(jnp.where(mine, by_row, 0.0), axis=1, keepdims=True)
    spread = jnp.broadcast_to(natural, (count, 128)).astype(BF)
    column = jnp.dot(pick, spread, preferred_element_type=F32)
    extra = jnp.concatenate([goal, column[:, : EXTRA - span]], axis=1).astype(BF)
    starts = [sum(o.shape[0] for o in outs[:n]) for n in range(4)]
    outs = list(zip(outs, starts))
    for ref, row in outs:
        ref[:, width:] = extra[row : row + ref.shape[0]]
    for n, at in enumerate(range(0, width, step)):
        copies[2 + n].wait()
        tokens = x_in[:, :, :, at : at + step].reshape(count, step)
        out = jnp.dot(pick, tokens, preferred_element_type=F32).astype(BF)
        for ref, row in outs:
            ref[:, at : at + step] = out[row : row + ref.shape[0]]


def windows_of(*tiles):
    return [[t.at[32 * w : 32 * w + 32] for t in tiles] for w in range(2)]


def attention_kernel(*refs):
    tiles, ctx_ref = windows_of(*refs[:4]), refs[4]
    part = ctx_ref.shape[1]
    is_last = lax.axis_index("lat") == lax.axis_size("lat") - 1
    same = (iota((512, 128), 0) % 128) // 64 == iota((512, 128), 1) // 64
    bias = jnp.where(jnp.logical_or(same, jnp.logical_not(is_last)), 0.0, -1e30)
    head = iota((128, 128), 1) // HDIM
    factor = math.log2(math.e) / math.sqrt(HDIM)
    for at in range(0, part, 128):
        for w in range(2):
            q, k, v = [
                jnp.concatenate(
                    [t[:, i * part + at : i * part + at + 128] for t in tiles[w]],
                    axis=0,
                )
                for i in range(3)
            ]
            zero = jnp.zeros_like(k)
            k4 = jnp.concatenate([jnp.where(head == h, k, zero) for h in range(4)], axis=0)
            v4 = jnp.concatenate([jnp.where(head == h, v, zero) for h in range(4)], axis=0)
            s = lax.dot_general(k4, q, (((1,), (1,)), ((), ())), preferred_element_type=F32)
            s = s + bias
            parts = []
            for h in range(4):
                sh = s[128 * h : 128 * h + 128]
                e = jnp.exp2((sh - jnp.max(sh, axis=0, keepdims=True)) * factor)
                parts.append((e * (1.0 / jnp.sum(e, axis=0, keepdims=True))).astype(BF))
            attn = jnp.concatenate(parts, axis=0)
            out = lax.dot_general(attn, v4, (((0,), (0,)), ((), ())), preferred_element_type=F32)
            ctx_ref[128 * w : 128 * w + 128, at : at + 128] = out.astype(BF)


def assemble(own_w, own_u, own_gain, pieces, w_all, ug_all):
    zi, part = lax.axis_index("dp"), lax.axis_index("lat")
    rows = own_w.shape[0]
    qr = rows // 4
    steps = len(pieces) // 4 + 1
    base = pl.multiple_of(zi * rows, 128)
    w_all[pl.ds(base, rows), :] = own_w[...]
    span = own_u.shape[0]
    ug_all[0:span, pl.ds(base, rows)] = own_u[...]
    ug_all[span : span + 16, pl.ds(base, rows)] = gain_rows(own_gain, rows)
    for k in range(1, steps):
        shard = lax.rem(zi - k + steps, steps)
        base = pl.multiple_of(shard * rows, 128)
        for bits, piece in zip((0, 2, 1, 3), pieces[4 * k - 4 : 4 * k]):
            from_part = part ^ bits
            row = pl.multiple_of(base + from_part * qr, 32)
            w_all[pl.ds(row, qr), :] = piece[0:qr, :]
            for j in range(4):
                urow = pl.multiple_of((4 * from_part + j) * 16, 16)
                ug_all[pl.ds(urow, 16), pl.ds(base, rows)] = piece[
                    qr : qr + 16, j * rows : (j + 1) * rows
                ]


def split3(x):
    hi = x.astype(BF).astype(F32)
    mid = (x - hi).astype(BF).astype(F32)
    return hi, mid, x - hi - mid


def loss_block(value, rows):
    hi, mid, lo = split3(value)
    lane = iota((rows, 128), 1)
    return jnp.where(lane == 0, hi, jnp.where(lane == 1, mid, jnp.where(lane == 2, lo, 0.0)))


def forward_kernel(lat_ref, var_ref, *refs):
    ctx_ref, refs = refs[0], refs[1:]
    extras, refs = refs[:4], refs[4:]
    owned, refs = refs[:3], refs[3:]
    pieces, refs = refs[:PIECES], refs[PIECES:]
    ts, refs = refs[:4], refs[4:]
    normed_ref, inv_ref, dfc_ref, hidden_ref, w_all, ug_all, term = refs
    lat_place = lax.axis_index("lat")
    assemble(*owned, pieces, w_all, ug_all)
    tokens, width = normed_ref.shape
    span = dfc_ref.shape[1]
    extra = jnp.concatenate([t[...] for tiles in windows_of(*extras) for t in tiles], axis=0)
    extra = extra.astype(F32)
    goal, valid = extra[:, :span], extra[:, span : span + 1]
    token = iota((tokens, 1), 0)
    row = (token // 4) % 4 + jnp.where((token // 32) % 4 >= 2, 4, 0)
    lat_w = jnp.zeros((tokens, 1), F32)
    for r in range(8):
        lat_w = jnp.where(row == r, lat_ref[lat_place * 8 + r], lat_w)
    lane = iota((1, span), 1) // (span // var_ref.shape[0])
    var_w = jnp.zeros((1, span), F32)
    for n in range(var_ref.shape[0]):
        var_w = jnp.where(lane == n, var_ref[n], var_w)
    weight = lat_w * valid * var_w
    mixed = jnp.dot(ctx_ref[...], w_all[...], preferred_element_type=F32)
    centre = jnp.mean(mixed, axis=-1, keepdims=True)
    off = mixed - centre
    inv = lax.rsqrt(jnp.mean(off * off, axis=-1, keepdims=True) + 1e-05)
    normed = off * inv
    normed_ref[...] = normed
    inv_ref[...] = jnp.broadcast_to(inv, inv_ref.shape)
    gain = ug_all[pl.ds(span, 16), :][0:1].astype(F32)
    hidden_ref[...] = (normed * gain).astype(BF)
    field = lax.dot_general(
        hidden_ref[...], ug_all[0:span, :], (((1,), (1,)), ((), ())), preferred_element_type=F32
    )
    misfit = field - goal
    dfc = (2.0 * weight * misfit).astype(BF)
    dfc_ref[...] = dfc
    term[...] = lax.dot_general(
        dfc, hidden_ref[...], (((0,), (0,)), ((), ())), preferred_element_type=F32
    )
    loss = jnp.sum(jnp.sum(weight * misfit * misfit, axis=1, keepdims=True), axis=0, keepdims=True)
    rows = ts[0].shape[0]
    block = loss_block(loss, rows).astype(BF)
    for b, ref in enumerate(ts):
        at = pl.multiple_of((lat_place ^ b) * rows, 8)
        ref[:, :width] = term[pl.ds(at, rows), :].astype(BF)
        ref[:, width:] = block


def backward_kernel(normed_ref, inv_ref, dfc_ref, *refs):
    owned, refs = refs[:3], refs[3:]
    pieces, (out_ref, w_all, ug_all) = refs[:PIECES], refs[PIECES:]
    assemble(*owned, pieces, w_all, ug_all)
    tokens, width = normed_ref.shape
    span = dfc_ref.shape[1]
    gain = ug_all[pl.ds(span, 16), :][0:1].astype(F32)
    g = jnp.dot(dfc_ref[...], ug_all[0:span, :], preferred_element_type=F32) * gain
    normed = normed_ref[...]
    mean_g = jnp.mean(g, axis=-1, keepdims=True)
    mean_gn = jnp.mean(g * normed, axis=-1, keepdims=True)
    dmixed = ((g - mean_g - normed * mean_gn) * inv_ref[:, 0:1]).astype(BF)
    place = iota((tokens, tokens), 0)
    row, col, level = (place // 8) % 8, place % 8, place // 64
    quad = jnp.where(row >= 4, 2, 0) + jnp.where(col >= 4, 1, 0)
    source = (level // 2) * 128 + quad * 32 + (level % 2) * 16 + (row % 4) * 4 + col % 4
    pick = (iota((tokens, tokens), 1) == source).astype(F32).astype(BF)
    dnat = jnp.dot(pick, dmixed, preferred_element_type=F32).astype(BF)
    out = lax.dot_general(dnat, w_all[...], (((1,), (1,)), ((), ())), preferred_element_type=F32)
    out_ref[...] = out.astype(BF)


def add4(a, b, c, d):
    return (a[...].astype(F32) + b[...].astype(F32)) + (c[...].astype(F32) + d[...].astype(F32))


def lat_sum_kernel(a, b, c, d, z0, z1, z2, z3, loss_ref, total_ref):
    total_ref[...] = add4(a, b, c, d)
    zi = lax.axis_index("dp")
    rows, width = z0.shape
    for k, ref in enumerate((z0, z1, z2, z3)):
        at = pl.multiple_of((zi ^ k) * width, 128)
        ref[...] = total_ref[:, pl.ds(at, width)].astype(BF)
    loss = jnp.sum(total_ref[0:1, 4 * width :], axis=1, keepdims=True)
    loss_ref[...] = jnp.broadcast_to(loss, loss_ref.shape)


def dp_sum_kernel(loss_ref, a, b, c, d, o_ref):
    rows, width = a.shape
    o_ref[0:rows, :] = add4(a, b, c, d).astype(BF)
    block = loss_block(loss_ref[0:1, 0:1], o_ref.shape[0] - rows)
    zeros = jnp.zeros((block.shape[0], width - 128), F32)
    o_ref[rows:, :] = jnp.concatenate([block, zeros], axis=1).astype(BF)


def pair_kernel(mine_ref, other_ref, o_ref):
    rows = mine_ref.shape[0]
    odd = lax.axis_index("lat") % 2
    o_ref[pl.ds(pl.multiple_of(odd * rows, 8), rows), :] = mine_ref[...]
    o_ref[pl.ds(pl.multiple_of((1 - odd) * rows, 8), rows), :] = other_ref[...]


def join_kernel(counts, *refs):
    pieces, (o_ref, loss_ref) = refs[:4], refs[4:]
    chip = lax.axis_index("lat") // 2
    held = pieces[0].shape[0] // 2
    rows = held - 8
    for a in range(2):
        for n in range(2):
            at = pl.multiple_of((2 * (chip ^ a) + n) * rows, 8)
            both = [pieces[2 * a + b][held * n : held * n + rows, :].astype(F32) for b in range(2)]
            o_ref[pl.ds(at, rows), :] = (both[0] + both[1]) / counts[0]
    sums = [
        jnp.sum(p[rows : rows + 1, 0:128].astype(F32), axis=1, keepdims=True) for p in pieces[:2]
    ]
    loss_ref[...] = jnp.broadcast_to((sums[0] + sums[1]) / counts[1], loss_ref.shape)


def swap(array, axis, bit):
    return lax.ppermute(array, axis, [(i, i ^ bit) for i in range(lax.axis_size(axis))])


def shape(dims, dtype):
    return jax.ShapeDtypeStruct(dims, dtype)


def shards(projected, targets, valid_cells, w_out, unpatch_matrix, norm_gain, var_weight):
    dp, lat, lon = lax.axis_size("dp"), lax.axis_size("lat"), lax.axis_size("lon")
    rows, width = w_out.shape
    levels = projected.shape[1]
    span = unpatch_matrix.shape[1]
    tokens = levels * 64
    lat_total = 8 * lat
    angle = math.pi * ((np.arange(lat_total) + 0.5) / lat_total - 0.5)
    cosine = np.cos(angle)
    lat_table = jnp.asarray(np.roll(cosine / cosine.mean(), -4), F32)
    barrier = lax.optimization_barrier

    unpatch_t = unpatch_matrix.T
    payload = pl.pallas_call(
        payload_kernel,
        out_shape=shape((rows // 4 + 16, width), BF),
        in_specs=[HBM, HBM, VMEM],
        out_specs=VMEM,
        scratch_shapes=[pltpu.VMEM((UGROWS, rows), BF), pltpu.SemaphoreType.DMA((2,))],
        compiler_params=params(60),
        name="payload",
    )(w_out, unpatch_t, norm_gain)
    ring1 = from_behind(payload, "dp", 1)
    own, *send = pl.pallas_call(
        pack_kernel,
        out_shape=[shape((n, 3 * width + EXTRA), BF) for n in (64, 64, 64, 64)],
        in_specs=[HBM] * 3,
        out_specs=[VMEM] * 4,
        scratch_shapes=[
            pltpu.VMEM((levels, 8, 8, 3 * width), BF),
            pltpu.VMEM((levels, 8, 8, span), BF),
            pltpu.VMEM((8, 8), jnp.int32),
            pltpu.SemaphoreType.DMA((2 + 3 * width // 512,)),
        ],
        compiler_params=params(50),
        name="pack",
    )(
        projected.reshape(levels, 8, 8, 3 * width),
        targets.reshape(levels, 8, 8, span),
        valid_cells,
    )
    corner = [
        (a * lon + b, ((a - 1) % lat) * lon + (b - 1) % lon) for a in range(lat) for b in range(lon)
    ]
    south = from_behind(send[1], "lat", -1)
    diag = lax.ppermute(send[2], ("lat", "lon"), corner)
    ring2 = from_behind(ring1, "dp", 1)
    across2 = swap(ring2, "lat", 2)
    ring2_after, east, south, diag = barrier((ring2, send[0], south, diag))
    ring3 = from_behind(ring2_after, "dp", 1)
    east = from_behind(east, "lon", -1)
    across3 = from_behind(across2, "dp", 1)
    ring1_late, across2 = barrier((ring1, across2))
    across1 = swap(ring1_late, "lat", 2)
    tiles = [own, east, south, diag]
    *tiles, ring1, across1, ring2 = barrier((*tiles, ring1, across1, ring2))
    ctx = pl.pallas_call(
        attention_kernel,
        out_shape=shape((tokens, width), BF),
        in_specs=[VMEM] * 4,
        out_specs=VMEM,
        compiler_params=params(16),
        name="attention",
    )(*tiles)
    ctx, across3 = barrier((ctx, across3))
    pieces = []
    for ring, across in ((ring1, across1), (ring2, across2), (ring3, across3)):
        pieces += [ring, across, swap(ring, "lat", 1), swap(across, "lat", 1)]

    piece = span // lat
    extra_specs = [
        pl.BlockSpec((t.shape[0], EXTRA), lambda i: (0, 3 * width // EXTRA)) for t in tiles
    ]
    assembly = [
        pltpu.VMEM((dp * rows, width), BF),
        pltpu.VMEM((UGROWS, dp * rows), BF),
    ]
    *terms, normed, inv, dfc = pl.pallas_call(
        forward_kernel,
        grid=(1,),
        out_shape=[shape((piece, width + 128), BF)] * 4
        + [shape((tokens, width), F32), shape((tokens, 128), F32), shape((tokens, span), BF)],
        in_specs=[SMEM] * 2 + [VMEM] + extra_specs + [VMEM] * (3 + PIECES),
        out_specs=[VMEM] * 7,
        scratch_shapes=[pltpu.VMEM((tokens, width), BF)]
        + assembly
        + [pltpu.VMEM((span, width), F32)],
        compiler_params=params(28),
        name="forward",
    )(lat_table, var_weight, ctx, *tiles, w_out, unpatch_t, norm_gain, *pieces)

    terms = [terms[0]] + [swap(terms[b], "lat", b) for b in (1, 2, 3)]
    grad_context = pl.pallas_call(
        backward_kernel,
        out_shape=shape((tokens, width), BF),
        in_specs=[VMEM] * (6 + PIECES),
        out_specs=VMEM,
        scratch_shapes=assembly,
        compiler_params=params(24),
        name="backward",
    )(normed, inv, dfc, w_out, unpatch_t, norm_gain, *pieces)
    *terms, grad_context = barrier((*terms, grad_context))

    *parts, loss = pl.pallas_call(
        lat_sum_kernel,
        out_shape=[shape((piece, rows), BF)] * 4 + [shape((8, 128), F32)],
        in_specs=[VMEM] * 4,
        out_specs=[VMEM] * 5,
        scratch_shapes=[pltpu.VMEM((piece, width + 128), F32)],
        compiler_params=params(4),
        name="lat_sum",
    )(*terms)
    parts = [parts[0]] + [swap(parts[k], "dp", k) for k in (1, 2, 3)]
    mine = pl.pallas_call(
        dp_sum_kernel,
        out_shape=shape((piece + 8, rows), BF),
        in_specs=[VMEM] * 5,
        out_specs=VMEM,
        compiler_params=params(4),
        name="dp_sum",
    )(loss, *parts)
    chip = pl.pallas_call(
        pair_kernel,
        out_shape=shape((2 * piece + 16, rows), BF),
        in_specs=[VMEM] * 2,
        out_specs=VMEM,
        compiler_params=params(4),
        name="pair",
    )(mine, swap(mine, "lat", 1))
    plane = [chip]
    for a, b in ((0, 1), (2, 0), (2, 1)):
        pairs = [(i * lon + j, (i ^ a) * lon + (j ^ b)) for i in range(lat) for j in range(lon)]
        plane.append(lax.ppermute(chip, ("lat", "lon"), pairs))
    count = levels * lat_total * 8 * lon
    counts = (float(count), float(count * (span // var_weight.shape[0])))
    joined, loss = pl.pallas_call(
        lambda *refs: join_kernel(counts, *refs),
        out_shape=[shape((span, rows), F32), shape((1, 1), F32)],
        in_specs=[VMEM] * 4,
        out_specs=[VMEM] * 2,
        compiler_params=params(4),
        name="join",
    )(*plane)
    return grad_context.reshape(1, levels, 8, 8, width), joined.T, loss.reshape(1)


def solution(mesh):
    placed = (
        P("dp", None, "lat", "lon", None),
        P("dp", None, "lat", "lon", None),
        P("lat", "lon"),
        P("dp", None),
        P("dp", None),
        P("dp"),
        P(),
    )
    fits = mesh.shape["dp"] == 4 and mesh.shape["lat"] == 4 and mesh.shape["lon"] == 2

    def program(*arrays):
        body = shards if fits else general_shards
        return jax.shard_map(
            body,
            mesh=mesh,
            in_specs=placed,
            out_specs=(P("dp", None, "lat", "lon", None), P("dp", None), P("dp")),
            check_vma=False,
        )(*arrays)

    return program
```

```python
import functools
import math

import jax
import jax.numpy as jnp
import numpy as np
from jax import lax
from jax.experimental import pallas as pl
from jax.experimental.pallas import tpu as pltpu
from jax.sharding import PartitionSpec as P

HEADS = 48
HDIM = 32
WLEV = 2
BF = jnp.bfloat16
F32 = jnp.float32
EXTRA = 256
UGROWS = 256
PIECES = 12
VMEM = pl.BlockSpec(memory_space=pltpu.VMEM)
SMEM = pl.BlockSpec(memory_space=pltpu.SMEM)
ANY = pl.BlockSpec(memory_space=pl.ANY)
HBM = pl.BlockSpec(memory_space=pltpu.HBM)


def from_behind(array, axis, by):
    length = lax.axis_size(axis)
    return lax.ppermute(array, axis, [(i, (i + by) % length) for i in range(length)])


def general_shards(projected, targets, valid_cells, w_out, unpatch_matrix, norm_gain, var_weight):
    tile_side = projected.shape[2]
    half_side = tile_side // 2
    levels = projected.shape[1]
    model_width = w_out.shape[1]
    predicted_span = unpatch_matrix.shape[1]
    lat_total = tile_side * lax.axis_size("lat")
    lon_total = tile_side * lax.axis_size("lon")
    lat_place = lax.axis_index("lat")
    moved = from_behind(
        (projected[:, :, :, :half_side], targets[:, :, :, :half_side], valid_cells[:, :half_side]),
        "lon",
        -1,
    )
    strip_proj = jnp.concatenate([projected[:, :, :, half_side:], moved[0]], axis=3)
    strip_goal = jnp.concatenate([targets[:, :, :, half_side:], moved[1]], axis=3)
    strip_valid = jnp.concatenate([valid_cells[:, half_side:], moved[2]], axis=1)
    moved_rows = from_behind(
        (strip_proj[:, :, :half_side], strip_goal[:, :, :half_side], strip_valid[:half_side]),
        "lat",
        -1,
    )
    local_proj = jnp.concatenate([strip_proj[:, :, half_side:], moved_rows[0]], axis=2)
    shard_reference = jnp.concatenate([strip_goal[:, :, half_side:], moved_rows[1]], axis=2)
    local_valid = jnp.concatenate([strip_valid[half_side:], moved_rows[2]], axis=0).astype(F32)
    win_count = levels // WLEV
    tokw = WLEV * tile_side * tile_side
    windows = local_proj.reshape(win_count, tokw, 3 * model_width)
    rows_here = lat_place * tile_side + jnp.arange(tile_side)
    region_rows = (rows_here >= lat_total - half_side).astype(jnp.int32)
    region = jnp.broadcast_to(region_rows[None, :, None], (WLEV, tile_side, tile_side)).reshape(-1)
    allowed = region[:, None] == region[None, :]
    queries = windows[..., :model_width].reshape(win_count, tokw, HEADS, -1)
    key_heads = windows[..., model_width : 2 * model_width].reshape(win_count, tokw, HEADS, -1)
    value_heads = windows[..., 2 * model_width :].reshape(win_count, tokw, HEADS, -1)
    scores = jnp.einsum("wqhd,wkhd->whqk", queries, key_heads, preferred_element_type=F32)
    scores = scores * (1.0 / math.sqrt(HDIM))
    scores = jnp.where(allowed[None, None], scores, -1e30)
    row_peak = jnp.max(scores, axis=-1, keepdims=True)
    lifted = jnp.exp(scores - row_peak)
    attn = (lifted / jnp.sum(lifted, axis=-1, keepdims=True)).astype(BF)
    context = jnp.einsum("whqk,wkhd->wqhd", attn, value_heads, preferred_element_type=F32)
    context = context.astype(BF).reshape(win_count * tokw, model_width)
    element_total = win_count * tokw
    out_all, unprojected_pieces, gain_all = (
        lax.all_gather(w_out, "dp", axis=0, tiled=True),
        lax.all_gather(unpatch_matrix, "dp", axis=0, tiled=True),
        lax.all_gather(norm_gain, "dp", axis=0, tiled=True),
    )
    mixed_rows = jnp.dot(context, out_all, preferred_element_type=F32)
    centre = jnp.mean(mixed_rows, axis=-1, keepdims=True)
    spread = jnp.mean((mixed_rows - centre) ** 2, axis=-1, keepdims=True)
    inv_spread = lax.rsqrt(spread + 1e-05)
    normed = (mixed_rows - centre) * inv_spread
    gain_f = gain_all.astype(F32)
    latent_activation = (normed * gain_f).astype(BF)
    prediction_field = jnp.dot(latent_activation, unprojected_pieces, preferred_element_type=F32)
    prediction_misfit = prediction_field - shard_reference.reshape(
        element_total, predicted_span
    ).astype(F32)
    all_rows = jnp.arange(lat_total).astype(F32)
    cosine_mean = jnp.mean(jnp.cos(math.pi * ((all_rows + 0.5) / lat_total - 0.5)))
    initial_rows = ((rows_here + half_side) % lat_total).astype(F32)
    lat_here = jnp.cos(math.pi * ((initial_rows + 0.5) / lat_total - 0.5)) / cosine_mean
    element_factor = jnp.broadcast_to(
        lat_here[None, :, None] * local_valid[None], (levels, tile_side, tile_side)
    ).reshape(element_total, 1)
    variable_factor = jnp.repeat(var_weight, predicted_span // var_weight.shape[0])[None, :]
    shard_penalty = jnp.sum(
        element_factor * variable_factor * prediction_misfit * prediction_misfit
    ) / (levels * lat_total * lon_total * (predicted_span // var_weight.shape[0]))
    prediction_gradient = (2.0 * element_factor * variable_factor * prediction_misfit).astype(BF)
    grad_shard = lax.psum_scatter(
        jnp.einsum(
            "td,to->do", latent_activation, prediction_gradient, preferred_element_type=F32
        ).astype(BF),
        "dp",
        scatter_dimension=0,
        tiled=True,
    ).astype(F32)
    grad_sum, loss_sum = lax.psum((grad_shard, shard_penalty), ("lat", "lon"))
    grad_recovery = grad_sum / (levels * lat_total * lon_total)
    grad_hidden = jnp.einsum(
        "to,do->td", prediction_gradient, unprojected_pieces, preferred_element_type=F32
    )
    scaled_grad = grad_hidden * gain_f
    grad_mixed = inv_spread * (
        scaled_grad
        - jnp.mean(scaled_grad, axis=-1, keepdims=True)
        - normed * jnp.mean(scaled_grad * normed, axis=-1, keepdims=True)
    )
    grad_mixed = grad_mixed.astype(BF)
    grad_context = jnp.einsum("tj,ij->ti", grad_mixed, out_all, preferred_element_type=F32)
    grad_context = grad_context.astype(BF).reshape(1, levels, tile_side, tile_side, model_width)
    return (grad_context, grad_recovery, loss_sum.reshape(1))


def params(mib):
    return pltpu.CompilerParams(vmem_limit_bytes=mib << 20)


def iota(shape, dim):
    return lax.broadcasted_iota(jnp.int32, shape, dim)


def payload_kernel(w_ref, unpatch_ref, gain_ref, payload_ref, ug, sems):
    part = lax.axis_index("lat")
    rows, width = w_ref.shape
    qr = rows // 4
    span = unpatch_ref.shape[0]
    start = pl.multiple_of(part * qr, 32)
    u_copy = pltpu.make_async_copy(unpatch_ref, ug.at[pl.ds(0, span), :], sems.at[0])
    u_copy.start()
    w_copy = pltpu.make_async_copy(
        w_ref.at[pl.ds(start, qr), :], payload_ref.at[pl.ds(0, qr), :], sems.at[1]
    )
    w_copy.start()
    ug[pl.ds(span, 16), :] = gain_rows(gain_ref, rows)
    ug[pl.ds(span + 16, UGROWS - span - 16), :] = jnp.zeros((UGROWS - span - 16, rows), BF)
    u_copy.wait()
    for j in range(4):
        at = pl.multiple_of((4 * part + j) * 16, 16)
        payload_ref[pl.ds(qr, 16), pl.ds(j * rows, rows)] = ug[pl.ds(at, 16), :]
    w_copy.wait()


def gain_rows(gain_ref, rows):
    return jnp.broadcast_to(gain_ref[...].astype(F32).reshape(1, rows), (16, rows)).astype(BF)


def pack_kernel(x_ref, t_ref, valid_ref, *refs):
    outs, (x_in, t_in, v_in, sems) = refs[:4], refs[4:]
    span = t_ref.shape[-1]
    count = x_ref.shape[0] * 64
    quarter = count // 4
    step = 512
    width = x_ref.shape[-1]
    copies = [
        pltpu.make_async_copy(t_ref, t_in, sems.at[0]),
        pltpu.make_async_copy(valid_ref, v_in, sems.at[1]),
    ]
    for at in range(0, width, step):
        lanes = (slice(None),) * 3 + (pl.ds(at, step),)
        copies.append(
            pltpu.make_async_copy(x_ref.at[lanes], x_in.at[lanes], sems.at[len(copies)])
        )
    for c in copies:
        c.start()
    place = iota((count, count), 0)
    quad, rest = place // quarter, place % quarter
    row = (rest // 4) % 4 + jnp.where(quad < 2, 4, 0)
    col = rest % 4 + jnp.where(quad % 2 == 0, 4, 0)
    source = (rest // 16) * 64 + row * 8 + col
    pick = (iota((count, count), 1) == source).astype(F32).astype(BF)
    copies[0].wait()
    copies[1].wait()
    goal = jnp.dot(pick, t_in[...].reshape(count, span), preferred_element_type=F32)
    token = iota((count, 8), 0)
    row_hot = ((token // 8) % 8 == iota((count, 8), 1)).astype(F32)
    by_row = jnp.dot(row_hot, v_in[...].astype(F32), preferred_element_type=F32)
    mine = token % 8 == iota((count, 8), 1)
    natural = jnp.sum(jnp.where(mine, by_row, 0.0), axis=1, keepdims=True)
    spread = jnp.broadcast_to(natural, (count, 128)).astype(BF)
    column = jnp.dot(pick, spread, preferred_element_type=F32)
    extra = jnp.concatenate([goal, column[:, : EXTRA - span]], axis=1).astype(BF)
    starts = [sum(o.shape[0] for o in outs[:n]) for n in range(4)]
    outs = list(zip(outs, starts))
    for ref, row in outs:
        ref[:, width:] = extra[row : row + ref.shape[0]]
    for n, at in enumerate(range(0, width, step)):
        copies[2 + n].wait()
        tokens = x_in[:, :, :, at : at + step].reshape(count, step)
        out = jnp.dot(pick, tokens, preferred_element_type=F32).astype(BF)
        for ref, row in outs:
            ref[:, at : at + step] = out[row : row + ref.shape[0]]


def windows_of(*tiles):
    return [[t.at[32 * w : 32 * w + 32] for t in tiles] for w in range(2)]


def attention_kernel(*refs):
    tiles, ctx_ref = windows_of(*refs[:4]), refs[4]
    part = ctx_ref.shape[1]
    is_last = lax.axis_index("lat") == lax.axis_size("lat") - 1
    same = (iota((512, 128), 0) % 128) // 64 == iota((512, 128), 1) // 64
    bias = jnp.where(jnp.logical_or(same, jnp.logical_not(is_last)), 0.0, -1e30)
    head = iota((128, 128), 1) // HDIM
    factor = math.log2(math.e) / math.sqrt(HDIM)
    for at in range(0, part, 128):
        for w in range(2):
            q, k, v = [
                jnp.concatenate(
                    [t[:, i * part + at : i * part + at + 128] for t in tiles[w]],
                    axis=0,
                )
                for i in range(3)
            ]
            zero = jnp.zeros_like(k)
            k4 = jnp.concatenate([jnp.where(head == h, k, zero) for h in range(4)], axis=0)
            v4 = jnp.concatenate([jnp.where(head == h, v, zero) for h in range(4)], axis=0)
            s = lax.dot_general(k4, q, (((1,), (1,)), ((), ())), preferred_element_type=F32)
            s = s + bias
            parts = []
            for h in range(4):
                sh = s[128 * h : 128 * h + 128]
                e = jnp.exp2((sh - jnp.max(sh, axis=0, keepdims=True)) * factor)
                parts.append((e * (1.0 / jnp.sum(e, axis=0, keepdims=True))).astype(BF))
            attn = jnp.concatenate(parts, axis=0)
            out = lax.dot_general(attn, v4, (((0,), (0,)), ((), ())), preferred_element_type=F32)
            ctx_ref[128 * w : 128 * w + 128, at : at + 128] = out.astype(BF)


def assemble(own_w, own_u, own_gain, pieces, w_all, ug_all):
    zi, part = lax.axis_index("dp"), lax.axis_index("lat")
    rows = own_w.shape[0]
    qr = rows // 4
    steps = len(pieces) // 4 + 1
    base = pl.multiple_of(zi * rows, 128)
    w_all[pl.ds(base, rows), :] = own_w[...]
    span = own_u.shape[0]
    ug_all[0:span, pl.ds(base, rows)] = own_u[...]
    ug_all[span : span + 16, pl.ds(base, rows)] = gain_rows(own_gain, rows)
    for k in range(1, steps):
        shard = lax.rem(zi - k + steps, steps)
        base = pl.multiple_of(shard * rows, 128)
        for bits, piece in zip((0, 2, 1, 3), pieces[4 * k - 4 : 4 * k]):
            from_part = part ^ bits
            row = pl.multiple_of(base + from_part * qr, 32)
            w_all[pl.ds(row, qr), :] = piece[0:qr, :]
            for j in range(4):
                urow = pl.multiple_of((4 * from_part + j) * 16, 16)
                ug_all[pl.ds(urow, 16), pl.ds(base, rows)] = piece[
                    qr : qr + 16, j * rows : (j + 1) * rows
                ]


def split3(x):
    hi = x.astype(BF).astype(F32)
    mid = (x - hi).astype(BF).astype(F32)
    return hi, mid, x - hi - mid


def loss_block(value, rows):
    hi, mid, lo = split3(value)
    lane = iota((rows, 128), 1)
    return jnp.where(lane == 0, hi, jnp.where(lane == 1, mid, jnp.where(lane == 2, lo, 0.0)))


def forward_kernel(lat_ref, var_ref, *refs):
    ctx_ref, refs = refs[0], refs[1:]
    extras, refs = refs[:4], refs[4:]
    owned, refs = refs[:3], refs[3:]
    pieces, refs = refs[:PIECES], refs[PIECES:]
    ts, refs = refs[:4], refs[4:]
    normed_ref, inv_ref, dfc_ref, loss_ref, hidden_ref, w_all, ug_all, term = refs
    lat_place = lax.axis_index("lat")
    assemble(*owned, pieces, w_all, ug_all)
    tokens, width = normed_ref.shape
    span = dfc_ref.shape[1]
    extra = jnp.concatenate([t[...] for tiles in windows_of(*extras) for t in tiles], axis=0)
    extra = extra.astype(F32)
    goal, valid = extra[:, :span], extra[:, span : span + 1]
    token = iota((tokens, 1), 0)
    row = (token // 4) % 4 + jnp.where((token // 32) % 4 >= 2, 4, 0)
    lat_w = jnp.zeros((tokens, 1), F32)
    for r in range(8):
        lat_w = jnp.where(row == r, lat_ref[lat_place * 8 + r], lat_w)
    lane = iota((1, span), 1) // (span // var_ref.shape[0])
    var_w = jnp.zeros((1, span), F32)
    for n in range(var_ref.shape[0]):
        var_w = jnp.where(lane == n, var_ref[n], var_w)
    weight = lat_w * valid * var_w
    mixed = jnp.dot(ctx_ref[...], w_all[...], preferred_element_type=F32)
    centre = jnp.mean(mixed, axis=-1, keepdims=True)
    off = mixed - centre
    inv = lax.rsqrt(jnp.mean(off * off, axis=-1, keepdims=True) + 1e-05)
    normed = off * inv
    normed_ref[...] = normed
    inv_ref[...] = jnp.broadcast_to(inv, inv_ref.shape)
    gain = ug_all[pl.ds(span, 16), :][0:1].astype(F32)
    hidden_ref[...] = (normed * gain).astype(BF)
    field = lax.dot_general(
        hidden_ref[...], ug_all[0:span, :], (((1,), (1,)), ((), ())), preferred_element_type=F32
    )
    misfit = field - goal
    dfc = (2.0 * weight * misfit).astype(BF)
    dfc_ref[...] = dfc
    term[...] = lax.dot_general(
        dfc, hidden_ref[...], (((0,), (0,)), ((), ())), preferred_element_type=F32
    )
    loss = jnp.sum(jnp.sum(weight * misfit * misfit, axis=1, keepdims=True), axis=0, keepdims=True)
    loss_ref[...] = jnp.broadcast_to(loss, loss_ref.shape)
    rows = ts[0].shape[0]
    for b, ref in enumerate(ts):
        at = pl.multiple_of((lat_place ^ b) * rows, 8)
        ref[...] = term[pl.ds(at, rows), :].astype(BF)


def backward_kernel(normed_ref, inv_ref, dfc_ref, *refs):
    owned, refs = refs[:3], refs[3:]
    pieces, (out_ref, w_all, ug_all) = refs[:PIECES], refs[PIECES:]
    assemble(*owned, pieces, w_all, ug_all)
    tokens, width = normed_ref.shape
    span = dfc_ref.shape[1]
    gain = ug_all[pl.ds(span, 16), :][0:1].astype(F32)
    g = jnp.dot(dfc_ref[...], ug_all[0:span, :], preferred_element_type=F32) * gain
    normed = normed_ref[...]
    mean_g = jnp.mean(g, axis=-1, keepdims=True)
    mean_gn = jnp.mean(g * normed, axis=-1, keepdims=True)
    dmixed = ((g - mean_g - normed * mean_gn) * inv_ref[:, 0:1]).astype(BF)
    place = iota((tokens, tokens), 0)
    row, col, level = (place // 8) % 8, place % 8, place // 64
    quad = jnp.where(row >= 4, 2, 0) + jnp.where(col >= 4, 1, 0)
    source = (level // 2) * 128 + quad * 32 + (level % 2) * 16 + (row % 4) * 4 + col % 4
    pick = (iota((tokens, tokens), 1) == source).astype(F32).astype(BF)
    dnat = jnp.dot(pick, dmixed, preferred_element_type=F32).astype(BF)
    out = lax.dot_general(dnat, w_all[...], (((1,), (1,)), ((), ())), preferred_element_type=F32)
    out_ref[...] = out.astype(BF)


def add4(a, b, c, d):
    return (a[...].astype(F32) + b[...].astype(F32)) + (c[...].astype(F32) + d[...].astype(F32))


def lat_sum_kernel(a, b, c, d, z0, z1, z2, z3, total_ref):
    total_ref[...] = add4(a, b, c, d)
    zi = lax.axis_index("dp")
    width = z0.shape[1]
    for k, ref in enumerate((z0, z1, z2, z3)):
        at = pl.multiple_of((zi ^ k) * width, 128)
        ref[...] = total_ref[:, pl.ds(at, width)].astype(BF)


def dp_sum_kernel(loss_ref, a, b, c, d, o_ref):
    rows, width = a.shape
    o_ref[0:rows, :] = add4(a, b, c, d).astype(BF)
    block = loss_block(loss_ref[0:1, 0:1], o_ref.shape[0] - rows)
    zeros = jnp.zeros((block.shape[0], width - 128), F32)
    o_ref[rows:, :] = jnp.concatenate([block, zeros], axis=1).astype(BF)


def pair_kernel(mine_ref, other_ref, o_ref):
    rows = mine_ref.shape[0]
    odd = lax.axis_index("lat") % 2
    o_ref[pl.ds(pl.multiple_of(odd * rows, 8), rows), :] = mine_ref[...]
    o_ref[pl.ds(pl.multiple_of((1 - odd) * rows, 8), rows), :] = other_ref[...]


def join_kernel(counts, *refs):
    pieces, (o_ref, loss_ref) = refs[:4], refs[4:]
    chip = lax.axis_index("lat") // 2
    held = pieces[0].shape[0] // 2
    rows = held - 8
    for a in range(2):
        for n in range(2):
            at = pl.multiple_of((2 * (chip ^ a) + n) * rows, 8)
            both = [pieces[2 * a + b][held * n : held * n + rows, :].astype(F32) for b in range(2)]
            o_ref[pl.ds(at, rows), :] = (both[0] + both[1]) / counts[0]
    def part(p, n):
        return jnp.sum(p[held * n + rows : held * n + rows + 1, 0:128].astype(F32), axis=1, keepdims=True)

    chips = [part(p, 0) + part(p, 1) for p in pieces]
    loss = (chips[0] + chips[1]) + (chips[2] + chips[3])
    loss_ref[...] = jnp.broadcast_to(loss / counts[1], loss_ref.shape)


def swap(array, axis, bit):
    return lax.ppermute(array, axis, [(i, i ^ bit) for i in range(lax.axis_size(axis))])


def shape(dims, dtype):
    return jax.ShapeDtypeStruct(dims, dtype)


def shards(projected, targets, valid_cells, w_out, unpatch_matrix, norm_gain, var_weight):
    dp, lat, lon = lax.axis_size("dp"), lax.axis_size("lat"), lax.axis_size("lon")
    rows, width = w_out.shape
    levels = projected.shape[1]
    span = unpatch_matrix.shape[1]
    tokens = levels * 64
    lat_total = 8 * lat
    angle = math.pi * ((np.arange(lat_total) + 0.5) / lat_total - 0.5)
    cosine = np.cos(angle)
    lat_table = jnp.asarray(np.roll(cosine / cosine.mean(), -4), F32)
    barrier = lax.optimization_barrier

    unpatch_t = unpatch_matrix.T
    payload = pl.pallas_call(
        payload_kernel,
        out_shape=shape((rows // 4 + 16, width), BF),
        in_specs=[HBM, HBM, VMEM],
        out_specs=VMEM,
        scratch_shapes=[pltpu.VMEM((UGROWS, rows), BF), pltpu.SemaphoreType.DMA((2,))],
        compiler_params=params(60),
        name="payload",
    )(w_out, unpatch_t, norm_gain)
    ring1 = from_behind(payload, "dp", 1)
    own, *send = pl.pallas_call(
        pack_kernel,
        out_shape=[shape((n, 3 * width + EXTRA), BF) for n in (64, 64, 64, 64)],
        in_specs=[HBM] * 3,
        out_specs=[VMEM] * 4,
        scratch_shapes=[
            pltpu.VMEM((levels, 8, 8, 3 * width), BF),
            pltpu.VMEM((levels, 8, 8, span), BF),
            pltpu.VMEM((8, 8), jnp.int32),
            pltpu.SemaphoreType.DMA((2 + 3 * width // 512,)),
        ],
        compiler_params=params(50),
        name="pack",
    )(
        projected.reshape(levels, 8, 8, 3 * width),
        targets.reshape(levels, 8, 8, span),
        valid_cells,
    )
    corner = [
        (a * lon + b, ((a - 1) % lat) * lon + (b - 1) % lon) for a in range(lat) for b in range(lon)
    ]
    south = from_behind(send[1], "lat", -1)
    diag = lax.ppermute(send[2], ("lat", "lon"), corner)
    ring2 = from_behind(ring1, "dp", 1)
    across2 = swap(ring2, "lat", 2)
    ring2_after, east, south, diag = barrier((ring2, send[0], south, diag))
    ring3 = from_behind(ring2_after, "dp", 1)
    east = from_behind(east, "lon", -1)
    across3 = from_behind(across2, "dp", 1)
    ring1_late, across2 = barrier((ring1, across2))
    across1 = swap(ring1_late, "lat", 2)
    tiles = [own, east, south, diag]
    across2_swapped = swap(across2, "lat", 1)
    *tiles, ring1, across1, ring2, across2_swapped = barrier(
        (*tiles, ring1, across1, ring2, across2_swapped)
    )
    ctx = pl.pallas_call(
        attention_kernel,
        out_shape=shape((tokens, width), BF),
        in_specs=[VMEM] * 4,
        out_specs=VMEM,
        compiler_params=params(16),
        name="attention",
    )(*tiles)
    ctx, across3 = barrier((ctx, across3))
    pieces = [ring1, across1, swap(ring1, "lat", 1), swap(across1, "lat", 1)]
    pieces += [ring2, across2, swap(ring2, "lat", 1), across2_swapped]
    pieces += [ring3, across3, swap(ring3, "lat", 1), swap(across3, "lat", 1)]

    piece = span // lat
    extra_specs = [
        pl.BlockSpec((t.shape[0], EXTRA), lambda i: (0, 3 * width // EXTRA)) for t in tiles
    ]
    assembly = [
        pltpu.VMEM((dp * rows, width), BF),
        pltpu.VMEM((UGROWS, dp * rows), BF),
    ]
    *terms, normed, inv, dfc, loss = pl.pallas_call(
        forward_kernel,
        grid=(1,),
        out_shape=[shape((piece, width), BF)] * 4
        + [shape((tokens, width), F32), shape((tokens, 128), F32), shape((tokens, span), BF)]
        + [shape((8, 128), F32)],
        in_specs=[SMEM] * 2 + [VMEM] + extra_specs + [VMEM] * (3 + PIECES),
        out_specs=[VMEM] * 8,
        scratch_shapes=[pltpu.VMEM((tokens, width), BF)]
        + assembly
        + [pltpu.VMEM((span, width), F32)],
        compiler_params=params(28),
        name="forward",
    )(lat_table, var_weight, ctx, *tiles, w_out, unpatch_t, norm_gain, *pieces)

    terms = [terms[0]] + [swap(terms[b], "lat", b) for b in (1, 2, 3)]
    grad_context = pl.pallas_call(
        backward_kernel,
        out_shape=shape((tokens, width), BF),
        in_specs=[VMEM] * (6 + PIECES),
        out_specs=VMEM,
        scratch_shapes=assembly,
        compiler_params=params(24),
        name="backward",
    )(normed, inv, dfc, w_out, unpatch_t, norm_gain, *pieces)
    *terms, grad_context = barrier((*terms, grad_context))

    parts = pl.pallas_call(
        lat_sum_kernel,
        out_shape=[shape((piece, rows), BF)] * 4,
        in_specs=[VMEM] * 4,
        out_specs=[VMEM] * 4,
        scratch_shapes=[pltpu.VMEM((piece, width), F32)],
        compiler_params=params(4),
        name="lat_sum",
    )(*terms)
    parts = [parts[0]] + [swap(parts[k], "dp", k) for k in (1, 2, 3)]
    mine = pl.pallas_call(
        dp_sum_kernel,
        out_shape=shape((piece + 8, rows), BF),
        in_specs=[VMEM] * 5,
        out_specs=VMEM,
        compiler_params=params(4),
        name="dp_sum",
    )(loss, *parts)
    chip = pl.pallas_call(
        pair_kernel,
        out_shape=shape((2 * piece + 16, rows), BF),
        in_specs=[VMEM] * 2,
        out_specs=VMEM,
        compiler_params=params(4),
        name="pair",
    )(mine, swap(mine, "lat", 1))
    plane = [chip]
    for a, b in ((0, 1), (2, 0), (2, 1)):
        pairs = [(i * lon + j, (i ^ a) * lon + (j ^ b)) for i in range(lat) for j in range(lon)]
        plane.append(lax.ppermute(chip, ("lat", "lon"), pairs))
    count = levels * lat_total * 8 * lon
    counts = (float(count), float(count * (span // var_weight.shape[0])))
    joined, loss = pl.pallas_call(
        lambda *refs: join_kernel(counts, *refs),
        out_shape=[shape((span, rows), F32), shape((1, 1), F32)],
        in_specs=[VMEM] * 4,
        out_specs=[VMEM] * 2,
        compiler_params=params(4),
        name="join",
    )(*plane)
    return grad_context.reshape(1, levels, 8, 8, width), joined.T, loss.reshape(1)


def solution(mesh):
    placed = (
        P("dp", None, "lat", "lon", None),
        P("dp", None, "lat", "lon", None),
        P("lat", "lon"),
        P("dp", None),
        P("dp", None),
        P("dp"),
        P(),
    )
    fits = mesh.shape["dp"] == 4 and mesh.shape["lat"] == 4 and mesh.shape["lon"] == 2

    def program(*arrays):
        body = shards if fits else general_shards
        return jax.shard_map(
            body,
            mesh=mesh,
            in_specs=placed,
            out_specs=(P("dp", None, "lat", "lon", None), P("dp", None), P("dp")),
            check_vma=False,
        )(*arrays)

    return program
```

```python
import functools
import math

import jax
import jax.numpy as jnp
import numpy as np
from jax import lax
from jax.experimental import pallas as pl
from jax.experimental.pallas import tpu as pltpu
from jax.sharding import PartitionSpec as P

HEADS = 48
HDIM = 32
WLEV = 2
BF = jnp.bfloat16
F32 = jnp.float32
EXTRA = 256
UGROWS = 256
PIECES = 12
VMEM = pl.BlockSpec(memory_space=pltpu.VMEM)
SMEM = pl.BlockSpec(memory_space=pltpu.SMEM)
ANY = pl.BlockSpec(memory_space=pl.ANY)
HBM = pl.BlockSpec(memory_space=pltpu.HBM)


def from_behind(array, axis, by):
    length = lax.axis_size(axis)
    return lax.ppermute(array, axis, [(i, (i + by) % length) for i in range(length)])


def general_shards(projected, targets, valid_cells, w_out, unpatch_matrix, norm_gain, var_weight):
    tile_side = projected.shape[2]
    half_side = tile_side // 2
    levels = projected.shape[1]
    model_width = w_out.shape[1]
    predicted_span = unpatch_matrix.shape[1]
    lat_total = tile_side * lax.axis_size("lat")
    lon_total = tile_side * lax.axis_size("lon")
    lat_place = lax.axis_index("lat")
    moved = from_behind(
        (projected[:, :, :, :half_side], targets[:, :, :, :half_side], valid_cells[:, :half_side]),
        "lon",
        -1,
    )
    strip_proj = jnp.concatenate([projected[:, :, :, half_side:], moved[0]], axis=3)
    strip_goal = jnp.concatenate([targets[:, :, :, half_side:], moved[1]], axis=3)
    strip_valid = jnp.concatenate([valid_cells[:, half_side:], moved[2]], axis=1)
    moved_rows = from_behind(
        (strip_proj[:, :, :half_side], strip_goal[:, :, :half_side], strip_valid[:half_side]),
        "lat",
        -1,
    )
    local_proj = jnp.concatenate([strip_proj[:, :, half_side:], moved_rows[0]], axis=2)
    shard_reference = jnp.concatenate([strip_goal[:, :, half_side:], moved_rows[1]], axis=2)
    local_valid = jnp.concatenate([strip_valid[half_side:], moved_rows[2]], axis=0).astype(F32)
    win_count = levels // WLEV
    tokw = WLEV * tile_side * tile_side
    windows = local_proj.reshape(win_count, tokw, 3 * model_width)
    rows_here = lat_place * tile_side + jnp.arange(tile_side)
    region_rows = (rows_here >= lat_total - half_side).astype(jnp.int32)
    region = jnp.broadcast_to(region_rows[None, :, None], (WLEV, tile_side, tile_side)).reshape(-1)
    allowed = region[:, None] == region[None, :]
    queries = windows[..., :model_width].reshape(win_count, tokw, HEADS, -1)
    key_heads = windows[..., model_width : 2 * model_width].reshape(win_count, tokw, HEADS, -1)
    value_heads = windows[..., 2 * model_width :].reshape(win_count, tokw, HEADS, -1)
    scores = jnp.einsum("wqhd,wkhd->whqk", queries, key_heads, preferred_element_type=F32)
    scores = scores * (1.0 / math.sqrt(HDIM))
    scores = jnp.where(allowed[None, None], scores, -1e30)
    row_peak = jnp.max(scores, axis=-1, keepdims=True)
    lifted = jnp.exp(scores - row_peak)
    attn = (lifted / jnp.sum(lifted, axis=-1, keepdims=True)).astype(BF)
    context = jnp.einsum("whqk,wkhd->wqhd", attn, value_heads, preferred_element_type=F32)
    context = context.astype(BF).reshape(win_count * tokw, model_width)
    element_total = win_count * tokw
    out_all, unprojected_pieces, gain_all = (
        lax.all_gather(w_out, "dp", axis=0, tiled=True),
        lax.all_gather(unpatch_matrix, "dp", axis=0, tiled=True),
        lax.all_gather(norm_gain, "dp", axis=0, tiled=True),
    )
    mixed_rows = jnp.dot(context, out_all, preferred_element_type=F32)
    centre = jnp.mean(mixed_rows, axis=-1, keepdims=True)
    spread = jnp.mean((mixed_rows - centre) ** 2, axis=-1, keepdims=True)
    inv_spread = lax.rsqrt(spread + 1e-05)
    normed = (mixed_rows - centre) * inv_spread
    gain_f = gain_all.astype(F32)
    latent_activation = (normed * gain_f).astype(BF)
    prediction_field = jnp.dot(latent_activation, unprojected_pieces, preferred_element_type=F32)
    prediction_misfit = prediction_field - shard_reference.reshape(
        element_total, predicted_span
    ).astype(F32)
    all_rows = jnp.arange(lat_total).astype(F32)
    cosine_mean = jnp.mean(jnp.cos(math.pi * ((all_rows + 0.5) / lat_total - 0.5)))
    initial_rows = ((rows_here + half_side) % lat_total).astype(F32)
    lat_here = jnp.cos(math.pi * ((initial_rows + 0.5) / lat_total - 0.5)) / cosine_mean
    element_factor = jnp.broadcast_to(
        lat_here[None, :, None] * local_valid[None], (levels, tile_side, tile_side)
    ).reshape(element_total, 1)
    variable_factor = jnp.repeat(var_weight, predicted_span // var_weight.shape[0])[None, :]
    shard_penalty = jnp.sum(
        element_factor * variable_factor * prediction_misfit * prediction_misfit
    ) / (levels * lat_total * lon_total * (predicted_span // var_weight.shape[0]))
    prediction_gradient = (2.0 * element_factor * variable_factor * prediction_misfit).astype(BF)
    grad_shard = lax.psum_scatter(
        jnp.einsum(
            "td,to->do", latent_activation, prediction_gradient, preferred_element_type=F32
        ).astype(BF),
        "dp",
        scatter_dimension=0,
        tiled=True,
    ).astype(F32)
    grad_sum, loss_sum = lax.psum((grad_shard, shard_penalty), ("lat", "lon"))
    grad_recovery = grad_sum / (levels * lat_total * lon_total)
    grad_hidden = jnp.einsum(
        "to,do->td", prediction_gradient, unprojected_pieces, preferred_element_type=F32
    )
    scaled_grad = grad_hidden * gain_f
    grad_mixed = inv_spread * (
        scaled_grad
        - jnp.mean(scaled_grad, axis=-1, keepdims=True)
        - normed * jnp.mean(scaled_grad * normed, axis=-1, keepdims=True)
    )
    grad_mixed = grad_mixed.astype(BF)
    grad_context = jnp.einsum("tj,ij->ti", grad_mixed, out_all, preferred_element_type=F32)
    grad_context = grad_context.astype(BF).reshape(1, levels, tile_side, tile_side, model_width)
    return (grad_context, grad_recovery, loss_sum.reshape(1))


def params(mib):
    return pltpu.CompilerParams(vmem_limit_bytes=mib << 20)


def iota(shape, dim):
    return lax.broadcasted_iota(jnp.int32, shape, dim)


def payload_kernel(w_ref, unpatch_ref, gain_ref, payload_ref, ug, sems):
    part = lax.axis_index("lat")
    rows, width = w_ref.shape
    qr = rows // 4
    span = unpatch_ref.shape[0]
    start = pl.multiple_of(part * qr, 32)
    u_copy = pltpu.make_async_copy(unpatch_ref, ug.at[pl.ds(0, span), :], sems.at[0])
    u_copy.start()
    w_copy = pltpu.make_async_copy(
        w_ref.at[pl.ds(start, qr), :], payload_ref.at[pl.ds(0, qr), :], sems.at[1]
    )
    w_copy.start()
    ug[pl.ds(span, 16), :] = gain_rows(gain_ref, rows)
    ug[pl.ds(span + 16, UGROWS - span - 16), :] = jnp.zeros((UGROWS - span - 16, rows), BF)
    u_copy.wait()
    for j in range(4):
        at = pl.multiple_of((4 * part + j) * 16, 16)
        payload_ref[pl.ds(qr, 16), pl.ds(j * rows, rows)] = ug[pl.ds(at, 16), :]
    w_copy.wait()


def gain_rows(gain_ref, rows):
    return jnp.broadcast_to(gain_ref[...].astype(F32).reshape(1, rows), (16, rows)).astype(BF)


def pack_kernel(x_ref, t_ref, valid_ref, *refs):
    outs, (x_in, t_in, v_in, sems) = refs[:4], refs[4:]
    span = t_ref.shape[-1]
    count = x_ref.shape[0] * 64
    quarter = count // 4
    step = 512
    width = x_ref.shape[-1]
    copies = [
        pltpu.make_async_copy(t_ref, t_in, sems.at[0]),
        pltpu.make_async_copy(valid_ref, v_in, sems.at[1]),
    ]
    for at in range(0, width, step):
        lanes = (slice(None),) * 3 + (pl.ds(at, step),)
        copies.append(
            pltpu.make_async_copy(x_ref.at[lanes], x_in.at[lanes], sems.at[len(copies)])
        )
    for c in copies:
        c.start()
    place = iota((count, count), 0)
    quad, rest = place // quarter, place % quarter
    row = (rest // 4) % 4 + jnp.where(quad < 2, 4, 0)
    col = rest % 4 + jnp.where(quad % 2 == 0, 4, 0)
    source = (rest // 16) * 64 + row * 8 + col
    pick = (iota((count, count), 1) == source).astype(F32).astype(BF)
    copies[0].wait()
    copies[1].wait()
    goal = jnp.dot(pick, t_in[...].reshape(count, span), preferred_element_type=F32)
    token = iota((count, 8), 0)
    row_hot = ((token // 8) % 8 == iota((count, 8), 1)).astype(F32)
    by_row = jnp.dot(row_hot, v_in[...].astype(F32), preferred_element_type=F32)
    mine = token % 8 == iota((count, 8), 1)
    natural = jnp.sum(jnp.where(mine, by_row, 0.0), axis=1, keepdims=True)
    spread = jnp.broadcast_to(natural, (count, 128)).astype(BF)
    column = jnp.dot(pick, spread, preferred_element_type=F32)
    extra = jnp.concatenate([goal, column[:, : EXTRA - span]], axis=1).astype(BF)
    starts = [sum(o.shape[0] for o in outs[:n]) for n in range(4)]
    outs = list(zip(outs, starts))
    for ref, row in outs:
        ref[:, width:] = extra[row : row + ref.shape[0]]
    for n, at in enumerate(range(0, width, step)):
        copies[2 + n].wait()
        tokens = x_in[:, :, :, at : at + step].reshape(count, step)
        out = jnp.dot(pick, tokens, preferred_element_type=F32).astype(BF)
        for ref, row in outs:
            ref[:, at : at + step] = out[row : row + ref.shape[0]]


def windows_of(*tiles):
    return [[t.at[32 * w : 32 * w + 32] for t in tiles] for w in range(2)]


def attention_kernel(*refs):
    tiles, ctx_ref = windows_of(*refs[:4]), refs[4]
    part = ctx_ref.shape[1]
    is_last = lax.axis_index("lat") == lax.axis_size("lat") - 1
    same = (iota((512, 128), 0) % 128) // 64 == iota((512, 128), 1) // 64
    bias = jnp.where(jnp.logical_or(same, jnp.logical_not(is_last)), 0.0, -1e30)
    head = iota((128, 128), 1) // HDIM
    factor = math.log2(math.e) / math.sqrt(HDIM)
    for at in range(0, part, 128):
        for w in range(2):
            q, k, v = [
                jnp.concatenate(
                    [t[:, i * part + at : i * part + at + 128] for t in tiles[w]],
                    axis=0,
                )
                for i in range(3)
            ]
            zero = jnp.zeros_like(k)
            k4 = jnp.concatenate([jnp.where(head == h, k, zero) for h in range(4)], axis=0)
            v4 = jnp.concatenate([jnp.where(head == h, v, zero) for h in range(4)], axis=0)
            s = lax.dot_general(k4, q, (((1,), (1,)), ((), ())), preferred_element_type=F32)
            s = s + bias
            parts = []
            for h in range(4):
                sh = s[128 * h : 128 * h + 128]
                e = jnp.exp2((sh - jnp.max(sh, axis=0, keepdims=True)) * factor)
                parts.append((e * (1.0 / jnp.sum(e, axis=0, keepdims=True))).astype(BF))
            attn = jnp.concatenate(parts, axis=0)
            out = lax.dot_general(attn, v4, (((0,), (0,)), ((), ())), preferred_element_type=F32)
            ctx_ref[128 * w : 128 * w + 128, at : at + 128] = out.astype(BF)


def assemble(own_w, own_u, own_gain, pieces, w_all, ug_all):
    zi, part = lax.axis_index("dp"), lax.axis_index("lat")
    rows = own_w.shape[0]
    qr = rows // 4
    steps = len(pieces) // 4 + 1
    base = pl.multiple_of(zi * rows, 128)
    w_all[pl.ds(base, rows), :] = own_w[...]
    span = own_u.shape[0]
    ug_all[0:span, pl.ds(base, rows)] = own_u[...]
    ug_all[span : span + 16, pl.ds(base, rows)] = gain_rows(own_gain, rows)
    for k in range(1, steps):
        shard = lax.rem(zi - k + steps, steps)
        base = pl.multiple_of(shard * rows, 128)
        for bits, piece in zip((0, 2, 1, 3), pieces[4 * k - 4 : 4 * k]):
            from_part = part ^ bits
            row = pl.multiple_of(base + from_part * qr, 32)
            w_all[pl.ds(row, qr), :] = piece[0:qr, :]
            for j in range(4):
                urow = pl.multiple_of((4 * from_part + j) * 16, 16)
                ug_all[pl.ds(urow, 16), pl.ds(base, rows)] = piece[
                    qr : qr + 16, j * rows : (j + 1) * rows
                ]


def split3(x):
    hi = x.astype(BF).astype(F32)
    mid = (x - hi).astype(BF).astype(F32)
    return hi, mid, x - hi - mid


def loss_block(value, rows):
    hi, mid, lo = split3(value)
    lane = iota((rows, 128), 1)
    return jnp.where(lane == 0, hi, jnp.where(lane == 1, mid, jnp.where(lane == 2, lo, 0.0)))


def forward_kernel(lat_ref, var_ref, *refs):
    ctx_ref, refs = refs[0], refs[1:]
    extras, refs = refs[:4], refs[4:]
    owned, refs = refs[:3], refs[3:]
    pieces, refs = refs[:PIECES], refs[PIECES:]
    ts, refs = refs[:4], refs[4:]
    normed_ref, inv_ref, dfc_ref, loss_ref, hidden_ref, w_all, ug_all, term = refs
    lat_place = lax.axis_index("lat")
    assemble(*owned, pieces, w_all, ug_all)
    tokens, width = normed_ref.shape
    span = dfc_ref.shape[1]
    extra = jnp.concatenate([t[...] for tiles in windows_of(*extras) for t in tiles], axis=0)
    extra = extra.astype(F32)
    goal, valid = extra[:, :span], extra[:, span : span + 1]
    token = iota((tokens, 1), 0)
    row = (token // 4) % 4 + jnp.where((token // 32) % 4 >= 2, 4, 0)
    lat_w = jnp.zeros((tokens, 1), F32)
    for r in range(8):
        lat_w = jnp.where(row == r, lat_ref[lat_place * 8 + r], lat_w)
    lane = iota((1, span), 1) // (span // var_ref.shape[0])
    var_w = jnp.zeros((1, span), F32)
    for n in range(var_ref.shape[0]):
        var_w = jnp.where(lane == n, var_ref[n], var_w)
    weight = lat_w * valid * var_w
    mixed = jnp.dot(ctx_ref[...], w_all[...], preferred_element_type=F32)
    centre = jnp.mean(mixed, axis=-1, keepdims=True)
    off = mixed - centre
    inv = lax.rsqrt(jnp.mean(off * off, axis=-1, keepdims=True) + 1e-05)
    normed = off * inv
    normed_ref[...] = normed
    inv_ref[...] = jnp.broadcast_to(inv, inv_ref.shape)
    gain = ug_all[pl.ds(span, 16), :][0:1].astype(F32)
    hidden_ref[...] = (normed * gain).astype(BF)
    field = lax.dot_general(
        hidden_ref[...], ug_all[0:span, :], (((1,), (1,)), ((), ())), preferred_element_type=F32
    )
    misfit = field - goal
    dfc = (2.0 * weight * misfit).astype(BF)
    dfc_ref[...] = dfc
    term[...] = lax.dot_general(
        dfc, hidden_ref[...], (((0,), (0,)), ((), ())), preferred_element_type=F32
    )
    loss = jnp.sum(jnp.sum(weight * misfit * misfit, axis=1, keepdims=True), axis=0, keepdims=True)
    loss_ref[...] = jnp.broadcast_to(loss, loss_ref.shape)
    rows = ts[0].shape[0]
    for b, ref in enumerate(ts):
        at = pl.multiple_of((lat_place ^ b) * rows, 8)
        ref[...] = term[pl.ds(at, rows), :].astype(BF)


def backward_kernel(normed_ref, inv_ref, dfc_ref, *refs):
    owned, refs = refs[:3], refs[3:]
    pieces, (out_ref, w_all, ug_all) = refs[:PIECES], refs[PIECES:]
    assemble(*owned, pieces, w_all, ug_all)
    tokens, width = normed_ref.shape
    span = dfc_ref.shape[1]
    gain = ug_all[pl.ds(span, 16), :][0:1].astype(F32)
    g = jnp.dot(dfc_ref[...], ug_all[0:span, :], preferred_element_type=F32) * gain
    normed = normed_ref[...]
    mean_g = jnp.mean(g, axis=-1, keepdims=True)
    mean_gn = jnp.mean(g * normed, axis=-1, keepdims=True)
    dmixed = ((g - mean_g - normed * mean_gn) * inv_ref[:, 0:1]).astype(BF)
    place = iota((tokens, tokens), 0)
    row, col, level = (place // 8) % 8, place % 8, place // 64
    quad = jnp.where(row >= 4, 2, 0) + jnp.where(col >= 4, 1, 0)
    source = (level // 2) * 128 + quad * 32 + (level % 2) * 16 + (row % 4) * 4 + col % 4
    pick = (iota((tokens, tokens), 1) == source).astype(F32).astype(BF)
    dnat = jnp.dot(pick, dmixed, preferred_element_type=F32).astype(BF)
    out = lax.dot_general(dnat, w_all[...], (((1,), (1,)), ((), ())), preferred_element_type=F32)
    out_ref[...] = out.astype(BF)


def add4(a, b, c, d):
    return (a[...].astype(F32) + b[...].astype(F32)) + (c[...].astype(F32) + d[...].astype(F32))


def lat_sum_kernel(a, b, c, d, z0, z1, z2, z3, total_ref):
    total_ref[...] = add4(a, b, c, d)
    zi = lax.axis_index("dp")
    width = z0.shape[1]
    for k, ref in enumerate((z0, z1, z2, z3)):
        at = pl.multiple_of((zi ^ k) * width, 128)
        ref[...] = total_ref[:, pl.ds(at, width)].astype(BF)


def dp_sum_kernel(loss_ref, a, b, c, d, o_ref):
    rows, width = a.shape
    o_ref[0:rows, :] = add4(a, b, c, d).astype(BF)
    block = loss_block(loss_ref[0:1, 0:1], o_ref.shape[0] - rows)
    zeros = jnp.zeros((block.shape[0], width - 128), F32)
    o_ref[rows:, :] = jnp.concatenate([block, zeros], axis=1).astype(BF)


def pair_kernel(mine_ref, other_ref, o_ref):
    rows = mine_ref.shape[0]
    odd = lax.axis_index("lat") % 2
    o_ref[pl.ds(pl.multiple_of(odd * rows, 8), rows), :] = mine_ref[...]
    o_ref[pl.ds(pl.multiple_of((1 - odd) * rows, 8), rows), :] = other_ref[...]


def join_kernel(counts, *refs):
    pieces, (o_ref, loss_ref) = refs[:4], refs[4:]
    chip = lax.axis_index("lat") // 2
    held = pieces[0].shape[0] // 2
    rows = held - 8
    for a in range(2):
        for n in range(2):
            at = pl.multiple_of((2 * (chip ^ a) + n) * rows, 8)
            both = [pieces[2 * a + b][held * n : held * n + rows, :].astype(F32) for b in range(2)]
            o_ref[pl.ds(at, rows), :] = (both[0] + both[1]) / counts[0]
    def part(p, n):
        return jnp.sum(p[held * n + rows : held * n + rows + 1, 0:128].astype(F32), axis=1, keepdims=True)

    chips = [part(p, 0) + part(p, 1) for p in pieces]
    loss = (chips[0] + chips[1]) + (chips[2] + chips[3])
    loss_ref[...] = jnp.broadcast_to(loss / counts[1], loss_ref.shape)


def swap(array, axis, bit):
    return lax.ppermute(array, axis, [(i, i ^ bit) for i in range(lax.axis_size(axis))])


def shape(dims, dtype):
    return jax.ShapeDtypeStruct(dims, dtype)


def shards(projected, targets, valid_cells, w_out, unpatch_matrix, norm_gain, var_weight):
    dp, lat, lon = lax.axis_size("dp"), lax.axis_size("lat"), lax.axis_size("lon")
    rows, width = w_out.shape
    levels = projected.shape[1]
    span = unpatch_matrix.shape[1]
    tokens = levels * 64
    lat_total = 8 * lat
    angle = math.pi * ((np.arange(lat_total) + 0.5) / lat_total - 0.5)
    cosine = np.cos(angle)
    lat_table = jnp.asarray(np.roll(cosine / cosine.mean(), -4), F32)
    barrier = lax.optimization_barrier

    unpatch_t = unpatch_matrix.T
    payload = pl.pallas_call(
        payload_kernel,
        out_shape=shape((rows // 4 + 16, width), BF),
        in_specs=[HBM, HBM, VMEM],
        out_specs=VMEM,
        scratch_shapes=[pltpu.VMEM((UGROWS, rows), BF), pltpu.SemaphoreType.DMA((2,))],
        compiler_params=params(60),
        name="payload",
    )(w_out, unpatch_t, norm_gain)
    ring1 = from_behind(payload, "dp", 1)
    own, *send = pl.pallas_call(
        pack_kernel,
        out_shape=[shape((n, 3 * width + EXTRA), BF) for n in (64, 64, 64, 64)],
        in_specs=[HBM] * 3,
        out_specs=[VMEM] * 4,
        scratch_shapes=[
            pltpu.VMEM((levels, 8, 8, 3 * width), BF),
            pltpu.VMEM((levels, 8, 8, span), BF),
            pltpu.VMEM((8, 8), jnp.int32),
            pltpu.SemaphoreType.DMA((2 + 3 * width // 512,)),
        ],
        compiler_params=params(50),
        name="pack",
    )(
        projected.reshape(levels, 8, 8, 3 * width),
        targets.reshape(levels, 8, 8, span),
        valid_cells,
    )
    corner = [
        (a * lon + b, ((a - 1) % lat) * lon + (b - 1) % lon) for a in range(lat) for b in range(lon)
    ]
    south = from_behind(send[1], "lat", -1)
    diag = lax.ppermute(send[2], ("lat", "lon"), corner)
    ring2 = from_behind(ring1, "dp", 1)
    across2 = swap(ring2, "lat", 2)
    ring2_after, east, south, diag = barrier((ring2, send[0], south, diag))
    ring3 = from_behind(ring2_after, "dp", 1)
    east = from_behind(east, "lon", -1)
    across3 = from_behind(across2, "dp", 1)
    ring1_late, across2 = barrier((ring1, across2))
    across1 = swap(ring1_late, "lat", 2)
    tiles = [own, east, south, diag]
    *tiles, ring1, across1, ring2 = barrier((*tiles, ring1, across1, ring2))
    ctx = pl.pallas_call(
        attention_kernel,
        out_shape=shape((tokens, width), BF),
        in_specs=[VMEM] * 4,
        out_specs=VMEM,
        compiler_params=params(16),
        name="attention",
    )(*tiles)
    ctx, across3 = barrier((ctx, across3))
    pieces = []
    for ring, across in ((ring1, across1), (ring2, across2), (ring3, across3)):
        pieces += [ring, across, swap(ring, "lat", 1), swap(across, "lat", 1)]

    piece = span // lat
    extra_specs = [
        pl.BlockSpec((t.shape[0], EXTRA), lambda i: (0, 3 * width // EXTRA)) for t in tiles
    ]
    assembly = [
        pltpu.VMEM((dp * rows, width), BF),
        pltpu.VMEM((UGROWS, dp * rows), BF),
    ]
    *terms, normed, inv, dfc, loss = pl.pallas_call(
        forward_kernel,
        grid=(1,),
        out_shape=[shape((piece, width), BF)] * 4
        + [shape((tokens, width), F32), shape((tokens, 128), F32), shape((tokens, span), BF)]
        + [shape((8, 128), F32)],
        in_specs=[SMEM] * 2 + [VMEM] + extra_specs + [VMEM] * (3 + PIECES),
        out_specs=[VMEM] * 8,
        scratch_shapes=[pltpu.VMEM((tokens, width), BF)]
        + assembly
        + [pltpu.VMEM((span, width), F32)],
        compiler_params=params(28),
        name="forward",
    )(lat_table, var_weight, ctx, *tiles, w_out, unpatch_t, norm_gain, *pieces)

    terms = [terms[0]] + [swap(terms[b], "lat", b) for b in (1, 2, 3)]
    grad_context = pl.pallas_call(
        backward_kernel,
        out_shape=shape((tokens, width), BF),
        in_specs=[VMEM] * (6 + PIECES),
        out_specs=VMEM,
        scratch_shapes=assembly,
        compiler_params=params(24),
        name="backward",
    )(normed, inv, dfc, w_out, unpatch_t, norm_gain, *pieces)
    *terms, grad_context = barrier((*terms, grad_context))

    parts = pl.pallas_call(
        lat_sum_kernel,
        out_shape=[shape((piece, rows), BF)] * 4,
        in_specs=[VMEM] * 4,
        out_specs=[VMEM] * 4,
        scratch_shapes=[pltpu.VMEM((piece, width), F32)],
        compiler_params=params(4),
        name="lat_sum",
    )(*terms)
    parts = [parts[0]] + [swap(parts[k], "dp", k) for k in (1, 2, 3)]
    mine = pl.pallas_call(
        dp_sum_kernel,
        out_shape=shape((piece + 8, rows), BF),
        in_specs=[VMEM] * 5,
        out_specs=VMEM,
        compiler_params=params(4),
        name="dp_sum",
    )(loss, *parts)
    chip = pl.pallas_call(
        pair_kernel,
        out_shape=shape((2 * piece + 16, rows), BF),
        in_specs=[VMEM] * 2,
        out_specs=VMEM,
        compiler_params=params(4),
        name="pair",
    )(mine, swap(mine, "lat", 1))
    plane = [chip]
    for a, b in ((0, 1), (2, 0), (2, 1)):
        pairs = [(i * lon + j, (i ^ a) * lon + (j ^ b)) for i in range(lat) for j in range(lon)]
        plane.append(lax.ppermute(chip, ("lat", "lon"), pairs))
    count = levels * lat_total * 8 * lon
    counts = (float(count), float(count * (span // var_weight.shape[0])))
    joined, loss = pl.pallas_call(
        lambda *refs: join_kernel(counts, *refs),
        out_shape=[shape((span, rows), F32), shape((1, 1), F32)],
        in_specs=[VMEM] * 4,
        out_specs=[VMEM] * 2,
        compiler_params=params(4),
        name="join",
    )(*plane)
    return grad_context.reshape(1, levels, 8, 8, width), joined.T, loss.reshape(1)


def solution(mesh):
    placed = (
        P("dp", None, "lat", "lon", None),
        P("dp", None, "lat", "lon", None),
        P("lat", "lon"),
        P("dp", None),
        P("dp", None),
        P("dp"),
        P(),
    )
    fits = mesh.shape["dp"] == 4 and mesh.shape["lat"] == 4 and mesh.shape["lon"] == 2

    def program(*arrays):
        body = shards if fits else general_shards
        return jax.shard_map(
            body,
            mesh=mesh,
            in_specs=placed,
            out_specs=(P("dp", None, "lat", "lon", None), P("dp", None), P("dp")),
            check_vma=False,
        )(*arrays)

    return program
```

```python
import functools
import math

import jax
import jax.numpy as jnp
import numpy as np
from jax import lax
from jax.experimental import pallas as pl
from jax.experimental.pallas import tpu as pltpu
from jax.sharding import PartitionSpec as P

HEADS = 48
HDIM = 32
WLEV = 2
BF = jnp.bfloat16
F32 = jnp.float32
EXTRA = 256
UGROWS = 256
PIECES = 12
VMEM = pl.BlockSpec(memory_space=pltpu.VMEM)
SMEM = pl.BlockSpec(memory_space=pltpu.SMEM)
ANY = pl.BlockSpec(memory_space=pl.ANY)
HBM = pl.BlockSpec(memory_space=pltpu.HBM)


def from_behind(array, axis, by):
    length = lax.axis_size(axis)
    return lax.ppermute(array, axis, [(i, (i + by) % length) for i in range(length)])


def general_shards(projected, targets, valid_cells, w_out, unpatch_matrix, norm_gain, var_weight):
    tile_side = projected.shape[2]
    half_side = tile_side // 2
    levels = projected.shape[1]
    model_width = w_out.shape[1]
    predicted_span = unpatch_matrix.shape[1]
    lat_total = tile_side * lax.axis_size("lat")
    lon_total = tile_side * lax.axis_size("lon")
    lat_place = lax.axis_index("lat")
    moved = from_behind(
        (projected[:, :, :, :half_side], targets[:, :, :, :half_side], valid_cells[:, :half_side]),
        "lon",
        -1,
    )
    strip_proj = jnp.concatenate([projected[:, :, :, half_side:], moved[0]], axis=3)
    strip_goal = jnp.concatenate([targets[:, :, :, half_side:], moved[1]], axis=3)
    strip_valid = jnp.concatenate([valid_cells[:, half_side:], moved[2]], axis=1)
    moved_rows = from_behind(
        (strip_proj[:, :, :half_side], strip_goal[:, :, :half_side], strip_valid[:half_side]),
        "lat",
        -1,
    )
    local_proj = jnp.concatenate([strip_proj[:, :, half_side:], moved_rows[0]], axis=2)
    shard_reference = jnp.concatenate([strip_goal[:, :, half_side:], moved_rows[1]], axis=2)
    local_valid = jnp.concatenate([strip_valid[half_side:], moved_rows[2]], axis=0).astype(F32)
    win_count = levels // WLEV
    tokw = WLEV * tile_side * tile_side
    windows = local_proj.reshape(win_count, tokw, 3 * model_width)
    rows_here = lat_place * tile_side + jnp.arange(tile_side)
    region_rows = (rows_here >= lat_total - half_side).astype(jnp.int32)
    region = jnp.broadcast_to(region_rows[None, :, None], (WLEV, tile_side, tile_side)).reshape(-1)
    allowed = region[:, None] == region[None, :]
    queries = windows[..., :model_width].reshape(win_count, tokw, HEADS, -1)
    key_heads = windows[..., model_width : 2 * model_width].reshape(win_count, tokw, HEADS, -1)
    value_heads = windows[..., 2 * model_width :].reshape(win_count, tokw, HEADS, -1)
    scores = jnp.einsum("wqhd,wkhd->whqk", queries, key_heads, preferred_element_type=F32)
    scores = scores * (1.0 / math.sqrt(HDIM))
    scores = jnp.where(allowed[None, None], scores, -1e30)
    row_peak = jnp.max(scores, axis=-1, keepdims=True)
    lifted = jnp.exp(scores - row_peak)
    attn = (lifted / jnp.sum(lifted, axis=-1, keepdims=True)).astype(BF)
    context = jnp.einsum("whqk,wkhd->wqhd", attn, value_heads, preferred_element_type=F32)
    context = context.astype(BF).reshape(win_count * tokw, model_width)
    element_total = win_count * tokw
    out_all, unprojected_pieces, gain_all = (
        lax.all_gather(w_out, "dp", axis=0, tiled=True),
        lax.all_gather(unpatch_matrix, "dp", axis=0, tiled=True),
        lax.all_gather(norm_gain, "dp", axis=0, tiled=True),
    )
    mixed_rows = jnp.dot(context, out_all, preferred_element_type=F32)
    centre = jnp.mean(mixed_rows, axis=-1, keepdims=True)
    spread = jnp.mean((mixed_rows - centre) ** 2, axis=-1, keepdims=True)
    inv_spread = lax.rsqrt(spread + 1e-05)
    normed = (mixed_rows - centre) * inv_spread
    gain_f = gain_all.astype(F32)
    latent_activation = (normed * gain_f).astype(BF)
    prediction_field = jnp.dot(latent_activation, unprojected_pieces, preferred_element_type=F32)
    prediction_misfit = prediction_field - shard_reference.reshape(
        element_total, predicted_span
    ).astype(F32)
    all_rows = jnp.arange(lat_total).astype(F32)
    cosine_mean = jnp.mean(jnp.cos(math.pi * ((all_rows + 0.5) / lat_total - 0.5)))
    initial_rows = ((rows_here + half_side) % lat_total).astype(F32)
    lat_here = jnp.cos(math.pi * ((initial_rows + 0.5) / lat_total - 0.5)) / cosine_mean
    element_factor = jnp.broadcast_to(
        lat_here[None, :, None] * local_valid[None], (levels, tile_side, tile_side)
    ).reshape(element_total, 1)
    variable_factor = jnp.repeat(var_weight, predicted_span // var_weight.shape[0])[None, :]
    shard_penalty = jnp.sum(
        element_factor * variable_factor * prediction_misfit * prediction_misfit
    ) / (levels * lat_total * lon_total * (predicted_span // var_weight.shape[0]))
    prediction_gradient = (2.0 * element_factor * variable_factor * prediction_misfit).astype(BF)
    grad_shard = lax.psum_scatter(
        jnp.einsum(
            "td,to->do", latent_activation, prediction_gradient, preferred_element_type=F32
        ).astype(BF),
        "dp",
        scatter_dimension=0,
        tiled=True,
    ).astype(F32)
    grad_sum, loss_sum = lax.psum((grad_shard, shard_penalty), ("lat", "lon"))
    grad_recovery = grad_sum / (levels * lat_total * lon_total)
    grad_hidden = jnp.einsum(
        "to,do->td", prediction_gradient, unprojected_pieces, preferred_element_type=F32
    )
    scaled_grad = grad_hidden * gain_f
    grad_mixed = inv_spread * (
        scaled_grad
        - jnp.mean(scaled_grad, axis=-1, keepdims=True)
        - normed * jnp.mean(scaled_grad * normed, axis=-1, keepdims=True)
    )
    grad_mixed = grad_mixed.astype(BF)
    grad_context = jnp.einsum("tj,ij->ti", grad_mixed, out_all, preferred_element_type=F32)
    grad_context = grad_context.astype(BF).reshape(1, levels, tile_side, tile_side, model_width)
    return (grad_context, grad_recovery, loss_sum.reshape(1))


def params(mib):
    return pltpu.CompilerParams(vmem_limit_bytes=mib << 20)


def iota(shape, dim):
    return lax.broadcasted_iota(jnp.int32, shape, dim)


def payload_kernel(w_ref, unpatch_ref, gain_ref, payload_ref, ug, sems):
    part = lax.axis_index("lat")
    rows, width = w_ref.shape
    qr = rows // 4
    span = unpatch_ref.shape[0]
    start = pl.multiple_of(part * qr, 32)
    u_copy = pltpu.make_async_copy(unpatch_ref, ug.at[pl.ds(0, span), :], sems.at[0])
    u_copy.start()
    w_copy = pltpu.make_async_copy(
        w_ref.at[pl.ds(start, qr), :], payload_ref.at[pl.ds(0, qr), :], sems.at[1]
    )
    w_copy.start()
    ug[pl.ds(span, 16), :] = gain_rows(gain_ref, rows)
    ug[pl.ds(span + 16, UGROWS - span - 16), :] = jnp.zeros((UGROWS - span - 16, rows), BF)
    u_copy.wait()
    for j in range(4):
        at = pl.multiple_of((4 * part + j) * 16, 16)
        payload_ref[pl.ds(qr, 16), pl.ds(j * rows, rows)] = ug[pl.ds(at, 16), :]
    w_copy.wait()


def gain_rows(gain_ref, rows):
    return jnp.broadcast_to(gain_ref[...].astype(F32).reshape(1, rows), (16, rows)).astype(BF)


def pack_kernel(x_ref, t_ref, valid_ref, *refs):
    outs, (x_in, t_in, v_in, sems) = refs[:4], refs[4:]
    span = t_ref.shape[-1]
    count = x_ref.shape[0] * 64
    quarter = count // 4
    step = 512
    width = x_ref.shape[-1]
    copies = [
        pltpu.make_async_copy(t_ref, t_in, sems.at[0]),
        pltpu.make_async_copy(valid_ref, v_in, sems.at[1]),
    ]
    for at in range(0, width, step):
        lanes = (slice(None),) * 3 + (pl.ds(at, step),)
        copies.append(
            pltpu.make_async_copy(x_ref.at[lanes], x_in.at[lanes], sems.at[len(copies)])
        )
    for c in copies:
        c.start()
    place = iota((count, count), 0)
    quad, rest = place // quarter, place % quarter
    row = (rest // 4) % 4 + jnp.where(quad < 2, 4, 0)
    col = rest % 4 + jnp.where(quad % 2 == 0, 4, 0)
    source = (rest // 16) * 64 + row * 8 + col
    pick = (iota((count, count), 1) == source).astype(F32).astype(BF)
    copies[0].wait()
    copies[1].wait()
    goal = jnp.dot(pick, t_in[...].reshape(count, span), preferred_element_type=F32)
    token = iota((count, 8), 0)
    row_hot = ((token // 8) % 8 == iota((count, 8), 1)).astype(F32)
    by_row = jnp.dot(row_hot, v_in[...].astype(F32), preferred_element_type=F32)
    mine = token % 8 == iota((count, 8), 1)
    natural = jnp.sum(jnp.where(mine, by_row, 0.0), axis=1, keepdims=True)
    spread = jnp.broadcast_to(natural, (count, 128)).astype(BF)
    column = jnp.dot(pick, spread, preferred_element_type=F32)
    extra = jnp.concatenate([goal, column[:, : EXTRA - span]], axis=1).astype(BF)
    starts = [sum(o.shape[0] for o in outs[:n]) for n in range(4)]
    outs = list(zip(outs, starts))
    for ref, row in outs:
        ref[:, width:] = extra[row : row + ref.shape[0]]
    for n, at in enumerate(range(0, width, step)):
        copies[2 + n].wait()
        tokens = x_in[:, :, :, at : at + step].reshape(count, step)
        out = jnp.dot(pick, tokens, preferred_element_type=F32).astype(BF)
        for ref, row in outs:
            ref[:, at : at + step] = out[row : row + ref.shape[0]]


def windows_of(*tiles):
    return [[t.at[32 * w : 32 * w + 32] for t in tiles] for w in range(2)]


def attention_kernel(*refs):
    tiles, ctx_ref = windows_of(*refs[:4]), refs[4]
    part = ctx_ref.shape[1]
    is_last = lax.axis_index("lat") == lax.axis_size("lat") - 1
    same = (iota((512, 128), 0) % 128) // 64 == iota((512, 128), 1) // 64
    bias = jnp.where(jnp.logical_or(same, jnp.logical_not(is_last)), 0.0, -1e30)
    head = iota((128, 128), 1) // HDIM
    factor = math.log2(math.e) / math.sqrt(HDIM)
    for at in range(0, part, 128):
        for w in range(2):
            q, k, v = [
                jnp.concatenate(
                    [t[:, i * part + at : i * part + at + 128] for t in tiles[w]],
                    axis=0,
                )
                for i in range(3)
            ]
            zero = jnp.zeros_like(k)
            k4 = jnp.concatenate([jnp.where(head == h, k, zero) for h in range(4)], axis=0)
            v4 = jnp.concatenate([jnp.where(head == h, v, zero) for h in range(4)], axis=0)
            s = lax.dot_general(k4, q, (((1,), (1,)), ((), ())), preferred_element_type=F32)
            s = s + bias
            parts = []
            for h in range(4):
                sh = s[128 * h : 128 * h + 128]
                e = jnp.exp2((sh - jnp.max(sh, axis=0, keepdims=True)) * factor)
                parts.append((e * (1.0 / jnp.sum(e, axis=0, keepdims=True))).astype(BF))
            attn = jnp.concatenate(parts, axis=0)
            out = lax.dot_general(attn, v4, (((0,), (0,)), ((), ())), preferred_element_type=F32)
            ctx_ref[128 * w : 128 * w + 128, at : at + 128] = out.astype(BF)


def assemble(own_w, own_u, own_gain, pieces, w_all, ug_all):
    zi, part = lax.axis_index("dp"), lax.axis_index("lat")
    rows = own_w.shape[0]
    qr = rows // 4
    steps = len(pieces) // 4 + 1
    base = pl.multiple_of(zi * rows, 128)
    w_all[pl.ds(base, rows), :] = own_w[...]
    span = own_u.shape[0]
    ug_all[0:span, pl.ds(base, rows)] = own_u[...]
    ug_all[span : span + 16, pl.ds(base, rows)] = gain_rows(own_gain, rows)
    for k in range(1, steps):
        shard = lax.rem(zi - k + steps, steps)
        base = pl.multiple_of(shard * rows, 128)
        for bits, piece in zip((0, 2, 1, 3), pieces[4 * k - 4 : 4 * k]):
            from_part = part ^ bits
            row = pl.multiple_of(base + from_part * qr, 32)
            w_all[pl.ds(row, qr), :] = piece[0:qr, :]
            for j in range(4):
                urow = pl.multiple_of((4 * from_part + j) * 16, 16)
                ug_all[pl.ds(urow, 16), pl.ds(base, rows)] = piece[
                    qr : qr + 16, j * rows : (j + 1) * rows
                ]


def split3(x):
    hi = x.astype(BF).astype(F32)
    mid = (x - hi).astype(BF).astype(F32)
    return hi, mid, x - hi - mid


def loss_block(value, rows):
    hi, mid, lo = split3(value)
    lane = iota((rows, 128), 1)
    return jnp.where(lane == 0, hi, jnp.where(lane == 1, mid, jnp.where(lane == 2, lo, 0.0)))


def forward_kernel(lat_ref, var_ref, *refs):
    ctx_ref, refs = refs[0], refs[1:]
    extras, refs = refs[:4], refs[4:]
    owned, refs = refs[:3], refs[3:]
    pieces, refs = refs[:PIECES], refs[PIECES:]
    ts, refs = refs[:4], refs[4:]
    normed_ref, inv_ref, dfc_ref, loss_ref, hidden_ref, w_all, ug_all, term = refs
    lat_place = lax.axis_index("lat")
    assemble(*owned, pieces, w_all, ug_all)
    tokens, width = normed_ref.shape
    span = dfc_ref.shape[1]
    extra = jnp.concatenate([t[...] for tiles in windows_of(*extras) for t in tiles], axis=0)
    extra = extra.astype(F32)
    goal, valid = extra[:, :span], extra[:, span : span + 1]
    token = iota((tokens, 1), 0)
    row = (token // 4) % 4 + jnp.where((token // 32) % 4 >= 2, 4, 0)
    lat_w = jnp.zeros((tokens, 1), F32)
    for r in range(8):
        lat_w = jnp.where(row == r, lat_ref[lat_place * 8 + r], lat_w)
    lane = iota((1, span), 1) // (span // var_ref.shape[0])
    var_w = jnp.zeros((1, span), F32)
    for n in range(var_ref.shape[0]):
        var_w = jnp.where(lane == n, var_ref[n], var_w)
    weight = lat_w * valid * var_w
    mixed = jnp.dot(ctx_ref[...], w_all[...], preferred_element_type=F32)
    centre = jnp.mean(mixed, axis=-1, keepdims=True)
    off = mixed - centre
    inv = lax.rsqrt(jnp.mean(off * off, axis=-1, keepdims=True) + 1e-05)
    normed = off * inv
    normed_ref[...] = normed
    inv_ref[...] = jnp.broadcast_to(inv, inv_ref.shape)
    gain = ug_all[pl.ds(span, 16), :][0:1].astype(F32)
    hidden_ref[...] = (normed * gain).astype(BF)
    field = lax.dot_general(
        hidden_ref[...], ug_all[0:span, :], (((1,), (1,)), ((), ())), preferred_element_type=F32
    )
    misfit = field - goal
    dfc = (2.0 * weight * misfit).astype(BF)
    dfc_ref[...] = dfc
    term[...] = lax.dot_general(
        dfc, hidden_ref[...], (((0,), (0,)), ((), ())), preferred_element_type=F32
    )
    loss = jnp.sum(jnp.sum(weight * misfit * misfit, axis=1, keepdims=True), axis=0, keepdims=True)
    loss_ref[...] = jnp.broadcast_to(loss, loss_ref.shape)
    rows = ts[0].shape[0]
    for b, ref in enumerate(ts):
        at = pl.multiple_of((lat_place ^ b) * rows, 8)
        ref[...] = term[pl.ds(at, rows), :].astype(BF)


def backward_kernel(normed_ref, inv_ref, dfc_ref, *refs):
    owned, refs = refs[:3], refs[3:]
    pieces, (out_ref, w_all, ug_all) = refs[:PIECES], refs[PIECES:]
    assemble(*owned, pieces, w_all, ug_all)
    tokens, width = normed_ref.shape
    span = dfc_ref.shape[1]
    gain = ug_all[pl.ds(span, 16), :][0:1].astype(F32)
    g = jnp.dot(dfc_ref[...], ug_all[0:span, :], preferred_element_type=F32) * gain
    normed = normed_ref[...]
    mean_g = jnp.mean(g, axis=-1, keepdims=True)
    mean_gn = jnp.mean(g * normed, axis=-1, keepdims=True)
    dmixed = ((g - mean_g - normed * mean_gn) * inv_ref[:, 0:1]).astype(BF)
    place = iota((tokens, tokens), 0)
    row, col, level = (place // 8) % 8, place % 8, place // 64
    quad = jnp.where(row >= 4, 2, 0) + jnp.where(col >= 4, 1, 0)
    source = (level // 2) * 128 + quad * 32 + (level % 2) * 16 + (row % 4) * 4 + col % 4
    pick = (iota((tokens, tokens), 1) == source).astype(F32).astype(BF)
    dnat = jnp.dot(pick, dmixed, preferred_element_type=F32).astype(BF)
    out = lax.dot_general(dnat, w_all[...], (((1,), (1,)), ((), ())), preferred_element_type=F32)
    out_ref[...] = out.astype(BF)


def add4(a, b, c, d):
    return (a[...].astype(F32) + b[...].astype(F32)) + (c[...].astype(F32) + d[...].astype(F32))


def lat_sum_kernel(a, b, c, d, z0, z1, z2, z3, total_ref):
    total_ref[...] = add4(a, b, c, d)
    zi = lax.axis_index("dp")
    width = z0.shape[1]
    for k, ref in enumerate((z0, z1, z2, z3)):
        at = pl.multiple_of((zi ^ k) * width, 128)
        ref[...] = total_ref[:, pl.ds(at, width)].astype(BF)


def dp_sum_kernel(loss_ref, a, b, c, d, o_ref):
    rows, width = a.shape
    o_ref[0:rows, :] = add4(a, b, c, d).astype(BF)
    block = loss_block(loss_ref[0:1, 0:1], o_ref.shape[0] - rows)
    zeros = jnp.zeros((block.shape[0], width - 128), F32)
    o_ref[rows:, :] = jnp.concatenate([block, zeros], axis=1).astype(BF)


def pair_kernel(mine_ref, other_ref, o_ref):
    rows = mine_ref.shape[0]
    odd = lax.axis_index("lat") % 2
    o_ref[pl.ds(pl.multiple_of(odd * rows, 8), rows), :] = mine_ref[...]
    o_ref[pl.ds(pl.multiple_of((1 - odd) * rows, 8), rows), :] = other_ref[...]


def join_kernel(counts, *refs):
    pieces, (o_ref, loss_ref) = refs[:4], refs[4:]
    chip = lax.axis_index("lat") // 2
    held = pieces[0].shape[0] // 2
    rows = held - 8
    for a in range(2):
        for n in range(2):
            at = pl.multiple_of((2 * (chip ^ a) + n) * rows, 8)
            both = [pieces[2 * a + b][held * n : held * n + rows, :].astype(F32) for b in range(2)]
            o_ref[pl.ds(at, rows), :] = (both[0] + both[1]) / counts[0]
    def part(p, n):
        return jnp.sum(p[held * n + rows : held * n + rows + 1, 0:128].astype(F32), axis=1, keepdims=True)

    chips = [part(p, 0) + part(p, 1) for p in pieces]
    loss = (chips[0] + chips[1]) + (chips[2] + chips[3])
    loss_ref[...] = jnp.broadcast_to(loss / counts[1], loss_ref.shape)


def swap(array, axis, bit):
    return lax.ppermute(array, axis, [(i, i ^ bit) for i in range(lax.axis_size(axis))])


def shape(dims, dtype):
    return jax.ShapeDtypeStruct(dims, dtype)


def shards(projected, targets, valid_cells, w_out, unpatch_matrix, norm_gain, var_weight):
    dp, lat, lon = lax.axis_size("dp"), lax.axis_size("lat"), lax.axis_size("lon")
    rows, width = w_out.shape
    levels = projected.shape[1]
    span = unpatch_matrix.shape[1]
    tokens = levels * 64
    lat_total = 8 * lat
    angle = math.pi * ((np.arange(lat_total) + 0.5) / lat_total - 0.5)
    cosine = np.cos(angle)
    lat_table = jnp.asarray(np.roll(cosine / cosine.mean(), -4), F32)
    barrier = lax.optimization_barrier

    unpatch_t = unpatch_matrix.T
    payload = pl.pallas_call(
        payload_kernel,
        out_shape=shape((rows // 4 + 16, width), BF),
        in_specs=[HBM, HBM, VMEM],
        out_specs=VMEM,
        scratch_shapes=[pltpu.VMEM((UGROWS, rows), BF), pltpu.SemaphoreType.DMA((2,))],
        compiler_params=params(60),
        name="payload",
    )(w_out, unpatch_t, norm_gain)
    ring1 = from_behind(payload, "dp", 1)
    own, *send = pl.pallas_call(
        pack_kernel,
        out_shape=[shape((n, 3 * width + EXTRA), BF) for n in (64, 64, 64, 64)],
        in_specs=[HBM] * 3,
        out_specs=[VMEM] * 4,
        scratch_shapes=[
            pltpu.VMEM((levels, 8, 8, 3 * width), BF),
            pltpu.VMEM((levels, 8, 8, span), BF),
            pltpu.VMEM((8, 8), jnp.int32),
            pltpu.SemaphoreType.DMA((2 + 3 * width // 512,)),
        ],
        compiler_params=params(50),
        name="pack",
    )(
        projected.reshape(levels, 8, 8, 3 * width),
        targets.reshape(levels, 8, 8, span),
        valid_cells,
    )
    corner = [
        (a * lon + b, ((a - 1) % lat) * lon + (b - 1) % lon) for a in range(lat) for b in range(lon)
    ]
    south = from_behind(send[1], "lat", -1)
    diag = lax.ppermute(send[2], ("lat", "lon"), corner)
    ring2 = from_behind(ring1, "dp", 1)
    across2 = swap(ring2, "lat", 2)
    ring2_after, east, south, diag = barrier((ring2, send[0], south, diag))
    ring3 = from_behind(ring2_after, "dp", 1)
    east = from_behind(east, "lon", -1)
    across3 = from_behind(across2, "dp", 1)
    ring1_late, across2 = barrier((ring1, across2))
    across1 = swap(ring1_late, "lat", 2)
    tiles = [own, east, south, diag]
    ring1_swapped = swap(ring1, "lat", 1)
    *tiles, across1, ring2, ring1_swapped = barrier((*tiles, across1, ring2, ring1_swapped))
    ctx = pl.pallas_call(
        attention_kernel,
        out_shape=shape((tokens, width), BF),
        in_specs=[VMEM] * 4,
        out_specs=VMEM,
        compiler_params=params(16),
        name="attention",
    )(*tiles)
    ctx, across3 = barrier((ctx, across3))
    pieces = [ring1, across1, ring1_swapped, swap(across1, "lat", 1)]
    for ring, across in ((ring2, across2), (ring3, across3)):
        pieces += [ring, across, swap(ring, "lat", 1), swap(across, "lat", 1)]

    piece = span // lat
    extra_specs = [
        pl.BlockSpec((t.shape[0], EXTRA), lambda i: (0, 3 * width // EXTRA)) for t in tiles
    ]
    assembly = [
        pltpu.VMEM((dp * rows, width), BF),
        pltpu.VMEM((UGROWS, dp * rows), BF),
    ]
    *terms, normed, inv, dfc, loss = pl.pallas_call(
        forward_kernel,
        grid=(1,),
        out_shape=[shape((piece, width), BF)] * 4
        + [shape((tokens, width), F32), shape((tokens, 128), F32), shape((tokens, span), BF)]
        + [shape((8, 128), F32)],
        in_specs=[SMEM] * 2 + [VMEM] + extra_specs + [VMEM] * (3 + PIECES),
        out_specs=[VMEM] * 8,
        scratch_shapes=[pltpu.VMEM((tokens, width), BF)]
        + assembly
        + [pltpu.VMEM((span, width), F32)],
        compiler_params=params(28),
        name="forward",
    )(lat_table, var_weight, ctx, *tiles, w_out, unpatch_t, norm_gain, *pieces)

    terms = [terms[0]] + [swap(terms[b], "lat", b) for b in (1, 2, 3)]
    grad_context = pl.pallas_call(
        backward_kernel,
        out_shape=shape((tokens, width), BF),
        in_specs=[VMEM] * (6 + PIECES),
        out_specs=VMEM,
        scratch_shapes=assembly,
        compiler_params=params(24),
        name="backward",
    )(normed, inv, dfc, w_out, unpatch_t, norm_gain, *pieces)
    *terms, grad_context = barrier((*terms, grad_context))

    parts = pl.pallas_call(
        lat_sum_kernel,
        out_shape=[shape((piece, rows), BF)] * 4,
        in_specs=[VMEM] * 4,
        out_specs=[VMEM] * 4,
        scratch_shapes=[pltpu.VMEM((piece, width), F32)],
        compiler_params=params(4),
        name="lat_sum",
    )(*terms)
    parts = [parts[0]] + [swap(parts[k], "dp", k) for k in (1, 2, 3)]
    mine = pl.pallas_call(
        dp_sum_kernel,
        out_shape=shape((piece + 8, rows), BF),
        in_specs=[VMEM] * 5,
        out_specs=VMEM,
        compiler_params=params(4),
        name="dp_sum",
    )(loss, *parts)
    chip = pl.pallas_call(
        pair_kernel,
        out_shape=shape((2 * piece + 16, rows), BF),
        in_specs=[VMEM] * 2,
        out_specs=VMEM,
        compiler_params=params(4),
        name="pair",
    )(mine, swap(mine, "lat", 1))
    plane = [chip]
    for a, b in ((0, 1), (2, 0), (2, 1)):
        pairs = [(i * lon + j, (i ^ a) * lon + (j ^ b)) for i in range(lat) for j in range(lon)]
        plane.append(lax.ppermute(chip, ("lat", "lon"), pairs))
    count = levels * lat_total * 8 * lon
    counts = (float(count), float(count * (span // var_weight.shape[0])))
    joined, loss = pl.pallas_call(
        lambda *refs: join_kernel(counts, *refs),
        out_shape=[shape((span, rows), F32), shape((1, 1), F32)],
        in_specs=[VMEM] * 4,
        out_specs=[VMEM] * 2,
        compiler_params=params(4),
        name="join",
    )(*plane)
    return grad_context.reshape(1, levels, 8, 8, width), joined.T, loss.reshape(1)


def solution(mesh):
    placed = (
        P("dp", None, "lat", "lon", None),
        P("dp", None, "lat", "lon", None),
        P("lat", "lon"),
        P("dp", None),
        P("dp", None),
        P("dp"),
        P(),
    )
    fits = mesh.shape["dp"] == 4 and mesh.shape["lat"] == 4 and mesh.shape["lon"] == 2

    def program(*arrays):
        body = shards if fits else general_shards
        return jax.shard_map(
            body,
            mesh=mesh,
            in_specs=placed,
            out_specs=(P("dp", None, "lat", "lon", None), P("dp", None), P("dp")),
            check_vma=False,
        )(*arrays)

    return program
```

```python
import functools
import math

import jax
import jax.numpy as jnp
import numpy as np
from jax import lax
from jax.experimental import pallas as pl
from jax.experimental.pallas import tpu as pltpu
from jax.sharding import PartitionSpec as P

HEADS = 48
HDIM = 32
WLEV = 2
BF = jnp.bfloat16
F32 = jnp.float32
EXTRA = 256
UGROWS = 256
PIECES = 12
VMEM = pl.BlockSpec(memory_space=pltpu.VMEM)
SMEM = pl.BlockSpec(memory_space=pltpu.SMEM)
ANY = pl.BlockSpec(memory_space=pl.ANY)
HBM = pl.BlockSpec(memory_space=pltpu.HBM)


def from_behind(array, axis, by):
    length = lax.axis_size(axis)
    return lax.ppermute(array, axis, [(i, (i + by) % length) for i in range(length)])


def general_shards(projected, targets, valid_cells, w_out, unpatch_matrix, norm_gain, var_weight):
    tile_side = projected.shape[2]
    half_side = tile_side // 2
    levels = projected.shape[1]
    model_width = w_out.shape[1]
    predicted_span = unpatch_matrix.shape[1]
    lat_total = tile_side * lax.axis_size("lat")
    lon_total = tile_side * lax.axis_size("lon")
    lat_place = lax.axis_index("lat")
    moved = from_behind(
        (projected[:, :, :, :half_side], targets[:, :, :, :half_side], valid_cells[:, :half_side]),
        "lon",
        -1,
    )
    strip_proj = jnp.concatenate([projected[:, :, :, half_side:], moved[0]], axis=3)
    strip_goal = jnp.concatenate([targets[:, :, :, half_side:], moved[1]], axis=3)
    strip_valid = jnp.concatenate([valid_cells[:, half_side:], moved[2]], axis=1)
    moved_rows = from_behind(
        (strip_proj[:, :, :half_side], strip_goal[:, :, :half_side], strip_valid[:half_side]),
        "lat",
        -1,
    )
    local_proj = jnp.concatenate([strip_proj[:, :, half_side:], moved_rows[0]], axis=2)
    shard_reference = jnp.concatenate([strip_goal[:, :, half_side:], moved_rows[1]], axis=2)
    local_valid = jnp.concatenate([strip_valid[half_side:], moved_rows[2]], axis=0).astype(F32)
    win_count = levels // WLEV
    tokw = WLEV * tile_side * tile_side
    windows = local_proj.reshape(win_count, tokw, 3 * model_width)
    rows_here = lat_place * tile_side + jnp.arange(tile_side)
    region_rows = (rows_here >= lat_total - half_side).astype(jnp.int32)
    region = jnp.broadcast_to(region_rows[None, :, None], (WLEV, tile_side, tile_side)).reshape(-1)
    allowed = region[:, None] == region[None, :]
    queries = windows[..., :model_width].reshape(win_count, tokw, HEADS, -1)
    key_heads = windows[..., model_width : 2 * model_width].reshape(win_count, tokw, HEADS, -1)
    value_heads = windows[..., 2 * model_width :].reshape(win_count, tokw, HEADS, -1)
    scores = jnp.einsum("wqhd,wkhd->whqk", queries, key_heads, preferred_element_type=F32)
    scores = scores * (1.0 / math.sqrt(HDIM))
    scores = jnp.where(allowed[None, None], scores, -1e30)
    row_peak = jnp.max(scores, axis=-1, keepdims=True)
    lifted = jnp.exp(scores - row_peak)
    attn = (lifted / jnp.sum(lifted, axis=-1, keepdims=True)).astype(BF)
    context = jnp.einsum("whqk,wkhd->wqhd", attn, value_heads, preferred_element_type=F32)
    context = context.astype(BF).reshape(win_count * tokw, model_width)
    element_total = win_count * tokw
    out_all, unprojected_pieces, gain_all = (
        lax.all_gather(w_out, "dp", axis=0, tiled=True),
        lax.all_gather(unpatch_matrix, "dp", axis=0, tiled=True),
        lax.all_gather(norm_gain, "dp", axis=0, tiled=True),
    )
    mixed_rows = jnp.dot(context, out_all, preferred_element_type=F32)
    centre = jnp.mean(mixed_rows, axis=-1, keepdims=True)
    spread = jnp.mean((mixed_rows - centre) ** 2, axis=-1, keepdims=True)
    inv_spread = lax.rsqrt(spread + 1e-05)
    normed = (mixed_rows - centre) * inv_spread
    gain_f = gain_all.astype(F32)
    latent_activation = (normed * gain_f).astype(BF)
    prediction_field = jnp.dot(latent_activation, unprojected_pieces, preferred_element_type=F32)
    prediction_misfit = prediction_field - shard_reference.reshape(
        element_total, predicted_span
    ).astype(F32)
    all_rows = jnp.arange(lat_total).astype(F32)
    cosine_mean = jnp.mean(jnp.cos(math.pi * ((all_rows + 0.5) / lat_total - 0.5)))
    initial_rows = ((rows_here + half_side) % lat_total).astype(F32)
    lat_here = jnp.cos(math.pi * ((initial_rows + 0.5) / lat_total - 0.5)) / cosine_mean
    element_factor = jnp.broadcast_to(
        lat_here[None, :, None] * local_valid[None], (levels, tile_side, tile_side)
    ).reshape(element_total, 1)
    variable_factor = jnp.repeat(var_weight, predicted_span // var_weight.shape[0])[None, :]
    shard_penalty = jnp.sum(
        element_factor * variable_factor * prediction_misfit * prediction_misfit
    ) / (levels * lat_total * lon_total * (predicted_span // var_weight.shape[0]))
    prediction_gradient = (2.0 * element_factor * variable_factor * prediction_misfit).astype(BF)
    grad_shard = lax.psum_scatter(
        jnp.einsum(
            "td,to->do", latent_activation, prediction_gradient, preferred_element_type=F32
        ).astype(BF),
        "dp",
        scatter_dimension=0,
        tiled=True,
    ).astype(F32)
    grad_sum, loss_sum = lax.psum((grad_shard, shard_penalty), ("lat", "lon"))
    grad_recovery = grad_sum / (levels * lat_total * lon_total)
    grad_hidden = jnp.einsum(
        "to,do->td", prediction_gradient, unprojected_pieces, preferred_element_type=F32
    )
    scaled_grad = grad_hidden * gain_f
    grad_mixed = inv_spread * (
        scaled_grad
        - jnp.mean(scaled_grad, axis=-1, keepdims=True)
        - normed * jnp.mean(scaled_grad * normed, axis=-1, keepdims=True)
    )
    grad_mixed = grad_mixed.astype(BF)
    grad_context = jnp.einsum("tj,ij->ti", grad_mixed, out_all, preferred_element_type=F32)
    grad_context = grad_context.astype(BF).reshape(1, levels, tile_side, tile_side, model_width)
    return (grad_context, grad_recovery, loss_sum.reshape(1))


def params(mib):
    return pltpu.CompilerParams(vmem_limit_bytes=mib << 20)


def iota(shape, dim):
    return lax.broadcasted_iota(jnp.int32, shape, dim)


def payload_kernel(w_ref, unpatch_ref, gain_ref, payload_ref, ug, sems):
    part = lax.axis_index("lat")
    rows, width = w_ref.shape
    qr = rows // 4
    span = unpatch_ref.shape[0]
    start = pl.multiple_of(part * qr, 32)
    u_copy = pltpu.make_async_copy(unpatch_ref, ug.at[pl.ds(0, span), :], sems.at[0])
    u_copy.start()
    w_copy = pltpu.make_async_copy(
        w_ref.at[pl.ds(start, qr), :], payload_ref.at[pl.ds(0, qr), :], sems.at[1]
    )
    w_copy.start()
    ug[pl.ds(span, 16), :] = gain_rows(gain_ref, rows)
    ug[pl.ds(span + 16, UGROWS - span - 16), :] = jnp.zeros((UGROWS - span - 16, rows), BF)
    u_copy.wait()
    for j in range(4):
        at = pl.multiple_of((4 * part + j) * 16, 16)
        payload_ref[pl.ds(qr, 16), pl.ds(j * rows, rows)] = ug[pl.ds(at, 16), :]
    w_copy.wait()


def gain_rows(gain_ref, rows):
    return jnp.broadcast_to(gain_ref[...].astype(F32).reshape(1, rows), (16, rows)).astype(BF)


def pack_kernel(x_ref, t_ref, valid_ref, *refs):
    outs, (x_in, t_in, v_in, sems) = refs[:4], refs[4:]
    span = t_ref.shape[-1]
    count = x_ref.shape[0] * 64
    quarter = count // 4
    step = 512
    width = x_ref.shape[-1]
    copies = [
        pltpu.make_async_copy(t_ref, t_in, sems.at[0]),
        pltpu.make_async_copy(valid_ref, v_in, sems.at[1]),
    ]
    for at in range(0, width, step):
        lanes = (slice(None),) * 3 + (pl.ds(at, step),)
        copies.append(
            pltpu.make_async_copy(x_ref.at[lanes], x_in.at[lanes], sems.at[len(copies)])
        )
    for c in copies:
        c.start()
    place = iota((count, count), 0)
    quad, rest = place // quarter, place % quarter
    row = (rest // 4) % 4 + jnp.where(quad < 2, 4, 0)
    col = rest % 4 + jnp.where(quad % 2 == 0, 4, 0)
    source = (rest // 16) * 64 + row * 8 + col
    pick = (iota((count, count), 1) == source).astype(F32).astype(BF)
    copies[0].wait()
    copies[1].wait()
    goal = jnp.dot(pick, t_in[...].reshape(count, span), preferred_element_type=F32)
    token = iota((count, 8), 0)
    row_hot = ((token // 8) % 8 == iota((count, 8), 1)).astype(F32)
    by_row = jnp.dot(row_hot, v_in[...].astype(F32), preferred_element_type=F32)
    mine = token % 8 == iota((count, 8), 1)
    natural = jnp.sum(jnp.where(mine, by_row, 0.0), axis=1, keepdims=True)
    spread = jnp.broadcast_to(natural, (count, 128)).astype(BF)
    column = jnp.dot(pick, spread, preferred_element_type=F32)
    extra = jnp.concatenate([goal, column[:, : EXTRA - span]], axis=1).astype(BF)
    starts = [sum(o.shape[0] for o in outs[:n]) for n in range(4)]
    outs = list(zip(outs, starts))
    for ref, row in outs:
        ref[:, width:] = extra[row : row + ref.shape[0]]
    for n, at in enumerate(range(0, width, step)):
        copies[2 + n].wait()
        tokens = x_in[:, :, :, at : at + step].reshape(count, step)
        out = jnp.dot(pick, tokens, preferred_element_type=F32).astype(BF)
        for ref, row in outs:
            ref[:, at : at + step] = out[row : row + ref.shape[0]]


def windows_of(*tiles):
    return [[t.at[32 * w : 32 * w + 32] for t in tiles] for w in range(2)]


def attention_kernel(*refs):
    tiles, ctx_ref = windows_of(*refs[:4]), refs[4]
    part = ctx_ref.shape[1]
    is_last = lax.axis_index("lat") == lax.axis_size("lat") - 1
    same = (iota((512, 128), 0) % 128) // 64 == iota((512, 128), 1) // 64
    bias = jnp.where(jnp.logical_or(same, jnp.logical_not(is_last)), 0.0, -1e30)
    head = iota((128, 128), 1) // HDIM
    factor = math.log2(math.e) / math.sqrt(HDIM)
    for at in range(0, part, 128):
        for w in range(2):
            q, k, v = [
                jnp.concatenate(
                    [t[:, i * part + at : i * part + at + 128] for t in tiles[w]],
                    axis=0,
                )
                for i in range(3)
            ]
            zero = jnp.zeros_like(k)
            k4 = jnp.concatenate([jnp.where(head == h, k, zero) for h in range(4)], axis=0)
            v4 = jnp.concatenate([jnp.where(head == h, v, zero) for h in range(4)], axis=0)
            s = lax.dot_general(k4, q, (((1,), (1,)), ((), ())), preferred_element_type=F32)
            s = s + bias
            parts = []
            for h in range(4):
                sh = s[128 * h : 128 * h + 128]
                e = jnp.exp2((sh - jnp.max(sh, axis=0, keepdims=True)) * factor)
                parts.append((e * (1.0 / jnp.sum(e, axis=0, keepdims=True))).astype(BF))
            attn = jnp.concatenate(parts, axis=0)
            out = lax.dot_general(attn, v4, (((0,), (0,)), ((), ())), preferred_element_type=F32)
            ctx_ref[128 * w : 128 * w + 128, at : at + 128] = out.astype(BF)


def assemble(own_w, own_u, own_gain, pieces, w_all, ug_all):
    zi, part = lax.axis_index("dp"), lax.axis_index("lat")
    rows = own_w.shape[0]
    qr = rows // 4
    steps = len(pieces) // 4 + 1
    base = pl.multiple_of(zi * rows, 128)
    w_all[pl.ds(base, rows), :] = own_w[...]
    span = own_u.shape[0]
    ug_all[0:span, pl.ds(base, rows)] = own_u[...]
    ug_all[span : span + 16, pl.ds(base, rows)] = gain_rows(own_gain, rows)
    for k in range(1, steps):
        shard = lax.rem(zi - k + steps, steps)
        base = pl.multiple_of(shard * rows, 128)
        for bits, piece in zip((0, 2, 1, 3), pieces[4 * k - 4 : 4 * k]):
            from_part = part ^ bits
            row = pl.multiple_of(base + from_part * qr, 32)
            w_all[pl.ds(row, qr), :] = piece[0:qr, :]
            for j in range(4):
                urow = pl.multiple_of((4 * from_part + j) * 16, 16)
                ug_all[pl.ds(urow, 16), pl.ds(base, rows)] = piece[
                    qr : qr + 16, j * rows : (j + 1) * rows
                ]


def split3(x):
    hi = x.astype(BF).astype(F32)
    mid = (x - hi).astype(BF).astype(F32)
    return hi, mid, x - hi - mid


def loss_block(value, rows):
    hi, mid, lo = split3(value)
    lane = iota((rows, 128), 1)
    return jnp.where(lane == 0, hi, jnp.where(lane == 1, mid, jnp.where(lane == 2, lo, 0.0)))


def forward_kernel(lat_ref, var_ref, *refs):
    ctx_ref, refs = refs[0], refs[1:]
    extras, refs = refs[:4], refs[4:]
    owned, refs = refs[:3], refs[3:]
    pieces, refs = refs[:PIECES], refs[PIECES:]
    ts, refs = refs[:4], refs[4:]
    normed_ref, inv_ref, dfc_ref, loss_ref, hidden_ref, w_all, ug_all, term = refs
    lat_place = lax.axis_index("lat")
    assemble(*owned, pieces, w_all, ug_all)
    tokens, width = normed_ref.shape
    span = dfc_ref.shape[1]
    extra = jnp.concatenate([t[...] for tiles in windows_of(*extras) for t in tiles], axis=0)
    extra = extra.astype(F32)
    goal, valid = extra[:, :span], extra[:, span : span + 1]
    token = iota((tokens, 1), 0)
    row = (token // 4) % 4 + jnp.where((token // 32) % 4 >= 2, 4, 0)
    lat_w = jnp.zeros((tokens, 1), F32)
    for r in range(8):
        lat_w = jnp.where(row == r, lat_ref[lat_place * 8 + r], lat_w)
    lane = iota((1, span), 1) // (span // var_ref.shape[0])
    var_w = jnp.zeros((1, span), F32)
    for n in range(var_ref.shape[0]):
        var_w = jnp.where(lane == n, var_ref[n], var_w)
    weight = lat_w * valid * var_w
    mixed = jnp.dot(ctx_ref[...], w_all[...], preferred_element_type=F32)
    centre = jnp.mean(mixed, axis=-1, keepdims=True)
    off = mixed - centre
    inv = lax.rsqrt(jnp.mean(off * off, axis=-1, keepdims=True) + 1e-05)
    normed = off * inv
    normed_ref[...] = normed
    inv_ref[...] = jnp.broadcast_to(inv, inv_ref.shape)
    gain = ug_all[pl.ds(span, 16), :][0:1].astype(F32)
    hidden_ref[...] = (normed * gain).astype(BF)
    field = lax.dot_general(
        hidden_ref[...], ug_all[0:span, :], (((1,), (1,)), ((), ())), preferred_element_type=F32
    )
    misfit = field - goal
    dfc = (2.0 * weight * misfit).astype(BF)
    dfc_ref[...] = dfc
    term[...] = lax.dot_general(
        dfc, hidden_ref[...], (((0,), (0,)), ((), ())), preferred_element_type=F32
    )
    loss = jnp.sum(jnp.sum(weight * misfit * misfit, axis=1, keepdims=True), axis=0, keepdims=True)
    loss_ref[...] = jnp.broadcast_to(loss, loss_ref.shape)
    rows = ts[0].shape[0]
    for b, ref in enumerate(ts):
        at = pl.multiple_of((lat_place ^ b) * rows, 8)
        ref[...] = term[pl.ds(at, rows), :].astype(BF)


def backward_kernel(normed_ref, inv_ref, dfc_ref, *refs):
    owned, refs = refs[:3], refs[3:]
    pieces, (out_ref, w_all, ug_all) = refs[:PIECES], refs[PIECES:]
    assemble(*owned, pieces, w_all, ug_all)
    tokens, width = normed_ref.shape
    span = dfc_ref.shape[1]
    gain = ug_all[pl.ds(span, 16), :][0:1].astype(F32)
    g = jnp.dot(dfc_ref[...], ug_all[0:span, :], preferred_element_type=F32) * gain
    normed = normed_ref[...]
    mean_g = jnp.mean(g, axis=-1, keepdims=True)
    mean_gn = jnp.mean(g * normed, axis=-1, keepdims=True)
    dmixed = ((g - mean_g - normed * mean_gn) * inv_ref[:, 0:1]).astype(BF)
    place = iota((tokens, tokens), 0)
    row, col, level = (place // 8) % 8, place % 8, place // 64
    quad = jnp.where(row >= 4, 2, 0) + jnp.where(col >= 4, 1, 0)
    source = (level // 2) * 128 + quad * 32 + (level % 2) * 16 + (row % 4) * 4 + col % 4
    pick = (iota((tokens, tokens), 1) == source).astype(F32).astype(BF)
    dnat = jnp.dot(pick, dmixed, preferred_element_type=F32).astype(BF)
    out = lax.dot_general(dnat, w_all[...], (((1,), (1,)), ((), ())), preferred_element_type=F32)
    out_ref[...] = out.astype(BF)


def add4(a, b, c, d):
    return (a[...].astype(F32) + b[...].astype(F32)) + (c[...].astype(F32) + d[...].astype(F32))


def lat_sum_kernel(a, b, c, d, z0, z1, z2, z3, total_ref):
    total_ref[...] = add4(a, b, c, d)
    zi = lax.axis_index("dp")
    width = z0.shape[1]
    for k, ref in enumerate((z0, z1, z2, z3)):
        at = pl.multiple_of((zi ^ k) * width, 128)
        ref[...] = total_ref[:, pl.ds(at, width)].astype(BF)


def dp_sum_kernel(loss_ref, a, b, c, d, o_ref):
    rows, width = a.shape
    o_ref[0:rows, :] = add4(a, b, c, d).astype(BF)
    block = loss_block(loss_ref[0:1, 0:1], o_ref.shape[0] - rows)
    zeros = jnp.zeros((block.shape[0], width - 128), F32)
    o_ref[rows:, :] = jnp.concatenate([block, zeros], axis=1).astype(BF)


def pair_kernel(mine_ref, other_ref, o_ref):
    rows = mine_ref.shape[0]
    odd = lax.axis_index("lat") % 2
    o_ref[pl.ds(pl.multiple_of(odd * rows, 8), rows), :] = mine_ref[...]
    o_ref[pl.ds(pl.multiple_of((1 - odd) * rows, 8), rows), :] = other_ref[...]


def join_kernel(counts, *refs):
    pieces, (o_ref, loss_ref) = refs[:4], refs[4:]
    chip = lax.axis_index("lat") // 2
    held = pieces[0].shape[0] // 2
    rows = held - 8
    for a in range(2):
        for n in range(2):
            at = pl.multiple_of((2 * (chip ^ a) + n) * rows, 8)
            both = [pieces[2 * a + b][held * n : held * n + rows, :].astype(F32) for b in range(2)]
            o_ref[pl.ds(at, rows), :] = (both[0] + both[1]) / counts[0]
    def part(p, n):
        return jnp.sum(p[held * n + rows : held * n + rows + 1, 0:128].astype(F32), axis=1, keepdims=True)

    chips = [part(p, 0) + part(p, 1) for p in pieces]
    loss = (chips[0] + chips[1]) + (chips[2] + chips[3])
    loss_ref[...] = jnp.broadcast_to(loss / counts[1], loss_ref.shape)


def swap(array, axis, bit):
    return lax.ppermute(array, axis, [(i, i ^ bit) for i in range(lax.axis_size(axis))])


def shape(dims, dtype):
    return jax.ShapeDtypeStruct(dims, dtype)


def shards(projected, targets, valid_cells, w_out, unpatch_matrix, norm_gain, var_weight):
    dp, lat, lon = lax.axis_size("dp"), lax.axis_size("lat"), lax.axis_size("lon")
    rows, width = w_out.shape
    levels = projected.shape[1]
    span = unpatch_matrix.shape[1]
    tokens = levels * 64
    lat_total = 8 * lat
    angle = math.pi * ((np.arange(lat_total) + 0.5) / lat_total - 0.5)
    cosine = np.cos(angle)
    lat_table = jnp.asarray(np.roll(cosine / cosine.mean(), -4), F32)
    barrier = lax.optimization_barrier

    unpatch_t = unpatch_matrix.T
    payload = pl.pallas_call(
        payload_kernel,
        out_shape=shape((rows // 4 + 16, width), BF),
        in_specs=[HBM, HBM, VMEM],
        out_specs=VMEM,
        scratch_shapes=[pltpu.VMEM((UGROWS, rows), BF), pltpu.SemaphoreType.DMA((2,))],
        compiler_params=params(60),
        name="payload",
    )(w_out, unpatch_t, norm_gain)
    ring1 = from_behind(payload, "dp", 1)
    own, *send = pl.pallas_call(
        pack_kernel,
        out_shape=[shape((n, 3 * width + EXTRA), BF) for n in (64, 64, 64, 64)],
        in_specs=[HBM] * 3,
        out_specs=[VMEM] * 4,
        scratch_shapes=[
            pltpu.VMEM((levels, 8, 8, 3 * width), BF),
            pltpu.VMEM((levels, 8, 8, span), BF),
            pltpu.VMEM((8, 8), jnp.int32),
            pltpu.SemaphoreType.DMA((2 + 3 * width // 512,)),
        ],
        compiler_params=params(50),
        name="pack",
    )(
        projected.reshape(levels, 8, 8, 3 * width),
        targets.reshape(levels, 8, 8, span),
        valid_cells,
    )
    corner = [
        (a * lon + b, ((a - 1) % lat) * lon + (b - 1) % lon) for a in range(lat) for b in range(lon)
    ]
    south = from_behind(send[1], "lat", -1)
    diag = lax.ppermute(send[2], ("lat", "lon"), corner)
    ring2 = from_behind(ring1, "dp", 1)
    across2 = swap(ring2, "lat", 2)
    ring2_after, east, south, diag = barrier((ring2, send[0], south, diag))
    ring3 = from_behind(ring2_after, "dp", 1)
    east = from_behind(east, "lon", -1)
    across3 = from_behind(across2, "dp", 1)
    ring1_late, across2 = barrier((ring1, across2))
    across1 = swap(ring1_late, "lat", 2)
    tiles = [own, east, south, diag]
    *tiles, ring1, across1, ring2 = barrier((*tiles, ring1, across1, ring2))
    ctx = pl.pallas_call(
        attention_kernel,
        out_shape=shape((tokens, width), BF),
        in_specs=[VMEM] * 4,
        out_specs=VMEM,
        compiler_params=params(16),
        name="attention",
    )(*tiles)
    ctx, across3 = barrier((ctx, across3))
    pieces = []
    for ring, across in ((ring1, across1), (ring2, across2), (ring3, across3)):
        pieces += [ring, across, swap(ring, "lat", 1), swap(across, "lat", 1)]

    piece = span // lat
    extra_specs = [
        pl.BlockSpec((t.shape[0], EXTRA), lambda i: (0, 3 * width // EXTRA)) for t in tiles
    ]
    assembly = [
        pltpu.VMEM((dp * rows, width), BF),
        pltpu.VMEM((UGROWS, dp * rows), BF),
    ]
    *terms, normed, inv, dfc, loss = pl.pallas_call(
        forward_kernel,
        grid=(1,),
        out_shape=[shape((piece, width), BF)] * 4
        + [shape((tokens, width), F32), shape((tokens, 128), F32), shape((tokens, span), BF)]
        + [shape((8, 128), F32)],
        in_specs=[SMEM] * 2 + [VMEM] + extra_specs + [VMEM] * (3 + PIECES),
        out_specs=[VMEM] * 8,
        scratch_shapes=[pltpu.VMEM((tokens, width), BF)]
        + assembly
        + [pltpu.VMEM((span, width), F32)],
        compiler_params=params(28),
        name="forward",
    )(lat_table, var_weight, ctx, *tiles, w_out, unpatch_t, norm_gain, *pieces)

    terms = [terms[0]] + [swap(terms[b], "lat", b) for b in (3, 2, 1)]
    grad_context = pl.pallas_call(
        backward_kernel,
        out_shape=shape((tokens, width), BF),
        in_specs=[VMEM] * (6 + PIECES),
        out_specs=VMEM,
        scratch_shapes=assembly,
        compiler_params=params(24),
        name="backward",
    )(normed, inv, dfc, w_out, unpatch_t, norm_gain, *pieces)
    *terms, grad_context = barrier((*terms, grad_context))

    parts = pl.pallas_call(
        lat_sum_kernel,
        out_shape=[shape((piece, rows), BF)] * 4,
        in_specs=[VMEM] * 4,
        out_specs=[VMEM] * 4,
        scratch_shapes=[pltpu.VMEM((piece, width), F32)],
        compiler_params=params(4),
        name="lat_sum",
    )(*terms)
    parts = [parts[0]] + [swap(parts[k], "dp", k) for k in (3, 2, 1)]
    mine = pl.pallas_call(
        dp_sum_kernel,
        out_shape=shape((piece + 8, rows), BF),
        in_specs=[VMEM] * 5,
        out_specs=VMEM,
        compiler_params=params(4),
        name="dp_sum",
    )(loss, *parts)
    chip = pl.pallas_call(
        pair_kernel,
        out_shape=shape((2 * piece + 16, rows), BF),
        in_specs=[VMEM] * 2,
        out_specs=VMEM,
        compiler_params=params(4),
        name="pair",
    )(mine, swap(mine, "lat", 1))
    plane = [chip]
    for a, b in ((0, 1), (2, 0), (2, 1)):
        pairs = [(i * lon + j, (i ^ a) * lon + (j ^ b)) for i in range(lat) for j in range(lon)]
        plane.append(lax.ppermute(chip, ("lat", "lon"), pairs))
    count = levels * lat_total * 8 * lon
    counts = (float(count), float(count * (span // var_weight.shape[0])))
    joined, loss = pl.pallas_call(
        lambda *refs: join_kernel(counts, *refs),
        out_shape=[shape((span, rows), F32), shape((1, 1), F32)],
        in_specs=[VMEM] * 4,
        out_specs=[VMEM] * 2,
        compiler_params=params(4),
        name="join",
    )(*plane)
    return grad_context.reshape(1, levels, 8, 8, width), joined.T, loss.reshape(1)


def solution(mesh):
    placed = (
        P("dp", None, "lat", "lon", None),
        P("dp", None, "lat", "lon", None),
        P("lat", "lon"),
        P("dp", None),
        P("dp", None),
        P("dp"),
        P(),
    )
    fits = mesh.shape["dp"] == 4 and mesh.shape["lat"] == 4 and mesh.shape["lon"] == 2

    def program(*arrays):
        body = shards if fits else general_shards
        return jax.shard_map(
            body,
            mesh=mesh,
            in_specs=placed,
            out_specs=(P("dp", None, "lat", "lon", None), P("dp", None), P("dp")),
            check_vma=False,
        )(*arrays)

    return program
```
